32 devices in a mesh: dp: 4 (over z), seq: 4 (over x, core), tensor: 2 (over y).
Axes of the slice: x: 2, y: 2, z: 4, core: 2. Of those that a mesh axis runs over, the one named last changes fastest.
Arguments:
- tokens: bfloat16 [8, 2048, 1024], P('dp', ('seq', 'tensor')), may hold values from -6 to 6
- cotangent: bfloat16 [8, 2048, 1024], P('dp', ('seq', 'tensor')), may hold values from -6 to 6
- species: int32 [8], P('dp'), may hold values from 0 to 849
- counts: int32 [8], P('dp'), may hold values from 0 to 2048, as said below
- species_scale: float32 [850], replicated, may hold values from 0.5 to 2
- norm1_gain: float32 [1024], P(('dp', 'seq', 'tensor')), may hold values from 0.5 to 1.5
- norm1_bias: float32 [1024], P(('dp', 'seq', 'tensor')), may hold values from -2.5 to 2.5
- w_query: bfloat16 [1024, 1024], P(('dp', 'seq'), 'tensor'), may hold values from -0.1875 to 0.1875
- w_key: bfloat16 [1024, 1024], P(('dp', 'seq'), 'tensor'), may hold values from -0.1875 to 0.1875
- w_value: bfloat16 [1024, 1024], P(('dp', 'seq'), 'tensor'), may hold values from -0.1875 to 0.1875
- w_out: bfloat16 [1024, 1024], P('tensor', ('dp', 'seq')), may hold values from -6 to 6
- norm2_gain: float32 [1024], P(('dp', 'seq', 'tensor')), may hold values from 0.5 to 1.5
- norm2_bias: float32 [1024], P(('dp', 'seq', 'tensor')), may hold values from -2.5 to 2.5
- w_gate: bfloat16 [1024, 4096], P(('dp', 'seq'), 'tensor'), may hold values from -0.1875 to 0.1875
- w_up: bfloat16 [1024, 4096], P(('dp', 'seq'), 'tensor'), may hold values from -0.1875 to 0.1875
- w_down: bfloat16 [4096, 1024], P('tensor', ('dp', 'seq')), may hold values from -0.09375 to 0.09375
Outputs:
- output: bfloat16 [8, 2048, 1024], P('dp', ('seq', 'tensor'))
- input_grad: float32 [8, 2048, 1024], P('dp', ('seq', 'tensor'))
- grad_norm1_gain: float32 [1024], P(('dp', 'seq', 'tensor'))
- grad_norm1_bias: float32 [1024], P(('dp', 'seq', 'tensor'))
- grad_query: float32 [1024, 1024], P(('dp', 'seq'), 'tensor')
- grad_key: float32 [1024, 1024], P(('dp', 'seq'), 'tensor')
- grad_value: float32 [1024, 1024], P(('dp', 'seq'), 'tensor')
- grad_out: float32 [1024, 1024], P('tensor', ('dp', 'seq'))
- grad_norm2_gain: float32 [1024], P(('dp', 'seq', 'tensor'))
- grad_norm2_bias: float32 [1024], P(('dp', 'seq', 'tensor'))
- grad_gate: float32 [1024, 4096], P(('dp', 'seq'), 'tensor')
- grad_up: float32 [1024, 4096], P(('dp', 'seq'), 'tensor')
- grad_down: float32 [4096, 1024], P('tensor', ('dp', 'seq'))
The draws below stay inside these ranges and needn't reach their ends.
Inputs may be any that keep to these rules, and one draw needn't show every extreme that they name: `counts`: A slot of count 0 is padding. Within the 2 slots of one index of dp the live slots come first, and there is at least one.
All inputs are finite; a program needn't handle non-finite values.
Results may differ from the reference program's by a relative error of at most 0.019.
Values may be sent and summed in bfloat16 or wider, within the bound.
A program may use at most 320 MiB of HBM per device.

```python
import math
import jax
import jax.numpy as jnp
from jax import lax

D = 1024
HEADS = 16
HEAD_DIM = 64
FF = 4096
WINDOW = 2048
WIN = 2
SPECIES = 850
WINDOWS = 8


def draw_counts(key, part):
    live_key, full_key, base_key = jax.random.split(key, 3)
    group_total = WINDOWS // WIN
    group_index = jnp.arange(WINDOWS, dtype=jnp.int32) // WIN
    slot_index = jnp.arange(WINDOWS, dtype=jnp.int32) % WIN
    groups = jnp.arange(group_total, dtype=jnp.int32)
    live_count = jax.random.randint(live_key, (group_total,), 1, WIN + 1)
    full_group = jax.random.randint(full_key, (), 0, group_total)
    live_count = jnp.where(groups == full_group, WIN, live_count)
    live_count = jnp.where(groups == (full_group + 1) % group_total, 1, live_count)
    base_count = jax.random.randint(base_key, (WINDOWS,), 64, 513)
    base_count = jnp.where(slot_index == 0, 512, base_count)
    is_live = slot_index < live_count[group_index]
    return jnp.where(is_live, base_count * (group_index + 1), 0).astype(jnp.int32)


def touch_ends(array, rng, least, largest):
    shape = array.shape
    spot = [jax.random.randint(jax.random.fold_in(rng, axis), (), 0, shape[axis]) for axis in range(len(shape))]
    array = array.at[tuple(spot)].set(least)
    longest = shape.index(max(shape))
    spot[longest] = (spot[longest] + 1) % shape[longest]
    return array.at[tuple(spot)].set(largest)


def steps_of(own_key, dims, shards, smallest, top_value):
    factor_of = 1.0
    for axis_at, parts in shards:
        heights = jax.random.uniform(jax.random.fold_in(jax.random.fold_in(own_key, 6), axis_at), (parts,), jnp.float32, smallest / len(shards), top_value / len(shards))
        factor_of = factor_of * jnp.repeat(jnp.exp(heights), dims[axis_at] // parts).reshape((-1,) + (1,) * (len(dims) - 1 - axis_at))
    return factor_of


def normal_values(key, extent, deviation, limit, cuts=(), held_as=jnp.bfloat16):
    values = jax.random.normal(key, extent, jnp.float32) * deviation
    if len(cuts) > 0:
        values = steps_of(key, extent, cuts, -0.22, 0.18) * values
    return jnp.clip(values, min=-limit, max=limit).astype(held_as)


def setup_inputs(seed: int = 0) -> dict:
    seeds = jax.random.split(jax.random.key(seed), 17)
    tokens = normal_values(seeds[0], (WINDOWS, WINDOW, D), 1.0, 6.0, ((0, 4), (1, 8)))
    cotangent = normal_values(seeds[1], (WINDOWS, WINDOW, D), 1.0, 6.0, ((0, 4), (1, 8)))
    species = touch_ends(jax.random.randint(seeds[2], (WINDOWS,), 0, SPECIES), jax.random.fold_in(seeds[2], 1), 0, SPECIES - 1).astype(jnp.int32)
    counts = draw_counts(jax.random.fold_in(seeds[16], 71), 0)
    species_scale = jnp.clip(jnp.exp(jax.random.uniform(seeds[4], (SPECIES,), jnp.float32, math.log(0.5), math.log(2.0))), 0.5, 2.0)
    norm1_gain = jnp.clip(1.0 + 0.1 * jax.random.normal(seeds[5], (D,), jnp.float32), 0.5, 1.5)
    norm1_bias = normal_values(seeds[6], (D,), 0.3, 2.5, ((0, 32),), jnp.float32)
    w_query = normal_values(seeds[7], (D, D), D ** -0.5, 0.1875, ((0, 16), (1, 2)))
    w_key = normal_values(seeds[8], (D, D), D ** -0.5, 0.1875, ((0, 16), (1, 2)))
    w_value = normal_values(seeds[9], (D, D), D ** -0.5, 0.1875, ((0, 16), (1, 2)))
    w_out = normal_values(seeds[10], (D, D), (max(1, D // WINDOW)) ** -0.5, 6.0, ((0, 2), (1, 16)))
    norm2_gain = jnp.clip(1.0 + 0.1 * jax.random.normal(seeds[11], (D,), jnp.float32), 0.5, 1.5)
    norm2_bias = normal_values(seeds[12], (D,), 0.3, 2.5, ((0, 32),), jnp.float32)
    w_gate = normal_values(seeds[13], (D, FF), D ** -0.5, 0.1875, ((0, 16), (1, 2)))
    w_up = normal_values(seeds[14], (D, FF), D ** -0.5, 0.1875, ((0, 16), (1, 2)))
    w_down = normal_values(seeds[15], (FF, D), FF ** -0.5, 0.09375, ((0, 2), (1, 16)))
    return {"tokens": tokens, "cotangent": cotangent, "species": species, "counts": counts, "species_scale": species_scale, "norm1_gain": norm1_gain, "norm1_bias": norm1_bias, "w_query": w_query, "w_key": w_key, "w_value": w_value, "w_out": w_out, "norm2_gain": norm2_gain, "norm2_bias": norm2_bias, "w_gate": w_gate, "w_up": w_up, "w_down": w_down}


@jax.custom_vjp
def low(v):
    return lax.optimization_barrier(v.astype(jnp.bfloat16)).astype(jnp.float32)

@jax.custom_vjp
def low_back(v):
    return v

def low_keep(v):
    return (low(v), None)

def low_pass(kept, grad):
    return (grad,)

def back_keep(v):
    return (v, None)

def back_low(kept, grad):
    return (low(grad),)
low.defvjp(low_keep, low_pass)
low_back.defvjp(back_keep, back_low)
EPSILON = 1e-05
ROPE_BASE = 10000.0

def rotate(matrix, cosine_table, sine_table):
    row_count, head_cols = matrix.shape
    half_dim = cosine_table.shape[1]
    halves = matrix.reshape(row_count, head_cols // (2 * half_dim), 2, half_dim)
    first_half = halves[:, :, 0, :]
    second_half = halves[:, :, 1, :]
    cos_wide = cosine_table[:, None, :]
    sin_wide = sine_table[:, None, :]
    turned = jnp.stack([first_half * cos_wide - second_half * sin_wide, second_half * cos_wide + first_half * sin_wide], axis=2)
    return turned.reshape(row_count, head_cols)

def angles(positions, head_dim):
    half_dim = head_dim // 2
    inverse = jnp.exp(-(math.log(ROPE_BASE) * 2.0 / head_dim) * jnp.arange(half_dim, dtype=jnp.float32))
    phase_angle = positions[:, None] * inverse[None, :]
    return (jnp.cos(phase_angle), jnp.sin(phase_angle))

def layer_norm(stream, norm_gain, norm_bias):
    row_mean = lax.optimization_barrier(jnp.mean(stream, axis=-1, keepdims=True))
    centred = stream - row_mean
    variance = lax.optimization_barrier(jnp.mean(centred * centred, axis=-1, keepdims=True))
    inv_std = lax.rsqrt(variance + EPSILON)
    normed = centred * inv_std
    return (normed, inv_std, normed * norm_gain + norm_bias)

def product(left_matrix, right_matrix):
    return jnp.dot(left_matrix, right_matrix, precision=lax.Precision.HIGHEST)

def window_layer(stream, norm1_gain, norm1_bias, w_query, w_key, w_value, w_out, norm2_gain, norm2_bias, w_gate, w_up, w_down):
    cosine_table, sine_table = angles(jnp.arange(WINDOW, dtype=jnp.float32), HEAD_DIM)
    normed_in = low(layer_norm(stream, norm1_gain, norm1_bias)[2])
    queries = low(rotate(low_back(product(normed_in, w_query)), cosine_table, sine_table))
    keys_all = low(rotate(low_back(product(normed_in, w_key)), cosine_table, sine_table))
    values_all = low(low_back(product(normed_in, w_value)))
    score_scale = 1.0 / math.sqrt(HEAD_DIM)

    def one_head(head_parts):
        head_query, head_keys, head_values = head_parts
        scores = low_back(product(head_query, head_keys.T) * score_scale)
        return product(low(jax.nn.softmax(scores, axis=-1)), head_values)

    def by_head(matrix):
        return matrix.reshape(WINDOW, HEADS, HEAD_DIM).transpose(1, 0, 2)
    mixed = lax.map(jax.checkpoint(one_head), (by_head(queries), by_head(keys_all), by_head(values_all)))
    attended = low(low_back(mixed.transpose(1, 0, 2).reshape(WINDOW, D)))
    middle = stream + low_back(product(attended, w_out))
    normed_mid = low(layer_norm(middle, norm2_gain, norm2_bias)[2])
    gate_values = low_back(product(normed_mid, w_gate))
    up_values = low_back(product(normed_mid, w_up))
    hidden = low(jax.nn.silu(gate_values) * up_values)
    return middle + low_back(product(hidden, w_down))

def whole_layer(tokens_all, norm1_gain, norm1_bias, w_query, w_key, w_value, w_out, norm2_gain, norm2_bias, w_gate, w_up, w_down):
    window_fn = jax.checkpoint(window_layer)

    def window_step(state_carry, stream):
        return (state_carry, window_fn(stream, norm1_gain, norm1_bias, w_query, w_key, w_value, w_out, norm2_gain, norm2_bias, w_gate, w_up, w_down))
    _, results = lax.scan(window_step, None, tokens_all)
    return results

def reference(tokens, cotangent, species, counts, species_scale, norm1_gain, norm1_bias, w_query, w_key, w_value, w_out, norm2_gain, norm2_bias, w_gate, w_up, w_down):
    chosen = species_scale[species]
    weighted = counts.astype(jnp.float32) * chosen
    factor = weighted * float(WINDOWS) / jnp.sum(weighted)
    floats = (tokens.astype(jnp.float32), norm1_gain.astype(jnp.float32), norm1_bias.astype(jnp.float32), w_query.astype(jnp.float32), w_key.astype(jnp.float32), w_value.astype(jnp.float32), w_out.astype(jnp.float32), norm2_gain.astype(jnp.float32), norm2_bias.astype(jnp.float32), w_gate.astype(jnp.float32), w_up.astype(jnp.float32), w_down.astype(jnp.float32))
    results, pullback = jax.vjp(whole_layer, *floats)
    grads = pullback(cotangent.astype(jnp.float32) * factor[:, None, None])
    return (results.astype(jnp.bfloat16), grads[0], grads[1], grads[2], grads[3], grads[4], grads[5], grads[6], grads[7], grads[8], grads[9], grads[10], grads[11])
```

```python
import functools
import math

import jax
import jax.numpy as jnp
from jax import lax
from jax.experimental import pallas as pl
from jax.experimental.pallas import tpu as pltpu
from jax.sharding import PartitionSpec as P

HEAD_DIM = 64
EPSILON = 1e-05
ROPE_BASE = 10000.0
PAIR = 2 * HEAD_DIM
LOG2E = math.log2(math.e)
BF16 = jnp.bfloat16
F32 = jnp.float32
VMEM_BYTES = 56 * 1024 * 1024


def angles(positions, head_dim):
    half_dim = head_dim // 2
    inverse = jnp.exp(
        -(math.log(ROPE_BASE) * 2.0 / head_dim) * jnp.arange(half_dim, dtype=F32)
    )
    phase_angle = positions[:, None] * inverse[None, :]
    return (jnp.cos(phase_angle), jnp.sin(phase_angle))


def layer_norm(stream, norm_gain, norm_bias):
    row_mean = jnp.mean(stream, axis=-1, keepdims=True)
    centred = stream - row_mean
    variance = jnp.mean(centred * centred, axis=-1, keepdims=True)
    inv_std = lax.rsqrt(variance + EPSILON)
    normed = centred * inv_std
    return (normed, inv_std, normed * norm_gain + norm_bias)


def norm_back(grad_normed, normed, inv_std, norm_gain):
    scaled_grad = grad_normed * norm_gain
    return inv_std * (
        scaled_grad
        - jnp.mean(scaled_grad, axis=-1, keepdims=True)
        - normed * jnp.mean(scaled_grad * normed, axis=-1, keepdims=True)
    )


def dot_nn(left, right):
    return lax.dot_general(left, right, (((1,), (0,)), ((), ())), preferred_element_type=F32)


def dot_nt(left, right):
    return lax.dot_general(left, right, (((1,), (1,)), ((), ())), preferred_element_type=F32)


def dot_tn(left, right):
    return lax.dot_general(left, right, (((0,), (0,)), ((), ())), preferred_element_type=F32)


def swap(array, axis, bit):
    size = lax.axis_size(axis)
    return lax.ppermute(array, axis, [(i, i ^ bit) for i in range(size)])


def spread(array, axis):
    blocks = [array]
    bit = 1
    while bit < lax.axis_size(axis):
        blocks = blocks + [swap(block, axis, bit) for block in blocks]
        bit *= 2
    return blocks


def gather_rows(array, axis):
    return jnp.concatenate(spread(array, axis), axis=0)


def scatter_rows(partial, axis):
    bit = lax.axis_size(axis) // 2
    while bit >= 1:
        rows = partial.shape[0] // 2
        arrived = swap(partial[rows:].astype(BF16), axis, bit)
        partial = partial[:rows] + arrived.astype(F32)
        bit //= 2
    return partial


def gather_ordered(array, axes):
    for axis in reversed(axes):
        bit = 1
        while bit < lax.axis_size(axis):
            arrived = swap(array, axis, bit)
            upper = (lax.axis_index(axis) // bit) % 2 == 1
            array = jnp.where(
                upper,
                jnp.concatenate([arrived, array], axis=0),
                jnp.concatenate([array, arrived], axis=0),
            )
            bit *= 2
    return array


def scatter_ordered(array, axes):
    for axis in axes:
        bit = lax.axis_size(axis) // 2
        while bit >= 1:
            rows = array.shape[0] // 2
            upper = (lax.axis_index(axis) // bit) % 2 == 1
            kept = jnp.where(upper, array[rows:], array[:rows])
            sent = jnp.where(upper, array[:rows], array[rows:])
            array = kept + swap(sent, axis, bit)
            bit //= 2
    return array


def first_head(shape):
    return lax.broadcasted_iota(jnp.int32, shape, 1) % PAIR < HEAD_DIM


def swap_halves(values):
    half = HEAD_DIM // 2
    lane = lax.broadcasted_iota(jnp.int32, values.shape, 1)
    ahead = pltpu.roll(values, PAIR - half, 1)
    behind = pltpu.roll(values, half, 1)
    return jnp.where(lane % HEAD_DIM < half, ahead, behind)


def qkv_kernel(x_ref, w_ref, cos_ref, sin_ref, q_ref, kv_ref):
    cols = q_ref.shape[1]
    rows = dot_nn(x_ref[...], w_ref[...])
    cosine = cos_ref[...]
    sine = sin_ref[...]
    for at in range(0, cols, PAIR):
        query = rows[:, at : at + PAIR]
        q_ref[:, at : at + PAIR] = (query * cosine + swap_halves(query) * sine).astype(BF16)
        key = rows[:, cols + at : cols + at + PAIR]
        kv_ref[0, :, at : at + PAIR] = (key * cosine + swap_halves(key) * sine).astype(BF16)
    kv_ref[1] = rows[:, 2 * cols :].astype(BF16)


def project_qkv(x_rows, w_qkv, cosine, sine):
    rows, width = x_rows.shape
    cols = w_qkv.shape[1] // 3
    step = min(256, rows)
    return pl.pallas_call(
        qkv_kernel,
        grid=(rows // step,),
        in_specs=[
            pl.BlockSpec((step, width), lambda i: (i, 0)),
            pl.BlockSpec((width, 3 * cols), lambda i: (0, 0)),
            pl.BlockSpec((step, PAIR), lambda i: (i, 0)),
            pl.BlockSpec((step, PAIR), lambda i: (i, 0)),
        ],
        out_specs=[
            pl.BlockSpec((step, cols), lambda i: (i, 0)),
            pl.BlockSpec((2, step, cols), lambda i: (0, i, 0)),
        ],
        out_shape=[
            jax.ShapeDtypeStruct((rows, cols), BF16),
            jax.ShapeDtypeStruct((2, rows, cols), BF16),
        ],
        compiler_params=pltpu.CompilerParams(vmem_limit_bytes=VMEM_BYTES),
        cost_estimate=pl.CostEstimate(
            flops=2 * rows * width * 3 * cols,
            bytes_accessed=2 * (rows * width + width * 3 * cols + rows * 3 * cols),
            transcendentals=0,
        ),
        name="project_qkv",
    )(x_rows, w_qkv, cosine, sine)


def attend_kernel(slots, last, first, exp_scale, *refs):
    refs = list(refs)
    q_ref = refs.pop(0)
    kv_refs = [refs.pop(0) for _ in range(slots)]
    if not first:
        acc_in, top_in, total_in = refs.pop(0), refs.pop(0), refs.pop(0)
    query = q_ref[...]
    is_first = first_head(query.shape)
    outs, tops = [], []
    for head in range(2):
        mine = is_first if head == 0 else jnp.logical_not(is_first)
        own_query = jnp.where(mine, query, jnp.zeros_like(query))
        scores = [dot_nt(own_query, kv[0]) for kv in kv_refs]
        top = scores[0].max(axis=1, keepdims=True)
        for one in scores[1:]:
            top = jnp.maximum(top, one.max(axis=1, keepdims=True))
        if not first:
            at = head * HEAD_DIM
            top = jnp.maximum(top, top_in[:, at : at + 1])
        shift = top * exp_scale
        mixed = None
        for one, kv in zip(scores, kv_refs):
            weight = jnp.exp2(one * exp_scale - shift).astype(BF16)
            value = kv[1]
            lane_first = first_head(value.shape)
            lane_mine = lane_first if head == 0 else jnp.logical_not(lane_first)
            term = dot_nn(weight, jnp.where(lane_mine, value, jnp.ones_like(value)))
            mixed = term if mixed is None else mixed + term
        outs.append(mixed)
        tops.append(jnp.broadcast_to(top, mixed.shape))
    acc = jnp.where(is_first, outs[0], outs[1])
    total = pltpu.roll(jnp.where(is_first, outs[1], outs[0]), HEAD_DIM, 1)
    top_wide = jnp.where(is_first, tops[0], tops[1])
    if not first:
        fade = jnp.exp2((top_in[...] - top_wide) * exp_scale)
        acc = acc + acc_in[...] * fade
        total = total + total_in[...] * fade
    if last:
        low_ref, wide_ref, log_ref = refs
        attended = acc / total
        low_ref[...] = attended.astype(BF16)
        wide_ref[...] = attended
        log_ref[...] = (top_wide * exp_scale + jnp.log2(total)).T
    else:
        acc_ref, top_ref, total_ref = refs
        acc_ref[...] = acc
        top_ref[...] = top_wide
        total_ref[...] = total


def attend(queries, blocks, carried, last):
    rows, cols = queries.shape
    keys = blocks[0].shape[1]
    slots = len(blocks)
    first = carried is None
    exp_scale = LOG2E / math.sqrt(HEAD_DIM)
    wide = pl.BlockSpec((rows, PAIR), lambda i: (0, i))
    block = pl.BlockSpec((2, keys, PAIR), lambda i: (0, 0, i))
    shape = jax.ShapeDtypeStruct((rows, cols), F32)
    if last:
        out_shape = [jax.ShapeDtypeStruct((rows, cols), BF16), shape, jax.ShapeDtypeStruct((cols, rows), F32)]
        out_specs = [wide, wide, pl.BlockSpec((PAIR, rows), lambda i: (i, 0))]
    else:
        out_shape = [shape] * 3
        out_specs = [wide] * 3
    scored = rows * keys * slots * (cols // HEAD_DIM)
    return pl.pallas_call(
        functools.partial(attend_kernel, slots, last, first, exp_scale),
        grid=(cols // PAIR,),
        in_specs=[wide] + [block] * slots + ([] if first else [wide] * 3),
        out_specs=out_specs,
        out_shape=out_shape,
        compiler_params=pltpu.CompilerParams(vmem_limit_bytes=VMEM_BYTES),
        cost_estimate=pl.CostEstimate(
            flops=scored * HEAD_DIM * 4 * 4,
            bytes_accessed=rows * cols * 20 + slots * keys * cols * 4,
            transcendentals=scored,
        ),
        name="attend",
    )(queries, *blocks, *([] if first else carried))


def attend_back_kernel(slots, last, first, exp_scale, score_scale, *refs):
    refs = list(refs)
    q_ref, do_ref, wide_ref, log_ref = [refs.pop(0) for _ in range(4)]
    kv_refs = [refs.pop(0) for _ in range(slots)]
    if not first:
        dq_in = refs.pop(0)
    if last:
        cos_ref, sin_ref = refs.pop(0), refs.pop(0)
    dq_ref = refs.pop(0)
    dkv_refs = refs
    query = q_ref[...]
    grad_out = do_ref[...]
    is_first = first_head(query.shape)
    overlap = (grad_out.astype(F32) * wide_ref[...]).T
    logs = log_ref[...]
    zero = jnp.zeros_like(query)
    own_q, own_do, row_log, row_sum = [], [], [], []
    for head in range(2):
        mine = is_first if head == 0 else jnp.logical_not(is_first)
        own_q.append(jnp.where(mine, query, zero))
        own_do.append(jnp.where(mine, grad_out, zero))
        at = head * HEAD_DIM
        row_log.append(logs[at : at + 1, :])
        row_sum.append(jnp.sum(overlap[at : at + HEAD_DIM, :], axis=0, keepdims=True))
    dq_parts = [None, None]
    for kv, dkv_ref in zip(kv_refs, dkv_refs):
        key, value = kv[0], kv[1]
        key_turned = key.T
        grad_key, grad_value = None, None
        for head in range(2):
            scores = dot_nt(key, own_q[head])
            probs = jnp.exp2(scores * exp_scale - row_log[head])
            grad_probs = dot_nt(value, own_do[head])
            grad_scores = (probs * (grad_probs - row_sum[head])).astype(BF16)
            term_v = dot_nn(probs.astype(BF16), own_do[head])
            term_k = dot_nn(grad_scores, own_q[head])
            at = head * HEAD_DIM
            term_q = dot_nn(key_turned[at : at + HEAD_DIM, :], grad_scores)
            grad_value = term_v if grad_value is None else grad_value + term_v
            grad_key = term_k if grad_key is None else grad_key + term_k
            dq_parts[head] = term_q if dq_parts[head] is None else dq_parts[head] + term_q
        dkv_ref[0] = (grad_key * score_scale).astype(BF16)
        dkv_ref[1] = grad_value.astype(BF16)
    grad_query = jnp.concatenate(dq_parts, axis=0).T * score_scale
    if not first:
        grad_query = grad_query + dq_in[...]
    if last:
        grad_query = grad_query * cos_ref[...] - swap_halves(grad_query) * sin_ref[...]
    dq_ref[...] = grad_query.astype(dq_ref.dtype)


def attend_back(queries, grad_out, wide, logs, blocks, carried, tables):
    rows, cols = queries.shape
    keys = blocks[0].shape[1]
    slots = len(blocks)
    first = carried is None
    last = tables is not None
    score_scale = 1.0 / math.sqrt(HEAD_DIM)
    row_spec = pl.BlockSpec((rows, PAIR), lambda i: (0, i))
    block = pl.BlockSpec((2, keys, PAIR), lambda i: (0, 0, i))
    table = pl.BlockSpec((rows, PAIR), lambda i: (0, 0))
    scored = rows * keys * slots * (cols // HEAD_DIM)
    return pl.pallas_call(
        functools.partial(
            attend_back_kernel, slots, last, first, score_scale * LOG2E, score_scale
        ),
        grid=(cols // PAIR,),
        in_specs=[row_spec] * 3
        + [pl.BlockSpec((PAIR, rows), lambda i: (i, 0))]
        + [block] * slots
        + ([] if first else [row_spec])
        + ([table] * 2 if last else []),
        out_specs=[row_spec] + [block] * slots,
        out_shape=[jax.ShapeDtypeStruct((rows, cols), BF16 if last else F32)]
        + [jax.ShapeDtypeStruct((2, keys, cols), BF16)] * slots,
        compiler_params=pltpu.CompilerParams(vmem_limit_bytes=VMEM_BYTES),
        cost_estimate=pl.CostEstimate(
            flops=scored * HEAD_DIM * 10 * 4,
            bytes_accessed=rows * cols * 20 + slots * keys * cols * 8,
            transcendentals=scored,
        ),
        name="attend_back",
    )(
        queries,
        grad_out,
        wide,
        logs,
        *blocks,
        *([] if first else [carried]),
        *(tables if last else []),
    )


def turn_back_kernel(dq_ref, own_ref, near_ref, far_ref, cos_ref, sin_ref, out_ref):
    cols = dq_ref.shape[1]
    out_ref[:, :cols] = dq_ref[...]
    cosine, sine = cos_ref[...], sin_ref[...]
    for at in range(0, cols, PAIR):
        part = slice(at, at + PAIR)
        key = (
            own_ref[0, :, part].astype(F32)
            + near_ref[0, :, part].astype(F32)
            + far_ref[0, :, part].astype(F32)
        )
        out_ref[:, cols + at : cols + at + PAIR] = (
            key * cosine - swap_halves(key) * sine
        ).astype(BF16)
    out_ref[:, 2 * cols :] = (
        own_ref[1].astype(F32) + near_ref[1].astype(F32) + far_ref[1].astype(F32)
    ).astype(BF16)


def turn_back(grad_query, own, near, far, cosine, sine):
    rows, cols = grad_query.shape
    step = min(256, rows)
    row_spec = pl.BlockSpec((step, cols), lambda i: (i, 0))
    block = pl.BlockSpec((2, step, cols), lambda i: (0, i, 0))
    table = pl.BlockSpec((step, PAIR), lambda i: (i, 0))
    return pl.pallas_call(
        turn_back_kernel,
        grid=(rows // step,),
        in_specs=[row_spec, block, block, block, table, table],
        out_specs=pl.BlockSpec((step, 3 * cols), lambda i: (i, 0)),
        out_shape=jax.ShapeDtypeStruct((rows, 3 * cols), BF16),
        compiler_params=pltpu.CompilerParams(vmem_limit_bytes=VMEM_BYTES),
        cost_estimate=pl.CostEstimate(
            flops=rows * cols * 10, bytes_accessed=rows * cols * 20, transcendentals=0
        ),
        name="turn_back",
    )(grad_query, own, near, far, cosine, sine)


def local(
    tokens,
    cotangent,
    species,
    counts,
    species_scale,
    norm1_gain,
    norm1_bias,
    w_query,
    w_key,
    w_value,
    w_out,
    norm2_gain,
    norm2_bias,
    w_gate,
    w_up,
    w_down,
):
    windows_here, own_rows, model_width = tokens.shape
    tensor_size = lax.axis_size("tensor")
    seq_size = lax.axis_size("seq")
    block_rows = own_rows * tensor_size
    head_cols = w_query.shape[1]
    hidden_cols = w_gate.shape[1]
    every = ("dp", "seq", "tensor")
    shards = ("dp", "seq")

    w_qkv = lax.all_gather(
        jnp.concatenate([w_query, w_key, w_value], axis=1), shards, axis=0, tiled=True
    )
    w_rest = lax.all_gather(
        jnp.concatenate([w_out.T, w_gate, w_up, w_down.T], axis=1), shards, axis=0, tiled=True
    )
    w_out_t = w_rest[:, :head_cols]
    w_pair = w_rest[:, head_cols : head_cols + 2 * hidden_cols]
    w_down_t = w_rest[:, head_cols + 2 * hidden_cols :]

    norms = gather_ordered(
        jnp.stack([norm1_gain, norm1_bias, norm2_gain, norm2_bias])[None], every
    )
    norms = norms.transpose(1, 0, 2).reshape(4, model_width)
    gain_one, bias_one, gain_two, bias_two = norms[0], norms[1], norms[2], norms[3]

    own_at = lax.axis_index("tensor")
    starts = jnp.concatenate(
        [
            lax.iota(jnp.int32, own_rows) + (own_at ^ other) * own_rows
            for other in range(tensor_size)
        ]
    )
    positions = (lax.axis_index("seq") * block_rows + starts).astype(F32)
    cos_half, sin_half = angles(positions, HEAD_DIM)
    cosine = jnp.concatenate([cos_half] * 4, axis=1)
    sine = jnp.concatenate([-sin_half, sin_half] * 2, axis=1)

    labels = lax.broadcasted_iota(jnp.int32, (windows_here, species_scale.shape[0]), 1)
    chosen = jnp.sum(jnp.where(species[:, None] == labels, species_scale[None, :], 0.0), axis=1)
    weighted = counts.astype(F32) * chosen
    weight_total = jnp.broadcast_to(jnp.sum(weighted), (8, 128))
    bit = 1
    while bit < lax.axis_size("dp"):
        weight_total = weight_total + swap(weight_total, "dp", bit)
        bit *= 2
    factor = weighted * float(windows_here * lax.axis_size("dp")) / weight_total[0, 0]

    windows = range(windows_here)
    streams = [tokens[w].astype(F32) for w in windows]
    grad_ys = [cotangent[w].astype(F32) * factor[w] for w in windows]

    token_rows = [gather_rows(tokens[w], "tensor") for w in windows]
    normed_rows, queries, near_blocks, far_blocks, states = [], [], [], [], []
    top_bit = seq_size // 2
    for w in windows:
        normed_in = layer_norm(token_rows[w].astype(F32), gain_one, bias_one)[2].astype(BF16)
        normed_rows.append(normed_in)
        query, own_kv = project_qkv(normed_in, w_qkv, cosine, sine)
        queries.append(query)
        far_own = swap(own_kv, "seq", top_bit)
        near, far = [own_kv], [far_own]
        bit = 1
        while bit < top_bit:
            near = near + [swap(block, "seq", bit) for block in near]
            far = far + [swap(block, "seq", bit) for block in far]
            bit *= 2
        near_blocks.append(near)
        far_blocks.append(far)
    for w in windows:
        states.append(attend(queries[w], near_blocks[w], None, False))
    grad_y_rows = [gather_rows(grad_ys[w].astype(BF16), "tensor") for w in windows]
    attended, wide_attended, logs, middles = [], [], [], []
    for w in windows:
        low, wide, log_row = attend(queries[w], far_blocks[w], states[w], True)
        attended.append(low)
        wide_attended.append(wide)
        logs.append(log_row)
        middles.append(streams[w] + scatter_rows(dot_nt(low, w_out_t), "tensor"))

    outputs, mid_rows, hiddens, grad_pairs, grad_middles, grad_mid_rows = [], [], [], [], [], []
    gain_two_sum = jnp.zeros((model_width,), F32)
    bias_two_sum = jnp.zeros((model_width,), F32)
    for w in windows:
        normed2, inv_std2, normed_mid = layer_norm(middles[w], gain_two, bias_two)
        gathered_mid = gather_rows(normed_mid.astype(BF16), "tensor")
        gate_up = dot_nn(gathered_mid, w_pair)
        gate_values = gate_up[:, :hidden_cols]
        up_values = gate_up[:, hidden_cols:]
        sigmoid_gate = jax.nn.sigmoid(gate_values)
        swish = gate_values * sigmoid_gate
        hidden = (swish * up_values).astype(BF16)
        grad_hidden = dot_nn(grad_y_rows[w], w_down_t)
        grad_pair = jnp.concatenate(
            [
                grad_hidden * up_values * sigmoid_gate * (1.0 + gate_values * (1.0 - sigmoid_gate)),
                grad_hidden * swish,
            ],
            axis=1,
        ).astype(BF16)
        grad_normed2 = scatter_rows(dot_nt(grad_pair, w_pair), "tensor")
        grad_middle = grad_ys[w] + norm_back(grad_normed2, normed2, inv_std2, gain_two)
        gain_two_sum = gain_two_sum + jnp.sum(grad_normed2 * normed2, axis=0)
        bias_two_sum = bias_two_sum + jnp.sum(grad_normed2, axis=0)
        grad_mid_rows.append(gather_rows(grad_middle.astype(BF16), "tensor"))
        result = middles[w] + scatter_rows(dot_nt(hidden, w_down_t), "tensor")
        outputs.append(result.astype(BF16))
        mid_rows.append(gathered_mid)
        hiddens.append(hidden)
        grad_pairs.append(grad_pair)
        grad_middles.append(grad_middle)

    mid_all = jnp.concatenate(mid_rows, axis=0)
    g_pair = dot_tn(mid_all, jnp.concatenate(grad_pairs, axis=0)).astype(BF16)
    grad_y_all = jnp.concatenate(grad_y_rows, axis=0)
    g_down = dot_tn(grad_y_all, jnp.concatenate(hiddens, axis=0)).astype(BF16)
    g_ffn = lax.psum_scatter(
        jnp.concatenate([g_pair, g_down], axis=1), shards, scatter_dimension=0, tiled=True
    ).astype(F32)

    grad_atts = [
        dot_nn(grad_mid_rows[w], w_out_t).astype(BF16) for w in windows
    ]
    grad_mid_all = jnp.concatenate(grad_mid_rows, axis=0)
    g_out = dot_tn(grad_mid_all, jnp.concatenate(attended, axis=0)).astype(BF16)

    def send_home(blocks):
        while len(blocks) > 1:
            half = len(blocks) // 2
            arrived = [swap(block, "seq", half) for block in blocks[half:]]
            blocks = [
                (kept.astype(F32) + new.astype(F32)).astype(BF16)
                for kept, new in zip(blocks[:half], arrived)
            ]
        return blocks[0]

    far_sums, dq_states = [], []
    for w in windows:
        results = attend_back(
            queries[w], grad_atts[w], wide_attended[w], logs[w], far_blocks[w], None, None
        )
        dq_states.append(results[0])
        far_sums.append(swap(send_home(list(results[1:])), "seq", top_bit))
    grad_qkvs = []
    for w in windows:
        results = attend_back(
            queries[w],
            grad_atts[w],
            wide_attended[w],
            logs[w],
            near_blocks[w],
            dq_states[w],
            (cosine, sine),
        )
        blocks = list(results[1:])
        while len(blocks) > 2:
            half = len(blocks) // 2
            arrived = [swap(block, "seq", half) for block in blocks[half:]]
            blocks = [
                (kept.astype(F32) + new.astype(F32)).astype(BF16)
                for kept, new in zip(blocks[:half], arrived)
            ]
        near_sum = swap(blocks[1], "seq", 1)
        grad_qkvs.append(turn_back(results[0], blocks[0], near_sum, far_sums[w], cosine, sine))

    gain_one_sum = jnp.zeros((model_width,), F32)
    bias_one_sum = jnp.zeros((model_width,), F32)
    input_grads = []
    for w in windows:
        grad_normed1 = scatter_rows(dot_nt(grad_qkvs[w], w_qkv), "tensor")
        normed1, inv_std1, _ = layer_norm(streams[w], gain_one, bias_one)
        input_grads.append(grad_middles[w] + norm_back(grad_normed1, normed1, inv_std1, gain_one))
        gain_one_sum = gain_one_sum + jnp.sum(grad_normed1 * normed1, axis=0)
        bias_one_sum = bias_one_sum + jnp.sum(grad_normed1, axis=0)
    g_qkv = dot_tn(
        jnp.concatenate(normed_rows, axis=0), jnp.concatenate(grad_qkvs, axis=0)
    ).astype(BF16)
    g_att = lax.psum_scatter(
        jnp.concatenate([g_qkv, g_out], axis=1), shards, scatter_dimension=0, tiled=True
    ).astype(F32)

    norm_sums = jnp.stack([gain_one_sum, bias_one_sum, gain_two_sum, bias_two_sum])
    devices = model_width // norm1_gain.shape[0]
    norm_sums = norm_sums.reshape(4, devices, -1).transpose(1, 0, 2)
    norm_sums = scatter_ordered(norm_sums, every)[0]

    return (
        jnp.stack(outputs),
        jnp.stack(input_grads),
        norm_sums[0],
        norm_sums[1],
        g_att[:, :head_cols],
        g_att[:, head_cols : 2 * head_cols],
        g_att[:, 2 * head_cols : 3 * head_cols],
        g_att[:, 3 * head_cols :].T,
        norm_sums[2],
        norm_sums[3],
        g_ffn[:, :hidden_cols],
        g_ffn[:, hidden_cols : 2 * hidden_cols],
        g_ffn[:, 2 * hidden_cols :].T,
    )


def solution(mesh):
    rows = P("dp", ("seq", "tensor"), None)
    vector = P(("dp", "seq", "tensor"))
    tall = P(("dp", "seq"), "tensor")
    flat = P("tensor", ("dp", "seq"))
    return jax.shard_map(
        local,
        mesh=mesh,
        in_specs=(
            rows, rows, P("dp"), P("dp"), P(), vector, vector,
            tall, tall, tall, flat, vector, vector, tall, tall, flat,
        ),
        out_specs=(
            rows, rows, vector, vector, tall, tall, tall, flat,
            vector, vector, tall, tall, flat,
        ),
        check_vma=False,
    )
```

```python
import functools
import math

import jax
import jax.numpy as jnp
from jax import lax
from jax.experimental import pallas as pl
from jax.experimental.pallas import tpu as pltpu
from jax.sharding import PartitionSpec as P

HEAD_DIM = 64
EPSILON = 1e-05
ROPE_BASE = 10000.0
PAIR = 2 * HEAD_DIM
LOG2E = math.log2(math.e)
BF16 = jnp.bfloat16
F32 = jnp.float32
VMEM_BYTES = 56 * 1024 * 1024


def angles(positions, head_dim):
    half_dim = head_dim // 2
    inverse = jnp.exp(
        -(math.log(ROPE_BASE) * 2.0 / head_dim) * jnp.arange(half_dim, dtype=F32)
    )
    phase_angle = positions[:, None] * inverse[None, :]
    return (jnp.cos(phase_angle), jnp.sin(phase_angle))


def dot_nn(left, right):
    return lax.dot_general(left, right, (((1,), (0,)), ((), ())), preferred_element_type=F32)


def dot_nt(left, right):
    return lax.dot_general(left, right, (((1,), (1,)), ((), ())), preferred_element_type=F32)


def dot_tn(left, right):
    return lax.dot_general(left, right, (((0,), (0,)), ((), ())), preferred_element_type=F32)


def swap(array, axis, bit):
    size = lax.axis_size(axis)
    return lax.ppermute(array, axis, [(i, i ^ bit) for i in range(size)])


def spread(array, axis):
    blocks = [array]
    bit = 1
    while bit < lax.axis_size(axis):
        blocks = blocks + [swap(block, axis, bit) for block in blocks]
        bit *= 2
    return blocks


def scatter_pair(kept, sent, axis):
    bit = lax.axis_size(axis) // 2
    while bit > 1:
        partial = kept + swap(sent, axis, bit).astype(F32)
        bit //= 2
        rows = partial.shape[0] // 2
        kept, sent = partial[:rows], partial[rows:].astype(BF16)
    return kept, swap(sent, axis, 1)


def hold(values, *others):
    return lax.optimization_barrier((values, others))[0]


def gather_ordered(array, axes):
    for axis in reversed(axes):
        bit = 1
        while bit < lax.axis_size(axis):
            arrived = swap(array, axis, bit)
            upper = (lax.axis_index(axis) // bit) % 2 == 1
            array = jnp.where(
                upper,
                jnp.concatenate([arrived, array], axis=0),
                jnp.concatenate([array, arrived], axis=0),
            )
            bit *= 2
    return array


def scatter_ordered(array, axes):
    for axis in axes:
        bit = lax.axis_size(axis) // 2
        while bit >= 1:
            rows = array.shape[0] // 2
            upper = (lax.axis_index(axis) // bit) % 2 == 1
            kept = jnp.where(upper, array[rows:], array[:rows])
            sent = jnp.where(upper, array[:rows], array[rows:])
            array = kept + swap(sent, axis, bit)
            bit //= 2
    return array


def gather_ordered(array, axes):
    for axis in reversed(axes):
        bit = 1
        while bit < lax.axis_size(axis):
            arrived = swap(array, axis, bit)
            upper = (lax.axis_index(axis) // bit) % 2 == 1
            array = jnp.where(
                upper,
                jnp.concatenate([arrived, array], axis=0),
                jnp.concatenate([array, arrived], axis=0),
            )
            bit *= 2
    return array


def scatter_ordered(array, axes):
    for axis in axes:
        bit = lax.axis_size(axis) // 2
        while bit >= 1:
            rows = array.shape[0] // 2
            upper = (lax.axis_index(axis) // bit) % 2 == 1
            kept = jnp.where(upper, array[rows:], array[:rows])
            sent = jnp.where(upper, array[:rows], array[rows:])
            array = kept + swap(sent, axis, bit)
            bit //= 2
    return array


def run(kernel, name, out_shape, flops, args, **options):
    args = [array for array in args]
    moved = sum(math.prod(array.shape) * array.dtype.itemsize for array in args)
    outs = out_shape if isinstance(out_shape, list) else [out_shape]
    moved += sum(math.prod(array.shape) * array.dtype.itemsize for array in outs)
    return pl.pallas_call(
        kernel,
        out_shape=out_shape,
        compiler_params=pltpu.CompilerParams(vmem_limit_bytes=VMEM_BYTES),
        cost_estimate=pl.CostEstimate(
            flops=int(flops), bytes_accessed=int(moved), transcendentals=0
        ),
        name=name,
        **options,
    )(*args)


def shaped(shape, dtype):
    return jax.ShapeDtypeStruct(shape, dtype)


SCALAR = pl.BlockSpec(memory_space=pltpu.SMEM)


def normalise(stream):
    row_mean = jnp.mean(stream, axis=-1, keepdims=True)
    centred = stream - row_mean
    variance = jnp.mean(centred * centred, axis=-1, keepdims=True)
    inv_std = lax.rsqrt(variance + EPSILON)
    return centred * inv_std, inv_std


def norm_back(grad_normed, normed, inv_std, norm_gain):
    scaled_grad = grad_normed * norm_gain
    return inv_std * (
        scaled_grad
        - jnp.mean(scaled_grad, axis=-1, keepdims=True)
        - normed * jnp.mean(scaled_grad * normed, axis=-1, keepdims=True)
    )


def first_head(shape):
    return lax.broadcasted_iota(jnp.int32, shape, 1) % PAIR < HEAD_DIM


def swap_halves(values):
    half = HEAD_DIM // 2
    lane = lax.broadcasted_iota(jnp.int32, values.shape, 1)
    ahead = pltpu.roll(values, PAIR - half, 1)
    behind = pltpu.roll(values, half, 1)
    return jnp.where(lane % HEAD_DIM < half, ahead, behind)


def project_kernel(blocks, norms_ref, w_ref, cos_ref, sin_ref, *refs):
    x_refs = refs[:blocks]
    normed_ref, q_ref, kv_ref = refs[blocks:]
    cols = q_ref.shape[1]
    gain, bias = norms_ref[0:1, :], norms_ref[1:2, :]
    at_row = 0
    for x_ref in x_refs:
        rows = slice(at_row, at_row + x_ref.shape[0])
        at_row += x_ref.shape[0]
        normed = (normalise(x_ref[...].astype(F32))[0] * gain + bias).astype(BF16)
        normed_ref[rows, :] = normed
        cosine, sine = cos_ref[rows, :], sin_ref[rows, :]
        query = dot_nn(normed, w_ref[:, :cols])
        key = dot_nn(normed, w_ref[:, cols : 2 * cols])
        for at in range(0, cols, PAIR):
            part = slice(at, at + PAIR)
            one = query[:, part]
            q_ref[rows, part] = (one * cosine + swap_halves(one) * sine).astype(BF16)
            one = key[:, part]
            kv_ref[0, rows, part] = (one * cosine + swap_halves(one) * sine).astype(BF16)
        kv_ref[1, rows, :] = dot_nn(normed, w_ref[:, 2 * cols : 3 * cols]).astype(BF16)


def project(x_blocks, norms, w_att, cosine, sine):
    width, cols = w_att.shape[0], w_att.shape[1] // 4
    rows = sum(block.shape[0] for block in x_blocks)
    return run(
        functools.partial(project_kernel, len(x_blocks)),
        "project",
        [
            shaped((rows, width), BF16),
            shaped((rows, cols), BF16),
            shaped((2, rows, cols), BF16),
        ],
        6 * rows * width * cols,
        [norms, w_att, cosine, sine, *x_blocks],
    )


def attend_kernel(slots, last, first, exp_scale, *refs):
    refs = list(refs)
    q_ref = refs.pop(0)
    kv_refs = [refs.pop(0) for _ in range(slots)]
    if not first:
        acc_in, top_in, total_in = refs.pop(0), refs.pop(0), refs.pop(0)
    query = q_ref[...]
    is_first = first_head(query.shape)
    outs, tops = [], []
    for head in range(2):
        mine = is_first if head == 0 else jnp.logical_not(is_first)
        own_query = jnp.where(mine, query, jnp.zeros_like(query))
        scores = [dot_nt(own_query, kv[0]) for kv in kv_refs]
        top = scores[0].max(axis=1, keepdims=True)
        for one in scores[1:]:
            top = jnp.maximum(top, one.max(axis=1, keepdims=True))
        if not first:
            at = head * HEAD_DIM
            top = jnp.maximum(top, top_in[:, at : at + 1])
        shift = top * exp_scale
        mixed = None
        for one, kv in zip(scores, kv_refs):
            weight = jnp.exp2(one * exp_scale - shift).astype(BF16)
            value = kv[1]
            lane_first = first_head(value.shape)
            lane_mine = lane_first if head == 0 else jnp.logical_not(lane_first)
            term = dot_nn(weight, jnp.where(lane_mine, value, jnp.ones_like(value)))
            mixed = term if mixed is None else mixed + term
        outs.append(mixed)
        tops.append(jnp.broadcast_to(top, mixed.shape))
    acc = jnp.where(is_first, outs[0], outs[1])
    total = pltpu.roll(jnp.where(is_first, outs[1], outs[0]), HEAD_DIM, 1)
    top_wide = jnp.where(is_first, tops[0], tops[1])
    if not first:
        fade = jnp.exp2((top_in[...] - top_wide) * exp_scale)
        acc = acc + acc_in[...] * fade
        total = total + total_in[...] * fade
    if last:
        w_ref, low_ref, wide_ref, log_ref, kept_ref, sent_ref, mixed_rows = refs
        attended = acc / total
        low = attended.astype(BF16)
        low_ref[...] = low
        wide_ref[...] = attended
        log_ref[...] = (top_wide * exp_scale + jnp.log2(total)).T
        term = dot_nt(low, w_ref[...])
        step = pl.program_id(0)

        @pl.when(step == 0)
        def _():
            mixed_rows[...] = term

        @pl.when(step > 0)
        def _():
            mixed_rows[...] += term

        @pl.when(step == pl.num_programs(0) - 1)
        def _():
            half = kept_ref.shape[0]
            kept_ref[...] = mixed_rows[:half]
            sent_ref[...] = mixed_rows[half:].astype(BF16)

    else:
        acc_ref, top_ref, total_ref = refs
        acc_ref[...] = acc
        top_ref[...] = top_wide
        total_ref[...] = total


def attend(queries, blocks, carried, w_att):
    rows, cols = queries.shape
    keys = blocks[0].shape[1]
    slots = len(blocks)
    first = carried is None
    last = w_att is not None
    wide = pl.BlockSpec((rows, PAIR), lambda i: (0, i))
    block = pl.BlockSpec((2, keys, PAIR), lambda i: (0, 0, i))
    shape = shaped((rows, cols), F32)
    args = [queries, *blocks, *([] if first else carried)]
    in_specs = [wide] + [block] * slots + ([] if first else [wide] * 3)
    scratch = []
    if last:
        width = w_att.shape[0]
        out_at = 3 * cols // PAIR
        args.append(w_att)
        in_specs.append(pl.BlockSpec((width, PAIR), lambda i: (0, out_at + i)))
        out_shape = [
            shaped((rows, cols), BF16),
            shape,
            shaped((cols, rows), F32),
            shaped((rows // 2, width), F32),
            shaped((rows // 2, width), BF16),
        ]
        half = pl.BlockSpec((rows // 2, width), lambda i: (0, 0))
        out_specs = [wide, wide, pl.BlockSpec((PAIR, rows), lambda i: (i, 0)), half, half]
        scratch = [pltpu.VMEM((rows, width), F32)]
    else:
        out_shape = [shape] * 3
        out_specs = [wide] * 3
    return run(
        functools.partial(attend_kernel, slots, last, first, LOG2E / math.sqrt(HEAD_DIM)),
        "attend_far" if last else "attend_near",
        out_shape,
        16 * rows * keys * slots * cols,
        args,
        grid=(cols // PAIR,),
        in_specs=in_specs,
        out_specs=out_specs,
        scratch_shapes=scratch,
    )


def attend_back_kernel(slots, first, grad_blocks, exp_scale, score_scale, *refs):
    refs = list(refs)
    q_ref, wide_ref, log_ref = [refs.pop(0) for _ in range(3)]
    if first:
        grad_refs = [refs.pop(0) for _ in range(grad_blocks)]
        w_ref = refs.pop(0)
    else:
        do_ref = refs.pop(0)
    kv_refs = [refs.pop(0) for _ in range(slots)]
    if not first:
        dq_in = refs.pop(0)
        cos_ref, sin_ref = refs.pop(0), refs.pop(0)
    dq_ref = refs.pop(0)
    dkv_refs = [refs.pop(0) for _ in range(slots)]
    query = q_ref[...]
    if first:
        do_ref, rows_ref = refs

        @pl.when(pl.program_id(0) == 0)
        def _():
            at_row = 0
            for grad_ref in grad_refs:
                rows_ref[at_row : at_row + grad_ref.shape[0], :] = grad_ref[...]
                at_row += grad_ref.shape[0]

        grad_out = dot_nn(rows_ref[...], w_ref[...]).astype(BF16)
        do_ref[...] = grad_out
    else:
        grad_out = do_ref[...]
    is_first = first_head(query.shape)
    overlap = (grad_out.astype(F32) * wide_ref[...]).T
    logs = log_ref[...]
    zero = jnp.zeros_like(query)
    own_q, own_do, row_log, row_sum = [], [], [], []
    for head in range(2):
        mine = is_first if head == 0 else jnp.logical_not(is_first)
        own_q.append(jnp.where(mine, query, zero))
        own_do.append(jnp.where(mine, grad_out, zero))
        at = head * HEAD_DIM
        row_log.append(logs[at : at + 1, :])
        row_sum.append(jnp.sum(overlap[at : at + HEAD_DIM, :], axis=0, keepdims=True))
    dq_parts = [None, None]
    for kv, dkv_ref in zip(kv_refs, dkv_refs):
        key, value = kv[0], kv[1]
        key_turned = key.T
        grad_key, grad_value = None, None
        for head in range(2):
            scores = dot_nt(key, own_q[head])
            probs = jnp.exp2(scores * exp_scale - row_log[head])
            grad_probs = dot_nt(value, own_do[head])
            grad_scores = (probs * (grad_probs - row_sum[head])).astype(BF16)
            term_v = dot_nn(probs.astype(BF16), own_do[head])
            term_k = dot_nn(grad_scores, own_q[head])
            at = head * HEAD_DIM
            term_q = dot_nn(key_turned[at : at + HEAD_DIM, :], grad_scores)
            grad_value = term_v if grad_value is None else grad_value + term_v
            grad_key = term_k if grad_key is None else grad_key + term_k
            dq_parts[head] = term_q if dq_parts[head] is None else dq_parts[head] + term_q
        dkv_ref[0] = (grad_key * score_scale).astype(BF16)
        dkv_ref[1] = grad_value.astype(BF16)
    grad_query = jnp.concatenate(dq_parts, axis=0).T * score_scale
    if not first:
        grad_query = grad_query + dq_in[...]
        grad_query = grad_query * cos_ref[...] - swap_halves(grad_query) * sin_ref[...]
    dq_ref[...] = grad_query.astype(dq_ref.dtype)


def attend_back(queries, wide, logs, blocks, grads, w_att, tables):
    rows, cols = queries.shape
    keys = blocks[0].shape[1]
    slots = len(blocks)
    first = tables is None
    score_scale = 1.0 / math.sqrt(HEAD_DIM)
    row_spec = pl.BlockSpec((rows, PAIR), lambda i: (0, i))
    block = pl.BlockSpec((2, keys, PAIR), lambda i: (0, 0, i))
    in_specs = [row_spec] * 2 + [pl.BlockSpec((PAIR, rows), lambda i: (i, 0))]
    args = [queries, wide, logs]
    out_shape = [shaped((rows, cols), F32 if first else BF16)]
    out_shape += [shaped((2, keys, cols), BF16)] * slots
    out_specs = [row_spec] + [block] * slots
    if first:
        width = w_att.shape[0]
        out_at = 3 * cols // PAIR
        args += [*grads, w_att]
        in_specs += [pl.BlockSpec(grad.shape, lambda i: (0, 0)) for grad in grads]
        in_specs += [pl.BlockSpec((width, PAIR), lambda i: (0, out_at + i))]
        out_shape += [shaped((rows, cols), BF16), shaped((rows, width), BF16)]
        out_specs += [row_spec, pl.BlockSpec((rows, width), lambda i: (0, 0))]
    else:
        args.append(grads[1])
        in_specs.append(row_spec)
    args += blocks
    in_specs += [block] * slots
    if not first:
        args += [grads[0], *tables]
        in_specs += [row_spec] + [pl.BlockSpec((rows, PAIR), lambda i: (0, 0))] * 2
    return run(
        functools.partial(
            attend_back_kernel, slots, first, len(grads), score_scale * LOG2E, score_scale
        ),
        "attend_back_far" if first else "attend_back_near",
        out_shape,
        40 * rows * keys * slots * cols,
        args,
        grid=(cols // PAIR,),
        in_specs=in_specs,
        out_specs=out_specs,
    )


def middle_kernel(x_ref, kept_ref, arrived_ref, norms_ref, middle_ref, normed_ref):
    middle = x_ref[...].astype(F32) + (kept_ref[...] + arrived_ref[...].astype(F32))
    middle_ref[...] = middle
    normed_ref[...] = (
        normalise(middle)[0] * norms_ref[2:3, :] + norms_ref[3:4, :]
    ).astype(BF16)


def second_norm(x_rows, kept, arrived, norms):
    return run(
        middle_kernel,
        "second_norm",
        [shaped(kept.shape, F32), shaped(kept.shape, BF16)],
        20 * kept.size,
        [x_rows, kept, arrived, norms],
    )


def feed_kernel(blocks, factor_ref, gate_w_ref, up_w_ref, down_w_ref, *refs):
    x_refs, cot_refs = refs[:blocks], refs[blocks : 2 * blocks]
    x_all, gy_all, hidden_ref, grad_gate_ref, grad_up_ref = refs[2 * blocks : 2 * blocks + 5]
    kept_ref, sent_ref, grad_kept_ref, grad_sent_ref, total, grad_total = refs[2 * blocks + 5 :]
    step = pl.program_id(0)

    @pl.when(step == 0)
    def _():
        at_row = 0
        for x_ref, cot_ref in zip(x_refs, cot_refs):
            rows = slice(at_row, at_row + x_ref.shape[0])
            at_row += x_ref.shape[0]
            x_all[rows, :] = x_ref[...]
            gy_all[rows, :] = (cot_ref[...].astype(F32) * factor_ref[0, 0]).astype(BF16)

    x_rows = x_all[...]
    gate = dot_nn(x_rows, gate_w_ref[...])
    up = dot_nn(x_rows, up_w_ref[...])
    grad_hidden = dot_nn(gy_all[...], down_w_ref[...])
    sig = jax.nn.sigmoid(gate)
    swish = gate * sig
    hidden = (swish * up).astype(BF16)
    grad_gate = (grad_hidden * up * sig * (1.0 + gate * (1.0 - sig))).astype(BF16)
    grad_up = (grad_hidden * swish).astype(BF16)
    hidden_ref[...] = hidden
    grad_gate_ref[...] = grad_gate
    grad_up_ref[...] = grad_up
    grad_term = dot_nt(grad_gate, gate_w_ref[...]) + dot_nt(grad_up, up_w_ref[...])
    term = dot_nt(hidden, down_w_ref[...])

    @pl.when(step == 0)
    def _():
        total[...] = term
        grad_total[...] = grad_term

    @pl.when(step > 0)
    def _():
        total[...] += term
        grad_total[...] += grad_term

    @pl.when(step == pl.num_programs(0) - 1)
    def _():
        half = kept_ref.shape[0]
        kept_ref[...] = total[:half]
        sent_ref[...] = total[half:].astype(BF16)
        grad_kept_ref[...] = grad_total[:half]
        grad_sent_ref[...] = grad_total[half:].astype(BF16)


def feed(x_blocks, cot_blocks, factor, weights):
    width = x_blocks[0].shape[1]
    rows = sum(block.shape[0] for block in x_blocks)
    hidden_cols = weights.shape[1] // 3
    step = min(512, hidden_cols)
    steps = hidden_cols // step
    full = pl.BlockSpec((rows, width), lambda i: (0, 0))
    half = pl.BlockSpec((rows // 2, width), lambda i: (0, 0))
    block = pl.BlockSpec((rows, step), lambda i: (0, i))
    return run(
        functools.partial(feed_kernel, len(x_blocks)),
        "feed",
        [shaped((rows, width), BF16)] * 2
        + [shaped((rows, hidden_cols), BF16)] * 3
        + [shaped((rows // 2, width), F32), shaped((rows // 2, width), BF16)] * 2,
        12 * rows * width * hidden_cols,
        [factor, weights, weights, weights, *x_blocks, *cot_blocks],
        grid=(steps,),
        in_specs=[SCALAR]
        + [
            pl.BlockSpec((width, step), functools.partial(lambda at, i: (0, at + i), k * steps))
            for k in range(3)
        ]
        + [pl.BlockSpec(array.shape, lambda i: (0, 0)) for array in (*x_blocks, *cot_blocks)],
        out_specs=[full] * 2 + [block] * 3 + [half] * 4,
        scratch_shapes=[pltpu.VMEM((rows, width), F32)] * 2,
    )


def weights_kernel(windows, starts, *refs):
    out_ref = refs[-1]
    at = pl.program_id(0)
    for group, (start, stop) in enumerate(starts):
        pairs = refs[2 * windows * group : 2 * windows * (group + 1)]

        @pl.when(jnp.logical_and(at >= start, at < stop))
        def _(pairs=pairs):
            total = None
            for left, right in zip(pairs[:windows], pairs[windows:]):
                term = dot_tn(left[...], right[...])
                total = term if total is None else total + term
            out_ref[...] = total.astype(BF16)


def weight_grads(groups, step, name):
    windows = len(groups[0][0])
    rows, width = groups[0][0][0].shape
    args, in_specs, starts = [], [], []
    at = 0
    for lefts, rights in groups:
        count = rights[0].shape[1] // step
        args += [*lefts, *rights]
        in_specs += [pl.BlockSpec((rows, width), lambda i: (0, 0))] * windows
        in_specs += [
            pl.BlockSpec(
                (rows, step),
                functools.partial(lambda at, count, i: (0, jnp.clip(i - at, 0, count - 1)), at, count),
            )
        ] * windows
        starts.append((at, at + count))
        at += count
    return run(
        functools.partial(weights_kernel, windows, starts),
        name,
        shaped((width, at * step), BF16),
        2 * windows * rows * width * at * step,
        args,
        grid=(at,),
        in_specs=in_specs,
        out_specs=pl.BlockSpec((width, step), lambda i: (0, i)),
    )


def norm_grad(kept_ref, arrived_ref, stream, gain, sums_ref):
    grad_normed = kept_ref[...] + arrived_ref[...].astype(F32)
    normed, inv_std = normalise(stream)
    sums_ref[0:1, :] = jnp.sum(grad_normed * normed, axis=0, keepdims=True)
    sums_ref[1:2, :] = jnp.sum(grad_normed, axis=0, keepdims=True)
    return norm_back(grad_normed, normed, inv_std, gain)


def middle_back_kernel(
    factor_ref, kept_ref, arrived_ref, middle_ref, cot_ref, norms_ref, grad_ref, low_ref, sums_ref
):
    grad_y = cot_ref[...].astype(F32) * factor_ref[0, 0]
    grad = grad_y + norm_grad(
        kept_ref, arrived_ref, middle_ref[...], norms_ref[2:3, :], sums_ref
    )
    grad_ref[...] = grad
    low_ref[...] = grad.astype(BF16)


def second_norm_back(factor, kept, arrived, middle, cot_rows, norms):
    return run(
        middle_back_kernel,
        "second_norm_back",
        [
            shaped(kept.shape, F32),
            shaped(kept.shape, BF16),
            shaped((2, kept.shape[1]), F32),
        ],
        40 * kept.size,
        [factor, kept, arrived, middle, cot_rows, norms],
        in_specs=[SCALAR] + [pl.BlockSpec(memory_space=pltpu.VMEM)] * 5,
    )


def turn_back_kernel(
    dq_ref, own_ref, near_ref, far_ref, cos_ref, sin_ref, w_ref, out_ref, kept_ref, sent_ref
):
    cols = dq_ref.shape[1]
    cosine, sine = cos_ref[...], sin_ref[...]
    out_ref[:, :cols] = dq_ref[...]
    for at in range(0, cols, PAIR):
        part = slice(at, at + PAIR)
        key = (
            own_ref[0, :, part].astype(F32)
            + near_ref[0, :, part].astype(F32)
            + far_ref[0, :, part].astype(F32)
        )
        out_ref[:, cols + at : cols + at + PAIR] = (
            key * cosine - swap_halves(key) * sine
        ).astype(BF16)
    out_ref[:, 2 * cols :] = (
        own_ref[1].astype(F32) + near_ref[1].astype(F32) + far_ref[1].astype(F32)
    ).astype(BF16)
    half = kept_ref.shape[0]
    sent_ref[...] = dot_nt(out_ref[half:, :], w_ref[:, : 3 * cols]).astype(BF16)
    kept_ref[...] = dot_nt(out_ref[:half, :], w_ref[:, : 3 * cols])


def turn_back(grad_query, own, near, far, cosine, sine, w_att):
    rows, cols = grad_query.shape
    width = w_att.shape[0]
    return run(
        turn_back_kernel,
        "turn_back",
        [
            shaped((rows, 3 * cols), BF16),
            shaped((rows // 2, width), F32),
            shaped((rows // 2, width), BF16),
        ],
        6 * rows * cols * width,
        [grad_query, own, near, far, cosine, sine, w_att],
    )


def input_back_kernel(window, kept_ref, arrived_ref, x_ref, grad_ref, norms_ref, *refs):
    out_ref, sums_ref = refs[-2:]
    out_ref[0] = grad_ref[...] + norm_grad(
        kept_ref, arrived_ref, x_ref[...].astype(F32), norms_ref[0:1, :], sums_ref
    )


def first_norm_back(window, windows, kept, arrived, x_rows, grad_middle, norms, earlier):
    rows, width = kept.shape
    args = [kept, arrived, x_rows, grad_middle, norms] + ([] if earlier is None else [earlier])
    whole = [pl.BlockSpec(array.shape, lambda i: (0, 0)) for array in args[:5]]
    return run(
        functools.partial(input_back_kernel, window),
        "first_norm_back",
        [shaped((windows, rows, width), F32), shaped((2, width), F32)],
        40 * rows * width,
        args,
        grid=(1,),
        in_specs=whole + ([] if earlier is None else [pl.BlockSpec(memory_space=pl.ANY)]),
        out_specs=[
            pl.BlockSpec((1, rows, width), lambda i: (window, 0, 0)),
            pl.BlockSpec((2, width), lambda i: (0, 0)),
        ],
        input_output_aliases={} if earlier is None else {5: 0},
    )


def result_kernel(windows, *refs):
    out_ref = refs[-1]
    for w in range(windows):
        middle_ref, kept_ref, arrived_ref = refs[3 * w : 3 * w + 3]
        out_ref[w] = (
            middle_ref[...] + (kept_ref[...] + arrived_ref[...].astype(F32))
        ).astype(BF16)


def results(parts):
    rows, width = parts[0][0].shape
    return run(
        functools.partial(result_kernel, len(parts)),
        "results",
        shaped((len(parts), rows, width), BF16),
        2 * len(parts) * rows * width,
        [array for part in parts for array in part],
    )


def local(
    tokens,
    cotangent,
    species,
    counts,
    species_scale,
    norm1_gain,
    norm1_bias,
    w_query,
    w_key,
    w_value,
    w_out,
    norm2_gain,
    norm2_bias,
    w_gate,
    w_up,
    w_down,
):
    windows_here, own_rows, model_width = tokens.shape
    tensor_size = lax.axis_size("tensor")
    seq_size = lax.axis_size("seq")
    block_rows = own_rows * tensor_size
    head_cols = w_query.shape[1]
    hidden_cols = w_gate.shape[1]
    every = ("dp", "seq", "tensor")
    shards = ("dp", "seq")

    w_att = lax.all_gather(
        jnp.concatenate([w_query, w_key, w_value, w_out.T], axis=1), shards, axis=0, tiled=True
    )
    w_ffn = lax.all_gather(
        jnp.concatenate([w_gate, w_up, w_down.T], axis=1), shards, axis=0, tiled=True
    )

    norms = gather_ordered(
        jnp.stack([norm1_gain, norm1_bias, norm2_gain, norm2_bias])[None], every
    )
    norms = norms.transpose(1, 0, 2).reshape(4, model_width)

    own_at = lax.axis_index("tensor")
    starts = jnp.concatenate(
        [
            lax.iota(jnp.int32, own_rows) + (own_at ^ other) * own_rows
            for other in range(tensor_size)
        ]
    )
    positions = (lax.axis_index("seq") * block_rows + starts).astype(F32)
    cos_half, sin_half = angles(positions, HEAD_DIM)
    cosine = jnp.concatenate([cos_half] * 4, axis=1)
    sine = jnp.concatenate([-sin_half, sin_half] * 2, axis=1)

    labels = lax.broadcasted_iota(jnp.int32, (windows_here, species_scale.shape[0]), 1)
    chosen = jnp.sum(jnp.where(species[:, None] == labels, species_scale[None, :], 0.0), axis=1)
    weighted = counts.astype(F32) * chosen
    weight_total = jnp.broadcast_to(jnp.sum(weighted), (8, 128))
    bit = 1
    while bit < lax.axis_size("dp"):
        weight_total = weight_total + swap(weight_total, "dp", bit)
        bit *= 2
    factor = weighted * float(windows_here * lax.axis_size("dp")) / weight_total[0, 0]

    windows = range(windows_here)
    factors = [factor[w].reshape(1, 1) for w in windows]
    top_bit = seq_size // 2

    def on_chip(block):
        blocks = [block]
        bit = 1
        while bit < top_bit:
            blocks = blocks + [swap(one, "seq", bit) for one in blocks]
            bit *= 2
        return blocks

    token_blocks = [spread(tokens[w], "tensor") for w in windows]
    normed_rows, queries, near_blocks, far_first = [], [], [], []
    for w in windows:
        normed, query, own_kv = project(token_blocks[w], norms, w_att, cosine, sine)
        normed_rows.append(normed)
        queries.append(query)
        far_first.append(swap(own_kv, "seq", top_bit))
        near_blocks.append(on_chip(own_kv))
    states = []
    for w in windows:
        query = hold(queries[w], states[-1] if states else ())
        states.append(attend(query, near_blocks[w], None, None))
    far_blocks = [on_chip(hold(far_first[w], states[w])) for w in windows]
    cot_blocks = [spread(hold(cotangent[w], states[0]), "tensor") for w in windows]
    attended, wide_attended, logs, middles, mid_blocks = [], [], [], [], []
    for w in windows:
        query = hold(queries[w], states[-1], attended[-1] if attended else ())
        low, wide, log_row, kept, sent = attend(query, far_blocks[w], states[w], w_att)
        attended.append(low)
        wide_attended.append(wide)
        logs.append(log_row)
        middle, normed_mid = second_norm(tokens[w], *scatter_pair(kept, sent, "tensor"), norms)
        middles.append(middle)
        mid_blocks.append(spread(normed_mid, "tensor"))

    fed = []
    for w in windows:
        blocks = hold(mid_blocks[w], fed[-1] if fed else ())
        fed.append(feed(blocks, cot_blocks[w], factors[w], w_ffn))
    mid_rows, grad_y_rows, hiddens, grad_gates, grad_ups = [
        [one[at] for one in fed] for at in range(5)
    ]
    grad_middles, grad_mid_blocks, second_sums = [], [], []

    def through_second_norm(w, *after):
        kept, arrived = scatter_pair(fed[w][7], fed[w][8], "tensor")
        grad_middle, low, sums = second_norm_back(
            factors[w], hold(kept, *after), arrived, middles[w], cotangent[w], norms
        )
        grad_middles.append(grad_middle)
        grad_mid_blocks.append(spread(low, "tensor"))
        second_sums.append(sums)

    for w in windows[:-1]:
        through_second_norm(w)
    g_ffn_part = weight_grads(
        [
            (mid_rows, grad_gates),
            (mid_rows, grad_ups),
            (grad_y_rows, hold(hiddens, grad_middles)),
        ],
        min(512, hidden_cols),
        "feed_weights",
    )
    g_ffn = lax.psum_scatter(g_ffn_part, shards, scatter_dimension=0, tiled=True).astype(F32)
    through_second_norm(windows[-1], g_ffn_part)

    def fold(blocks, down_to):
        while len(blocks) > down_to:
            half = len(blocks) // 2
            arrived = [swap(block, "seq", half) for block in blocks[half:]]
            blocks = [
                (kept.astype(F32) + new.astype(F32)).astype(BF16)
                for kept, new in zip(blocks[:half], arrived)
            ]
        return blocks

    slots = seq_size // 2
    far_sums, dq_states, grad_mid_rows = [], [], []
    for w in windows:
        query = hold(queries[w], dq_states[-1][0] if dq_states else grad_middles[-1])
        parts = attend_back(
            query, wide_attended[w], logs[w], far_blocks[w], grad_mid_blocks[w], w_att, None
        )
        dq_states.append((parts[0], parts[1 + slots]))
        grad_mid_rows.append(parts[2 + slots])
        far_sums.append(swap(fold(list(parts[1 : 1 + slots]), 1)[0], "seq", top_bit))
    result_parts = [
        (middles[w], *scatter_pair(fed[w][5], hold(fed[w][6], dq_states[0]), "tensor"))
        for w in windows
    ]
    grad_queries, near_pairs = [], []
    for w in windows:
        query = hold(queries[w], grad_queries[-1] if grad_queries else dq_states[-1][0])
        parts = attend_back(
            query, wide_attended[w], logs[w], near_blocks[w], dq_states[w], None, (cosine, sine)
        )
        grad_queries.append(parts[0])
        blocks = fold(list(parts[1:]), 2)
        near_pairs.append((blocks[0], swap(blocks[1], "seq", 1)))
    output = results(result_parts)

    grad_qkvs, first_parts = [], []
    for w in windows:
        grad_qkv, kept, sent = turn_back(
            grad_queries[w], *near_pairs[w], far_sums[w], cosine, sine, w_att
        )
        grad_qkvs.append(grad_qkv)
        first_parts.append(scatter_pair(kept, sent, "tensor"))
    g_att_part = weight_grads(
        [(normed_rows, grad_qkvs), (grad_mid_rows, attended)], head_cols, "attend_weights"
    )
    g_att = lax.psum_scatter(
        hold(g_att_part, g_ffn), shards, scatter_dimension=0, tiled=True
    ).astype(F32)
    input_grad = None
    first_sums = []
    for w in windows:
        kept, arrived = first_parts[w]
        input_grad, sums = first_norm_back(
            w,
            windows_here,
            hold(kept, g_att_part),
            arrived,
            tokens[w],
            grad_middles[w],
            norms,
            input_grad,
        )
        first_sums.append(sums)

    norm_sums = jnp.concatenate([sum(first_sums), sum(second_sums)], axis=0)
    devices = model_width // norm1_gain.shape[0]
    norm_sums = norm_sums.reshape(4, devices, -1).transpose(1, 0, 2)
    norm_sums = scatter_ordered(norm_sums, every)[0]

    return (
        output,
        input_grad,
        norm_sums[0],
        norm_sums[1],
        g_att[:, :head_cols],
        g_att[:, head_cols : 2 * head_cols],
        g_att[:, 2 * head_cols : 3 * head_cols],
        g_att[:, 3 * head_cols :].T,
        norm_sums[2],
        norm_sums[3],
        g_ffn[:, :hidden_cols],
        g_ffn[:, hidden_cols : 2 * hidden_cols],
        g_ffn[:, 2 * hidden_cols :].T,
    )


def solution(mesh):
    rows = P("dp", ("seq", "tensor"), None)
    vector = P(("dp", "seq", "tensor"))
    tall = P(("dp", "seq"), "tensor")
    flat = P("tensor", ("dp", "seq"))
    return jax.shard_map(
        local,
        mesh=mesh,
        in_specs=(
            rows, rows, P("dp"), P("dp"), P(), vector, vector,
            tall, tall, tall, flat, vector, vector, tall, tall, flat,
        ),
        out_specs=(
            rows, rows, vector, vector, tall, tall, tall, flat,
            vector, vector, tall, tall, flat,
        ),
        check_vma=False,
    )
```

```python
import functools
import math

import jax
import jax.numpy as jnp
from jax import lax
from jax.experimental import pallas as pl
from jax.experimental.pallas import tpu as pltpu
from jax.sharding import PartitionSpec as P

HEAD_DIM = 64
EPSILON = 1e-05
ROPE_BASE = 10000.0
PAIR = 2 * HEAD_DIM
LOG2E = math.log2(math.e)
BF16 = jnp.bfloat16
F32 = jnp.float32
VMEM_BYTES = 56 * 1024 * 1024
MESH = pl.DeviceIdType.MESH


def angles(positions, head_dim):
    half_dim = head_dim // 2
    inverse = jnp.exp(
        -(math.log(ROPE_BASE) * 2.0 / head_dim) * jnp.arange(half_dim, dtype=F32)
    )
    phase_angle = positions[:, None] * inverse[None, :]
    return (jnp.cos(phase_angle), jnp.sin(phase_angle))


def dot_nn(left, right):
    return lax.dot_general(left, right, (((1,), (0,)), ((), ())), preferred_element_type=F32)


def dot_nt(left, right):
    return lax.dot_general(left, right, (((1,), (1,)), ((), ())), preferred_element_type=F32)


def dot_tn(left, right):
    return lax.dot_general(left, right, (((0,), (0,)), ((), ())), preferred_element_type=F32)


def swap(array, axis, bit):
    size = lax.axis_size(axis)
    return lax.ppermute(array, axis, [(i, i ^ bit) for i in range(size)])


def spread(array, axis):
    blocks = [array]
    bit = 1
    while bit < lax.axis_size(axis):
        blocks = blocks + [swap(block, axis, bit) for block in blocks]
        bit *= 2
    return blocks


def scatter_pair(kept, sent, axis):
    bit = lax.axis_size(axis) // 2
    while bit > 1:
        partial = kept + swap(sent, axis, bit).astype(F32)
        bit //= 2
        rows = partial.shape[0] // 2
        kept, sent = partial[:rows], partial[rows:].astype(BF16)
    return kept, swap(sent, axis, 1)


def hold(values, *others):
    return lax.optimization_barrier((values, others))[0]


def gather_ordered(array, axes):
    for axis in reversed(axes):
        bit = 1
        while bit < lax.axis_size(axis):
            arrived = swap(array, axis, bit)
            upper = (lax.axis_index(axis) // bit) % 2 == 1
            array = jnp.where(
                upper,
                jnp.concatenate([arrived, array], axis=0),
                jnp.concatenate([array, arrived], axis=0),
            )
            bit *= 2
    return array


def scatter_ordered(array, axes):
    for axis in axes:
        bit = lax.axis_size(axis) // 2
        while bit >= 1:
            rows = array.shape[0] // 2
            upper = (lax.axis_index(axis) // bit) % 2 == 1
            kept = jnp.where(upper, array[rows:], array[:rows])
            sent = jnp.where(upper, array[:rows], array[rows:])
            array = kept + swap(sent, axis, bit)
            bit //= 2
    return array


def gather_ordered(array, axes):
    for axis in reversed(axes):
        bit = 1
        while bit < lax.axis_size(axis):
            arrived = swap(array, axis, bit)
            upper = (lax.axis_index(axis) // bit) % 2 == 1
            array = jnp.where(
                upper,
                jnp.concatenate([arrived, array], axis=0),
                jnp.concatenate([array, arrived], axis=0),
            )
            bit *= 2
    return array


def scatter_ordered(array, axes):
    for axis in axes:
        bit = lax.axis_size(axis) // 2
        while bit >= 1:
            rows = array.shape[0] // 2
            upper = (lax.axis_index(axis) // bit) % 2 == 1
            kept = jnp.where(upper, array[rows:], array[:rows])
            sent = jnp.where(upper, array[:rows], array[rows:])
            array = kept + swap(sent, axis, bit)
            bit //= 2
    return array


def run(kernel, name, out_shape, flops, args, collective_id=None, **options):
    trading = {} if collective_id is None else dict(collective_id=collective_id, has_side_effects=True)
    moved = sum(math.prod(array.shape) * array.dtype.itemsize for array in args)
    outs = out_shape if isinstance(out_shape, list) else [out_shape]
    moved += sum(math.prod(array.shape) * array.dtype.itemsize for array in outs)
    return pl.pallas_call(
        kernel,
        out_shape=out_shape,
        compiler_params=pltpu.CompilerParams(vmem_limit_bytes=VMEM_BYTES, **trading),
        cost_estimate=pl.CostEstimate(
            flops=int(flops), bytes_accessed=int(moved), transcendentals=0
        ),
        name=name,
        **options,
    )(*args)


def shaped(shape, dtype):
    return jax.ShapeDtypeStruct(shape, dtype)


SCALAR = pl.BlockSpec(memory_space=pltpu.SMEM)


def normalise(stream):
    row_mean = jnp.mean(stream, axis=-1, keepdims=True)
    centred = stream - row_mean
    variance = jnp.mean(centred * centred, axis=-1, keepdims=True)
    inv_std = lax.rsqrt(variance + EPSILON)
    return centred * inv_std, inv_std


def norm_back(grad_normed, normed, inv_std, norm_gain):
    scaled_grad = grad_normed * norm_gain
    return inv_std * (
        scaled_grad
        - jnp.mean(scaled_grad, axis=-1, keepdims=True)
        - normed * jnp.mean(scaled_grad * normed, axis=-1, keepdims=True)
    )


def first_head(shape):
    return lax.broadcasted_iota(jnp.int32, shape, 1) % PAIR < HEAD_DIM


def swap_halves(values):
    half = HEAD_DIM // 2
    lane = lax.broadcasted_iota(jnp.int32, values.shape, 1)
    ahead = pltpu.roll(values, PAIR - half, 1)
    behind = pltpu.roll(values, half, 1)
    return jnp.where(lane % HEAD_DIM < half, ahead, behind)


def project_kernel(blocks, norms_ref, w_ref, cos_ref, sin_ref, *refs):
    x_refs = refs[:blocks]
    normed_ref, q_ref, kv_ref = refs[blocks:]
    cols = q_ref.shape[2]
    gain, bias = norms_ref[0:1, :], norms_ref[1:2, :]
    at_row = 0
    for x_ref in x_refs:
        rows = slice(at_row, at_row + x_ref.shape[1])
        at_row += x_ref.shape[1]
        normed = (normalise(x_ref[0].astype(F32))[0] * gain + bias).astype(BF16)
        normed_ref[0, rows, :] = normed
        cosine, sine = cos_ref[rows, :], sin_ref[rows, :]
        query = dot_nn(normed, w_ref[:, :cols])
        key = dot_nn(normed, w_ref[:, cols : 2 * cols])
        for at in range(0, cols, PAIR):
            part = slice(at, at + PAIR)
            one = query[:, part]
            q_ref[0, rows, part] = (one * cosine + swap_halves(one) * sine).astype(BF16)
            one = key[:, part]
            kv_ref[0, 0, rows, part] = (one * cosine + swap_halves(one) * sine).astype(BF16)
        kv_ref[0, 1, rows, :] = dot_nn(normed, w_ref[:, 2 * cols : 3 * cols]).astype(BF16)


def project(x_blocks, norms, w_att, cosine, sine):
    windows = x_blocks[0].shape[0]
    width, cols = w_att.shape[0], w_att.shape[1] // 4
    rows = sum(block.shape[1] for block in x_blocks)
    args = [norms, w_att, cosine, sine, *x_blocks]
    return run(
        functools.partial(project_kernel, len(x_blocks)),
        "project",
        [
            shaped((windows, rows, width), BF16),
            shaped((windows, rows, cols), BF16),
            shaped((windows, 2, rows, cols), BF16),
        ],
        6 * windows * rows * width * cols,
        args,
        grid=(windows,),
        in_specs=[pl.BlockSpec(array.shape, lambda i: (0, 0)) for array in args[:4]]
        + [pl.BlockSpec((1,) + block.shape[1:], lambda i: (i, 0, 0)) for block in x_blocks],
        out_specs=[
            pl.BlockSpec((1, rows, width), lambda i: (i, 0, 0)),
            pl.BlockSpec((1, rows, cols), lambda i: (i, 0, 0)),
            pl.BlockSpec((1, 2, rows, cols), lambda i: (i, 0, 0, 0)),
        ],
    )


def flipped(index, mask):
    bit = 1
    while bit <= mask:
        if mask & bit:
            index = index + bit - 2 * bit * ((index // bit) % 2)
        bit *= 2
    return index


def greet(peers):
    barrier = pltpu.get_barrier_semaphore()
    for peer in peers:
        pl.semaphore_signal(barrier, inc=1, device_id=peer, device_id_type=MESH)
    pl.semaphore_wait(barrier, len(peers))


def send(source, target, send_sem, recv_sem, peer):
    return pltpu.make_async_remote_copy(
        src_ref=source,
        dst_ref=target,
        send_sem=send_sem,
        recv_sem=recv_sem,
        device_id=peer,
        device_id_type=MESH,
    )


def attend_kernel(windows, pairs, trades, exp_scale, *refs):
    q_ref, w_ref, kv_ref, cot_ref = refs[:4]
    low_ref, wide_ref, log_ref, kept_ref, sent_ref, slots_ref, cots_ref = refs[4:11]
    slots, acc_all, top_all, total_all, mixed_rows = refs[11:16]
    own_sem, send_sem, recv_sem, save_sem, cot_send, cot_recv = refs[16:]
    step = pl.program_id(0)
    near_steps = windows * pairs
    steps = 2 * near_steps
    seq, tensor = lax.axis_index("seq"), lax.axis_index("tensor")
    core_peer = {"seq": flipped(seq, 1)}
    far_peer = {"seq": flipped(seq, 2)}
    cot_peers = [{"tensor": flipped(tensor, other + 1)} for other in range(trades)]

    def piece(number):
        columns = pl.ds(pl.multiple_of((number % pairs) * PAIR, PAIR), PAIR)
        return kv_ref.at[number // pairs, :, :, columns]

    def own_copy(number):
        return pltpu.make_async_copy(piece(number), slots.at[number, 0], own_sem.at[number])

    def trade(number, slot):
        peer = far_peer if slot == 2 else core_peer
        source = slots.at[number, 2] if slot == 3 else piece(number)
        return send(
            source,
            slots.at[number, slot],
            send_sem.at[number, slot - 1],
            recv_sem.at[number, slot - 1],
            peer,
        )

    def cot_trade(other):
        return send(
            cot_ref, cots_ref.at[other], cot_send.at[other], cot_recv.at[other], cot_peers[other]
        )

    def save(number, slot):
        return pltpu.make_async_copy(
            slots.at[number, slot], slots_ref.at[number, slot], save_sem.at[number, slot]
        )

    @pl.when(step == 0)
    def _():
        greet([core_peer, far_peer] + cot_peers)

        @pl.loop(0, near_steps)
        def _(number):
            own_copy(number).start()
            trade(number, 1).start()
            trade(number, 2).start()

        for other in range(trades):
            cot_trade(other).start()

    relayed = step - (near_steps - 1)

    @pl.when(jnp.logical_and(relayed >= 0, relayed < near_steps))
    def _():
        trade(relayed, 2).wait_recv()
        trade(relayed, 3).start()
        save(relayed, 2).start()

    query = q_ref[0]
    is_first = first_head(query.shape)

    def partial_of(number, used, carried_top):
        outs, tops = [], []
        for head in range(2):
            mine = is_first if head == 0 else jnp.logical_not(is_first)
            own_query = jnp.where(mine, query, jnp.zeros_like(query))
            scores = [dot_nt(own_query, slots[number, slot, 0]) for slot in used]
            top = scores[0].max(axis=1, keepdims=True)
            for one in scores[1:]:
                top = jnp.maximum(top, one.max(axis=1, keepdims=True))
            if carried_top is not None:
                at = head * HEAD_DIM
                top = jnp.maximum(top, carried_top[:, at : at + 1])
            shift = top * exp_scale
            mixed = None
            for one, slot in zip(scores, used):
                weight = jnp.exp2(one * exp_scale - shift).astype(BF16)
                value = slots[number, slot, 1]
                lane_first = first_head(value.shape)
                lane_mine = lane_first if head == 0 else jnp.logical_not(lane_first)
                term = dot_nn(weight, jnp.where(lane_mine, value, jnp.ones_like(value)))
                mixed = term if mixed is None else mixed + term
            outs.append(mixed)
            tops.append(jnp.broadcast_to(top, mixed.shape))
        acc = jnp.where(is_first, outs[0], outs[1])
        total = pltpu.roll(jnp.where(is_first, outs[1], outs[0]), HEAD_DIM, 1)
        return acc, jnp.where(is_first, tops[0], tops[1]), total

    @pl.when(step < near_steps)
    def _():
        own_copy(step).wait()
        trade(step, 1).wait_recv()
        save(step, 0).start()
        save(step, 1).start()
        acc, top, total = partial_of(step, (0, 1), None)
        acc_all[step] = acc
        top_all[step] = top
        total_all[step] = total

    @pl.when(step >= near_steps)
    def _():
        number = step - near_steps
        trade(number, 3).wait_recv()
        save(number, 3).start()
        carried_top = top_all[number]
        acc, top, total = partial_of(number, (2, 3), carried_top)
        fade = jnp.exp2((carried_top - top) * exp_scale)
        acc = acc + acc_all[number] * fade
        total = total + total_all[number] * fade
        attended = acc / total
        low = attended.astype(BF16)
        low_ref[0] = low
        wide_ref[0] = attended
        log_ref[0] = (top * exp_scale + jnp.log2(total)).T
        term = dot_nt(low, w_ref[...])
        pair = number % pairs

        @pl.when(pair == 0)
        def _():
            mixed_rows[...] = term

        @pl.when(pair > 0)
        def _():
            mixed_rows[...] += term

        @pl.when(pair == pairs - 1)
        def _():
            half = kept_ref.shape[1]
            kept_ref[0] = mixed_rows[:half]
            sent_ref[0] = mixed_rows[half:].astype(BF16)

    @pl.when(step == steps - 1)
    def _():
        @pl.loop(0, near_steps)
        def _(number):
            for slot in range(1, 4):
                trade(number, slot).wait_send()
            for slot in range(4):
                save(number, slot).wait()

        for other in range(trades):
            cot_trade(other).wait_send()
            cot_trade(other).wait_recv()


def attend(queries, own_kv, w_att, cotangent, trades):
    windows, rows, cols = queries.shape
    width = w_att.shape[0]
    pairs = cols // PAIR
    near = windows * pairs
    out_at = 3 * pairs

    def far(i):
        return jnp.maximum(i - near, 0)

    anywhere = pl.BlockSpec(memory_space=pl.ANY)
    wide = pl.BlockSpec((1, rows, PAIR), lambda i: (far(i) // pairs, 0, far(i) % pairs))
    half = pl.BlockSpec((1, rows // 2, width), lambda i: (far(i) // pairs, 0, 0))
    state = pltpu.VMEM((near, rows, PAIR), F32)
    dma = pltpu.SemaphoreType.DMA
    return run(
        functools.partial(attend_kernel, windows, pairs, trades, LOG2E / math.sqrt(HEAD_DIM)),
        "attend",
        [
            shaped((windows, rows, cols), BF16),
            shaped((windows, rows, cols), F32),
            shaped((windows, cols, rows), F32),
            shaped((windows, rows // 2, width), F32),
            shaped((windows, rows // 2, width), BF16),
            shaped((near, 4, 2, rows, PAIR), BF16),
            shaped((trades,) + cotangent.shape, BF16),
        ],
        64 * windows * rows * rows * cols,
        [queries, w_att, own_kv, cotangent],
        collective_id=0,
        grid=(2 * near,),
        in_specs=[
            pl.BlockSpec((1, rows, PAIR), lambda i: ((i // pairs) % windows, 0, i % pairs)),
            pl.BlockSpec((width, PAIR), lambda i: (0, out_at + far(i) % pairs)),
            anywhere,
            anywhere,
        ],
        out_specs=[
            wide,
            wide,
            pl.BlockSpec((1, PAIR, rows), lambda i: (far(i) // pairs, far(i) % pairs, 0)),
            half,
            half,
            anywhere,
            anywhere,
        ],
        scratch_shapes=[
            pltpu.VMEM((near, 4, 2, rows, PAIR), BF16),
            state,
            state,
            state,
            pltpu.VMEM((rows, width), F32),
            dma((near,)),
            dma((near, 3)),
            dma((near, 3)),
            dma((near, 4)),
            dma((trades,)),
            dma((trades,)),
        ],
    )


def attend_back_kernel(slots, first, grad_blocks, exp_scale, score_scale, *refs):
    refs = list(refs)
    q_ref, wide_ref, log_ref = [refs.pop(0) for _ in range(3)]
    if first:
        grad_refs = [refs.pop(0) for _ in range(grad_blocks)]
        w_ref = refs.pop(0)
    else:
        do_ref = refs.pop(0)
    slots_ref = refs.pop(0)
    if not first:
        dq_in = refs.pop(0)
        cos_ref, sin_ref = refs.pop(0), refs.pop(0)
    dq_ref = refs.pop(0)
    dkv_refs = [refs.pop(0) for _ in range(slots)]
    query = q_ref[0]
    if first:
        do_ref, rows_ref = refs

        @pl.when(pl.program_id(0) == 0)
        def _():
            at_row = 0
            for grad_ref in grad_refs:
                rows_ref[at_row : at_row + grad_ref.shape[0], :] = grad_ref[...]
                at_row += grad_ref.shape[0]

        grad_out = dot_nn(rows_ref[...], w_ref[...]).astype(BF16)
        do_ref[...] = grad_out
    else:
        grad_out = do_ref[...]
    is_first = first_head(query.shape)
    overlap = (grad_out.astype(F32) * wide_ref[0]).T
    logs = log_ref[0]
    zero = jnp.zeros_like(query)
    own_q, own_do, row_log, row_sum = [], [], [], []
    for head in range(2):
        mine = is_first if head == 0 else jnp.logical_not(is_first)
        own_q.append(jnp.where(mine, query, zero))
        own_do.append(jnp.where(mine, grad_out, zero))
        at = head * HEAD_DIM
        row_log.append(logs[at : at + 1, :])
        row_sum.append(jnp.sum(overlap[at : at + HEAD_DIM, :], axis=0, keepdims=True))
    dq_parts = [None, None]
    for slot, dkv_ref in enumerate(dkv_refs):
        key, value = slots_ref[0, slot, 0], slots_ref[0, slot, 1]
        key_turned = key.T
        grad_key, grad_value = None, None
        for head in range(2):
            scores = dot_nt(key, own_q[head])
            probs = jnp.exp2(scores * exp_scale - row_log[head])
            grad_probs = dot_nt(value, own_do[head])
            grad_scores = (probs * (grad_probs - row_sum[head])).astype(BF16)
            term_v = dot_nn(probs.astype(BF16), own_do[head])
            term_k = dot_nn(grad_scores, own_q[head])
            at = head * HEAD_DIM
            term_q = dot_nn(key_turned[at : at + HEAD_DIM, :], grad_scores)
            grad_value = term_v if grad_value is None else grad_value + term_v
            grad_key = term_k if grad_key is None else grad_key + term_k
            dq_parts[head] = term_q if dq_parts[head] is None else dq_parts[head] + term_q
        dkv_ref[0] = (grad_key * score_scale).astype(BF16)
        dkv_ref[1] = grad_value.astype(BF16)
    grad_query = jnp.concatenate(dq_parts, axis=0).T * score_scale
    if not first:
        grad_query = grad_query + dq_in[...]
        grad_query = grad_query * cos_ref[...] - swap_halves(grad_query) * sin_ref[...]
    dq_ref[...] = grad_query.astype(dq_ref.dtype)


def attend_back(window, queries, wide, logs, slots_all, grads, w_att, tables):
    rows, cols = queries.shape[1:]
    keys = rows
    slots = slots_all.shape[1] // 2
    pairs = cols // PAIR
    first = tables is None
    score_scale = 1.0 / math.sqrt(HEAD_DIM)
    row_spec = pl.BlockSpec((rows, PAIR), lambda i: (0, i))
    block = pl.BlockSpec((2, keys, PAIR), lambda i: (0, 0, i))
    stacked = pl.BlockSpec((1, rows, PAIR), lambda i: (window, 0, i))
    in_specs = [stacked] * 2 + [pl.BlockSpec((1, PAIR, rows), lambda i: (window, i, 0))]
    args = [queries, wide, logs]
    out_shape = [shaped((rows, cols), F32 if first else BF16)]
    out_shape += [shaped((2, keys, cols), BF16)] * slots
    out_specs = [row_spec] + [block] * slots
    if first:
        width = w_att.shape[0]
        out_at = 3 * cols // PAIR
        args += [*grads, w_att]
        in_specs += [pl.BlockSpec(grad.shape, lambda i: (0, 0)) for grad in grads]
        in_specs += [pl.BlockSpec((width, PAIR), lambda i: (0, out_at + i))]
        out_shape += [shaped((rows, cols), BF16), shaped((rows, width), BF16)]
        out_specs += [row_spec, pl.BlockSpec((rows, width), lambda i: (0, 0))]
    else:
        args.append(grads[1])
        in_specs.append(row_spec)
    args.append(slots_all)
    half = 1 if first else 0
    in_specs.append(
        pl.BlockSpec((1, slots, 2, keys, PAIR), lambda i: (window * pairs + i, half, 0, 0, 0))
    )
    if not first:
        args += [grads[0], *tables]
        in_specs += [row_spec] + [pl.BlockSpec((rows, PAIR), lambda i: (0, 0))] * 2
    return run(
        functools.partial(
            attend_back_kernel, slots, first, len(grads), score_scale * LOG2E, score_scale
        ),
        "attend_back_far" if first else "attend_back_near",
        out_shape,
        40 * rows * keys * slots * cols,
        args,
        grid=(cols // PAIR,),
        in_specs=in_specs,
        out_specs=out_specs,
    )


def middle_kernel(x_ref, kept_ref, arrived_ref, norms_ref, middle_ref, normed_ref):
    middle = x_ref[...].astype(F32) + (kept_ref[...] + arrived_ref[...].astype(F32))
    middle_ref[...] = middle
    normed_ref[...] = (
        normalise(middle)[0] * norms_ref[2:3, :] + norms_ref[3:4, :]
    ).astype(BF16)


def second_norm(x_rows, kept, arrived, norms):
    return run(
        middle_kernel,
        "second_norm",
        [shaped(kept.shape, F32), shaped(kept.shape, BF16)],
        20 * kept.size,
        [x_rows, kept, arrived, norms],
    )


def feed_kernel(blocks, factor_ref, gate_w_ref, up_w_ref, down_w_ref, *refs):
    x_refs, cot_refs = refs[:blocks], refs[blocks : 2 * blocks]
    x_all, gy_all, hidden_ref, grad_gate_ref, grad_up_ref = refs[2 * blocks : 2 * blocks + 5]
    kept_ref, sent_ref, grad_kept_ref, grad_sent_ref, total, grad_total = refs[2 * blocks + 5 :]
    step = pl.program_id(0)

    @pl.when(step == 0)
    def _():
        at_row = 0
        for x_ref, cot_ref in zip(x_refs, cot_refs):
            rows = slice(at_row, at_row + x_ref.shape[0])
            at_row += x_ref.shape[0]
            x_all[rows, :] = x_ref[...]
            gy_all[rows, :] = (cot_ref[...].astype(F32) * factor_ref[0, 0]).astype(BF16)

    x_rows = x_all[...]
    gate = dot_nn(x_rows, gate_w_ref[...])
    up = dot_nn(x_rows, up_w_ref[...])
    grad_hidden = dot_nn(gy_all[...], down_w_ref[...])
    sig = jax.nn.sigmoid(gate)
    swish = gate * sig
    hidden = (swish * up).astype(BF16)
    grad_gate = (grad_hidden * up * sig * (1.0 + gate * (1.0 - sig))).astype(BF16)
    grad_up = (grad_hidden * swish).astype(BF16)
    hidden_ref[...] = hidden
    grad_gate_ref[...] = grad_gate
    grad_up_ref[...] = grad_up
    grad_term = dot_nt(grad_gate, gate_w_ref[...]) + dot_nt(grad_up, up_w_ref[...])
    term = dot_nt(hidden, down_w_ref[...])

    @pl.when(step == 0)
    def _():
        total[...] = term
        grad_total[...] = grad_term

    @pl.when(step > 0)
    def _():
        total[...] += term
        grad_total[...] += grad_term

    @pl.when(step == pl.num_programs(0) - 1)
    def _():
        half = kept_ref.shape[0]
        kept_ref[...] = total[:half]
        sent_ref[...] = total[half:].astype(BF16)
        grad_kept_ref[...] = grad_total[:half]
        grad_sent_ref[...] = grad_total[half:].astype(BF16)


def feed(x_blocks, cot_blocks, factor, weights):
    width = x_blocks[0].shape[1]
    rows = sum(block.shape[0] for block in x_blocks)
    hidden_cols = weights.shape[1] // 3
    step = min(512, hidden_cols)
    steps = hidden_cols // step
    full = pl.BlockSpec((rows, width), lambda i: (0, 0))
    half = pl.BlockSpec((rows // 2, width), lambda i: (0, 0))
    block = pl.BlockSpec((rows, step), lambda i: (0, i))
    return run(
        functools.partial(feed_kernel, len(x_blocks)),
        "feed",
        [shaped((rows, width), BF16)] * 2
        + [shaped((rows, hidden_cols), BF16)] * 3
        + [shaped((rows // 2, width), F32), shaped((rows // 2, width), BF16)] * 2,
        12 * rows * width * hidden_cols,
        [factor, weights, weights, weights, *x_blocks, *cot_blocks],
        grid=(steps,),
        in_specs=[SCALAR]
        + [
            pl.BlockSpec((width, step), functools.partial(lambda at, i: (0, at + i), k * steps))
            for k in range(3)
        ]
        + [pl.BlockSpec(array.shape, lambda i: (0, 0)) for array in (*x_blocks, *cot_blocks)],
        out_specs=[full] * 2 + [block] * 3 + [half] * 4,
        scratch_shapes=[pltpu.VMEM((rows, width), F32)] * 2,
    )


def weights_kernel(windows, starts, *refs):
    out_ref = refs[-1]
    at = pl.program_id(0)
    for group, (start, stop) in enumerate(starts):
        pairs = refs[2 * windows * group : 2 * windows * (group + 1)]

        @pl.when(jnp.logical_and(at >= start, at < stop))
        def _(pairs=pairs):
            total = None
            for left, right in zip(pairs[:windows], pairs[windows:]):
                term = dot_tn(left[...], right[...])
                total = term if total is None else total + term
            out_ref[...] = total.astype(BF16)


def weight_grads(groups, step, name):
    windows = len(groups[0][0])
    rows, width = groups[0][0][0].shape
    args, in_specs, starts = [], [], []
    at = 0
    for lefts, rights in groups:
        count = rights[0].shape[1] // step
        args += [*lefts, *rights]
        in_specs += [pl.BlockSpec((rows, width), lambda i: (0, 0))] * windows
        in_specs += [
            pl.BlockSpec(
                (rows, step),
                functools.partial(lambda at, count, i: (0, jnp.clip(i - at, 0, count - 1)), at, count),
            )
        ] * windows
        starts.append((at, at + count))
        at += count
    return run(
        functools.partial(weights_kernel, windows, starts),
        name,
        shaped((width, at * step), BF16),
        2 * windows * rows * width * at * step,
        args,
        grid=(at,),
        in_specs=in_specs,
        out_specs=pl.BlockSpec((width, step), lambda i: (0, i)),
    )


def norm_grad(kept_ref, arrived_ref, stream, gain, sums_ref):
    grad_normed = kept_ref[...] + arrived_ref[...].astype(F32)
    normed, inv_std = normalise(stream)
    sums_ref[0:1, :] = jnp.sum(grad_normed * normed, axis=0, keepdims=True)
    sums_ref[1:2, :] = jnp.sum(grad_normed, axis=0, keepdims=True)
    return norm_back(grad_normed, normed, inv_std, gain)


def middle_back_kernel(
    factor_ref, kept_ref, arrived_ref, middle_ref, cot_ref, norms_ref, grad_ref, low_ref, sums_ref
):
    grad_y = cot_ref[...].astype(F32) * factor_ref[0, 0]
    grad = grad_y + norm_grad(
        kept_ref, arrived_ref, middle_ref[...], norms_ref[2:3, :], sums_ref
    )
    grad_ref[...] = grad
    low_ref[...] = grad.astype(BF16)


def second_norm_back(factor, kept, arrived, middle, cot_rows, norms):
    return run(
        middle_back_kernel,
        "second_norm_back",
        [
            shaped(kept.shape, F32),
            shaped(kept.shape, BF16),
            shaped((2, kept.shape[1]), F32),
        ],
        40 * kept.size,
        [factor, kept, arrived, middle, cot_rows, norms],
        in_specs=[SCALAR] + [pl.BlockSpec(memory_space=pltpu.VMEM)] * 5,
    )


def turn_back_kernel(
    dq_ref, own_ref, near_ref, far_ref, cos_ref, sin_ref, w_ref, out_ref, kept_ref, sent_ref
):
    cols = dq_ref.shape[1]
    cosine, sine = cos_ref[...], sin_ref[...]
    out_ref[:, :cols] = dq_ref[...]
    for at in range(0, cols, PAIR):
        part = slice(at, at + PAIR)
        key = (
            own_ref[0, :, part].astype(F32)
            + near_ref[0, :, part].astype(F32)
            + far_ref[0, :, part].astype(F32)
        )
        out_ref[:, cols + at : cols + at + PAIR] = (
            key * cosine - swap_halves(key) * sine
        ).astype(BF16)
    out_ref[:, 2 * cols :] = (
        own_ref[1].astype(F32) + near_ref[1].astype(F32) + far_ref[1].astype(F32)
    ).astype(BF16)
    half = kept_ref.shape[0]
    sent_ref[...] = dot_nt(out_ref[half:, :], w_ref[:, : 3 * cols]).astype(BF16)
    kept_ref[...] = dot_nt(out_ref[:half, :], w_ref[:, : 3 * cols])


def turn_back(grad_query, own, near, far, cosine, sine, w_att):
    rows, cols = grad_query.shape
    width = w_att.shape[0]
    return run(
        turn_back_kernel,
        "turn_back",
        [
            shaped((rows, 3 * cols), BF16),
            shaped((rows // 2, width), F32),
            shaped((rows // 2, width), BF16),
        ],
        6 * rows * cols * width,
        [grad_query, own, near, far, cosine, sine, w_att],
    )


def input_back_kernel(window, kept_ref, arrived_ref, x_ref, grad_ref, norms_ref, *refs):
    out_ref, sums_ref = refs[-2:]
    out_ref[0] = grad_ref[...] + norm_grad(
        kept_ref, arrived_ref, x_ref[...].astype(F32), norms_ref[0:1, :], sums_ref
    )


def first_norm_back(window, windows, kept, arrived, x_rows, grad_middle, norms, earlier):
    rows, width = kept.shape
    args = [kept, arrived, x_rows, grad_middle, norms] + ([] if earlier is None else [earlier])
    whole = [pl.BlockSpec(array.shape, lambda i: (0, 0)) for array in args[:5]]
    return run(
        functools.partial(input_back_kernel, window),
        "first_norm_back",
        [shaped((windows, rows, width), F32), shaped((2, width), F32)],
        40 * rows * width,
        args,
        grid=(1,),
        in_specs=whole + ([] if earlier is None else [pl.BlockSpec(memory_space=pl.ANY)]),
        out_specs=[
            pl.BlockSpec((1, rows, width), lambda i: (window, 0, 0)),
            pl.BlockSpec((2, width), lambda i: (0, 0)),
        ],
        input_output_aliases={} if earlier is None else {5: 0},
    )


def result_kernel(windows, *refs):
    out_ref = refs[-1]
    for w in range(windows):
        middle_ref, kept_ref, arrived_ref = refs[3 * w : 3 * w + 3]
        out_ref[w] = (
            middle_ref[...] + (kept_ref[...] + arrived_ref[...].astype(F32))
        ).astype(BF16)


def results(parts):
    rows, width = parts[0][0].shape
    return run(
        functools.partial(result_kernel, len(parts)),
        "results",
        shaped((len(parts), rows, width), BF16),
        2 * len(parts) * rows * width,
        [array for part in parts for array in part],
    )


def local(
    tokens,
    cotangent,
    species,
    counts,
    species_scale,
    norm1_gain,
    norm1_bias,
    w_query,
    w_key,
    w_value,
    w_out,
    norm2_gain,
    norm2_bias,
    w_gate,
    w_up,
    w_down,
):
    windows_here, own_rows, model_width = tokens.shape
    tensor_size = lax.axis_size("tensor")
    seq_size = lax.axis_size("seq")
    block_rows = own_rows * tensor_size
    head_cols = w_query.shape[1]
    hidden_cols = w_gate.shape[1]
    every = ("dp", "seq", "tensor")
    shards = ("dp", "seq")

    w_att = lax.all_gather(
        jnp.concatenate([w_query, w_key, w_value, w_out.T], axis=1), shards, axis=0, tiled=True
    )
    w_ffn = lax.all_gather(
        jnp.concatenate([w_gate, w_up, w_down.T], axis=1), shards, axis=0, tiled=True
    )

    norms = gather_ordered(
        jnp.stack([norm1_gain, norm1_bias, norm2_gain, norm2_bias])[None], every
    )
    norms = norms.transpose(1, 0, 2).reshape(4, model_width)

    own_at = lax.axis_index("tensor")
    starts = jnp.concatenate(
        [
            lax.iota(jnp.int32, own_rows) + (own_at ^ other) * own_rows
            for other in range(tensor_size)
        ]
    )
    positions = (lax.axis_index("seq") * block_rows + starts).astype(F32)
    cos_half, sin_half = angles(positions, HEAD_DIM)
    cosine = jnp.concatenate([cos_half] * 4, axis=1)
    sine = jnp.concatenate([-sin_half, sin_half] * 2, axis=1)

    labels = lax.broadcasted_iota(jnp.int32, (windows_here, species_scale.shape[0]), 1)
    chosen = jnp.sum(jnp.where(species[:, None] == labels, species_scale[None, :], 0.0), axis=1)
    weighted = counts.astype(F32) * chosen
    weight_total = jnp.broadcast_to(jnp.sum(weighted), (8, 128))
    bit = 1
    while bit < lax.axis_size("dp"):
        weight_total = weight_total + swap(weight_total, "dp", bit)
        bit *= 2
    factor = weighted * float(windows_here * lax.axis_size("dp")) / weight_total[0, 0]

    windows = range(windows_here)
    factors = [factor[w].reshape(1, 1) for w in windows]
    top_bit = seq_size // 2

    token_blocks = spread(tokens, "tensor")
    normed_rows, queries, own_kv = project(token_blocks, norms, w_att, cosine, sine)
    attended, wide_attended, logs, kept_all, sent_all, slots_all, cots = attend(
        queries, own_kv, w_att, cotangent, tensor_size - 1
    )
    cot_blocks = [
        [cotangent[w]] + [cots[other, w] for other in range(tensor_size - 1)] for w in windows
    ]
    middles, mid_blocks = [], []
    for w in windows:
        middle, normed_mid = second_norm(
            tokens[w], *scatter_pair(kept_all[w], sent_all[w], "tensor"), norms
        )
        middles.append(middle)
        mid_blocks.append(spread(normed_mid, "tensor"))

    fed = []
    for w in windows:
        blocks = hold(mid_blocks[w], fed[-1] if fed else ())
        fed.append(feed(blocks, cot_blocks[w], factors[w], w_ffn))
    mid_rows, grad_y_rows, hiddens, grad_gates, grad_ups = [
        [one[at] for one in fed] for at in range(5)
    ]
    grad_middles, grad_mid_blocks, second_sums = [], [], []

    def through_second_norm(w, *after):
        kept, arrived = scatter_pair(fed[w][7], fed[w][8], "tensor")
        grad_middle, low, sums = second_norm_back(
            factors[w], hold(kept, *after), arrived, middles[w], cotangent[w], norms
        )
        grad_middles.append(grad_middle)
        grad_mid_blocks.append(spread(low, "tensor"))
        second_sums.append(sums)

    for w in windows[:-1]:
        through_second_norm(w)
    g_ffn_part = weight_grads(
        [
            (mid_rows, grad_gates),
            (mid_rows, grad_ups),
            (grad_y_rows, hold(hiddens, grad_middles)),
        ],
        min(512, hidden_cols),
        "feed_weights",
    )
    g_ffn = lax.psum_scatter(g_ffn_part, shards, scatter_dimension=0, tiled=True).astype(F32)
    through_second_norm(windows[-1], g_ffn_part)

    def fold(blocks, down_to):
        while len(blocks) > down_to:
            half = len(blocks) // 2
            arrived = [swap(block, "seq", half) for block in blocks[half:]]
            blocks = [
                (kept.astype(F32) + new.astype(F32)).astype(BF16)
                for kept, new in zip(blocks[:half], arrived)
            ]
        return blocks

    slots = seq_size // 2
    far_sums, dq_states, grad_mid_rows = [], [], []
    for w in windows:
        query = hold(queries, dq_states[-1][0] if dq_states else grad_middles[-1])
        parts = attend_back(
            w, query, wide_attended, logs, slots_all, grad_mid_blocks[w], w_att, None
        )
        dq_states.append((parts[0], parts[1 + slots]))
        grad_mid_rows.append(parts[2 + slots])
        far_sums.append(swap(fold(list(parts[1 : 1 + slots]), 1)[0], "seq", top_bit))
    result_parts = [
        (middles[w], *scatter_pair(fed[w][5], hold(fed[w][6], dq_states[0]), "tensor"))
        for w in windows
    ]
    grad_queries, near_pairs = [], []
    for w in windows:
        query = hold(queries, grad_queries[-1] if grad_queries else dq_states[-1][0])
        parts = attend_back(
            w, query, wide_attended, logs, slots_all, dq_states[w], None, (cosine, sine)
        )
        grad_queries.append(parts[0])
        blocks = fold(list(parts[1:]), 2)
        near_pairs.append((blocks[0], swap(blocks[1], "seq", 1)))
    output = results(result_parts)

    grad_qkvs, first_parts = [], []
    for w in windows:
        grad_qkv, kept, sent = turn_back(
            grad_queries[w], *near_pairs[w], far_sums[w], cosine, sine, w_att
        )
        grad_qkvs.append(grad_qkv)
        first_parts.append(scatter_pair(kept, sent, "tensor"))
    g_att_part = weight_grads(
        [
            ([normed_rows[w] for w in windows], grad_qkvs),
            (grad_mid_rows, [attended[w] for w in windows]),
        ],
        head_cols,
        "attend_weights",
    )
    g_att = lax.psum_scatter(
        hold(g_att_part, g_ffn), shards, scatter_dimension=0, tiled=True
    ).astype(F32)
    input_grad = None
    first_sums = []
    for w in windows:
        kept, arrived = first_parts[w]
        input_grad, sums = first_norm_back(
            w,
            windows_here,
            hold(kept, g_att_part),
            arrived,
            tokens[w],
            grad_middles[w],
            norms,
            input_grad,
        )
        first_sums.append(sums)

    norm_sums = jnp.concatenate([sum(first_sums), sum(second_sums)], axis=0)
    devices = model_width // norm1_gain.shape[0]
    norm_sums = norm_sums.reshape(4, devices, -1).transpose(1, 0, 2)
    norm_sums = scatter_ordered(norm_sums, every)[0]

    return (
        output,
        input_grad,
        norm_sums[0],
        norm_sums[1],
        g_att[:, :head_cols],
        g_att[:, head_cols : 2 * head_cols],
        g_att[:, 2 * head_cols : 3 * head_cols],
        g_att[:, 3 * head_cols :].T,
        norm_sums[2],
        norm_sums[3],
        g_ffn[:, :hidden_cols],
        g_ffn[:, hidden_cols : 2 * hidden_cols],
        g_ffn[:, 2 * hidden_cols :].T,
    )


def solution(mesh):
    rows = P("dp", ("seq", "tensor"), None)
    vector = P(("dp", "seq", "tensor"))
    tall = P(("dp", "seq"), "tensor")
    flat = P("tensor", ("dp", "seq"))
    return jax.shard_map(
        local,
        mesh=mesh,
        in_specs=(
            rows, rows, P("dp"), P("dp"), P(), vector, vector,
            tall, tall, tall, flat, vector, vector, tall, tall, flat,
        ),
        out_specs=(
            rows, rows, vector, vector, tall, tall, tall, flat,
            vector, vector, tall, tall, flat,
        ),
        check_vma=False,
    )
```

```python
import functools
import math

import jax
import jax.numpy as jnp
from jax import lax
from jax.experimental import pallas as pl
from jax.experimental.pallas import tpu as pltpu
from jax.sharding import PartitionSpec as P

HEAD_DIM = 64
EPSILON = 1e-05
ROPE_BASE = 10000.0
PAIR = 2 * HEAD_DIM
LOG2E = math.log2(math.e)
BF16 = jnp.bfloat16
F32 = jnp.float32
VMEM_BYTES = 56 * 1024 * 1024
MESH = pl.DeviceIdType.MESH


def angles(positions, head_dim):
    half_dim = head_dim // 2
    inverse = jnp.exp(
        -(math.log(ROPE_BASE) * 2.0 / head_dim) * jnp.arange(half_dim, dtype=F32)
    )
    phase_angle = positions[:, None] * inverse[None, :]
    return (jnp.cos(phase_angle), jnp.sin(phase_angle))


def dot_nn(left, right):
    return lax.dot_general(left, right, (((1,), (0,)), ((), ())), preferred_element_type=F32)


def dot_nt(left, right):
    return lax.dot_general(left, right, (((1,), (1,)), ((), ())), preferred_element_type=F32)


def dot_tn(left, right):
    return lax.dot_general(left, right, (((0,), (0,)), ((), ())), preferred_element_type=F32)


def swap(array, axis, bit):
    size = lax.axis_size(axis)
    return lax.ppermute(array, axis, [(i, i ^ bit) for i in range(size)])


def spread(array, axis):
    blocks = [array]
    bit = 1
    while bit < lax.axis_size(axis):
        blocks = blocks + [swap(block, axis, bit) for block in blocks]
        bit *= 2
    return blocks


def scatter_pair(kept, sent, axis):
    bit = lax.axis_size(axis) // 2
    while bit > 1:
        partial = kept + swap(sent, axis, bit).astype(F32)
        bit //= 2
        rows = partial.shape[0] // 2
        kept, sent = partial[:rows], partial[rows:].astype(BF16)
    return kept, swap(sent, axis, 1)


def hold(values, *others):
    return lax.optimization_barrier((values, others))[0]


def scatter_ordered(array, axes):
    for axis in axes:
        bit = lax.axis_size(axis) // 2
        while bit >= 1:
            rows = array.shape[0] // 2
            upper = (lax.axis_index(axis) // bit) % 2 == 1
            kept = jnp.where(upper, array[rows:], array[:rows])
            sent = jnp.where(upper, array[:rows], array[rows:])
            array = kept + swap(sent, axis, bit)
            bit //= 2
    return array


def gather_ordered(array, axes):
    for axis in reversed(axes):
        bit = 1
        while bit < lax.axis_size(axis):
            arrived = swap(array, axis, bit)
            upper = (lax.axis_index(axis) // bit) % 2 == 1
            array = jnp.where(
                upper,
                jnp.concatenate([arrived, array], axis=0),
                jnp.concatenate([array, arrived], axis=0),
            )
            bit *= 2
    return array


def scatter_ordered(array, axes):
    for axis in axes:
        bit = lax.axis_size(axis) // 2
        while bit >= 1:
            rows = array.shape[0] // 2
            upper = (lax.axis_index(axis) // bit) % 2 == 1
            kept = jnp.where(upper, array[rows:], array[:rows])
            sent = jnp.where(upper, array[:rows], array[rows:])
            array = kept + swap(sent, axis, bit)
            bit //= 2
    return array


def run(kernel, name, out_shape, flops, args, collective_id=None, **options):
    trading = {} if collective_id is None else dict(collective_id=collective_id, has_side_effects=True)
    moved = sum(math.prod(array.shape) * array.dtype.itemsize for array in args)
    outs = out_shape if isinstance(out_shape, list) else [out_shape]
    moved += sum(math.prod(array.shape) * array.dtype.itemsize for array in outs)
    return pl.pallas_call(
        kernel,
        out_shape=out_shape,
        compiler_params=pltpu.CompilerParams(vmem_limit_bytes=VMEM_BYTES, **trading),
        cost_estimate=pl.CostEstimate(
            flops=int(flops), bytes_accessed=int(moved), transcendentals=0
        ),
        name=name,
        **options,
    )(*args)


def shaped(shape, dtype):
    return jax.ShapeDtypeStruct(shape, dtype)


SCALAR = pl.BlockSpec(memory_space=pltpu.SMEM)


def normalise(stream):
    row_mean = jnp.mean(stream, axis=-1, keepdims=True)
    centred = stream - row_mean
    variance = jnp.mean(centred * centred, axis=-1, keepdims=True)
    inv_std = lax.rsqrt(variance + EPSILON)
    return centred * inv_std, inv_std


def norm_back(grad_normed, normed, inv_std, norm_gain):
    scaled_grad = grad_normed * norm_gain
    return inv_std * (
        scaled_grad
        - jnp.mean(scaled_grad, axis=-1, keepdims=True)
        - normed * jnp.mean(scaled_grad * normed, axis=-1, keepdims=True)
    )


def first_head(shape):
    return lax.broadcasted_iota(jnp.int32, shape, 1) % PAIR < HEAD_DIM


def swap_halves(values):
    half = HEAD_DIM // 2
    lane = lax.broadcasted_iota(jnp.int32, values.shape, 1)
    ahead = pltpu.roll(values, PAIR - half, 1)
    behind = pltpu.roll(values, half, 1)
    return jnp.where(lane % HEAD_DIM < half, ahead, behind)


def project_kernel(blocks, norms_ref, w_ref, cos_ref, sin_ref, *refs):
    x_refs = refs[:blocks]
    normed_ref, q_ref, kv_ref = refs[blocks:]
    cols = q_ref.shape[2]
    gain, bias = norms_ref[0:1, :], norms_ref[1:2, :]
    at_row = 0
    for x_ref in x_refs:
        rows = slice(at_row, at_row + x_ref.shape[1])
        at_row += x_ref.shape[1]
        normed = (normalise(x_ref[0].astype(F32))[0] * gain + bias).astype(BF16)
        normed_ref[0, rows, :] = normed
        cosine, sine = cos_ref[rows, :], sin_ref[rows, :]
        query = dot_nn(normed, w_ref[:, :cols])
        key = dot_nn(normed, w_ref[:, cols : 2 * cols])
        for at in range(0, cols, PAIR):
            part = slice(at, at + PAIR)
            one = query[:, part]
            q_ref[0, rows, part] = (one * cosine + swap_halves(one) * sine).astype(BF16)
            one = key[:, part]
            kv_ref[0, 0, rows, part] = (one * cosine + swap_halves(one) * sine).astype(BF16)
        kv_ref[0, 1, rows, :] = dot_nn(normed, w_ref[:, 2 * cols : 3 * cols]).astype(BF16)


def project(x_blocks, norms, w_att, cosine, sine):
    windows = x_blocks[0].shape[0]
    width, cols = w_att.shape[0], w_att.shape[1] // 4
    rows = sum(block.shape[1] for block in x_blocks)
    args = [norms, w_att, cosine, sine, *x_blocks]
    return run(
        functools.partial(project_kernel, len(x_blocks)),
        "project",
        [
            shaped((windows, rows, width), BF16),
            shaped((windows, rows, cols), BF16),
            shaped((windows, 2, rows, cols), BF16),
        ],
        6 * windows * rows * width * cols,
        args,
        grid=(windows,),
        in_specs=[pl.BlockSpec(array.shape, lambda i: (0, 0)) for array in args[:4]]
        + [pl.BlockSpec((1,) + block.shape[1:], lambda i: (i, 0, 0)) for block in x_blocks],
        out_specs=[
            pl.BlockSpec((1, rows, width), lambda i: (i, 0, 0)),
            pl.BlockSpec((1, rows, cols), lambda i: (i, 0, 0)),
            pl.BlockSpec((1, 2, rows, cols), lambda i: (i, 0, 0, 0)),
        ],
    )


def flipped(index, mask):
    bit = 1
    while bit <= mask:
        if mask & bit:
            index = index + bit - 2 * bit * ((index // bit) % 2)
        bit *= 2
    return index


def greet(peers):
    barrier = pltpu.get_barrier_semaphore()
    for peer in peers:
        pl.semaphore_signal(barrier, inc=1, device_id=peer, device_id_type=MESH)
    pl.semaphore_wait(barrier, len(peers))


def send(source, target, send_sem, recv_sem, peer):
    return pltpu.make_async_remote_copy(
        src_ref=source,
        dst_ref=target,
        send_sem=send_sem,
        recv_sem=recv_sem,
        device_id=peer,
        device_id_type=MESH,
    )


def half_chip_peers():
    seq, depth = lax.axis_index("seq"), lax.axis_index("dp")
    size = lax.axis_size("dp")
    return {
        "far": {"seq": flipped(seq, 2)},
        "up": {"dp": (depth + 1) % size},
        "down": {"dp": (depth + size - 1) % size},
        "core": {"seq": flipped(seq, 1)},
    }


class Route:
    PARTS = ((0, 0), (0, 1), (3, 0), (1, 0), (3, 1), (1, 1), (2, 0), (2, 1))

    def __init__(self, whole, rows, send_sem, recv_sem, own=None):
        self.whole, self.rows = whole, rows
        self.send_sem, self.recv_sem = send_sem, recv_sem
        self.seq, self.depth = lax.axis_index("seq"), lax.axis_index("dp")
        self.peers = half_chip_peers()
        self.own = self.part((0, 0)) if own is None else own

    def part(self, place, half=None):
        turn, other = place
        seq = flipped(self.seq, 2) if other else self.seq
        at = (((self.depth + turn) % lax.axis_size("dp")) * lax.axis_size("seq") + seq) * self.rows
        count = self.rows if half is None else self.rows // 2
        if half == 1:
            at = at + count
        return self.whole.at[pl.ds(pl.multiple_of(at, count), count), :]

    def message(self, number):
        if number >= 9:
            place, peer, half = self.PARTS[number - 9], "core", None
        else:
            place, peer, half = (
                ((0, 0), "far", None),
                ((0, 0), "up", None),
                ((0, 0), "down", None),
                ((0, 1), "up", None),
                ((0, 1), "down", None),
                ((3, 0), "up", 0),
                ((1, 0), "down", 1),
                ((3, 1), "up", 0),
                ((1, 1), "down", 1),
            )[number]
        target = self.part(place, half)
        return send(
            self.own if place == (0, 0) else target,
            target,
            self.send_sem.at[number],
            self.recv_sem.at[number],
            self.peers[peer],
        )

    def start(self, *numbers):
        for number in numbers:
            self.message(number).start()

    def arrived(self, *numbers):
        for number in numbers:
            self.message(number).wait_recv()

    def sent(self, *numbers):
        for number in numbers:
            self.message(number).wait_send()


MESSAGES = 17


def gather_kernel(trades, att_ref, ffn_ref, tile_ref, tokens_ref, *refs):
    att_all, ffn_all, norms_ref, tokens_all = refs[:4]
    tiles, pair_of_tiles = refs[4:6]
    att_send, att_recv, ffn_send, ffn_recv, tile_send, tile_recv = refs[6:12]
    own_sem, tokens_send, tokens_recv, pair_send, pair_recv = refs[12:]
    tensor = lax.axis_index("tensor")
    others = [{"tensor": flipped(tensor, other + 1)} for other in range(trades)]
    rows = att_ref.shape[0]
    att = Route(att_all, rows, att_send, att_recv, att_ref)
    ffn = Route(ffn_all, rows, ffn_send, ffn_recv, ffn_ref)
    tile_rows = tile_ref.shape[0]
    group = pair_of_tiles.shape[0]
    small = Route(tiles, group, tile_send, tile_recv, pair_of_tiles)

    def tokens_trade(other):
        return send(
            tokens_ref,
            tokens_all.at[other],
            tokens_send.at[other],
            tokens_recv.at[other],
            others[other],
        )

    own_rows = pl.ds(pl.multiple_of(tensor * tile_rows, tile_rows), tile_rows)

    def pair_trade(other):
        return send(
            tile_ref,
            pair_of_tiles.at[own_rows, :],
            pair_send.at[other],
            pair_recv.at[other],
            others[other],
        )

    own_copies = [
        pltpu.make_async_copy(att_ref, att.part((0, 0)), own_sem.at[0]),
        pltpu.make_async_copy(ffn_ref, ffn.part((0, 0)), own_sem.at[1]),
        pltpu.make_async_copy(tile_ref, pair_of_tiles.at[own_rows, :], own_sem.at[2]),
        pltpu.make_async_copy(pair_of_tiles, small.part((0, 0)), own_sem.at[3]),
    ]

    greet(list(att.peers.values()) + others)
    for other in range(trades):
        pair_trade(other).start()
    att.start(0, 1, 2, 9)
    own_copies[2].start()
    own_copies[0].start()
    own_copies[1].start()
    for other in range(trades):
        tokens_trade(other).start()
    own_copies[2].wait()
    for other in range(trades):
        pair_trade(other).wait_recv()
    own_copies[3].start()
    small.start(0, 1, 2, 9)
    ffn.start(0)
    att.arrived(0)
    att.start(3, 4, 10)
    small.arrived(0)
    small.start(3, 4, 10)
    for route in (att, small):
        route.arrived(1, 2)
        route.start(5, 6, 11, 12)
    for route in (att, small):
        route.arrived(3, 4)
        route.start(7, 8, 13, 14)
    for route in (small, att):
        route.arrived(5, 6)
        route.start(15)
        route.arrived(7, 8)
        route.start(16)
        route.arrived(*range(9, 17))
    own_copies[3].wait()
    shard = norms_ref.shape[1] // (tiles.shape[0] // tile_rows)
    total = None
    for device in range(tiles.shape[0] // tile_rows):
        tile = tiles[device * tile_rows : (device + 1) * tile_rows, :]
        norms_ref[:, device * shard : (device + 1) * shard] = tile[:, :shard]
    for depth in range(lax.axis_size("dp")):
        at = depth * (tiles.shape[0] // lax.axis_size("dp"))
        one = tiles[at + 4 : at + 5, :]
        total = one if total is None else total + one
    norms_ref[4:5, : total.shape[1]] = total
    for route in (att, small):
        route.sent(*range(MESSAGES))
    ffn.arrived(0)
    ffn.sent(0)
    own_copies[0].wait()
    own_copies[1].wait()
    for other in range(trades):
        pair_trade(other).wait_send()
        tokens_trade(other).wait_recv()
        tokens_trade(other).wait_send()


def gather(att, ffn, tile, tokens, trades):
    count = lax.axis_size("dp") * lax.axis_size("seq")
    rows = att.shape[0]
    group = tile.shape[0] * (trades + 1)
    anywhere = pl.BlockSpec(memory_space=pl.ANY)
    vmem = pl.BlockSpec(memory_space=pltpu.VMEM)
    dma = pltpu.SemaphoreType.DMA
    return run(
        functools.partial(gather_kernel, trades),
        "gather",
        [
            shaped((count * rows, att.shape[1]), BF16),
            shaped((count * rows, ffn.shape[1]), BF16),
            shaped((tile.shape[0], count * rows), F32),
            shaped((trades,) + tokens.shape, BF16),
        ],
        0,
        [att, ffn, tile, tokens],
        collective_id=1,
        in_specs=[vmem, vmem, vmem, anywhere],
        out_specs=[anywhere, anywhere, vmem, anywhere],
        scratch_shapes=[pltpu.VMEM((count * group, 128), F32), pltpu.VMEM((group, 128), F32)]
        + [dma((MESSAGES,))] * 6
        + [dma((4,)), dma((trades,)), dma((trades,)), dma((trades,)), dma((trades,))],
    )


def attend_kernel(windows, pairs, trades, exp_scale, *refs):
    q_ref, w_ref, kv_ref, cot_ref = refs[:4]
    low_ref, wide_ref, log_ref, kept_ref, sent_ref, slots_ref, cots_ref, ffn_ref = refs[5:13]
    slots, acc_all, top_all, total_all, mixed_rows = refs[13:18]
    own_sem, send_sem, recv_sem, save_sem, cot_send, cot_recv, ffn_send, ffn_recv = refs[18:]
    shards = lax.axis_size("dp") * lax.axis_size("seq")
    ffn = Route(ffn_ref, ffn_ref.shape[0] // shards, ffn_send, ffn_recv)
    step = pl.program_id(0)
    near_steps = windows * pairs
    steps = 2 * near_steps
    seq, tensor = lax.axis_index("seq"), lax.axis_index("tensor")
    core_peer = {"seq": flipped(seq, 1)}
    far_peer = {"seq": flipped(seq, 2)}
    cot_peers = [{"tensor": flipped(tensor, other + 1)} for other in range(trades)]

    def piece(number):
        columns = pl.ds(pl.multiple_of((number % pairs) * PAIR, PAIR), PAIR)
        return kv_ref.at[number // pairs, :, :, columns]

    def own_copy(number):
        return pltpu.make_async_copy(piece(number), slots.at[number, 0], own_sem.at[number])

    def trade(number, slot):
        peer = far_peer if slot == 2 else core_peer
        source = slots.at[number, 2] if slot == 3 else piece(number)
        return send(
            source,
            slots.at[number, slot],
            send_sem.at[number, slot - 1],
            recv_sem.at[number, slot - 1],
            peer,
        )

    def cot_trade(other):
        return send(
            cot_ref, cots_ref.at[other], cot_send.at[other], cot_recv.at[other], cot_peers[other]
        )

    def save(number, slot):
        return pltpu.make_async_copy(
            slots.at[number, slot], slots_ref.at[number, slot], save_sem.at[number, slot]
        )

    @pl.when(step == 0)
    def _():
        greet(list(ffn.peers.values()) + cot_peers)
        ffn.start(1, 2, 3, 4, 9, 10)

        @pl.loop(0, near_steps)
        def _(number):
            own_copy(number).start()
            trade(number, 1).start()
            trade(number, 2).start()

        for other in range(trades):
            cot_trade(other).start()

    @pl.when(step == near_steps - 1)
    def _():
        ffn.arrived(1, 2)
        ffn.start(5, 6, 11, 12)

    @pl.when(step == near_steps + near_steps // 2)
    def _():
        ffn.arrived(3, 4)
        ffn.start(7, 8, 13, 14)

    relayed = step - (near_steps - 1)

    @pl.when(jnp.logical_and(relayed >= 0, relayed < near_steps))
    def _():
        trade(relayed, 2).wait_recv()
        trade(relayed, 3).start()
        save(relayed, 2).start()

    query = q_ref[0]
    is_first = first_head(query.shape)

    def partial_of(number, used, carried_top):
        outs, tops = [], []
        for head in range(2):
            mine = is_first if head == 0 else jnp.logical_not(is_first)
            own_query = jnp.where(mine, query, jnp.zeros_like(query))
            scores = [dot_nt(own_query, slots[number, slot, 0]) for slot in used]
            top = scores[0].max(axis=1, keepdims=True)
            for one in scores[1:]:
                top = jnp.maximum(top, one.max(axis=1, keepdims=True))
            if carried_top is not None:
                at = head * HEAD_DIM
                top = jnp.maximum(top, carried_top[:, at : at + 1])
            shift = top * exp_scale
            mixed = None
            for one, slot in zip(scores, used):
                weight = jnp.exp2(one * exp_scale - shift).astype(BF16)
                value = slots[number, slot, 1]
                lane_first = first_head(value.shape)
                lane_mine = lane_first if head == 0 else jnp.logical_not(lane_first)
                term = dot_nn(weight, jnp.where(lane_mine, value, jnp.ones_like(value)))
                mixed = term if mixed is None else mixed + term
            outs.append(mixed)
            tops.append(jnp.broadcast_to(top, mixed.shape))
        acc = jnp.where(is_first, outs[0], outs[1])
        total = pltpu.roll(jnp.where(is_first, outs[1], outs[0]), HEAD_DIM, 1)
        return acc, jnp.where(is_first, tops[0], tops[1]), total

    @pl.when(step < near_steps)
    def _():
        own_copy(step).wait()
        trade(step, 1).wait_recv()
        save(step, 0).start()
        save(step, 1).start()
        acc, top, total = partial_of(step, (0, 1), None)
        acc_all[step] = acc
        top_all[step] = top
        total_all[step] = total

    @pl.when(step >= near_steps)
    def _():
        number = step - near_steps
        trade(number, 3).wait_recv()
        save(number, 3).start()
        carried_top = top_all[number]
        acc, top, total = partial_of(number, (2, 3), carried_top)
        fade = jnp.exp2((carried_top - top) * exp_scale)
        acc = acc + acc_all[number] * fade
        total = total + total_all[number] * fade
        attended = acc / total
        low = attended.astype(BF16)
        low_ref[0] = low
        wide_ref[0] = attended
        log_ref[0] = (top * exp_scale + jnp.log2(total)).T
        term = dot_nt(low, w_ref[...])
        pair = number % pairs

        @pl.when(pair == 0)
        def _():
            mixed_rows[...] = term

        @pl.when(pair > 0)
        def _():
            mixed_rows[...] += term

        @pl.when(pair == pairs - 1)
        def _():
            half = kept_ref.shape[1]
            kept_ref[0] = mixed_rows[:half]
            sent_ref[0] = mixed_rows[half:].astype(BF16)

    @pl.when(step == steps - 1)
    def _():
        ffn.arrived(5, 6)
        ffn.start(15)
        ffn.arrived(7, 8)
        ffn.start(16)

        @pl.loop(0, near_steps)
        def _(number):
            for slot in range(1, 4):
                trade(number, slot).wait_send()
            for slot in range(4):
                save(number, slot).wait()

        for other in range(trades):
            cot_trade(other).wait_send()
            cot_trade(other).wait_recv()
        ffn.arrived(*range(9, MESSAGES))
        ffn.sent(*range(1, MESSAGES))


def attend(queries, own_kv, w_att, cotangent, w_ffn, trades):
    windows, rows, cols = queries.shape
    width = w_att.shape[0]
    pairs = cols // PAIR
    near = windows * pairs
    out_at = 3 * pairs

    def far(i):
        return jnp.maximum(i - near, 0)

    anywhere = pl.BlockSpec(memory_space=pl.ANY)
    wide = pl.BlockSpec((1, rows, PAIR), lambda i: (far(i) // pairs, 0, far(i) % pairs))
    half = pl.BlockSpec((1, rows // 2, width), lambda i: (far(i) // pairs, 0, 0))
    state = pltpu.VMEM((near, rows, PAIR), F32)
    dma = pltpu.SemaphoreType.DMA
    return run(
        functools.partial(attend_kernel, windows, pairs, trades, LOG2E / math.sqrt(HEAD_DIM)),
        "attend",
        [
            shaped((windows, rows, cols), BF16),
            shaped((windows, rows, cols), F32),
            shaped((windows, cols, rows), F32),
            shaped((windows, rows // 2, width), F32),
            shaped((windows, rows // 2, width), BF16),
            shaped((near, 4, 2, rows, PAIR), BF16),
            shaped((trades,) + cotangent.shape, BF16),
            shaped(w_ffn.shape, BF16),
        ],
        64 * windows * rows * rows * cols,
        [queries, w_att, own_kv, cotangent, w_ffn],
        collective_id=0,
        input_output_aliases={4: 7},
        grid=(2 * near,),
        in_specs=[
            pl.BlockSpec((1, rows, PAIR), lambda i: ((i // pairs) % windows, 0, i % pairs)),
            pl.BlockSpec((width, PAIR), lambda i: (0, out_at + far(i) % pairs)),
            anywhere,
            anywhere,
            anywhere,
        ],
        out_specs=[
            wide,
            wide,
            pl.BlockSpec((1, PAIR, rows), lambda i: (far(i) // pairs, far(i) % pairs, 0)),
            half,
            half,
            anywhere,
            anywhere,
            anywhere,
        ],
        scratch_shapes=[
            pltpu.VMEM((near, 4, 2, rows, PAIR), BF16),
            state,
            state,
            state,
            pltpu.VMEM((rows, width), F32),
            dma((near,)),
            dma((near, 3)),
            dma((near, 3)),
            dma((near, 4)),
            dma((trades,)),
            dma((trades,)),
            dma((MESSAGES,)),
            dma((MESSAGES,)),
        ],
    )


def attend_back_kernel(slots, first, grad_blocks, exp_scale, score_scale, *refs):
    refs = list(refs)
    q_ref, wide_ref, log_ref = [refs.pop(0) for _ in range(3)]
    if first:
        grad_refs = [refs.pop(0) for _ in range(grad_blocks)]
        w_ref = refs.pop(0)
    else:
        do_ref = refs.pop(0)
    slots_ref = refs.pop(0)
    if not first:
        dq_in = refs.pop(0)
        cos_ref, sin_ref = refs.pop(0), refs.pop(0)
    dq_ref = refs.pop(0)
    dkv_refs = [refs.pop(0) for _ in range(slots)]
    query = q_ref[0]
    if first:
        do_ref, rows_ref = refs

        @pl.when(pl.program_id(0) == 0)
        def _():
            at_row = 0
            for grad_ref in grad_refs:
                rows_ref[at_row : at_row + grad_ref.shape[0], :] = grad_ref[...]
                at_row += grad_ref.shape[0]

        grad_out = dot_nn(rows_ref[...], w_ref[...]).astype(BF16)
        do_ref[...] = grad_out
    else:
        grad_out = do_ref[...]
    is_first = first_head(query.shape)
    overlap = (grad_out.astype(F32) * wide_ref[0]).T
    logs = log_ref[0]
    zero = jnp.zeros_like(query)
    own_q, own_do, row_log, row_sum = [], [], [], []
    for head in range(2):
        mine = is_first if head == 0 else jnp.logical_not(is_first)
        own_q.append(jnp.where(mine, query, zero))
        own_do.append(jnp.where(mine, grad_out, zero))
        at = head * HEAD_DIM
        row_log.append(logs[at : at + 1, :])
        row_sum.append(jnp.sum(overlap[at : at + HEAD_DIM, :], axis=0, keepdims=True))
    dq_parts = [None, None]
    for slot, dkv_ref in enumerate(dkv_refs):
        key, value = slots_ref[0, slot, 0], slots_ref[0, slot, 1]
        key_turned = key.T
        grad_key, grad_value = None, None
        for head in range(2):
            scores = dot_nt(key, own_q[head])
            probs = jnp.exp2(scores * exp_scale - row_log[head])
            grad_probs = dot_nt(value, own_do[head])
            grad_scores = (probs * (grad_probs - row_sum[head])).astype(BF16)
            term_v = dot_nn(probs.astype(BF16), own_do[head])
            term_k = dot_nn(grad_scores, own_q[head])
            at = head * HEAD_DIM
            term_q = dot_nn(key_turned[at : at + HEAD_DIM, :], grad_scores)
            grad_value = term_v if grad_value is None else grad_value + term_v
            grad_key = term_k if grad_key is None else grad_key + term_k
            dq_parts[head] = term_q if dq_parts[head] is None else dq_parts[head] + term_q
        dkv_ref[0] = (grad_key * score_scale).astype(BF16)
        dkv_ref[1] = grad_value.astype(BF16)
    grad_query = jnp.concatenate(dq_parts, axis=0).T * score_scale
    if not first:
        grad_query = grad_query + dq_in[...]
        grad_query = grad_query * cos_ref[...] - swap_halves(grad_query) * sin_ref[...]
    dq_ref[...] = grad_query.astype(dq_ref.dtype)


def attend_back(window, queries, wide, logs, slots_all, grads, w_att, tables):
    rows, cols = queries.shape[1:]
    keys = rows
    slots = slots_all.shape[1] // 2
    pairs = cols // PAIR
    first = tables is None
    score_scale = 1.0 / math.sqrt(HEAD_DIM)
    row_spec = pl.BlockSpec((rows, PAIR), lambda i: (0, i))
    block = pl.BlockSpec((2, keys, PAIR), lambda i: (0, 0, i))
    stacked = pl.BlockSpec((1, rows, PAIR), lambda i: (window, 0, i))
    in_specs = [stacked] * 2 + [pl.BlockSpec((1, PAIR, rows), lambda i: (window, i, 0))]
    args = [queries, wide, logs]
    out_shape = [shaped((rows, cols), F32 if first else BF16)]
    out_shape += [shaped((2, keys, cols), BF16)] * slots
    out_specs = [row_spec] + [block] * slots
    if first:
        width = w_att.shape[0]
        out_at = 3 * cols // PAIR
        args += [*grads, w_att]
        in_specs += [pl.BlockSpec(grad.shape, lambda i: (0, 0)) for grad in grads]
        in_specs += [pl.BlockSpec((width, PAIR), lambda i: (0, out_at + i))]
        out_shape += [shaped((rows, cols), BF16), shaped((rows, width), BF16)]
        out_specs += [row_spec, pl.BlockSpec((rows, width), lambda i: (0, 0))]
    else:
        args.append(grads[1])
        in_specs.append(row_spec)
    args.append(slots_all)
    half = 1 if first else 0
    in_specs.append(
        pl.BlockSpec((1, slots, 2, keys, PAIR), lambda i: (window * pairs + i, half, 0, 0, 0))
    )
    if not first:
        args += [grads[0], *tables]
        in_specs += [row_spec] + [pl.BlockSpec((rows, PAIR), lambda i: (0, 0))] * 2
    return run(
        functools.partial(
            attend_back_kernel, slots, first, len(grads), score_scale * LOG2E, score_scale
        ),
        "attend_back_far" if first else "attend_back_near",
        out_shape,
        40 * rows * keys * slots * cols,
        args,
        grid=(cols // PAIR,),
        in_specs=in_specs,
        out_specs=out_specs,
    )


def middle_kernel(x_ref, kept_ref, arrived_ref, norms_ref, middle_ref, normed_ref):
    middle = x_ref[...].astype(F32) + (kept_ref[...] + arrived_ref[...].astype(F32))
    middle_ref[...] = middle
    normed_ref[...] = (
        normalise(middle)[0] * norms_ref[2:3, :] + norms_ref[3:4, :]
    ).astype(BF16)


def second_norm(x_rows, kept, arrived, norms):
    return run(
        middle_kernel,
        "second_norm",
        [shaped(kept.shape, F32), shaped(kept.shape, BF16)],
        20 * kept.size,
        [x_rows, kept, arrived, norms],
    )


def feed_kernel(blocks, factor_ref, gate_w_ref, up_w_ref, down_w_ref, *refs):
    x_refs, cot_refs = refs[:blocks], refs[blocks : 2 * blocks]
    x_all, gy_all, hidden_ref, grad_gate_ref, grad_up_ref = refs[2 * blocks : 2 * blocks + 5]
    kept_ref, sent_ref, grad_kept_ref, grad_sent_ref, total, grad_total = refs[2 * blocks + 5 :]
    step = pl.program_id(0)

    @pl.when(step == 0)
    def _():
        at_row = 0
        for x_ref, cot_ref in zip(x_refs, cot_refs):
            rows = slice(at_row, at_row + x_ref.shape[0])
            at_row += x_ref.shape[0]
            x_all[rows, :] = x_ref[...]
            gy_all[rows, :] = (cot_ref[...].astype(F32) * factor_ref[0, 0]).astype(BF16)

    x_rows = x_all[...]
    gate = dot_nn(x_rows, gate_w_ref[...])
    up = dot_nn(x_rows, up_w_ref[...])
    grad_hidden = dot_nn(gy_all[...], down_w_ref[...])
    sig = jax.nn.sigmoid(gate)
    swish = gate * sig
    hidden = (swish * up).astype(BF16)
    grad_gate = (grad_hidden * up * sig * (1.0 + gate * (1.0 - sig))).astype(BF16)
    grad_up = (grad_hidden * swish).astype(BF16)
    hidden_ref[...] = hidden
    grad_gate_ref[...] = grad_gate
    grad_up_ref[...] = grad_up
    grad_term = dot_nt(grad_gate, gate_w_ref[...]) + dot_nt(grad_up, up_w_ref[...])
    term = dot_nt(hidden, down_w_ref[...])

    @pl.when(step == 0)
    def _():
        total[...] = term
        grad_total[...] = grad_term

    @pl.when(step > 0)
    def _():
        total[...] += term
        grad_total[...] += grad_term

    @pl.when(step == pl.num_programs(0) - 1)
    def _():
        half = kept_ref.shape[0]
        kept_ref[...] = total[:half]
        sent_ref[...] = total[half:].astype(BF16)
        grad_kept_ref[...] = grad_total[:half]
        grad_sent_ref[...] = grad_total[half:].astype(BF16)


def feed(x_blocks, cot_blocks, factor, weights):
    width = x_blocks[0].shape[1]
    rows = sum(block.shape[0] for block in x_blocks)
    hidden_cols = weights.shape[1] // 3
    step = min(512, hidden_cols)
    steps = hidden_cols // step
    full = pl.BlockSpec((rows, width), lambda i: (0, 0))
    half = pl.BlockSpec((rows // 2, width), lambda i: (0, 0))
    block = pl.BlockSpec((rows, step), lambda i: (0, i))
    return run(
        functools.partial(feed_kernel, len(x_blocks)),
        "feed",
        [shaped((rows, width), BF16)] * 2
        + [shaped((rows, hidden_cols), BF16)] * 3
        + [shaped((rows // 2, width), F32), shaped((rows // 2, width), BF16)] * 2,
        12 * rows * width * hidden_cols,
        [factor, weights, weights, weights, *x_blocks, *cot_blocks],
        grid=(steps,),
        in_specs=[SCALAR]
        + [
            pl.BlockSpec((width, step), functools.partial(lambda at, i: (0, at + i), k * steps))
            for k in range(3)
        ]
        + [pl.BlockSpec(array.shape, lambda i: (0, 0)) for array in (*x_blocks, *cot_blocks)],
        out_specs=[full] * 2 + [block] * 3 + [half] * 4,
        scratch_shapes=[pltpu.VMEM((rows, width), F32)] * 2,
    )


def weights_kernel(windows, starts, *refs):
    out_ref = refs[-1]
    at = pl.program_id(0)
    for group, (start, stop) in enumerate(starts):
        pairs = refs[2 * windows * group : 2 * windows * (group + 1)]

        @pl.when(jnp.logical_and(at >= start, at < stop))
        def _(pairs=pairs):
            total = None
            for left, right in zip(pairs[:windows], pairs[windows:]):
                term = dot_tn(left[...], right[...])
                total = term if total is None else total + term
            out_ref[...] = total.astype(BF16)


def weight_grads(groups, step, name):
    windows = len(groups[0][0])
    rows, width = groups[0][0][0].shape
    args, in_specs, starts = [], [], []
    at = 0
    for lefts, rights in groups:
        count = rights[0].shape[1] // step
        args += [*lefts, *rights]
        in_specs += [pl.BlockSpec((rows, width), lambda i: (0, 0))] * windows
        in_specs += [
            pl.BlockSpec(
                (rows, step),
                functools.partial(lambda at, count, i: (0, jnp.clip(i - at, 0, count - 1)), at, count),
            )
        ] * windows
        starts.append((at, at + count))
        at += count
    return run(
        functools.partial(weights_kernel, windows, starts),
        name,
        shaped((width, at * step), BF16),
        2 * windows * rows * width * at * step,
        args,
        grid=(at,),
        in_specs=in_specs,
        out_specs=pl.BlockSpec((width, step), lambda i: (0, i)),
    )


def norm_grad(kept_ref, arrived_ref, stream, gain, sums_ref):
    grad_normed = kept_ref[...] + arrived_ref[...].astype(F32)
    normed, inv_std = normalise(stream)
    sums_ref[0:1, :] = jnp.sum(grad_normed * normed, axis=0, keepdims=True)
    sums_ref[1:2, :] = jnp.sum(grad_normed, axis=0, keepdims=True)
    return norm_back(grad_normed, normed, inv_std, gain)


def middle_back_kernel(
    factor_ref, kept_ref, arrived_ref, middle_ref, cot_ref, norms_ref, grad_ref, low_ref, sums_ref
):
    grad_y = cot_ref[...].astype(F32) * factor_ref[0, 0]
    grad = grad_y + norm_grad(
        kept_ref, arrived_ref, middle_ref[...], norms_ref[2:3, :], sums_ref
    )
    grad_ref[...] = grad
    low_ref[...] = grad.astype(BF16)


def second_norm_back(factor, kept, arrived, middle, cot_rows, norms):
    return run(
        middle_back_kernel,
        "second_norm_back",
        [
            shaped(kept.shape, F32),
            shaped(kept.shape, BF16),
            shaped((2, kept.shape[1]), F32),
        ],
        40 * kept.size,
        [factor, kept, arrived, middle, cot_rows, norms],
        in_specs=[SCALAR] + [pl.BlockSpec(memory_space=pltpu.VMEM)] * 5,
    )


def turn_back_kernel(
    dq_ref, own_ref, near_ref, far_ref, cos_ref, sin_ref, w_ref, out_ref, kept_ref, sent_ref
):
    cols = dq_ref.shape[1]
    cosine, sine = cos_ref[...], sin_ref[...]
    out_ref[:, :cols] = dq_ref[...]
    for at in range(0, cols, PAIR):
        part = slice(at, at + PAIR)
        key = (
            own_ref[0, :, part].astype(F32)
            + near_ref[0, :, part].astype(F32)
            + far_ref[0, :, part].astype(F32)
        )
        out_ref[:, cols + at : cols + at + PAIR] = (
            key * cosine - swap_halves(key) * sine
        ).astype(BF16)
    out_ref[:, 2 * cols :] = (
        own_ref[1].astype(F32) + near_ref[1].astype(F32) + far_ref[1].astype(F32)
    ).astype(BF16)
    half = kept_ref.shape[0]
    sent_ref[...] = dot_nt(out_ref[half:, :], w_ref[:, : 3 * cols]).astype(BF16)
    kept_ref[...] = dot_nt(out_ref[:half, :], w_ref[:, : 3 * cols])


def turn_back(grad_query, own, near, far, cosine, sine, w_att):
    rows, cols = grad_query.shape
    width = w_att.shape[0]
    return run(
        turn_back_kernel,
        "turn_back",
        [
            shaped((rows, 3 * cols), BF16),
            shaped((rows // 2, width), F32),
            shaped((rows // 2, width), BF16),
        ],
        6 * rows * cols * width,
        [grad_query, own, near, far, cosine, sine, w_att],
    )


def input_back_kernel(window, kept_ref, arrived_ref, x_ref, grad_ref, norms_ref, *refs):
    out_ref, sums_ref = refs[-2:]
    out_ref[0] = grad_ref[...] + norm_grad(
        kept_ref, arrived_ref, x_ref[...].astype(F32), norms_ref[0:1, :], sums_ref
    )


def first_norm_back(window, windows, kept, arrived, x_rows, grad_middle, norms, earlier):
    rows, width = kept.shape
    args = [kept, arrived, x_rows, grad_middle, norms] + ([] if earlier is None else [earlier])
    whole = [pl.BlockSpec(array.shape, lambda i: (0, 0)) for array in args[:5]]
    return run(
        functools.partial(input_back_kernel, window),
        "first_norm_back",
        [shaped((windows, rows, width), F32), shaped((2, width), F32)],
        40 * rows * width,
        args,
        grid=(1,),
        in_specs=whole + ([] if earlier is None else [pl.BlockSpec(memory_space=pl.ANY)]),
        out_specs=[
            pl.BlockSpec((1, rows, width), lambda i: (window, 0, 0)),
            pl.BlockSpec((2, width), lambda i: (0, 0)),
        ],
        input_output_aliases={} if earlier is None else {5: 0},
    )


def result_kernel(windows, *refs):
    out_ref = refs[-1]
    for w in range(windows):
        middle_ref, kept_ref, arrived_ref = refs[3 * w : 3 * w + 3]
        out_ref[w] = (
            middle_ref[...] + (kept_ref[...] + arrived_ref[...].astype(F32))
        ).astype(BF16)


def results(parts):
    rows, width = parts[0][0].shape
    return run(
        functools.partial(result_kernel, len(parts)),
        "results",
        shaped((len(parts), rows, width), BF16),
        2 * len(parts) * rows * width,
        [array for part in parts for array in part],
    )


def local(
    tokens,
    cotangent,
    species,
    counts,
    species_scale,
    norm1_gain,
    norm1_bias,
    w_query,
    w_key,
    w_value,
    w_out,
    norm2_gain,
    norm2_bias,
    w_gate,
    w_up,
    w_down,
):
    windows_here, own_rows, model_width = tokens.shape
    tensor_size = lax.axis_size("tensor")
    seq_size = lax.axis_size("seq")
    block_rows = own_rows * tensor_size
    head_cols = w_query.shape[1]
    hidden_cols = w_gate.shape[1]
    every = ("dp", "seq", "tensor")
    shards = ("dp", "seq")

    own_at = lax.axis_index("tensor")
    starts = jnp.concatenate(
        [
            lax.iota(jnp.int32, own_rows) + (own_at ^ other) * own_rows
            for other in range(tensor_size)
        ]
    )
    positions = (lax.axis_index("seq") * block_rows + starts).astype(F32)
    cos_half, sin_half = angles(positions, HEAD_DIM)
    cosine = jnp.concatenate([cos_half] * 4, axis=1)
    sine = jnp.concatenate([-sin_half, sin_half] * 2, axis=1)

    labels = lax.broadcasted_iota(jnp.int32, (windows_here, species_scale.shape[0]), 1)
    chosen = jnp.sum(jnp.where(species[:, None] == labels, species_scale[None, :], 0.0), axis=1)
    weighted = counts.astype(F32) * chosen

    lanes = jnp.zeros((8, 128), F32)
    vectors = jnp.stack([norm1_gain, norm1_bias, norm2_gain, norm2_bias])
    tile = lanes.at[:4, : vectors.shape[1]].set(vectors).at[4, :].set(jnp.sum(weighted))
    w_att, w_ffn, norms, arrived_tokens = gather(
        jnp.concatenate([w_query, w_key, w_value, w_out.T], axis=1),
        jnp.concatenate([w_gate, w_up, w_down.T], axis=1),
        tile,
        tokens,
        tensor_size - 1,
    )
    factor = weighted * float(windows_here * lax.axis_size("dp")) / norms[4, 0]

    windows = range(windows_here)
    factors = [factor[w].reshape(1, 1) for w in windows]
    top_bit = seq_size // 2

    token_blocks = [tokens] + [arrived_tokens[other] for other in range(tensor_size - 1)]
    normed_rows, queries, own_kv = project(token_blocks, norms, w_att, cosine, sine)
    attended, wide_attended, logs, kept_all, sent_all, slots_all, cots, w_ffn = attend(
        queries, own_kv, w_att, cotangent, w_ffn, tensor_size - 1
    )
    cot_blocks = [
        [cotangent[w]] + [cots[other, w] for other in range(tensor_size - 1)] for w in windows
    ]
    middles, mid_blocks = [], []
    for w in windows:
        middle, normed_mid = second_norm(
            tokens[w], *scatter_pair(kept_all[w], sent_all[w], "tensor"), norms
        )
        middles.append(middle)
        mid_blocks.append(spread(normed_mid, "tensor"))

    fed = []
    for w in windows:
        blocks = hold(mid_blocks[w], fed[-1] if fed else ())
        fed.append(feed(blocks, cot_blocks[w], factors[w], w_ffn))
    mid_rows, grad_y_rows, hiddens, grad_gates, grad_ups = [
        [one[at] for one in fed] for at in range(5)
    ]
    grad_middles, grad_mid_blocks, second_sums = [], [], []

    def through_second_norm(w, *after):
        kept, arrived = scatter_pair(fed[w][7], fed[w][8], "tensor")
        grad_middle, low, sums = second_norm_back(
            factors[w], hold(kept, *after), arrived, middles[w], cotangent[w], norms
        )
        grad_middles.append(grad_middle)
        grad_mid_blocks.append(spread(low, "tensor"))
        second_sums.append(sums)

    for w in windows[:-1]:
        through_second_norm(w)
    g_ffn_part = weight_grads(
        [
            (mid_rows, grad_gates),
            (mid_rows, grad_ups),
            (grad_y_rows, hold(hiddens, grad_middles)),
        ],
        min(512, hidden_cols),
        "feed_weights",
    )
    g_ffn = lax.psum_scatter(g_ffn_part, shards, scatter_dimension=0, tiled=True).astype(F32)
    through_second_norm(windows[-1], g_ffn_part)

    def fold(blocks, down_to):
        while len(blocks) > down_to:
            half = len(blocks) // 2
            arrived = [swap(block, "seq", half) for block in blocks[half:]]
            blocks = [
                (kept.astype(F32) + new.astype(F32)).astype(BF16)
                for kept, new in zip(blocks[:half], arrived)
            ]
        return blocks

    slots = seq_size // 2
    far_sums, dq_states, grad_mid_rows = [], [], []
    for w in windows:
        query = hold(queries, dq_states[-1][0] if dq_states else grad_middles[-1])
        parts = attend_back(
            w, query, wide_attended, logs, slots_all, grad_mid_blocks[w], w_att, None
        )
        dq_states.append((parts[0], parts[1 + slots]))
        grad_mid_rows.append(parts[2 + slots])
        far_sums.append(swap(fold(list(parts[1 : 1 + slots]), 1)[0], "seq", top_bit))
    result_parts = [
        (middles[w], *scatter_pair(fed[w][5], hold(fed[w][6], dq_states[0]), "tensor"))
        for w in windows
    ]
    grad_queries, near_pairs = [], []
    for w in windows:
        query = hold(queries, grad_queries[-1] if grad_queries else dq_states[-1][0])
        parts = attend_back(
            w, query, wide_attended, logs, slots_all, dq_states[w], None, (cosine, sine)
        )
        grad_queries.append(parts[0])
        blocks = fold(list(parts[1:]), 2)
        near_pairs.append((blocks[0], swap(blocks[1], "seq", 1)))
    output = results(result_parts)

    grad_qkvs, first_parts = [], []
    for w in windows:
        grad_qkv, kept, sent = turn_back(
            grad_queries[w], *near_pairs[w], far_sums[w], cosine, sine, w_att
        )
        grad_qkvs.append(grad_qkv)
        first_parts.append(scatter_pair(kept, sent, "tensor"))
    g_att_part = weight_grads(
        [
            ([normed_rows[w] for w in windows], grad_qkvs),
            (grad_mid_rows, [attended[w] for w in windows]),
        ],
        head_cols,
        "attend_weights",
    )
    g_att = lax.psum_scatter(
        hold(g_att_part, g_ffn), shards, scatter_dimension=0, tiled=True
    ).astype(F32)
    input_grad = None
    first_sums = []
    for w in windows:
        kept, arrived = first_parts[w]
        input_grad, sums = first_norm_back(
            w,
            windows_here,
            hold(kept, g_att_part),
            arrived,
            tokens[w],
            grad_middles[w],
            norms,
            input_grad,
        )
        first_sums.append(sums)

    norm_sums = jnp.concatenate([sum(first_sums), sum(second_sums)], axis=0)
    devices = model_width // norm1_gain.shape[0]
    norm_sums = norm_sums.reshape(4, devices, -1).transpose(1, 0, 2)
    norm_sums = scatter_ordered(norm_sums, every)[0]

    return (
        output,
        input_grad,
        norm_sums[0],
        norm_sums[1],
        g_att[:, :head_cols],
        g_att[:, head_cols : 2 * head_cols],
        g_att[:, 2 * head_cols : 3 * head_cols],
        g_att[:, 3 * head_cols :].T,
        norm_sums[2],
        norm_sums[3],
        g_ffn[:, :hidden_cols],
        g_ffn[:, hidden_cols : 2 * hidden_cols],
        g_ffn[:, 2 * hidden_cols :].T,
    )


def solution(mesh):
    rows = P("dp", ("seq", "tensor"), None)
    vector = P(("dp", "seq", "tensor"))
    tall = P(("dp", "seq"), "tensor")
    flat = P("tensor", ("dp", "seq"))
    return jax.shard_map(
        local,
        mesh=mesh,
        in_specs=(
            rows, rows, P("dp"), P("dp"), P(), vector, vector,
            tall, tall, tall, flat, vector, vector, tall, tall, flat,
        ),
        out_specs=(
            rows, rows, vector, vector, tall, tall, tall, flat,
            vector, vector, tall, tall, flat,
        ),
        check_vma=False,
    )
```

```python
import functools
import math

import jax
import jax.numpy as jnp
from jax import lax
from jax.experimental import pallas as pl
from jax.experimental.pallas import tpu as pltpu
from jax.sharding import PartitionSpec as P

HEAD_DIM = 64
EPSILON = 1e-05
ROPE_BASE = 10000.0
PAIR = 2 * HEAD_DIM
LOG2E = math.log2(math.e)
BF16 = jnp.bfloat16
F32 = jnp.float32
VMEM_BYTES = 56 * 1024 * 1024
MESH = pl.DeviceIdType.MESH


def angles(positions, head_dim):
    half_dim = head_dim // 2
    inverse = jnp.exp(
        -(math.log(ROPE_BASE) * 2.0 / head_dim) * jnp.arange(half_dim, dtype=F32)
    )
    phase_angle = positions[:, None] * inverse[None, :]
    return (jnp.cos(phase_angle), jnp.sin(phase_angle))


def dot_nn(left, right):
    return lax.dot_general(left, right, (((1,), (0,)), ((), ())), preferred_element_type=F32)


def dot_nt(left, right):
    return lax.dot_general(left, right, (((1,), (1,)), ((), ())), preferred_element_type=F32)


def dot_tn(left, right):
    return lax.dot_general(left, right, (((0,), (0,)), ((), ())), preferred_element_type=F32)


def swap(array, axis, bit):
    size = lax.axis_size(axis)
    return lax.ppermute(array, axis, [(i, i ^ bit) for i in range(size)])


def spread(array, axis):
    blocks = [array]
    bit = 1
    while bit < lax.axis_size(axis):
        blocks = blocks + [swap(block, axis, bit) for block in blocks]
        bit *= 2
    return blocks


def scatter_pair(kept, sent, axis):
    return later_pair(kept, swap(sent, axis, lax.axis_size(axis) // 2), axis)


def later_pair(kept, arrived, axis):
    bit = lax.axis_size(axis) // 2
    while bit > 1:
        partial = kept + arrived.astype(F32)
        bit //= 2
        rows = partial.shape[0] // 2
        kept, arrived = partial[:rows], swap(partial[rows:].astype(BF16), axis, bit)
    return kept, arrived


def hold(values, *others):
    return lax.optimization_barrier((values, others))[0]


def run(kernel, name, out_shape, flops, args, collective_id=None, **options):
    trading = {} if collective_id is None else dict(collective_id=collective_id, has_side_effects=True)
    moved = sum(math.prod(array.shape) * array.dtype.itemsize for array in args)
    outs = out_shape if isinstance(out_shape, list) else [out_shape]
    moved += sum(math.prod(array.shape) * array.dtype.itemsize for array in outs)
    return pl.pallas_call(
        kernel,
        out_shape=out_shape,
        compiler_params=pltpu.CompilerParams(vmem_limit_bytes=VMEM_BYTES, **trading),
        cost_estimate=pl.CostEstimate(
            flops=int(flops), bytes_accessed=int(moved), transcendentals=0
        ),
        name=name,
        **options,
    )(*args)


def shaped(shape, dtype):
    return jax.ShapeDtypeStruct(shape, dtype)


SCALAR = pl.BlockSpec(memory_space=pltpu.SMEM)


def normalise(stream):
    row_mean = jnp.mean(stream, axis=-1, keepdims=True)
    centred = stream - row_mean
    variance = jnp.mean(centred * centred, axis=-1, keepdims=True)
    inv_std = lax.rsqrt(variance + EPSILON)
    return centred * inv_std, inv_std


def norm_back(grad_normed, normed, inv_std, norm_gain):
    scaled_grad = grad_normed * norm_gain
    return inv_std * (
        scaled_grad
        - jnp.mean(scaled_grad, axis=-1, keepdims=True)
        - normed * jnp.mean(scaled_grad * normed, axis=-1, keepdims=True)
    )


def first_head(shape):
    return lax.broadcasted_iota(jnp.int32, shape, 1) % PAIR < HEAD_DIM


def swap_halves(values):
    half = HEAD_DIM // 2
    lane = lax.broadcasted_iota(jnp.int32, values.shape, 1)
    ahead = pltpu.roll(values, PAIR - half, 1)
    behind = pltpu.roll(values, half, 1)
    return jnp.where(lane % HEAD_DIM < half, ahead, behind)


def project_kernel(blocks, norms_ref, w_ref, cos_ref, sin_ref, *refs):
    x_refs = refs[:blocks]
    normed_ref, q_ref, kv_ref = refs[blocks:]
    cols = q_ref.shape[2]
    gain, bias = norms_ref[0:1, :], norms_ref[1:2, :]
    at_row = 0
    for x_ref in x_refs:
        rows = slice(at_row, at_row + x_ref.shape[1])
        at_row += x_ref.shape[1]
        normed = (normalise(x_ref[0].astype(F32))[0] * gain + bias).astype(BF16)
        normed_ref[0, rows, :] = normed
        cosine, sine = cos_ref[rows, :], sin_ref[rows, :]
        query = dot_nn(normed, w_ref[:, :cols])
        key = dot_nn(normed, w_ref[:, cols : 2 * cols])
        for at in range(0, cols, PAIR):
            part = slice(at, at + PAIR)
            one = query[:, part]
            q_ref[0, rows, part] = (one * cosine + swap_halves(one) * sine).astype(BF16)
            one = key[:, part]
            kv_ref[0, 0, rows, part] = (one * cosine + swap_halves(one) * sine).astype(BF16)
        kv_ref[0, 1, rows, :] = dot_nn(normed, w_ref[:, 2 * cols : 3 * cols]).astype(BF16)


def project(x_blocks, norms, w_att, cosine, sine):
    windows = x_blocks[0].shape[0]
    width, cols = w_att.shape[0], w_att.shape[1] // 4
    rows = sum(block.shape[1] for block in x_blocks)
    args = [norms, w_att, cosine, sine, *x_blocks]
    return run(
        functools.partial(project_kernel, len(x_blocks)),
        "project",
        [
            shaped((windows, rows, width), BF16),
            shaped((windows, rows, cols), BF16),
            shaped((windows, 2, rows, cols), BF16),
        ],
        6 * windows * rows * width * cols,
        args,
        grid=(windows,),
        in_specs=[pl.BlockSpec(array.shape, lambda i: (0, 0)) for array in args[:4]]
        + [pl.BlockSpec((1,) + block.shape[1:], lambda i: (i, 0, 0)) for block in x_blocks],
        out_specs=[
            pl.BlockSpec((1, rows, width), lambda i: (i, 0, 0)),
            pl.BlockSpec((1, rows, cols), lambda i: (i, 0, 0)),
            pl.BlockSpec((1, 2, rows, cols), lambda i: (i, 0, 0, 0)),
        ],
    )


def flipped(index, mask):
    bit = 1
    while bit <= mask:
        if mask & bit:
            index = index + bit - 2 * bit * ((index // bit) % 2)
        bit *= 2
    return index


def greet(peers):
    barrier = pltpu.get_barrier_semaphore()
    for peer in peers:
        pl.semaphore_signal(barrier, inc=1, device_id=peer, device_id_type=MESH)
    pl.semaphore_wait(barrier, len(peers))


def send(source, target, send_sem, recv_sem, peer):
    return pltpu.make_async_remote_copy(
        src_ref=source,
        dst_ref=target,
        send_sem=send_sem,
        recv_sem=recv_sem,
        device_id=peer,
        device_id_type=MESH,
    )


def half_chip_peers():
    seq, depth = lax.axis_index("seq"), lax.axis_index("dp")
    size = lax.axis_size("dp")
    return {
        "far": {"seq": flipped(seq, 2)},
        "up": {"dp": (depth + 1) % size},
        "down": {"dp": (depth + size - 1) % size},
        "core": {"seq": flipped(seq, 1)},
    }


class Route:
    PARTS = ((0, 0), (3, 0), (1, 0), (2, 0), (0, 1), (3, 1), (1, 1), (2, 1))

    def __init__(self, whole, rows, send_sem, recv_sem, own):
        self.whole, self.rows, self.own = whole, rows, own
        self.send_sem, self.recv_sem = send_sem, recv_sem
        self.seq, self.depth = lax.axis_index("seq"), lax.axis_index("dp")
        self.peers = half_chip_peers()

    def part(self, place):
        turn, other = place
        seq = flipped(self.seq, 2) if other else self.seq
        at = (((self.depth + turn) % lax.axis_size("dp")) * lax.axis_size("seq") + seq) * self.rows
        return self.whole.at[pl.ds(pl.multiple_of(at, self.rows), self.rows), :]

    def message(self, number):
        if number >= 7:
            place, peer = self.PARTS[number - 7], "core"
        else:
            place, peer = (
                ((0, 0), "up"),
                ((0, 0), "down"),
                ((3, 0), "up"),
                ((0, 0), "far"),
                ((3, 0), "far"),
                ((1, 0), "far"),
                ((2, 0), "far"),
            )[number]
        target = self.part(place)
        return send(
            self.own if place == (0, 0) else target,
            target,
            self.send_sem.at[number],
            self.recv_sem.at[number],
            self.peers[peer],
        )

    def start(self, *numbers):
        for number in numbers:
            self.message(number).start()

    def arrived(self, *numbers):
        for number in numbers:
            self.message(number).wait_recv()

    def sent(self, *numbers):
        for number in numbers:
            self.message(number).wait_send()


MESSAGES = 15


def gather_kernel(trades, att_ref, tile_ref, tokens_ref, *refs):
    att_all, norms_ref, tokens_all = refs[:3]
    tiles, pair_of_tiles = refs[3:5]
    att_send, att_recv, tile_send, tile_recv = refs[5:9]
    own_sem, tokens_send, tokens_recv, pair_send, pair_recv = refs[9:]
    tensor = lax.axis_index("tensor")
    others = [{"tensor": flipped(tensor, other + 1)} for other in range(trades)]
    att = Route(att_all, att_ref.shape[0], att_send, att_recv, att_ref)
    tile_rows = tile_ref.shape[0]
    small = Route(tiles, pair_of_tiles.shape[0], tile_send, tile_recv, pair_of_tiles)

    def tokens_trade(other):
        return send(
            tokens_ref,
            tokens_all.at[other],
            tokens_send.at[other],
            tokens_recv.at[other],
            others[other],
        )

    own_rows = pl.ds(pl.multiple_of(tensor * tile_rows, tile_rows), tile_rows)

    def pair_trade(other):
        return send(
            tile_ref,
            pair_of_tiles.at[own_rows, :],
            pair_send.at[other],
            pair_recv.at[other],
            others[other],
        )

    own_copies = [
        pltpu.make_async_copy(att_ref, att.part((0, 0)), own_sem.at[0]),
        pltpu.make_async_copy(tile_ref, pair_of_tiles.at[own_rows, :], own_sem.at[1]),
        pltpu.make_async_copy(pair_of_tiles, small.part((0, 0)), own_sem.at[2]),
    ]

    greet(list(att.peers.values()) + others)
    for other in range(trades):
        pair_trade(other).start()
    own_copies[1].start()
    own_copies[1].wait()
    for other in range(trades):
        pair_trade(other).wait_recv()
    for route in (small, att):
        route.start(0, 1, 3, 7)
    own_copies[0].start()
    own_copies[2].start()
    for other in range(trades):
        tokens_trade(other).start()
    for route in (small, att):
        route.arrived(0)
        route.start(2, 4, 8)
    for route in (small, att):
        route.arrived(3)
        route.start(11)
    for route in (small, att):
        route.arrived(1)
        route.start(5, 9)
    for route in (small, att):
        route.arrived(2)
        route.start(6, 10)
    for route in (small, att):
        route.arrived(4)
        route.start(12)
        route.arrived(5)
        route.start(13)
        route.arrived(6)
        route.start(14)
    for route in (small, att):
        route.arrived(*range(7, MESSAGES))
    own_copies[2].wait()
    shard = norms_ref.shape[1] // (tiles.shape[0] // tile_rows)
    total = None
    for device in range(tiles.shape[0] // tile_rows):
        tile = tiles[device * tile_rows : (device + 1) * tile_rows, :]
        norms_ref[:, device * shard : (device + 1) * shard] = tile[:, :shard]
    for depth in range(lax.axis_size("dp")):
        at = depth * (tiles.shape[0] // lax.axis_size("dp"))
        one = tiles[at + 4 : at + 5, :]
        total = one if total is None else total + one
    norms_ref[4:5, : total.shape[1]] = total
    for route in (att, small):
        route.sent(*range(MESSAGES))
    own_copies[0].wait()
    for other in range(trades):
        pair_trade(other).wait_send()
        tokens_trade(other).wait_recv()
        tokens_trade(other).wait_send()


def gather(att, tile, tokens, trades):
    count = lax.axis_size("dp") * lax.axis_size("seq")
    rows = att.shape[0]
    group = tile.shape[0] * (trades + 1)
    anywhere = pl.BlockSpec(memory_space=pl.ANY)
    vmem = pl.BlockSpec(memory_space=pltpu.VMEM)
    dma = pltpu.SemaphoreType.DMA
    return run(
        functools.partial(gather_kernel, trades),
        "gather",
        [
            shaped((count * rows, att.shape[1]), BF16),
            shaped((tile.shape[0], count * rows), F32),
            shaped((trades,) + tokens.shape, BF16),
        ],
        0,
        [att, tile, tokens],
        collective_id=1,
        in_specs=[vmem, vmem, anywhere],
        out_specs=[anywhere, vmem, anywhere],
        scratch_shapes=[pltpu.VMEM((count * group, 128), F32), pltpu.VMEM((group, 128), F32)]
        + [dma((MESSAGES,))] * 4
        + [dma((3,)), dma((trades,)), dma((trades,)), dma((trades,)), dma((trades,))],
    )


def attend_kernel(windows, pairs, trades, exp_scale, *refs):
    q_ref, w_ref, kv_ref, cot_ref = refs[:4]
    low_ref, wide_ref, log_ref, kept_ref, sent_ref, slots_ref, cots_ref = refs[4:11]
    slots, acc_all, top_all, total_all, mixed_rows = refs[11:16]
    own_sem, send_sem, recv_sem, save_sem, cot_send, cot_recv = refs[16:]
    step = pl.program_id(0)
    near_steps = windows * pairs
    steps = 2 * near_steps
    seq, tensor = lax.axis_index("seq"), lax.axis_index("tensor")
    core_peer = {"seq": flipped(seq, 1)}
    far_peer = {"seq": flipped(seq, 2)}
    cot_peers = [{"tensor": flipped(tensor, other + 1)} for other in range(trades)]

    def piece(number):
        columns = pl.ds(pl.multiple_of((number % pairs) * PAIR, PAIR), PAIR)
        return kv_ref.at[number // pairs, :, :, columns]

    def own_copy(number):
        return pltpu.make_async_copy(piece(number), slots.at[number, 0], own_sem.at[number])

    def trade(number, slot):
        peer = far_peer if slot == 2 else core_peer
        source = slots.at[number, 2] if slot == 3 else piece(number)
        return send(
            source,
            slots.at[number, slot],
            send_sem.at[number, slot - 1],
            recv_sem.at[number, slot - 1],
            peer,
        )

    def cot_trade(other):
        return send(
            cot_ref, cots_ref.at[other], cot_send.at[other], cot_recv.at[other], cot_peers[other]
        )

    def save(number, slot):
        return pltpu.make_async_copy(
            slots.at[number, slot], slots_ref.at[number, slot], save_sem.at[number, slot]
        )

    @pl.when(step == 0)
    def _():
        greet([core_peer, far_peer] + cot_peers)

        @pl.loop(0, near_steps)
        def _(number):
            own_copy(number).start()
            trade(number, 1).start()
            trade(number, 2).start()

        for other in range(trades):
            cot_trade(other).start()

    relayed = step - (near_steps - 1)

    @pl.when(jnp.logical_and(relayed >= 0, relayed < near_steps))
    def _():
        trade(relayed, 2).wait_recv()
        trade(relayed, 3).start()
        save(relayed, 2).start()

    query = q_ref[0]
    is_first = first_head(query.shape)

    def partial_of(number, used, carried_top):
        outs, tops = [], []
        for head in range(2):
            mine = is_first if head == 0 else jnp.logical_not(is_first)
            own_query = jnp.where(mine, query, jnp.zeros_like(query))
            scores = [dot_nt(own_query, slots[number, slot, 0]) for slot in used]
            top = scores[0].max(axis=1, keepdims=True)
            for one in scores[1:]:
                top = jnp.maximum(top, one.max(axis=1, keepdims=True))
            if carried_top is not None:
                at = head * HEAD_DIM
                top = jnp.maximum(top, carried_top[:, at : at + 1])
            shift = top * exp_scale
            mixed = None
            for one, slot in zip(scores, used):
                weight = jnp.exp2(one * exp_scale - shift).astype(BF16)
                value = slots[number, slot, 1]
                lane_first = first_head(value.shape)
                lane_mine = lane_first if head == 0 else jnp.logical_not(lane_first)
                term = dot_nn(weight, jnp.where(lane_mine, value, jnp.ones_like(value)))
                mixed = term if mixed is None else mixed + term
            outs.append(mixed)
            tops.append(jnp.broadcast_to(top, mixed.shape))
        acc = jnp.where(is_first, outs[0], outs[1])
        total = pltpu.roll(jnp.where(is_first, outs[1], outs[0]), HEAD_DIM, 1)
        return acc, jnp.where(is_first, tops[0], tops[1]), total

    @pl.when(step < near_steps)
    def _():
        own_copy(step).wait()
        trade(step, 1).wait_recv()
        save(step, 0).start()
        save(step, 1).start()
        acc, top, total = partial_of(step, (0, 1), None)
        acc_all[step] = acc
        top_all[step] = top
        total_all[step] = total

    @pl.when(step >= near_steps)
    def _():
        number = step - near_steps
        trade(number, 3).wait_recv()
        save(number, 3).start()
        carried_top = top_all[number]
        acc, top, total = partial_of(number, (2, 3), carried_top)
        fade = jnp.exp2((carried_top - top) * exp_scale)
        acc = acc + acc_all[number] * fade
        total = total + total_all[number] * fade
        attended = acc / total
        low = attended.astype(BF16)
        low_ref[0] = low
        wide_ref[0] = attended
        log_ref[0] = (top * exp_scale + jnp.log2(total)).T
        term = dot_nt(low, w_ref[...])
        pair = number % pairs

        @pl.when(pair == 0)
        def _():
            mixed_rows[...] = term

        @pl.when(pair > 0)
        def _():
            mixed_rows[...] += term

        @pl.when(pair == pairs - 1)
        def _():
            half = kept_ref.shape[1]
            kept_ref[0] = mixed_rows[:half]
            sent_ref[0] = mixed_rows[half:].astype(BF16)

    @pl.when(step == steps - 1)
    def _():
        @pl.loop(0, near_steps)
        def _(number):
            for slot in range(1, 4):
                trade(number, slot).wait_send()
            for slot in range(4):
                save(number, slot).wait()

        for other in range(trades):
            cot_trade(other).wait_send()
            cot_trade(other).wait_recv()


def attend(queries, own_kv, w_att, cotangent, trades):
    windows, rows, cols = queries.shape
    width = w_att.shape[0]
    pairs = cols // PAIR
    near = windows * pairs
    out_at = 3 * pairs

    def far(i):
        return jnp.maximum(i - near, 0)

    anywhere = pl.BlockSpec(memory_space=pl.ANY)
    wide = pl.BlockSpec((1, rows, PAIR), lambda i: (far(i) // pairs, 0, far(i) % pairs))
    half = pl.BlockSpec((1, rows // 2, width), lambda i: (far(i) // pairs, 0, 0))
    state = pltpu.VMEM((near, rows, PAIR), F32)
    dma = pltpu.SemaphoreType.DMA
    return run(
        functools.partial(attend_kernel, windows, pairs, trades, LOG2E / math.sqrt(HEAD_DIM)),
        "attend",
        [
            shaped((windows, rows, cols), BF16),
            shaped((windows, rows, cols), F32),
            shaped((windows, cols, rows), F32),
            shaped((windows, rows // 2, width), F32),
            shaped((windows, rows // 2, width), BF16),
            shaped((near, 4, 2, rows, PAIR), BF16),
            shaped((trades,) + cotangent.shape, BF16),
        ],
        64 * windows * rows * rows * cols,
        [queries, w_att, own_kv, cotangent],
        collective_id=0,
        grid=(2 * near,),
        in_specs=[
            pl.BlockSpec((1, rows, PAIR), lambda i: ((i // pairs) % windows, 0, i % pairs)),
            pl.BlockSpec((width, PAIR), lambda i: (0, out_at + far(i) % pairs)),
            anywhere,
            anywhere,
        ],
        out_specs=[
            wide,
            wide,
            pl.BlockSpec((1, PAIR, rows), lambda i: (far(i) // pairs, far(i) % pairs, 0)),
            half,
            half,
            anywhere,
            anywhere,
        ],
        scratch_shapes=[
            pltpu.VMEM((near, 4, 2, rows, PAIR), BF16),
            state,
            state,
            state,
            pltpu.VMEM((rows, width), F32),
            dma((near,)),
            dma((near, 3)),
            dma((near, 3)),
            dma((near, 4)),
            dma((trades,)),
            dma((trades,)),
        ],
    )


def attend_back_kernel(windows, pairs, blocks, exp_scale, score_scale, *refs):
    q_ref, wide_ref, log_ref, slots_ref, w_ref, cos_ref, sin_ref = refs[:7]
    grad_refs = refs[7 : 7 + windows * blocks]
    refs = refs[7 + windows * blocks :]
    sent_refs, refs = refs[:windows], refs[windows:]
    gq_ref, gk_ref, gv_ref, rows_ref = refs[:4]
    arrived_refs, refs = refs[4 : 4 + windows], refs[4 + windows :]
    dq_all, do_all, far_kept, far_sent, far_core, far_x, near_kept, near_sent, near_core = refs[:9]
    send_sem, recv_sem, result_send, result_recv = refs[9:]
    step = pl.program_id(0)
    count = windows * pairs
    seq, tensor = lax.axis_index("seq"), lax.axis_index("tensor")
    core_peer = {"seq": flipped(seq, 1)}
    far_peer = {"seq": flipped(seq, 2)}
    result_peer = {"tensor": flipped(tensor, lax.axis_size("tensor") // 2)}

    def trade(kind, number):
        source, target, peer = (
            (far_sent, far_core, core_peer),
            (far_kept, far_x, far_peer),
            (near_sent, near_core, core_peer),
        )[kind]
        return send(
            source.at[number],
            target.at[number],
            send_sem.at[kind, number],
            recv_sem.at[kind, number],
            peer,
        )

    def result_trade(w):
        return send(
            sent_refs[w], arrived_refs[w], result_send.at[w], result_recv.at[w], result_peer
        )

    @pl.when(step == 0)
    def _():
        greet([core_peer, far_peer, result_peer])
        for w in range(windows):
            result_trade(w).start()

    def at_step(first, body):
        number = step - first

        @pl.when(jnp.logical_and(number >= 0, number < count))
        def _():
            body(number)

    def send_far(number):
        trade(0, number).start()

    def add_far(number):
        trade(0, number).wait_recv()
        far_kept[number] = (
            far_kept[number].astype(F32) + far_core[number].astype(F32)
        ).astype(BF16)

    def send_x(number):
        trade(1, number).start()

    def send_near(number):
        trade(2, number).start()

    def finish(number):
        trade(2, number).wait_recv()
        trade(1, number).wait_recv()
        total = (
            near_kept[number].astype(F32)
            + near_core[number].astype(F32)
            + far_x[number].astype(F32)
        )
        key = total[0]
        gk_ref[0] = (key * cos_ref[...] - swap_halves(key) * sin_ref[...]).astype(BF16)
        gv_ref[0] = total[1].astype(BF16)

    at_step(1, send_far)
    at_step(3, send_x)
    at_step(count + 1, send_near)
    at_step(2, add_far)
    at_step(count + 2, finish)

    for w in range(windows):

        @pl.when(step == w * pairs)
        def _(w=w):
            at_row = 0
            for grad_ref in grad_refs[w * blocks : (w + 1) * blocks]:
                rows_ref[0, at_row : at_row + grad_ref.shape[0], :] = grad_ref[...]
                at_row += grad_ref.shape[0]

    def gradients(number, grad_out, kept, sent):
        query = q_ref[0]
        is_first = first_head(query.shape)
        overlap = (grad_out.astype(F32) * wide_ref[0]).T
        logs = log_ref[0]
        zero = jnp.zeros_like(query)
        own_q, own_do, row_log, row_sum = [], [], [], []
        for head in range(2):
            mine = is_first if head == 0 else jnp.logical_not(is_first)
            own_q.append(jnp.where(mine, query, zero))
            own_do.append(jnp.where(mine, grad_out, zero))
            at = head * HEAD_DIM
            row_log.append(logs[at : at + 1, :])
            row_sum.append(jnp.sum(overlap[at : at + HEAD_DIM, :], axis=0, keepdims=True))
        dq_parts = [None, None]
        for slot, target in enumerate((kept, sent)):
            key, value = slots_ref[0, slot, 0], slots_ref[0, slot, 1]
            key_turned = key.T
            grad_key, grad_value = None, None
            for head in range(2):
                scores = dot_nt(key, own_q[head])
                probs = jnp.exp2(scores * exp_scale - row_log[head])
                grad_probs = dot_nt(value, own_do[head])
                grad_scores = (probs * (grad_probs - row_sum[head])).astype(BF16)
                term_v = dot_nn(probs.astype(BF16), own_do[head])
                term_k = dot_nn(grad_scores, own_q[head])
                at = head * HEAD_DIM
                term_q = dot_nn(key_turned[at : at + HEAD_DIM, :], grad_scores)
                grad_value = term_v if grad_value is None else grad_value + term_v
                grad_key = term_k if grad_key is None else grad_key + term_k
                dq_parts[head] = term_q if dq_parts[head] is None else dq_parts[head] + term_q
            target[number, 0] = (grad_key * score_scale).astype(BF16)
            target[number, 1] = grad_value.astype(BF16)
        return jnp.concatenate(dq_parts, axis=0).T * score_scale

    @pl.when(step < count)
    def _():
        grad_out = dot_nn(rows_ref[0], w_ref[...]).astype(BF16)
        do_all[step] = grad_out
        dq_all[step] = gradients(step, grad_out, far_kept, far_sent)

    @pl.when(jnp.logical_and(step >= count, step < 2 * count))
    def _():
        number = step - count
        grad_query = dq_all[number] + gradients(number, do_all[number], near_kept, near_sent)
        gq_ref[0] = (grad_query * cos_ref[...] - swap_halves(grad_query) * sin_ref[...]).astype(
            BF16
        )

    @pl.when(step == pl.num_programs(0) - 1)
    def _():
        @pl.loop(0, count)
        def _(number):
            for kind in range(3):
                trade(kind, number).wait_send()

        for w in range(windows):
            result_trade(w).wait_send()
            result_trade(w).wait_recv()


def attend_back(queries, wide, logs, slots_all, grad_blocks, w_att, tables, sent):
    windows, rows, cols = queries.shape
    width = w_att.shape[0]
    pairs = cols // PAIR
    count = windows * pairs
    out_at = 3 * pairs
    score_scale = 1.0 / math.sqrt(HEAD_DIM)
    blocks = len(grad_blocks[0])
    grads = [block for one in grad_blocks for block in one]

    def spot(lag, last=None):
        def index(i):
            number = jnp.clip(i - lag, 0, count - 1)
            return (number // pairs, 0, number % pairs)

        return pl.BlockSpec((1, rows, PAIR), index)

    def both(i):
        return jnp.minimum(i, 2 * count - 1) % count

    dma = pltpu.SemaphoreType.DMA
    piece = pltpu.VMEM((count, 2, rows, PAIR), BF16)
    anywhere = pl.BlockSpec(memory_space=pl.ANY)
    return run(
        functools.partial(
            attend_back_kernel, windows, pairs, blocks, score_scale * LOG2E, score_scale
        ),
        "attend_back",
        [shaped((windows, rows, cols), BF16)] * 3
        + [shaped((windows, rows, width), BF16)]
        + [shaped(one.shape, BF16) for one in sent],
        160 * windows * rows * rows * cols,
        [queries, wide, logs, slots_all, w_att, *tables, *grads, *sent],
        collective_id=2,
        grid=(2 * count + 2,),
        in_specs=[
            pl.BlockSpec((1, rows, PAIR), lambda i: (both(i) // pairs, 0, both(i) % pairs)),
            pl.BlockSpec((1, rows, PAIR), lambda i: (both(i) // pairs, 0, both(i) % pairs)),
            pl.BlockSpec((1, PAIR, rows), lambda i: (both(i) // pairs, both(i) % pairs, 0)),
            pl.BlockSpec(
                (1, 2, 2, rows, PAIR),
                lambda i: (both(i), jnp.where(i < count, 1, 0), 0, 0, 0),
            ),
            pl.BlockSpec((width, PAIR), lambda i: (0, out_at + jnp.minimum(i, count - 1) % pairs)),
            pl.BlockSpec((rows, PAIR), lambda i: (0, 0)),
            pl.BlockSpec((rows, PAIR), lambda i: (0, 0)),
        ]
        + [pl.BlockSpec(block.shape, lambda i: (0, 0)) for block in grads]
        + [anywhere] * windows,
        out_specs=[
            spot(count),
            spot(count + 2),
            spot(count + 2),
            pl.BlockSpec((1, rows, width), lambda i: (jnp.minimum(i // pairs, windows - 1), 0, 0)),
        ]
        + [anywhere] * windows,
        scratch_shapes=[pltpu.VMEM((count, rows, PAIR), F32), pltpu.VMEM((count, rows, PAIR), BF16)]
        + [piece] * 7
        + [dma((3, count)), dma((3, count)), dma((windows,)), dma((windows,))],
    )


def middle_kernel(x_ref, kept_ref, arrived_ref, norms_ref, middle_ref, normed_ref):
    middle = x_ref[...].astype(F32) + (kept_ref[...] + arrived_ref[...].astype(F32))
    middle_ref[...] = middle
    normed_ref[...] = (
        normalise(middle)[0] * norms_ref[2:3, :] + norms_ref[3:4, :]
    ).astype(BF16)


def second_norm(x_rows, kept, arrived, norms):
    return run(
        middle_kernel,
        "second_norm",
        [shaped(kept.shape, F32), shaped(kept.shape, BF16)],
        20 * kept.size,
        [x_rows, kept, arrived, norms],
    )


def feed_step(x_rows, gy_rows, w_refs, out_refs):
    gate_w_ref, up_w_ref, down_w_ref = w_refs
    hidden_ref, grad_gate_ref, grad_up_ref = out_refs
    gate = dot_nn(x_rows, gate_w_ref[...])
    up = dot_nn(x_rows, up_w_ref[...])
    grad_hidden = dot_nn(gy_rows, down_w_ref[...])
    sig = jax.nn.sigmoid(gate)
    swish = gate * sig
    hidden = (swish * up).astype(BF16)
    grad_gate = (grad_hidden * up * sig * (1.0 + gate * (1.0 - sig))).astype(BF16)
    grad_up = (grad_hidden * swish).astype(BF16)
    hidden_ref[...] = hidden
    grad_gate_ref[...] = grad_gate
    grad_up_ref[...] = grad_up
    grad_term = dot_nt(grad_gate, gate_w_ref[...]) + dot_nt(grad_up, up_w_ref[...])
    return dot_nt(hidden, down_w_ref[...]), grad_term


def feed_first_kernel(blocks, factor_ref, *refs):
    w_refs, refs = refs[:3], refs[3:]
    x_refs, cot_refs = refs[:blocks], refs[blocks : 2 * blocks]
    x_all, gy_all = refs[2 * blocks : 2 * blocks + 2]
    total, grad_total = refs[2 * blocks + 5 :]
    step = pl.program_id(0)

    @pl.when(step == 0)
    def _():
        at_row = 0
        for x_ref, cot_ref in zip(x_refs, cot_refs):
            rows = slice(at_row, at_row + x_ref.shape[0])
            at_row += x_ref.shape[0]
            x_all[rows, :] = x_ref[...]
            gy_all[rows, :] = (cot_ref[...].astype(F32) * factor_ref[0, 0]).astype(BF16)

    term, grad_term = feed_step(
        x_all[...], gy_all[...], w_refs, refs[2 * blocks + 2 : 2 * blocks + 5]
    )

    @pl.when(step == 0)
    def _():
        total[...] = term
        grad_total[...] = grad_term

    @pl.when(step > 0)
    def _():
        total[...] += term
        grad_total[...] += grad_term


def feed_last_kernel(*refs):
    w_refs = refs[:3]
    x_ref, gy_ref, total_in, grad_in = refs[3:7]
    kept_ref, sent_ref, grad_kept_ref, grad_sent_ref, total, grad_total = refs[13:]
    step = pl.program_id(0)
    term, grad_term = feed_step(x_ref[...], gy_ref[...], w_refs, refs[10:13])

    @pl.when(step == 0)
    def _():
        total[...] = total_in[...] + term
        grad_total[...] = grad_in[...] + grad_term

    @pl.when(step > 0)
    def _():
        total[...] += term
        grad_total[...] += grad_term

    @pl.when(step == pl.num_programs(0) - 1)
    def _():
        half = kept_ref.shape[0]
        kept_ref[...] = total[:half]
        sent_ref[...] = total[half:].astype(BF16)
        grad_kept_ref[...] = grad_total[:half]
        grad_sent_ref[...] = grad_total[half:].astype(BF16)


def feed_specs(weights):
    width, part_cols = weights.shape[0], weights.shape[1] // 3
    step = min(512, part_cols)
    steps = part_cols // step
    specs = [
        pl.BlockSpec((width, step), functools.partial(lambda at, i: (0, at + i), k * steps))
        for k in range(3)
    ]
    return step, steps, specs


def feed_first(x_blocks, cot_blocks, factor, weights):
    width = x_blocks[0].shape[1]
    rows = sum(block.shape[0] for block in x_blocks)
    step, steps, w_specs = feed_specs(weights)
    hidden_cols = 2 * step * steps
    full = pl.BlockSpec((rows, width), lambda i: (0, 0))
    return run(
        functools.partial(feed_first_kernel, len(x_blocks)),
        "feed_first",
        [shaped((rows, width), BF16)] * 2
        + [shaped((rows, hidden_cols), BF16)] * 3
        + [shaped((rows, width), F32)] * 2,
        6 * rows * width * hidden_cols,
        [factor, weights, weights, weights, *x_blocks, *cot_blocks],
        grid=(steps,),
        in_specs=[SCALAR]
        + w_specs
        + [pl.BlockSpec(array.shape, lambda i: (0, 0)) for array in (*x_blocks, *cot_blocks)],
        out_specs=[full] * 2 + [pl.BlockSpec((rows, step), lambda i: (0, i))] * 3 + [full] * 2,
    )


def feed_last(x_rows, gy_rows, totals, earlier, weights):
    rows, width = x_rows.shape
    step, steps, w_specs = feed_specs(weights)
    hidden_cols = 2 * step * steps
    full = pl.BlockSpec((rows, width), lambda i: (0, 0))
    half = pl.BlockSpec((rows // 2, width), lambda i: (0, 0))
    return run(
        feed_last_kernel,
        "feed_last",
        [shaped((rows, hidden_cols), BF16)] * 3
        + [shaped((rows // 2, width), F32), shaped((rows // 2, width), BF16)] * 2,
        6 * rows * width * hidden_cols,
        [weights, weights, weights, x_rows, gy_rows, *totals, *earlier],
        grid=(steps,),
        in_specs=w_specs + [full] * 4 + [pl.BlockSpec(memory_space=pl.ANY)] * 3,
        out_specs=[pl.BlockSpec((rows, step), lambda i: (0, steps + i))] * 3 + [half] * 4,
        scratch_shapes=[pltpu.VMEM((rows, width), F32)] * 2,
        input_output_aliases={7: 0, 8: 1, 9: 2},
    )


def weights_kernel(windows, starts, *refs):
    out_ref = refs[-1]
    at = pl.program_id(0)
    for group, (start, stop) in enumerate(starts):
        pairs = refs[2 * windows * group : 2 * windows * (group + 1)]

        @pl.when(jnp.logical_and(at >= start, at < stop))
        def _(pairs=pairs):
            total = None
            for left, right in zip(pairs[:windows], pairs[windows:]):
                term = dot_tn(left[...], right[...])
                total = term if total is None else total + term
            out_ref[...] = total.astype(BF16)


def weight_grads(groups, step, name, first=0, parts=1):
    windows = len(groups[0][0])
    rows, width = groups[0][0][0].shape
    args, in_specs, starts = [], [], []
    at = 0
    for lefts, rights in groups:
        count = rights[0].shape[1] // (step * parts)
        args += [*lefts, *rights]
        in_specs += [pl.BlockSpec((rows, width), lambda i: (0, 0))] * windows
        in_specs += [
            pl.BlockSpec(
                (rows, step),
                functools.partial(
                    lambda at, count, i: (0, first * count + jnp.clip(i - at, 0, count - 1)),
                    at,
                    count,
                ),
            )
        ] * windows
        starts.append((at, at + count))
        at += count
    return run(
        functools.partial(weights_kernel, windows, starts),
        name,
        shaped((width, at * step), BF16),
        2 * windows * rows * width * at * step,
        args,
        grid=(at,),
        in_specs=in_specs,
        out_specs=pl.BlockSpec((width, step), lambda i: (0, i)),
    )


def norm_grad(kept_ref, arrived_ref, stream, gain, sums_ref):
    grad_normed = kept_ref[...] + arrived_ref[...].astype(F32)
    normed, inv_std = normalise(stream)
    sums_ref[0:1, :] = jnp.sum(grad_normed * normed, axis=0, keepdims=True)
    sums_ref[1:2, :] = jnp.sum(grad_normed, axis=0, keepdims=True)
    return norm_back(grad_normed, normed, inv_std, gain)


def middle_back_kernel(
    factor_ref, kept_ref, arrived_ref, middle_ref, cot_ref, norms_ref, grad_ref, low_ref, sums_ref
):
    grad_y = cot_ref[...].astype(F32) * factor_ref[0, 0]
    grad = grad_y + norm_grad(
        kept_ref, arrived_ref, middle_ref[...], norms_ref[2:3, :], sums_ref
    )
    grad_ref[...] = grad
    low_ref[...] = grad.astype(BF16)


def second_norm_back(factor, kept, arrived, middle, cot_rows, norms):
    return run(
        middle_back_kernel,
        "second_norm_back",
        [
            shaped(kept.shape, F32),
            shaped(kept.shape, BF16),
            shaped((2, kept.shape[1]), F32),
        ],
        40 * kept.size,
        [factor, kept, arrived, middle, cot_rows, norms],
        in_specs=[SCALAR] + [pl.BlockSpec(memory_space=pltpu.VMEM)] * 5,
    )


def turn_back_kernel(gq_ref, gk_ref, gv_ref, w_ref, kept_ref, sent_ref):
    cols = gq_ref.shape[2]
    half = kept_ref.shape[0]

    def rows_of(part):
        total = None
        for at, ref in enumerate((gq_ref, gk_ref, gv_ref)):
            term = dot_nt(ref[0, part, :], w_ref[:, at * cols : (at + 1) * cols])
            total = term if total is None else total + term
        return total

    sent_ref[...] = rows_of(slice(half, 2 * half)).astype(BF16)
    kept_ref[...] = rows_of(slice(0, half))


def turn_back(window, grads, w_att):
    windows, rows, cols = grads[0].shape
    width = w_att.shape[0]
    half = pl.BlockSpec((rows // 2, width), lambda i: (0, 0))
    return run(
        turn_back_kernel,
        "turn_back",
        [shaped((rows // 2, width), F32), shaped((rows // 2, width), BF16)],
        6 * rows * cols * width,
        [*grads, w_att],
        grid=(1,),
        in_specs=[pl.BlockSpec((1, rows, cols), lambda i: (window, 0, 0))] * 3
        + [pl.BlockSpec((width, 3 * cols), lambda i: (0, 0))],
        out_specs=[half, half],
    )


def input_back_kernel(window, kept_ref, arrived_ref, x_ref, grad_ref, norms_ref, *refs):
    out_ref, sums_ref = refs[-2:]
    out_ref[0] = grad_ref[...] + norm_grad(
        kept_ref, arrived_ref, x_ref[...].astype(F32), norms_ref[0:1, :], sums_ref
    )


def first_norm_back(window, windows, kept, arrived, x_rows, grad_middle, norms, earlier):
    rows, width = kept.shape
    args = [kept, arrived, x_rows, grad_middle, norms] + ([] if earlier is None else [earlier])
    whole = [pl.BlockSpec(array.shape, lambda i: (0, 0)) for array in args[:5]]
    return run(
        functools.partial(input_back_kernel, window),
        "first_norm_back",
        [shaped((windows, rows, width), F32), shaped((2, width), F32)],
        40 * rows * width,
        args,
        grid=(1,),
        in_specs=whole + ([] if earlier is None else [pl.BlockSpec(memory_space=pl.ANY)]),
        out_specs=[
            pl.BlockSpec((1, rows, width), lambda i: (window, 0, 0)),
            pl.BlockSpec((2, width), lambda i: (0, 0)),
        ],
        input_output_aliases={} if earlier is None else {5: 0},
    )


class SumRoute:
    def __init__(self, part, rows, core_in, mine, x_in, z_in, send_sem, recv_sem):
        self.read, self.rows = part, rows
        self.core_in, self.mine, self.x_in, self.z_in = core_in, mine, x_in, z_in
        self.send_sem, self.recv_sem = send_sem, recv_sem
        self.seq, self.depth = lax.axis_index("seq"), lax.axis_index("dp")
        self.peers = half_chip_peers()

    def place(self, number, other_core):
        seq = flipped(self.seq, 2) if number >= 4 else self.seq
        seq = flipped(seq, 1) if other_core else seq
        turn = (self.depth + number % 4) % lax.axis_size("dp")
        return pl.ds(
            pl.multiple_of((turn * lax.axis_size("seq") + seq) * self.rows, self.rows), self.rows
        )

    def message(self, number):
        if number < 8:
            source, target, peer = self.read.at[self.place(number, True), :], self.core_in, "core"
            target = target.at[number]
        elif number < 12:
            source, target, peer = self.mine.at[number - 4], self.x_in.at[number - 8], "far"
        else:
            turn, peer = ((2, "up"), (1, "up"), (3, "down"))[number - 12]
            source, target = self.mine.at[turn], self.z_in.at[number - 12]
        return send(
            source, target, self.send_sem.at[number], self.recv_sem.at[number], self.peers[peer]
        )

    def start(self, *numbers):
        for number in numbers:
            self.message(number).start()

    def add_core(self, number):
        self.message(number).wait_recv()
        own = self.read[self.place(number, False), :].astype(F32)
        self.mine[number] = (own + self.core_in[number].astype(F32)).astype(self.mine.dtype)

    def add_x(self, number):
        self.message(8 + number).wait_recv()
        total = self.mine[number].astype(F32) + self.x_in[number].astype(F32)
        self.mine[number] = total.astype(self.mine.dtype)

    def add_up(self):
        self.message(12).wait_recv()
        total = self.mine[1].astype(F32) + self.z_in[0].astype(F32)
        self.mine[1] = total.astype(self.mine.dtype)

    def total(self):
        self.message(13).wait_recv()
        self.message(14).wait_recv()
        return (
            self.mine[0].astype(F32) + self.z_in[1].astype(F32) + self.z_in[2].astype(F32)
        )

    def sent(self):
        for number in range(SUM_MESSAGES):
            self.message(number).wait_send()


SUM_MESSAGES = 15


def reduce_kernel(trades, windows, part_ref, *refs):
    first_refs, second_refs = refs[:windows], refs[windows : 2 * windows]
    out_ref, vectors_ref = refs[2 * windows : 2 * windows + 2]
    refs = refs[2 * windows + 2 :]
    tiles, own_tiles, arrived_tiles = refs[:3]
    big = refs[3:9]
    small = refs[9:15]
    tile_send, tile_recv = refs[15:]
    tensor = lax.axis_index("tensor")
    others = [{"tensor": flipped(tensor, other + 1)} for other in range(trades)]
    shards = lax.axis_size("dp") * lax.axis_size("seq")
    devices = shards * (trades + 1)
    group = tiles.shape[0] // shards
    routes = (
        SumRoute(tiles, group, *small),
        SumRoute(part_ref, part_ref.shape[0] // shards, *big),
    )
    small_route, big_route = routes
    first = sum(ref[...] for ref in first_refs)
    second = sum(ref[...] for ref in second_refs)
    span = first.shape[1] // devices
    tiles[...] = jnp.zeros_like(tiles)
    for device in range(devices):
        at = device * 8
        part = slice(device * span, (device + 1) * span)
        tiles[at : at + 2, :span] = first[:, part]
        tiles[at + 2 : at + 4, :span] = second[:, part]
    greet(list(big_route.peers.values()) + others)
    small_route.start(6, 5, 7, 4, 2, 1, 3, 0)
    big_route.start(6, 5, 7, 4, 2, 1, 3, 0)
    for number in (6, 5, 7, 4, 2, 1, 3, 0):
        small_route.add_core(number)
    big_route.add_core(6)
    small_route.start(10, 9, 11, 8)
    big_route.add_core(5)
    big_route.start(10)
    big_route.add_core(7)
    big_route.start(9)
    big_route.add_core(4)
    big_route.start(11)
    big_route.add_core(2)
    big_route.start(8)
    for number in (2, 1, 3, 0):
        small_route.add_x(number)
    big_route.add_core(1)
    small_route.start(12, 14)
    big_route.add_core(3)
    big_route.add_core(0)
    small_route.add_up()
    big_route.add_x(2)
    small_route.start(13)
    own = small_route.total()
    big_route.start(12)
    own_tiles[...] = own
    big_route.add_x(1)
    big_route.add_up()
    out_ref[...] = jnp.zeros_like(out_ref)
    big_route.start(13)
    big_route.add_x(3)
    out_ref[...] = jnp.zeros_like(out_ref)
    big_route.start(14)
    big_route.add_x(0)
    out_ref[...] = big_route.total()

    def tile_trade(other):
        rows = pl.ds(pl.multiple_of(flipped(tensor, other + 1) * 8, 8), 8)
        return send(
            own_tiles.at[rows, :],
            arrived_tiles.at[other],
            tile_send.at[other],
            tile_recv.at[other],
            others[other],
        )

    for other in range(trades):
        tile_trade(other).start()
    vectors = own_tiles[pl.ds(pl.multiple_of(tensor * 8, 8), 8), :]
    for other in range(trades):
        tile_trade(other).wait_recv()
        vectors = vectors + arrived_tiles[other]
    vectors_ref[...] = vectors
    for route in routes:
        route.sent()
    for other in range(trades):
        tile_trade(other).wait_send()


def reduce_grads(part, first_sums, second_sums, trades):
    shards = lax.axis_size("dp") * lax.axis_size("seq")
    rows, cols = part.shape[0] // shards, part.shape[1]
    group = 8 * (trades + 1)
    windows = len(first_sums)
    dma = pltpu.SemaphoreType.DMA

    def buffers(shape, dtype):
        return [pltpu.VMEM((count,) + shape, dtype) for count in (8, 8, 4, 3)] + [
            dma((SUM_MESSAGES,)),
            dma((SUM_MESSAGES,)),
        ]

    return run(
        functools.partial(reduce_kernel, trades, windows),
        "reduce_grads",
        [shaped((rows, cols), F32), shaped((8, 128), F32)],
        0,
        [part, *first_sums, *second_sums],
        collective_id=3,
        scratch_shapes=[
            pltpu.VMEM((shards * group, 128), F32),
            pltpu.VMEM((group, 128), F32),
            pltpu.VMEM((trades, 8, 128), F32),
        ]
        + buffers((rows, cols), BF16)
        + buffers((group, 128), F32)
        + [dma((trades,)), dma((trades,))],
    )


def result_kernel(windows, *refs):
    out_ref = refs[-1]
    for w in range(windows):
        middle_ref, kept_ref, arrived_ref = refs[3 * w : 3 * w + 3]
        out_ref[w] = (
            middle_ref[...] + (kept_ref[...] + arrived_ref[...].astype(F32))
        ).astype(BF16)


def results(parts):
    rows, width = parts[0][0].shape
    return run(
        functools.partial(result_kernel, len(parts)),
        "results",
        shaped((len(parts), rows, width), BF16),
        2 * len(parts) * rows * width,
        [array for part in parts for array in part],
    )


def local(
    tokens,
    cotangent,
    species,
    counts,
    species_scale,
    norm1_gain,
    norm1_bias,
    w_query,
    w_key,
    w_value,
    w_out,
    norm2_gain,
    norm2_bias,
    w_gate,
    w_up,
    w_down,
):
    windows_here, own_rows, model_width = tokens.shape
    tensor_size = lax.axis_size("tensor")
    seq_size = lax.axis_size("seq")
    block_rows = own_rows * tensor_size
    head_cols = w_query.shape[1]
    hidden_cols = w_gate.shape[1]
    shards = ("dp", "seq")

    own_at = lax.axis_index("tensor")
    starts = jnp.concatenate(
        [
            lax.iota(jnp.int32, own_rows) + (own_at ^ other) * own_rows
            for other in range(tensor_size)
        ]
    )
    positions = (lax.axis_index("seq") * block_rows + starts).astype(F32)
    cos_half, sin_half = angles(positions, HEAD_DIM)
    cosine = jnp.concatenate([cos_half] * 4, axis=1)
    sine = jnp.concatenate([-sin_half, sin_half] * 2, axis=1)

    labels = lax.broadcasted_iota(jnp.int32, (windows_here, species_scale.shape[0]), 1)
    chosen = jnp.sum(jnp.where(species[:, None] == labels, species_scale[None, :], 0.0), axis=1)
    weighted = counts.astype(F32) * chosen

    lanes = jnp.zeros((8, 128), F32)
    vectors = jnp.stack([norm1_gain, norm1_bias, norm2_gain, norm2_bias])
    tile = lanes.at[:4, : vectors.shape[1]].set(vectors).at[4, :].set(jnp.sum(weighted))
    part = hidden_cols // 2
    turned = w_down.T
    first_ffn = jnp.concatenate([w_gate[:, :part], w_up[:, :part], turned[:, :part]], axis=1)
    last_ffn = jnp.concatenate([w_gate[:, part:], w_up[:, part:], turned[:, part:]], axis=1)
    first_ffn = lax.all_gather(first_ffn, shards, axis=0, tiled=True)
    w_att, norms, arrived_tokens = gather(
        jnp.concatenate([w_query, w_key, w_value, w_out.T], axis=1),
        tile,
        tokens,
        tensor_size - 1,
    )
    factor = weighted * float(windows_here * lax.axis_size("dp")) / norms[4, 0]

    windows = range(windows_here)
    factors = [factor[w].reshape(1, 1) for w in windows]
    top_bit = seq_size // 2

    token_blocks = [tokens] + [arrived_tokens[other] for other in range(tensor_size - 1)]
    normed_rows, queries, own_kv = project(token_blocks, norms, w_att, cosine, sine)
    attended, wide_attended, logs, kept_all, sent_all, slots_all, cots = attend(
        queries, own_kv, w_att, cotangent, tensor_size - 1
    )
    last_ffn = lax.all_gather(hold(last_ffn, kept_all), shards, axis=0, tiled=True)
    cot_blocks = [
        [cotangent[w]] + [cots[other, w] for other in range(tensor_size - 1)] for w in windows
    ]
    middles, mid_blocks = [], []
    for w in windows:
        middle, normed_mid = second_norm(
            tokens[w], *scatter_pair(kept_all[w], sent_all[w], "tensor"), norms
        )
        middles.append(middle)
        mid_blocks.append(spread(normed_mid, "tensor"))

    begun = []
    for w in windows:
        blocks = hold(mid_blocks[w], begun[-1] if begun else ())
        begun.append(feed_first(blocks, cot_blocks[w], factors[w], first_ffn))
    step = min(512, part)

    def feed_weights(done, half):
        return weight_grads(
            [
                ([one[0] for one in done], [one[3] for one in done]),
                ([one[0] for one in done], [one[4] for one in done]),
                ([one[1] for one in done], [one[2] for one in done]),
            ],
            step,
            "feed_weights",
            half,
            2,
        )

    g_first_part = feed_weights(begun, 0)
    g_first = lax.psum_scatter(g_first_part, shards, scatter_dimension=0, tiled=True)
    fed = []
    for w in windows:
        x_rows, gy_rows, *parts = hold(begun[w], fed[-1] if fed else g_first_part)
        ended = feed_last(x_rows, gy_rows, parts[3:], parts[:3], last_ffn)
        fed.append((x_rows, gy_rows, *ended))
    grad_middles, grad_mid_blocks, second_sums = [], [], []

    def through_second_norm(w, *after):
        kept, arrived = scatter_pair(fed[w][7], fed[w][8], "tensor")
        grad_middle, low, sums = second_norm_back(
            factors[w], hold(kept, *after), arrived, middles[w], cotangent[w], norms
        )
        grad_middles.append(grad_middle)
        grad_mid_blocks.append(spread(low, "tensor"))
        second_sums.append(sums)

    for w in windows[:-1]:
        through_second_norm(w)
    g_ffn_part = feed_weights(hold(fed, grad_middles), 1)
    g_last = lax.psum_scatter(g_ffn_part, shards, scatter_dimension=0, tiled=True)
    through_second_norm(windows[-1], g_ffn_part)

    grad_q, grad_k, grad_v, grad_mid_rows, *arrived_results = attend_back(
        hold(queries, g_ffn_part),
        wide_attended,
        logs,
        slots_all,
        grad_mid_blocks,
        w_att,
        (cosine, sine),
        [fed[w][6] for w in windows],
    )
    output = results(
        [
            (middles[w], *later_pair(fed[w][5], arrived_results[w], "tensor"))
            for w in windows
        ]
    )

    first_parts = []
    for w in windows:
        kept, sent = turn_back(w, (grad_q, grad_k, grad_v), w_att)
        first_parts.append(scatter_pair(kept, sent, "tensor"))
    g_att_part = weight_grads(
        [
            ([normed_rows[w] for w in windows], [grad[w] for w in windows])
            for grad in (grad_q, grad_k, grad_v)
        ]
        + [([grad_mid_rows[w] for w in windows], [attended[w] for w in windows])],
        head_cols,
        "attend_weights",
    )
    input_grad = None
    first_sums = []
    for w in windows:
        kept, arrived = first_parts[w]
        input_grad, sums = first_norm_back(
            w,
            windows_here,
            hold(kept, g_att_part),
            arrived,
            tokens[w],
            grad_middles[w],
            norms,
            input_grad,
        )
        first_sums.append(sums)

    g_att, vectors = reduce_grads(g_att_part, first_sums, second_sums, tensor_size - 1)
    norm_sums = vectors[:4, : norm1_gain.shape[0]]
    ffn_grads = [
        jnp.concatenate(
            [g_first[:, at * part : (at + 1) * part], g_last[:, at * part : (at + 1) * part]],
            axis=1,
        ).astype(F32)
        for at in range(3)
    ]

    return (
        output,
        input_grad,
        norm_sums[0],
        norm_sums[1],
        g_att[:, :head_cols],
        g_att[:, head_cols : 2 * head_cols],
        g_att[:, 2 * head_cols : 3 * head_cols],
        g_att[:, 3 * head_cols :].T,
        norm_sums[2],
        norm_sums[3],
        ffn_grads[0],
        ffn_grads[1],
        ffn_grads[2].T,
    )


def solution(mesh):
    rows = P("dp", ("seq", "tensor"), None)
    vector = P(("dp", "seq", "tensor"))
    tall = P(("dp", "seq"), "tensor")
    flat = P("tensor", ("dp", "seq"))
    return jax.shard_map(
        local,
        mesh=mesh,
        in_specs=(
            rows, rows, P("dp"), P("dp"), P(), vector, vector,
            tall, tall, tall, flat, vector, vector, tall, tall, flat,
        ),
        out_specs=(
            rows, rows, vector, vector, tall, tall, tall, flat,
            vector, vector, tall, tall, flat,
        ),
        check_vma=False,
    )
```

```python
import functools
import math

import jax
import jax.numpy as jnp
from jax import lax
from jax.experimental import pallas as pl
from jax.experimental.pallas import tpu as pltpu
from jax.sharding import PartitionSpec as P

HEAD_DIM = 64
EPSILON = 1e-05
ROPE_BASE = 10000.0
PAIR = 2 * HEAD_DIM
LOG2E = math.log2(math.e)
BF16 = jnp.bfloat16
F32 = jnp.float32
VMEM_BYTES = 56 * 1024 * 1024
MESH = pl.DeviceIdType.MESH


def angles(positions, head_dim):
    half_dim = head_dim // 2
    inverse = jnp.exp(
        -(math.log(ROPE_BASE) * 2.0 / head_dim) * jnp.arange(half_dim, dtype=F32)
    )
    phase_angle = positions[:, None] * inverse[None, :]
    return (jnp.cos(phase_angle), jnp.sin(phase_angle))


def dot_nn(left, right):
    return lax.dot_general(left, right, (((1,), (0,)), ((), ())), preferred_element_type=F32)


def dot_nt(left, right):
    return lax.dot_general(left, right, (((1,), (1,)), ((), ())), preferred_element_type=F32)


def dot_tn(left, right):
    return lax.dot_general(left, right, (((0,), (0,)), ((), ())), preferred_element_type=F32)


def swap(array, axis, bit):
    size = lax.axis_size(axis)
    return lax.ppermute(array, axis, [(i, i ^ bit) for i in range(size)])


def spread(array, axis):
    blocks = [array]
    bit = 1
    while bit < lax.axis_size(axis):
        blocks = blocks + [swap(block, axis, bit) for block in blocks]
        bit *= 2
    return blocks


def scatter_pair(kept, sent, axis):
    return later_pair(kept, swap(sent, axis, lax.axis_size(axis) // 2), axis)


def later_pair(kept, arrived, axis):
    bit = lax.axis_size(axis) // 2
    while bit > 1:
        partial = kept + arrived.astype(F32)
        bit //= 2
        rows = partial.shape[0] // 2
        kept, arrived = partial[:rows], swap(partial[rows:].astype(BF16), axis, bit)
    return kept, arrived


def hold(values, *others):
    return lax.optimization_barrier((values, others))[0]


def run(kernel, name, out_shape, flops, args, collective_id=None, **options):
    trading = {} if collective_id is None else dict(collective_id=collective_id, has_side_effects=True)
    moved = sum(math.prod(array.shape) * array.dtype.itemsize for array in args)
    outs = out_shape if isinstance(out_shape, list) else [out_shape]
    moved += sum(math.prod(array.shape) * array.dtype.itemsize for array in outs)
    return pl.pallas_call(
        kernel,
        out_shape=out_shape,
        compiler_params=pltpu.CompilerParams(vmem_limit_bytes=VMEM_BYTES, **trading),
        cost_estimate=pl.CostEstimate(
            flops=int(flops), bytes_accessed=int(moved), transcendentals=0
        ),
        name=name,
        **options,
    )(*args)


def shaped(shape, dtype):
    return jax.ShapeDtypeStruct(shape, dtype)


SCALAR = pl.BlockSpec(memory_space=pltpu.SMEM)


def plane(operand, block=None, index=None):
    array, at = operand if isinstance(operand, tuple) else (operand, ())
    shape = array.shape[len(at) :] if block is None else block
    place = (lambda *i: (0,) * len(shape)) if index is None else index
    return array, pl.BlockSpec((None,) * len(at) + tuple(shape), lambda *i: at + place(*i))


def normalise(stream):
    row_mean = jnp.mean(stream, axis=-1, keepdims=True)
    centred = stream - row_mean
    variance = jnp.mean(centred * centred, axis=-1, keepdims=True)
    inv_std = lax.rsqrt(variance + EPSILON)
    return centred * inv_std, inv_std


def norm_back(grad_normed, normed, inv_std, norm_gain):
    scaled_grad = grad_normed * norm_gain
    return inv_std * (
        scaled_grad
        - jnp.mean(scaled_grad, axis=-1, keepdims=True)
        - normed * jnp.mean(scaled_grad * normed, axis=-1, keepdims=True)
    )


def first_head(shape):
    return lax.broadcasted_iota(jnp.int32, shape, 1) % PAIR < HEAD_DIM


def swap_halves(values):
    half = HEAD_DIM // 2
    lane = lax.broadcasted_iota(jnp.int32, values.shape, 1)
    ahead = pltpu.roll(values, PAIR - half, 1)
    behind = pltpu.roll(values, half, 1)
    return jnp.where(lane % HEAD_DIM < half, ahead, behind)


def project_kernel(blocks, norms_ref, w_ref, cos_ref, sin_ref, *refs):
    x_refs = refs[:blocks]
    normed_ref, q_ref, kv_ref = refs[blocks:]
    cols = q_ref.shape[2]
    gain, bias = norms_ref[0:1, :], norms_ref[1:2, :]
    at_row = 0
    for x_ref in x_refs:
        rows = slice(at_row, at_row + x_ref.shape[1])
        at_row += x_ref.shape[1]
        normed = (normalise(x_ref[0].astype(F32))[0] * gain + bias).astype(BF16)
        normed_ref[0, rows, :] = normed
        cosine, sine = cos_ref[rows, :], sin_ref[rows, :]
        query = dot_nn(normed, w_ref[:, :cols])
        key = dot_nn(normed, w_ref[:, cols : 2 * cols])
        for at in range(0, cols, PAIR):
            part = slice(at, at + PAIR)
            one = query[:, part]
            q_ref[0, rows, part] = (one * cosine + swap_halves(one) * sine).astype(BF16)
            one = key[:, part]
            kv_ref[0, 0, rows, part] = (one * cosine + swap_halves(one) * sine).astype(BF16)
        kv_ref[0, 1, rows, :] = dot_nn(normed, w_ref[:, 2 * cols : 3 * cols]).astype(BF16)


def project(x_blocks, norms, w_att, cosine, sine):
    windows = x_blocks[0].shape[0]
    width, cols = w_att.shape[0], w_att.shape[1] // 4
    rows = sum(block.shape[1] for block in x_blocks)
    args = [norms, w_att, cosine, sine, *x_blocks]
    return run(
        functools.partial(project_kernel, len(x_blocks)),
        "project",
        [
            shaped((windows, rows, width), BF16),
            shaped((windows, rows, cols), BF16),
            shaped((windows, 2, rows, cols), BF16),
        ],
        6 * windows * rows * width * cols,
        args,
        grid=(windows,),
        in_specs=[pl.BlockSpec(array.shape, lambda i: (0, 0)) for array in args[:4]]
        + [pl.BlockSpec((1,) + block.shape[1:], lambda i: (i, 0, 0)) for block in x_blocks],
        out_specs=[
            pl.BlockSpec((1, rows, width), lambda i: (i, 0, 0)),
            pl.BlockSpec((1, rows, cols), lambda i: (i, 0, 0)),
            pl.BlockSpec((1, 2, rows, cols), lambda i: (i, 0, 0, 0)),
        ],
    )


def flipped(index, mask):
    bit = 1
    while bit <= mask:
        if mask & bit:
            index = index + bit - 2 * bit * ((index // bit) % 2)
        bit *= 2
    return index


def greet(peers):
    barrier = pltpu.get_barrier_semaphore()
    for peer in peers:
        pl.semaphore_signal(barrier, inc=1, device_id=peer, device_id_type=MESH)
    pl.semaphore_wait(barrier, len(peers))


def send(source, target, send_sem, recv_sem, peer):
    return pltpu.make_async_remote_copy(
        src_ref=source,
        dst_ref=target,
        send_sem=send_sem,
        recv_sem=recv_sem,
        device_id=peer,
        device_id_type=MESH,
    )


def half_chip_peers():
    seq, depth = lax.axis_index("seq"), lax.axis_index("dp")
    size = lax.axis_size("dp")
    return {
        "far": {"seq": flipped(seq, 2)},
        "up": {"dp": (depth + 1) % size},
        "down": {"dp": (depth + size - 1) % size},
        "core": {"seq": flipped(seq, 1)},
    }


class Route:
    PARTS = ((0, 0), (3, 0), (1, 0), (2, 0), (0, 1), (3, 1), (1, 1), (2, 1))

    def __init__(self, whole, rows, send_sem, recv_sem, own):
        self.whole, self.rows, self.own = whole, rows, own
        self.send_sem, self.recv_sem = send_sem, recv_sem
        self.seq, self.depth = lax.axis_index("seq"), lax.axis_index("dp")
        self.peers = half_chip_peers()

    def part(self, place):
        turn, other = place
        seq = flipped(self.seq, 2) if other else self.seq
        at = (((self.depth + turn) % lax.axis_size("dp")) * lax.axis_size("seq") + seq) * self.rows
        return self.whole.at[pl.ds(pl.multiple_of(at, self.rows), self.rows), :]

    def message(self, number):
        if number >= 7:
            place, peer = self.PARTS[number - 7], "core"
        else:
            place, peer = (
                ((0, 0), "up"),
                ((0, 0), "down"),
                ((3, 0), "up"),
                ((0, 0), "far"),
                ((3, 0), "far"),
                ((1, 0), "far"),
                ((2, 0), "far"),
            )[number]
        target = self.part(place)
        return send(
            self.own if place == (0, 0) else target,
            target,
            self.send_sem.at[number],
            self.recv_sem.at[number],
            self.peers[peer],
        )

    def start(self, *numbers):
        for number in numbers:
            self.message(number).start()

    def arrived(self, *numbers):
        for number in numbers:
            self.message(number).wait_recv()

    def sent(self, *numbers):
        for number in numbers:
            self.message(number).wait_send()


MESSAGES = 15


def gather_kernel(trades, att_ref, tile_ref, tokens_ref, *refs):
    att_all, norms_ref, tokens_all = refs[:3]
    tiles, pair_of_tiles = refs[3:5]
    att_send, att_recv, tile_send, tile_recv = refs[5:9]
    own_sem, tokens_send, tokens_recv, pair_send, pair_recv = refs[9:]
    tensor = lax.axis_index("tensor")
    others = [{"tensor": flipped(tensor, other + 1)} for other in range(trades)]
    att = Route(att_all, att_ref.shape[0], att_send, att_recv, att_ref)
    tile_rows = tile_ref.shape[0]
    small = Route(tiles, pair_of_tiles.shape[0], tile_send, tile_recv, pair_of_tiles)

    def tokens_trade(other):
        return send(
            tokens_ref,
            tokens_all.at[other],
            tokens_send.at[other],
            tokens_recv.at[other],
            others[other],
        )

    own_rows = pl.ds(pl.multiple_of(tensor * tile_rows, tile_rows), tile_rows)

    def pair_trade(other):
        return send(
            tile_ref,
            pair_of_tiles.at[own_rows, :],
            pair_send.at[other],
            pair_recv.at[other],
            others[other],
        )

    own_copies = [
        pltpu.make_async_copy(att_ref, att.part((0, 0)), own_sem.at[0]),
        pltpu.make_async_copy(tile_ref, pair_of_tiles.at[own_rows, :], own_sem.at[1]),
        pltpu.make_async_copy(pair_of_tiles, small.part((0, 0)), own_sem.at[2]),
    ]

    greet(list(att.peers.values()) + others)
    for other in range(trades):
        pair_trade(other).start()
    own_copies[1].start()
    own_copies[1].wait()
    for other in range(trades):
        pair_trade(other).wait_recv()
    for route in (small, att):
        route.start(0, 1, 3, 7)
    own_copies[0].start()
    own_copies[2].start()
    for other in range(trades):
        tokens_trade(other).start()
    for route in (small, att):
        route.arrived(0)
        route.start(2, 4, 8)
    for route in (small, att):
        route.arrived(3)
        route.start(11)
    for route in (small, att):
        route.arrived(1)
        route.start(5, 9)
    for route in (small, att):
        route.arrived(2)
        route.start(6, 10)
    for route in (small, att):
        route.arrived(4)
        route.start(12)
        route.arrived(5)
        route.start(13)
        route.arrived(6)
        route.start(14)
    for route in (small, att):
        route.arrived(*range(7, MESSAGES))
    own_copies[2].wait()
    shard = norms_ref.shape[1] // (tiles.shape[0] // tile_rows)
    total = None
    for device in range(tiles.shape[0] // tile_rows):
        tile = tiles[device * tile_rows : (device + 1) * tile_rows, :]
        norms_ref[:, device * shard : (device + 1) * shard] = tile[:, :shard]
    for depth in range(lax.axis_size("dp")):
        at = depth * (tiles.shape[0] // lax.axis_size("dp"))
        one = tiles[at + 4 : at + 5, :]
        total = one if total is None else total + one
    norms_ref[4:5, : total.shape[1]] = total
    for route in (att, small):
        route.sent(*range(MESSAGES))
    own_copies[0].wait()
    for other in range(trades):
        pair_trade(other).wait_send()
        tokens_trade(other).wait_recv()
        tokens_trade(other).wait_send()


def gather(att, tile, tokens, trades):
    count = lax.axis_size("dp") * lax.axis_size("seq")
    rows = att.shape[0]
    group = tile.shape[0] * (trades + 1)
    anywhere = pl.BlockSpec(memory_space=pl.ANY)
    vmem = pl.BlockSpec(memory_space=pltpu.VMEM)
    dma = pltpu.SemaphoreType.DMA
    return run(
        functools.partial(gather_kernel, trades),
        "gather",
        [
            shaped((count * rows, att.shape[1]), BF16),
            shaped((tile.shape[0], count * rows), F32),
            shaped((trades,) + tokens.shape, BF16),
        ],
        0,
        [att, tile, tokens],
        collective_id=1,
        in_specs=[vmem, vmem, anywhere],
        out_specs=[anywhere, vmem, anywhere],
        scratch_shapes=[pltpu.VMEM((count * group, 128), F32), pltpu.VMEM((group, 128), F32)]
        + [dma((MESSAGES,))] * 4
        + [dma((3,)), dma((trades,)), dma((trades,)), dma((trades,)), dma((trades,))],
    )


def attend_kernel(windows, pairs, trades, exp_scale, *refs):
    stages = (trades + 1).bit_length() - 1
    q_ref, w_ref, kv_ref, cot_ref, x_ref, norms_ref = refs[:6]
    low_ref, wide_ref, log_ref, kept_ref, sent_ref, slots_ref, cots_ref = refs[6:13]
    middle_ref, normed_ref, others_ref = refs[13:16]
    slots, acc_all, top_all, total_all, mixed_rows = refs[16:21]
    own_sem, send_sem, recv_sem, save_sem, cot_send, cot_recv = refs[21:27]
    early_kept, early_normed, early_sem, early_recv, normed_sem, normed_recv = refs[27:33]
    early_sent, early_arrived = refs[33 : 33 + stages], refs[33 + stages :]
    step = pl.program_id(0)
    near_steps = windows * pairs
    steps = 2 * near_steps
    seq, tensor = lax.axis_index("seq"), lax.axis_index("tensor")
    core_peer = {"seq": flipped(seq, 1)}
    far_peer = {"seq": flipped(seq, 2)}
    cot_peers = [{"tensor": flipped(tensor, other + 1)} for other in range(trades)]

    def piece(number):
        columns = pl.ds(pl.multiple_of((number % pairs) * PAIR, PAIR), PAIR)
        return kv_ref.at[number // pairs, :, :, columns]

    def own_copy(number):
        return pltpu.make_async_copy(piece(number), slots.at[number, 0], own_sem.at[number])

    def trade(number, slot):
        peer = far_peer if slot == 2 else core_peer
        source = slots.at[number, 2] if slot == 3 else piece(number)
        return send(
            source,
            slots.at[number, slot],
            send_sem.at[number, slot - 1],
            recv_sem.at[number, slot - 1],
            peer,
        )

    def cot_trade(other):
        return send(
            cot_ref, cots_ref.at[other], cot_send.at[other], cot_recv.at[other], cot_peers[other]
        )

    def early_trade(stage):
        return send(
            early_sent[stage],
            early_arrived[stage],
            early_sem.at[stage],
            early_recv.at[stage],
            {"tensor": flipped(tensor, (trades + 1) >> (stage + 1))},
        )

    def normed_trade(other):
        return send(
            early_normed,
            others_ref.at[other],
            normed_sem.at[other],
            normed_recv.at[other],
            cot_peers[other],
        )

    def save(number, slot):
        return pltpu.make_async_copy(
            slots.at[number, slot], slots_ref.at[number, slot], save_sem.at[number, slot]
        )

    @pl.when(step == 0)
    def _():
        greet([core_peer, far_peer] + cot_peers)

        @pl.loop(0, near_steps)
        def _(number):
            own_copy(number).start()
            trade(number, 1).start()
            trade(number, 2).start()

        for other in range(trades):
            cot_trade(other).start()

    @pl.when(step == near_steps + pairs)
    def _():
        early_trade(0).start()

    @pl.when(step == steps - 2)
    def _():
        kept = early_kept[...]
        for stage in range(stages):
            early_trade(stage).wait_recv()
            kept = kept + early_arrived[stage][...].astype(F32)
            if stage + 1 < stages:
                half = kept.shape[0] // 2
                early_sent[stage + 1][...] = kept[half:].astype(BF16)
                early_trade(stage + 1).start()
                kept = kept[:half]
        middle = x_ref[...].astype(F32) + kept
        middle_ref[...] = middle
        normed = (normalise(middle)[0] * norms_ref[2:3, :] + norms_ref[3:4, :]).astype(BF16)
        normed_ref[...] = normed
        early_normed[...] = normed

    @pl.when(step == steps - 1)
    def _():
        for other in range(trades):
            normed_trade(other).start()

    relayed = step - (near_steps - 1)

    @pl.when(jnp.logical_and(relayed >= 0, relayed < near_steps))
    def _():
        trade(relayed, 2).wait_recv()
        trade(relayed, 3).start()
        save(relayed, 2).start()

    query = q_ref[0]
    is_first = first_head(query.shape)

    def partial_of(number, used, carried_top):
        outs, tops = [], []
        for head in range(2):
            mine = is_first if head == 0 else jnp.logical_not(is_first)
            own_query = jnp.where(mine, query, jnp.zeros_like(query))
            scores = [dot_nt(own_query, slots[number, slot, 0]) for slot in used]
            top = scores[0].max(axis=1, keepdims=True)
            for one in scores[1:]:
                top = jnp.maximum(top, one.max(axis=1, keepdims=True))
            if carried_top is not None:
                at = head * HEAD_DIM
                top = jnp.maximum(top, carried_top[:, at : at + 1])
            shift = top * exp_scale
            mixed = None
            for one, slot in zip(scores, used):
                weight = jnp.exp2(one * exp_scale - shift).astype(BF16)
                value = slots[number, slot, 1]
                lane_first = first_head(value.shape)
                lane_mine = lane_first if head == 0 else jnp.logical_not(lane_first)
                term = dot_nn(weight, jnp.where(lane_mine, value, jnp.ones_like(value)))
                mixed = term if mixed is None else mixed + term
            outs.append(mixed)
            tops.append(jnp.broadcast_to(top, mixed.shape))
        acc = jnp.where(is_first, outs[0], outs[1])
        total = pltpu.roll(jnp.where(is_first, outs[1], outs[0]), HEAD_DIM, 1)
        return acc, jnp.where(is_first, tops[0], tops[1]), total

    @pl.when(step < near_steps)
    def _():
        own_copy(step).wait()
        trade(step, 1).wait_recv()
        save(step, 0).start()
        save(step, 1).start()
        acc, top, total = partial_of(step, (0, 1), None)
        acc_all[step] = acc
        top_all[step] = top
        total_all[step] = total

    @pl.when(step >= near_steps)
    def _():
        number = step - near_steps
        trade(number, 3).wait_recv()
        save(number, 3).start()
        carried_top = top_all[number]
        acc, top, total = partial_of(number, (2, 3), carried_top)
        fade = jnp.exp2((carried_top - top) * exp_scale)
        acc = acc + acc_all[number] * fade
        total = total + total_all[number] * fade
        attended = acc / total
        low = attended.astype(BF16)
        low_ref[0] = low
        wide_ref[0] = attended
        log_ref[0] = (top * exp_scale + jnp.log2(total)).T
        term = dot_nt(low, w_ref[...])
        pair = number % pairs

        @pl.when(pair == 0)
        def _():
            mixed_rows[...] = term

        @pl.when(pair > 0)
        def _():
            mixed_rows[...] += term

        @pl.when(jnp.logical_and(pair == pairs - 1, number >= pairs))
        def _():
            half = kept_ref.shape[1]
            kept_ref[0] = mixed_rows[:half]
            sent_ref[0] = mixed_rows[half:].astype(BF16)

        @pl.when(number == pairs - 1)
        def _():
            half = kept_ref.shape[1]
            early_kept[...] = mixed_rows[:half]
            early_sent[0][...] = mixed_rows[half:].astype(BF16)

    @pl.when(step == steps - 1)
    def _():
        @pl.loop(0, near_steps)
        def _(number):
            for slot in range(1, 4):
                trade(number, slot).wait_send()
            for slot in range(4):
                save(number, slot).wait()

        for stage in range(stages):
            early_trade(stage).wait_send()
        for other in range(trades):
            cot_trade(other).wait_send()
            cot_trade(other).wait_recv()
            normed_trade(other).wait_send()
            normed_trade(other).wait_recv()


def attend(queries, own_kv, w_att, cotangent, tokens, norms, trades):
    windows, rows, cols = queries.shape
    width = w_att.shape[0]
    pairs = cols // PAIR
    near = windows * pairs
    out_at = 3 * pairs

    def far(i):
        return jnp.maximum(i - near, 0)

    anywhere = pl.BlockSpec(memory_space=pl.ANY)
    wide = pl.BlockSpec((1, rows, PAIR), lambda i: (far(i) // pairs, 0, far(i) % pairs))
    half = pl.BlockSpec((1, rows // 2, width), lambda i: (jnp.maximum(far(i) // pairs, 1) - 1, 0, 0))
    own_rows = tokens.shape[1]
    own = pl.BlockSpec((own_rows, width), lambda i: (0, 0))
    stages = [rows >> (stage + 1) for stage in range((trades + 1).bit_length() - 1)]
    state = pltpu.VMEM((near, rows, PAIR), F32)
    dma = pltpu.SemaphoreType.DMA
    return run(
        functools.partial(attend_kernel, windows, pairs, trades, LOG2E / math.sqrt(HEAD_DIM)),
        "attend",
        [
            shaped((windows, rows, cols), BF16),
            shaped((windows, rows, cols), F32),
            shaped((windows, cols, rows), F32),
            shaped((windows - 1, rows // 2, width), F32),
            shaped((windows - 1, rows // 2, width), BF16),
            shaped((near, 4, 2, rows, PAIR), BF16),
            shaped((trades,) + cotangent.shape, BF16),
            shaped((own_rows, width), F32),
            shaped((own_rows, width), BF16),
            shaped((trades, own_rows, width), BF16),
        ],
        64 * windows * rows * rows * cols,
        [queries, w_att, own_kv, cotangent, tokens, norms],
        collective_id=0,
        grid=(2 * near,),
        in_specs=[
            pl.BlockSpec((1, rows, PAIR), lambda i: ((i // pairs) % windows, 0, i % pairs)),
            pl.BlockSpec((width, PAIR), lambda i: (0, out_at + far(i) % pairs)),
            anywhere,
            anywhere,
            pl.BlockSpec((None, own_rows, width), lambda i: (0, 0, 0)),
            pl.BlockSpec(norms.shape, lambda i: (0, 0)),
        ],
        out_specs=[
            wide,
            wide,
            pl.BlockSpec((1, PAIR, rows), lambda i: (far(i) // pairs, far(i) % pairs, 0)),
            half,
            half,
            anywhere,
            anywhere,
            own,
            own,
            anywhere,
        ],
        scratch_shapes=[
            pltpu.VMEM((near, 4, 2, rows, PAIR), BF16),
            state,
            state,
            state,
            pltpu.VMEM((rows, width), F32),
            dma((near,)),
            dma((near, 3)),
            dma((near, 3)),
            dma((near, 4)),
            dma((trades,)),
            dma((trades,)),
            pltpu.VMEM((rows // 2, width), F32),
            pltpu.VMEM((own_rows, width), BF16),
            dma((len(stages),)),
            dma((len(stages),)),
            dma((trades,)),
            dma((trades,)),
        ]
        + [pltpu.VMEM((count, width), BF16) for count in stages] * 2,
    )


def attend_back_kernel(windows, pairs, blocks, exp_scale, score_scale, *refs):
    q_ref, wide_ref, log_ref, slots_ref, w_ref, cos_ref, sin_ref, last_ref = refs[:8]
    trades = blocks - 1
    known = (windows - 1) * blocks + 1
    grad_refs = list(refs[8 : 8 + known])
    refs = refs[8 + known :]
    sent_refs, refs = refs[:windows], refs[windows:]
    gq_ref, gk_ref, gv_ref, rows_ref = refs[:4]
    arrived_refs, refs = refs[4 : 4 + windows], refs[4 + windows :]
    dq_all, do_all, far_kept, far_sent, far_core, far_x, near_kept, near_sent, near_core = refs[:9]
    send_sem, recv_sem, result_send, result_recv, last_send, last_recv, last_others = refs[9:]
    grad_refs += [last_others.at[other] for other in range(trades)]
    step = pl.program_id(0)
    count = windows * pairs
    seq, tensor = lax.axis_index("seq"), lax.axis_index("tensor")
    core_peer = {"seq": flipped(seq, 1)}
    far_peer = {"seq": flipped(seq, 2)}
    result_peer = {"tensor": flipped(tensor, lax.axis_size("tensor") // 2)}

    def trade(kind, number):
        source, target, peer = (
            (far_sent, far_core, core_peer),
            (far_kept, far_x, far_peer),
            (near_sent, near_core, core_peer),
        )[kind]
        return send(
            source.at[number],
            target.at[number],
            send_sem.at[kind, number],
            recv_sem.at[kind, number],
            peer,
        )

    def result_trade(w):
        return send(
            sent_refs[w], arrived_refs[w], result_send.at[w], result_recv.at[w], result_peer
        )

    others = [{"tensor": flipped(tensor, other + 1)} for other in range(trades)]

    def last_trade(other):
        return send(
            last_ref, last_others.at[other], last_send.at[other], last_recv.at[other], others[other]
        )

    @pl.when(step == 0)
    def _():
        greet([core_peer, far_peer] + others)
        for other in range(trades):
            last_trade(other).start()
        for w in range(windows):
            result_trade(w).start()

    def at_step(first, body):
        number = step - first

        @pl.when(jnp.logical_and(number >= 0, number < count))
        def _():
            body(number)

    def send_far(number):
        trade(0, number).start()

    def add_far(number):
        trade(0, number).wait_recv()
        far_kept[number] = (
            far_kept[number].astype(F32) + far_core[number].astype(F32)
        ).astype(BF16)

    def send_x(number):
        trade(1, number).start()

    def send_near(number):
        trade(2, number).start()

    def finish(number):
        trade(2, number).wait_recv()
        trade(1, number).wait_recv()
        total = (
            near_kept[number].astype(F32)
            + near_core[number].astype(F32)
            + far_x[number].astype(F32)
        )
        key = total[0]
        gk_ref[0] = (key * cos_ref[...] - swap_halves(key) * sin_ref[...]).astype(BF16)
        gv_ref[0] = total[1].astype(BF16)

    at_step(1, send_far)
    at_step(3, send_x)
    at_step(count + 1, send_near)
    at_step(2, add_far)
    at_step(count + 2, finish)

    for w in range(windows):

        @pl.when(step == w * pairs)
        def _(w=w):
            if w == windows - 1:
                for other in range(trades):
                    last_trade(other).wait_recv()
            at_row = 0
            for grad_ref in grad_refs[w * blocks : (w + 1) * blocks]:
                rows_ref[0, at_row : at_row + grad_ref.shape[0], :] = grad_ref[...]
                at_row += grad_ref.shape[0]

    def gradients(number, grad_out, kept, sent):
        query = q_ref[0]
        is_first = first_head(query.shape)
        overlap = (grad_out.astype(F32) * wide_ref[0]).T
        logs = log_ref[0]
        zero = jnp.zeros_like(query)
        own_q, own_do, row_log, row_sum = [], [], [], []
        for head in range(2):
            mine = is_first if head == 0 else jnp.logical_not(is_first)
            own_q.append(jnp.where(mine, query, zero))
            own_do.append(jnp.where(mine, grad_out, zero))
            at = head * HEAD_DIM
            row_log.append(logs[at : at + 1, :])
            row_sum.append(jnp.sum(overlap[at : at + HEAD_DIM, :], axis=0, keepdims=True))
        dq_parts = [None, None]
        for slot, target in enumerate((kept, sent)):
            key, value = slots_ref[0, slot, 0], slots_ref[0, slot, 1]
            key_turned = key.T
            grad_key, grad_value = None, None
            for head in range(2):
                scores = dot_nt(key, own_q[head])
                probs = jnp.exp2(scores * exp_scale - row_log[head])
                grad_probs = dot_nt(value, own_do[head])
                grad_scores = (probs * (grad_probs - row_sum[head])).astype(BF16)
                term_v = dot_nn(probs.astype(BF16), own_do[head])
                term_k = dot_nn(grad_scores, own_q[head])
                at = head * HEAD_DIM
                term_q = dot_nn(key_turned[at : at + HEAD_DIM, :], grad_scores)
                grad_value = term_v if grad_value is None else grad_value + term_v
                grad_key = term_k if grad_key is None else grad_key + term_k
                dq_parts[head] = term_q if dq_parts[head] is None else dq_parts[head] + term_q
            target[number, 0] = (grad_key * score_scale).astype(BF16)
            target[number, 1] = grad_value.astype(BF16)
        return jnp.concatenate(dq_parts, axis=0).T * score_scale

    @pl.when(step < count)
    def _():
        grad_out = dot_nn(rows_ref[0], w_ref[...]).astype(BF16)
        do_all[step] = grad_out
        dq_all[step] = gradients(step, grad_out, far_kept, far_sent)

    @pl.when(jnp.logical_and(step >= count, step < 2 * count))
    def _():
        number = step - count
        grad_query = dq_all[number] + gradients(number, do_all[number], near_kept, near_sent)
        gq_ref[0] = (grad_query * cos_ref[...] - swap_halves(grad_query) * sin_ref[...]).astype(
            BF16
        )

    @pl.when(step == pl.num_programs(0) - 1)
    def _():
        @pl.loop(0, count)
        def _(number):
            for kind in range(3):
                trade(kind, number).wait_send()

        for other in range(trades):
            last_trade(other).wait_send()
        for w in range(windows):
            result_trade(w).wait_send()
            result_trade(w).wait_recv()


def attend_back(queries, wide, logs, slots_all, grad_blocks, w_att, tables, sent):
    windows, rows, cols = queries.shape
    width = w_att.shape[0]
    pairs = cols // PAIR
    count = windows * pairs
    out_at = 3 * pairs
    score_scale = 1.0 / math.sqrt(HEAD_DIM)
    blocks = lax.axis_size("tensor")
    grads = [block for one in grad_blocks for block in one]
    last = grads[-1]

    def spot(lag, last=None):
        def index(i):
            number = jnp.clip(i - lag, 0, count - 1)
            return (number // pairs, 0, number % pairs)

        return pl.BlockSpec((1, rows, PAIR), index)

    def both(i):
        return jnp.minimum(i, 2 * count - 1) % count

    dma = pltpu.SemaphoreType.DMA
    piece = pltpu.VMEM((count, 2, rows, PAIR), BF16)
    anywhere = pl.BlockSpec(memory_space=pl.ANY)
    return run(
        functools.partial(
            attend_back_kernel, windows, pairs, blocks, score_scale * LOG2E, score_scale
        ),
        "attend_back",
        [shaped((windows, rows, cols), BF16)] * 3
        + [shaped((windows, rows, width), BF16)]
        + [shaped(one.shape, BF16) for one in sent],
        160 * windows * rows * rows * cols,
        [queries, wide, logs, slots_all, w_att, *tables, last, *grads, *sent],
        collective_id=2,
        grid=(2 * count + 2,),
        in_specs=[
            pl.BlockSpec((1, rows, PAIR), lambda i: (both(i) // pairs, 0, both(i) % pairs)),
            pl.BlockSpec((1, rows, PAIR), lambda i: (both(i) // pairs, 0, both(i) % pairs)),
            pl.BlockSpec((1, PAIR, rows), lambda i: (both(i) // pairs, both(i) % pairs, 0)),
            pl.BlockSpec(
                (1, 2, 2, rows, PAIR),
                lambda i: (both(i), jnp.where(i < count, 1, 0), 0, 0, 0),
            ),
            pl.BlockSpec((width, PAIR), lambda i: (0, out_at + jnp.minimum(i, count - 1) % pairs)),
            pl.BlockSpec((rows, PAIR), lambda i: (0, 0)),
            pl.BlockSpec((rows, PAIR), lambda i: (0, 0)),
            anywhere,
        ]
        + [pl.BlockSpec(block.shape, lambda i: (0, 0)) for block in grads]
        + [anywhere] * windows,
        out_specs=[
            spot(count),
            spot(count + 2),
            spot(count + 2),
            pl.BlockSpec((1, rows, width), lambda i: (jnp.minimum(i // pairs, windows - 1), 0, 0)),
        ]
        + [anywhere] * windows,
        scratch_shapes=[pltpu.VMEM((count, rows, PAIR), F32), pltpu.VMEM((count, rows, PAIR), BF16)]
        + [piece] * 7
        + [dma((3, count)), dma((3, count)), dma((windows,)), dma((windows,))]
        + [dma((blocks - 1,)), dma((blocks - 1,)), pltpu.VMEM((blocks - 1,) + last.shape, BF16)],
    )


def middle_kernel(x_ref, kept_ref, arrived_ref, norms_ref, middle_ref, normed_ref):
    middle = x_ref[...].astype(F32) + (kept_ref[...] + arrived_ref[...].astype(F32))
    middle_ref[...] = middle
    normed_ref[...] = (
        normalise(middle)[0] * norms_ref[2:3, :] + norms_ref[3:4, :]
    ).astype(BF16)


def second_norm(x_rows, kept, arrived, norms):
    args, in_specs = zip(*[plane(one) for one in (x_rows, kept, arrived, norms)])
    rows, width = in_specs[1].block_shape[-2:]
    full = pl.BlockSpec((rows, width), lambda i: (0, 0))
    return run(
        middle_kernel,
        "second_norm",
        [shaped((rows, width), F32), shaped((rows, width), BF16)],
        20 * rows * width,
        args,
        grid=(1,),
        in_specs=list(in_specs),
        out_specs=[full, full],
    )


def feed_step(x_rows, gy_rows, w_refs, out_refs):
    gate_w_ref, up_w_ref, down_w_ref = w_refs
    hidden_ref, grad_gate_ref, grad_up_ref = out_refs
    gate = dot_nn(x_rows, gate_w_ref[...])
    up = dot_nn(x_rows, up_w_ref[...])
    grad_hidden = dot_nn(gy_rows, down_w_ref[...])
    sig = jax.nn.sigmoid(gate)
    swish = gate * sig
    hidden = (swish * up).astype(BF16)
    grad_gate = (grad_hidden * up * sig * (1.0 + gate * (1.0 - sig))).astype(BF16)
    grad_up = (grad_hidden * swish).astype(BF16)
    hidden_ref[...] = hidden
    grad_gate_ref[...] = grad_gate
    grad_up_ref[...] = grad_up
    grad_term = dot_nt(grad_gate, gate_w_ref[...]) + dot_nt(grad_up, up_w_ref[...])
    return dot_nt(hidden, down_w_ref[...]), grad_term


def feed_first_kernel(blocks, factor_ref, *refs):
    w_refs, refs = refs[:3], refs[3:]
    x_refs, cot_refs = refs[:blocks], refs[blocks : 2 * blocks]
    x_all, gy_all = refs[2 * blocks : 2 * blocks + 2]
    total, grad_total = refs[2 * blocks + 5 :]
    step = pl.program_id(0)

    @pl.when(step == 0)
    def _():
        at_row = 0
        for x_ref, cot_ref in zip(x_refs, cot_refs):
            rows = slice(at_row, at_row + x_ref.shape[0])
            at_row += x_ref.shape[0]
            x_all[rows, :] = x_ref[...]
            gy_all[rows, :] = (cot_ref[...].astype(F32) * factor_ref[0, 0]).astype(BF16)

    term, grad_term = feed_step(
        x_all[...], gy_all[...], w_refs, refs[2 * blocks + 2 : 2 * blocks + 5]
    )

    @pl.when(step == 0)
    def _():
        total[...] = term
        grad_total[...] = grad_term

    @pl.when(step > 0)
    def _():
        total[...] += term
        grad_total[...] += grad_term


def feed_last_kernel(*refs):
    w_refs = refs[:3]
    x_ref, gy_ref, total_in, grad_in = refs[3:7]
    kept_ref, sent_ref, grad_kept_ref, grad_sent_ref, total, grad_total = refs[13:]
    step = pl.program_id(0)
    term, grad_term = feed_step(x_ref[...], gy_ref[...], w_refs, refs[10:13])

    @pl.when(step == 0)
    def _():
        total[...] = total_in[...] + term
        grad_total[...] = grad_in[...] + grad_term

    @pl.when(step > 0)
    def _():
        total[...] += term
        grad_total[...] += grad_term

    @pl.when(step == pl.num_programs(0) - 1)
    def _():
        half = kept_ref.shape[0]
        kept_ref[...] = total[:half]
        sent_ref[...] = total[half:].astype(BF16)
        grad_kept_ref[...] = grad_total[:half]
        grad_sent_ref[...] = grad_total[half:].astype(BF16)


def feed_specs(weights):
    width, part_cols = weights.shape[0], weights.shape[1] // 3
    step = min(512, part_cols)
    steps = part_cols // step
    specs = [
        pl.BlockSpec((width, step), functools.partial(lambda at, i: (0, at + i), k * steps))
        for k in range(3)
    ]
    return step, steps, specs


def feed_first(x_blocks, cot_blocks, factor, weights):
    blocks, block_specs = zip(*[plane(block) for block in (*x_blocks, *cot_blocks)])
    width = x_blocks[0].shape[1]
    rows = sum(block.shape[0] for block in x_blocks)
    step, steps, w_specs = feed_specs(weights)
    hidden_cols = 2 * step * steps
    full = pl.BlockSpec((rows, width), lambda i: (0, 0))
    return run(
        functools.partial(feed_first_kernel, len(x_blocks)),
        "feed_first",
        [shaped((rows, width), BF16)] * 2
        + [shaped((rows, hidden_cols), BF16)] * 3
        + [shaped((rows, width), F32)] * 2,
        6 * rows * width * hidden_cols,
        [factor, weights, weights, weights, *blocks],
        grid=(steps,),
        in_specs=[SCALAR] + w_specs + list(block_specs),
        out_specs=[full] * 2 + [pl.BlockSpec((rows, step), lambda i: (0, i))] * 3 + [full] * 2,
    )


def feed_last(x_rows, gy_rows, totals, earlier, weights):
    rows, width = x_rows.shape
    step, steps, w_specs = feed_specs(weights)
    hidden_cols = 2 * step * steps
    full = pl.BlockSpec((rows, width), lambda i: (0, 0))
    half = pl.BlockSpec((rows // 2, width), lambda i: (0, 0))
    return run(
        feed_last_kernel,
        "feed_last",
        [shaped((rows, hidden_cols), BF16)] * 3
        + [shaped((rows // 2, width), F32), shaped((rows // 2, width), BF16)] * 2,
        6 * rows * width * hidden_cols,
        [weights, weights, weights, x_rows, gy_rows, *totals, *earlier],
        grid=(steps,),
        in_specs=w_specs + [full] * 4 + [pl.BlockSpec(memory_space=pl.ANY)] * 3,
        out_specs=[pl.BlockSpec((rows, step), lambda i: (0, steps + i))] * 3 + [half] * 4,
        scratch_shapes=[pltpu.VMEM((rows, width), F32)] * 2,
        input_output_aliases={7: 0, 8: 1, 9: 2},
    )


def weights_kernel(windows, starts, masks, *refs):
    inputs = 2 * windows * len(starts)
    sources = refs[inputs : inputs + len(masks)]
    out_ref = refs[inputs + len(masks)]
    targets = refs[inputs + len(masks) + 1 : inputs + 2 * len(masks) + 1]
    at = pl.program_id(0)
    trades = []
    if masks:
        send_sem, recv_sem = refs[inputs + 2 * len(masks) + 1 :]
        tensor = lax.axis_index("tensor")
        for source, target, kinds in zip(sources, targets, masks):
            for number, mask in enumerate(kinds):
                sems = (send_sem.at[len(trades)], recv_sem.at[len(trades)])
                peer = {"tensor": flipped(tensor, mask)}
                trades.append(send(source, target.at[number], *sems, peer))

        @pl.when(at == 0)
        def _():
            greet(
                [
                    {"tensor": flipped(tensor, mask)}
                    for mask in sorted({mask for kinds in masks for mask in kinds})
                ]
            )
            for trade in trades:
                trade.start()

    for group, (start, stop) in enumerate(starts):
        pairs = refs[2 * windows * group : 2 * windows * (group + 1)]

        @pl.when(jnp.logical_and(at >= start, at < stop))
        def _(pairs=pairs):
            total = None
            for left, right in zip(pairs[:windows], pairs[windows:]):
                term = dot_tn(left[...], right[...])
                total = term if total is None else total + term
            out_ref[...] = total.astype(BF16)

    if masks:

        @pl.when(at == pl.num_programs(0) - 1)
        def _():
            for trade in trades:
                trade.wait()


def weight_grads(groups, step, name, first=0, parts=1, swaps=(), collective_id=None):
    windows = len(groups[0][0])
    args, in_specs, starts = [], [], []
    at = 0
    for lefts, rights in groups:
        for left in lefts:
            array, spec = plane(left)
            rows, width = array.shape[-2:]
            args.append(array)
            in_specs.append(spec)
        for right in rights:
            cols = plane(right)[0].shape[-1]
            count = cols // (step * parts)
            place = functools.partial(
                lambda at, count, i: (0, first * count + jnp.clip(i - at, 0, count - 1)), at, count
            )
            array, spec = plane(right, (rows, step), place)
            args.append(array)
            in_specs.append(spec)
        starts.append((at, at + count))
        at += count
    masks = [kinds for _, kinds in swaps]
    anywhere = pl.BlockSpec(memory_space=pl.ANY)
    out_shape = [shaped((width, at * step), BF16)]
    out_shape += [shaped((len(kinds),) + array.shape, BF16) for array, kinds in swaps]
    total = sum(len(kinds) for kinds in masks)
    outs = run(
        functools.partial(weights_kernel, windows, starts, masks),
        name,
        out_shape,
        2 * windows * rows * width * at * step,
        args + [array for array, _ in swaps],
        collective_id=collective_id,
        grid=(at,),
        in_specs=in_specs + [anywhere] * len(swaps),
        out_specs=[pl.BlockSpec((width, step), lambda i: (0, i))] + [anywhere] * len(swaps),
        scratch_shapes=[pltpu.SemaphoreType.DMA((total,))] * 2 if total else [],
    )
    return outs if swaps else outs[0]


def norm_grad(kept_ref, arrived_ref, stream, gain, sums_ref):
    grad_normed = kept_ref[...] + arrived_ref[...].astype(F32)
    normed, inv_std = normalise(stream)
    sums_ref[0:1, :] = jnp.sum(grad_normed * normed, axis=0, keepdims=True)
    sums_ref[1:2, :] = jnp.sum(grad_normed, axis=0, keepdims=True)
    return norm_back(grad_normed, normed, inv_std, gain)


def middle_back_kernel(
    factor_ref, kept_ref, arrived_ref, middle_ref, cot_ref, norms_ref, grad_ref, low_ref, sums_ref
):
    grad_y = cot_ref[...].astype(F32) * factor_ref[0, 0]
    grad = grad_y + norm_grad(
        kept_ref, arrived_ref, middle_ref[...], norms_ref[2:3, :], sums_ref
    )
    grad_ref[...] = grad
    low_ref[...] = grad.astype(BF16)


def second_norm_back(factor, kept, arrived, middle, cot_rows, norms):
    args, in_specs = zip(*[plane(one) for one in (kept, arrived, middle, cot_rows, norms)])
    full = pl.BlockSpec(kept.shape, lambda i: (0, 0))
    return run(
        middle_back_kernel,
        "second_norm_back",
        [
            shaped(kept.shape, F32),
            shaped(kept.shape, BF16),
            shaped((2, kept.shape[1]), F32),
        ],
        40 * kept.size,
        [factor, *args],
        grid=(1,),
        in_specs=[SCALAR, *in_specs],
        out_specs=[full, full, pl.BlockSpec((2, kept.shape[1]), lambda i: (0, 0))],
    )


def turn_back_kernel(gq_ref, gk_ref, gv_ref, w_ref, kept_ref, sent_ref):
    cols = gq_ref.shape[2]
    half = kept_ref.shape[0]

    def rows_of(part):
        total = None
        for at, ref in enumerate((gq_ref, gk_ref, gv_ref)):
            term = dot_nt(ref[0, part, :], w_ref[:, at * cols : (at + 1) * cols])
            total = term if total is None else total + term
        return total

    sent_ref[...] = rows_of(slice(half, 2 * half)).astype(BF16)
    kept_ref[...] = rows_of(slice(0, half))


def turn_back(window, grads, w_att):
    windows, rows, cols = grads[0].shape
    width = w_att.shape[0]
    half = pl.BlockSpec((rows // 2, width), lambda i: (0, 0))
    return run(
        turn_back_kernel,
        "turn_back",
        [shaped((rows // 2, width), F32), shaped((rows // 2, width), BF16)],
        6 * rows * cols * width,
        [*grads, w_att],
        grid=(1,),
        in_specs=[pl.BlockSpec((1, rows, cols), lambda i: (window, 0, 0))] * 3
        + [pl.BlockSpec((width, 3 * cols), lambda i: (0, 0))],
        out_specs=[half, half],
    )


def input_back_kernel(window, kept_ref, arrived_ref, x_ref, grad_ref, norms_ref, *refs):
    out_ref, sums_ref = refs[-2:]
    out_ref[0] = grad_ref[...] + norm_grad(
        kept_ref, arrived_ref, x_ref[...].astype(F32), norms_ref[0:1, :], sums_ref
    )


def first_norm_back(window, windows, kept, arrived, x_rows, grad_middle, norms, earlier):
    rows, width = kept.shape
    args, whole = zip(*[plane(one) for one in (kept, arrived, x_rows, grad_middle, norms)])
    args, whole = list(args), list(whole)
    args += [] if earlier is None else [earlier]
    return run(
        functools.partial(input_back_kernel, window),
        "first_norm_back",
        [shaped((windows, rows, width), F32), shaped((2, width), F32)],
        40 * rows * width,
        args,
        grid=(1,),
        in_specs=whole + ([] if earlier is None else [pl.BlockSpec(memory_space=pl.ANY)]),
        out_specs=[
            pl.BlockSpec((1, rows, width), lambda i: (window, 0, 0)),
            pl.BlockSpec((2, width), lambda i: (0, 0)),
        ],
        input_output_aliases={} if earlier is None else {5: 0},
    )


class SumRoute:
    def __init__(self, part, rows, core_in, mine, x_in, z_in, send_sem, recv_sem):
        self.read, self.rows = part, rows
        self.core_in, self.mine, self.x_in, self.z_in = core_in, mine, x_in, z_in
        self.send_sem, self.recv_sem = send_sem, recv_sem
        self.seq, self.depth = lax.axis_index("seq"), lax.axis_index("dp")
        self.peers = half_chip_peers()

    def place(self, number, other_core):
        seq = flipped(self.seq, 2) if number >= 4 else self.seq
        seq = flipped(seq, 1) if other_core else seq
        turn = (self.depth + number % 4) % lax.axis_size("dp")
        return pl.ds(
            pl.multiple_of((turn * lax.axis_size("seq") + seq) * self.rows, self.rows), self.rows
        )

    def message(self, number):
        if number < 8:
            source, target, peer = self.read.at[self.place(number, True), :], self.core_in, "core"
            target = target.at[number]
        elif number < 12:
            source, target, peer = self.mine.at[number - 4], self.x_in.at[number - 8], "far"
        else:
            turn, peer = ((2, "up"), (1, "up"), (3, "down"))[number - 12]
            source, target = self.mine.at[turn], self.z_in.at[number - 12]
        return send(
            source, target, self.send_sem.at[number], self.recv_sem.at[number], self.peers[peer]
        )

    def start(self, *numbers):
        for number in numbers:
            self.message(number).start()

    def add_core(self, number):
        self.message(number).wait_recv()
        own = self.read[self.place(number, False), :].astype(F32)
        self.mine[number] = (own + self.core_in[number].astype(F32)).astype(self.mine.dtype)

    def add_x(self, number):
        self.message(8 + number).wait_recv()
        total = self.mine[number].astype(F32) + self.x_in[number].astype(F32)
        self.mine[number] = total.astype(self.mine.dtype)

    def add_up(self):
        self.message(12).wait_recv()
        total = self.mine[1].astype(F32) + self.z_in[0].astype(F32)
        self.mine[1] = total.astype(self.mine.dtype)

    def total(self):
        self.message(13).wait_recv()
        self.message(14).wait_recv()
        return (
            self.mine[0].astype(F32) + self.z_in[1].astype(F32) + self.z_in[2].astype(F32)
        )

    def sent(self):
        for number in range(SUM_MESSAGES):
            self.message(number).wait_send()


SUM_MESSAGES = 15


def reduce_kernel(trades, windows, part_ref, *refs):
    first_refs, second_refs = refs[:windows], refs[windows : 2 * windows]
    out_ref, vectors_ref = refs[2 * windows : 2 * windows + 2]
    refs = refs[2 * windows + 2 :]
    tiles, own_tiles, arrived_tiles = refs[:3]
    big = refs[3:9]
    small = refs[9:15]
    tile_send, tile_recv = refs[15:]
    tensor = lax.axis_index("tensor")
    others = [{"tensor": flipped(tensor, other + 1)} for other in range(trades)]
    shards = lax.axis_size("dp") * lax.axis_size("seq")
    devices = shards * (trades + 1)
    group = tiles.shape[0] // shards
    routes = (
        SumRoute(tiles, group, *small),
        SumRoute(part_ref, part_ref.shape[0] // shards, *big),
    )
    small_route, big_route = routes
    first = sum(ref[...] for ref in first_refs)
    second = sum(ref[...] for ref in second_refs)
    span = first.shape[1] // devices
    tiles[...] = jnp.zeros_like(tiles)
    for device in range(devices):
        at = device * 8
        part = slice(device * span, (device + 1) * span)
        tiles[at : at + 2, :span] = first[:, part]
        tiles[at + 2 : at + 4, :span] = second[:, part]
    greet(list(big_route.peers.values()) + others)
    small_route.start(6, 5, 7, 4, 2, 1, 3, 0)
    big_route.start(6, 5, 7, 4, 2, 1, 3, 0)
    for number in (6, 5, 7, 4, 2, 1, 3, 0):
        small_route.add_core(number)
    big_route.add_core(6)
    small_route.start(10, 9, 11, 8)
    big_route.add_core(5)
    big_route.start(10)
    big_route.add_core(7)
    big_route.start(9)
    big_route.add_core(4)
    big_route.start(11)
    big_route.add_core(2)
    big_route.start(8)
    for number in (2, 1, 3, 0):
        small_route.add_x(number)
    big_route.add_core(1)
    small_route.start(12, 14)
    big_route.add_core(3)
    big_route.add_core(0)
    small_route.add_up()
    big_route.add_x(2)
    small_route.start(13)
    own = small_route.total()
    big_route.start(12)
    own_tiles[...] = own
    big_route.add_x(1)
    big_route.add_up()
    out_ref[...] = jnp.zeros_like(out_ref)
    big_route.start(13)
    big_route.add_x(3)
    out_ref[...] = jnp.zeros_like(out_ref)
    big_route.start(14)
    big_route.add_x(0)
    out_ref[...] = big_route.total()

    def tile_trade(other):
        rows = pl.ds(pl.multiple_of(flipped(tensor, other + 1) * 8, 8), 8)
        return send(
            own_tiles.at[rows, :],
            arrived_tiles.at[other],
            tile_send.at[other],
            tile_recv.at[other],
            others[other],
        )

    for other in range(trades):
        tile_trade(other).start()
    vectors = own_tiles[pl.ds(pl.multiple_of(tensor * 8, 8), 8), :]
    for other in range(trades):
        tile_trade(other).wait_recv()
        vectors = vectors + arrived_tiles[other]
    vectors_ref[...] = vectors
    for route in routes:
        route.sent()
    for other in range(trades):
        tile_trade(other).wait_send()


def reduce_grads(part, first_sums, second_sums, trades):
    shards = lax.axis_size("dp") * lax.axis_size("seq")
    rows, cols = part.shape[0] // shards, part.shape[1]
    group = 8 * (trades + 1)
    windows = len(first_sums)
    dma = pltpu.SemaphoreType.DMA

    def buffers(shape, dtype):
        return [pltpu.VMEM((count,) + shape, dtype) for count in (8, 8, 4, 3)] + [
            dma((SUM_MESSAGES,)),
            dma((SUM_MESSAGES,)),
        ]

    return run(
        functools.partial(reduce_kernel, trades, windows),
        "reduce_grads",
        [shaped((rows, cols), F32), shaped((8, 128), F32)],
        0,
        [part, *first_sums, *second_sums],
        collective_id=3,
        scratch_shapes=[
            pltpu.VMEM((shards * group, 128), F32),
            pltpu.VMEM((group, 128), F32),
            pltpu.VMEM((trades, 8, 128), F32),
        ]
        + buffers((rows, cols), BF16)
        + buffers((group, 128), F32)
        + [dma((trades,)), dma((trades,))],
    )


def result_kernel(windows, *refs):
    out_ref = refs[-1]
    for w in range(windows):
        middle_ref, kept_ref, arrived_ref = refs[3 * w : 3 * w + 3]
        out_ref[w] = (
            middle_ref[...] + (kept_ref[...] + arrived_ref[...].astype(F32))
        ).astype(BF16)


def results(parts):
    rows, width = parts[0][0].shape
    return run(
        functools.partial(result_kernel, len(parts)),
        "results",
        shaped((len(parts), rows, width), BF16),
        2 * len(parts) * rows * width,
        [array for part in parts for array in part],
    )


def local(
    tokens,
    cotangent,
    species,
    counts,
    species_scale,
    norm1_gain,
    norm1_bias,
    w_query,
    w_key,
    w_value,
    w_out,
    norm2_gain,
    norm2_bias,
    w_gate,
    w_up,
    w_down,
):
    windows_here, own_rows, model_width = tokens.shape
    tensor_size = lax.axis_size("tensor")
    seq_size = lax.axis_size("seq")
    block_rows = own_rows * tensor_size
    head_cols = w_query.shape[1]
    hidden_cols = w_gate.shape[1]
    shards = ("dp", "seq")

    own_at = lax.axis_index("tensor")
    starts = jnp.concatenate(
        [
            lax.iota(jnp.int32, own_rows) + (own_at ^ other) * own_rows
            for other in range(tensor_size)
        ]
    )
    positions = (lax.axis_index("seq") * block_rows + starts).astype(F32)
    cos_half, sin_half = angles(positions, HEAD_DIM)
    cosine = jnp.concatenate([cos_half] * 4, axis=1)
    sine = jnp.concatenate([-sin_half, sin_half] * 2, axis=1)

    labels = lax.broadcasted_iota(jnp.int32, (windows_here, species_scale.shape[0]), 1)
    chosen = jnp.sum(jnp.where(species[:, None] == labels, species_scale[None, :], 0.0), axis=1)
    weighted = counts.astype(F32) * chosen

    lanes = jnp.zeros((8, 128), F32)
    vectors = jnp.stack([norm1_gain, norm1_bias, norm2_gain, norm2_bias])
    tile = lanes.at[:4, : vectors.shape[1]].set(vectors).at[4, :].set(jnp.sum(weighted))
    part = hidden_cols // 2
    turned = w_down.T
    first_ffn = jnp.concatenate([w_gate[:, :part], w_up[:, :part], turned[:, :part]], axis=1)
    last_ffn = jnp.concatenate([w_gate[:, part:], w_up[:, part:], turned[:, part:]], axis=1)
    first_ffn = lax.all_gather(first_ffn, shards, axis=0, tiled=True)
    w_att, norms, arrived_tokens = gather(
        jnp.concatenate([w_query, w_key, w_value, w_out.T], axis=1),
        tile,
        tokens,
        tensor_size - 1,
    )
    factor = weighted * float(windows_here * lax.axis_size("dp")) / norms[4, 0]

    windows = range(windows_here)
    factors = [factor[w].reshape(1, 1) for w in windows]
    top_bit = seq_size // 2

    token_blocks = [tokens] + [arrived_tokens[other] for other in range(tensor_size - 1)]
    normed_rows, queries, own_kv = project(token_blocks, norms, w_att, cosine, sine)
    (
        attended,
        wide_attended,
        logs,
        kept_all,
        sent_all,
        slots_all,
        cots,
        first_middle,
        first_normed,
        first_others,
    ) = attend(queries, own_kv, w_att, cotangent, tokens, norms, tensor_size - 1)
    last_ffn = lax.all_gather(hold(last_ffn, kept_all), shards, axis=0, tiled=True)
    others = range(tensor_size - 1)
    cot_blocks = [
        [(cotangent, (w,))] + [(cots, (other, w)) for other in others] for w in windows
    ]
    middles = [first_middle]

    begun = [
        feed_first(
            [first_normed] + [first_others[other] for other in others],
            cot_blocks[0],
            factors[0],
            first_ffn,
        )
    ]
    for w in windows[1:]:
        kept, arrived = scatter_pair(kept_all[w - 1], sent_all[w - 1], "tensor")
        middle, normed_mid = second_norm(
            (tokens, (w,)), hold(kept, begun[-1]), arrived, norms
        )
        middles.append(middle)
        begun.append(
            feed_first(spread(normed_mid, "tensor"), cot_blocks[w], factors[w], first_ffn)
        )
    step = min(512, part)

    def feed_weights(done, half, swaps, collective_id):
        return weight_grads(
            [
                ([one[0] for one in done], [one[3] for one in done]),
                ([one[0] for one in done], [one[4] for one in done]),
                ([one[1] for one in done], [one[2] for one in done]),
            ],
            step,
            "feed_weights",
            half,
            2,
            swaps,
            collective_id,
        )

    g_first_part = feed_weights(begun, 0, (), None)
    g_first = lax.psum_scatter(g_first_part, shards, scatter_dimension=0, tiled=True)
    fed = []
    for w in windows:
        x_rows, gy_rows, *parts = hold(begun[w], fed[-1] if fed else g_first_part)
        ended = feed_last(x_rows, gy_rows, parts[3:], parts[:3], last_ffn)
        fed.append((x_rows, gy_rows, *ended))
    grad_middles, second_sums = [], []

    def through_second_norm(w, kept, arrived):
        grad_middle, low, sums = second_norm_back(
            factors[w], kept, arrived, middles[w], (cotangent, (w,)), norms
        )
        grad_middles.append(grad_middle)
        second_sums.append(sums)
        return low

    lows = []
    for w in windows[:-1]:
        kept, arrived = scatter_pair(fed[w][7], fed[w][8], "tensor")
        lows.append(through_second_norm(w, hold(kept, fed[w + 1]), arrived))
    masks = [other + 1 for other in others]
    g_last_part, arrived, *arrived_lows = feed_weights(
        hold(fed, grad_middles),
        1,
        [(fed[-1][8], [tensor_size // 2])] + [(low, masks) for low in lows],
        4,
    )
    g_last = lax.psum_scatter(g_last_part, shards, scatter_dimension=0, tiled=True)
    kept, arrived = later_pair(fed[-1][7], arrived[0], "tensor")
    last_low = through_second_norm(windows[-1], hold(kept, g_last_part), arrived)
    grad_mid_blocks = [
        [low] + [arrived[other] for other in others] for low, arrived in zip(lows, arrived_lows)
    ] + [[last_low]]

    grad_q, grad_k, grad_v, grad_mid_rows, *arrived_results = attend_back(
        hold(queries, g_last_part),
        wide_attended,
        logs,
        slots_all,
        grad_mid_blocks,
        w_att,
        (cosine, sine),
        [fed[w][6] for w in windows],
    )
    output = results(
        [
            (middles[w], *later_pair(fed[w][5], arrived_results[w], "tensor"))
            for w in windows
        ]
    )

    first_parts = []
    for w in windows:
        kept, sent = turn_back(w, (grad_q, grad_k, grad_v), w_att)
        first_parts.append(scatter_pair(kept, sent, "tensor"))
    g_att_part = weight_grads(
        [
            ([(normed_rows, (w,)) for w in windows], [(grad, (w,)) for w in windows])
            for grad in (grad_q, grad_k, grad_v)
        ]
        + [([(grad_mid_rows, (w,)) for w in windows], [(attended, (w,)) for w in windows])],
        head_cols,
        "attend_weights",
    )
    input_grad = None
    first_sums = []
    for w in windows:
        kept, arrived = first_parts[w]
        input_grad, sums = first_norm_back(
            w,
            windows_here,
            hold(kept, g_att_part),
            arrived,
            (tokens, (w,)),
            grad_middles[w],
            norms,
            input_grad,
        )
        first_sums.append(sums)

    g_att, vectors = reduce_grads(g_att_part, first_sums, second_sums, tensor_size - 1)
    norm_sums = vectors[:4, : norm1_gain.shape[0]]
    ffn_grads = [
        jnp.concatenate(
            [g_first[:, at * part : (at + 1) * part], g_last[:, at * part : (at + 1) * part]],
            axis=1,
        ).astype(F32)
        for at in range(3)
    ]

    return (
        output,
        input_grad,
        norm_sums[0],
        norm_sums[1],
        g_att[:, :head_cols],
        g_att[:, head_cols : 2 * head_cols],
        g_att[:, 2 * head_cols : 3 * head_cols],
        g_att[:, 3 * head_cols :].T,
        norm_sums[2],
        norm_sums[3],
        ffn_grads[0],
        ffn_grads[1],
        ffn_grads[2].T,
    )


def solution(mesh):
    rows = P("dp", ("seq", "tensor"), None)
    vector = P(("dp", "seq", "tensor"))
    tall = P(("dp", "seq"), "tensor")
    flat = P("tensor", ("dp", "seq"))
    return jax.shard_map(
        local,
        mesh=mesh,
        in_specs=(
            rows, rows, P("dp"), P("dp"), P(), vector, vector,
            tall, tall, tall, flat, vector, vector, tall, tall, flat,
        ),
        out_specs=(
            rows, rows, vector, vector, tall, tall, tall, flat,
            vector, vector, tall, tall, flat,
        ),
        check_vma=False,
    )
```

```python
import functools
import math

import jax
import jax.numpy as jnp
from jax import lax
from jax.experimental import pallas as pl
from jax.experimental.pallas import tpu as pltpu
from jax.sharding import PartitionSpec as P

HEAD_DIM = 64
EPSILON = 1e-05
ROPE_BASE = 10000.0
PAIR = 2 * HEAD_DIM
LOG2E = math.log2(math.e)
BF16 = jnp.bfloat16
F32 = jnp.float32
VMEM_BYTES = 56 * 1024 * 1024
MESH = pl.DeviceIdType.MESH


def angles(positions, head_dim):
    half_dim = head_dim // 2
    inverse = jnp.exp(
        -(math.log(ROPE_BASE) * 2.0 / head_dim) * jnp.arange(half_dim, dtype=F32)
    )
    phase_angle = positions[:, None] * inverse[None, :]
    return (jnp.cos(phase_angle), jnp.sin(phase_angle))


def dot_nn(left, right):
    return lax.dot_general(left, right, (((1,), (0,)), ((), ())), preferred_element_type=F32)


def dot_nt(left, right):
    return lax.dot_general(left, right, (((1,), (1,)), ((), ())), preferred_element_type=F32)


def dot_tn(left, right):
    return lax.dot_general(left, right, (((0,), (0,)), ((), ())), preferred_element_type=F32)


def swap(array, axis, bit):
    size = lax.axis_size(axis)
    return lax.ppermute(array, axis, [(i, i ^ bit) for i in range(size)])


def spread(array, axis):
    blocks = [array]
    bit = 1
    while bit < lax.axis_size(axis):
        blocks = blocks + [swap(block, axis, bit) for block in blocks]
        bit *= 2
    return blocks


def scatter_pair(kept, sent, axis):
    return later_pair(kept, swap(sent, axis, lax.axis_size(axis) // 2), axis)


def later_pair(kept, arrived, axis):
    bit = lax.axis_size(axis) // 2
    while bit > 1:
        partial = kept + arrived.astype(F32)
        bit //= 2
        rows = partial.shape[0] // 2
        kept, arrived = partial[:rows], swap(partial[rows:].astype(BF16), axis, bit)
    return kept, arrived


def hold(values, *others):
    return lax.optimization_barrier((values, others))[0]


def run(kernel, name, out_shape, flops, args, collective_id=None, **options):
    trading = {} if collective_id is None else dict(collective_id=collective_id, has_side_effects=True)
    moved = sum(math.prod(array.shape) * array.dtype.itemsize for array in args)
    outs = out_shape if isinstance(out_shape, list) else [out_shape]
    moved += sum(math.prod(array.shape) * array.dtype.itemsize for array in outs)
    return pl.pallas_call(
        kernel,
        out_shape=out_shape,
        compiler_params=pltpu.CompilerParams(vmem_limit_bytes=VMEM_BYTES, **trading),
        cost_estimate=pl.CostEstimate(
            flops=int(flops), bytes_accessed=int(moved), transcendentals=0
        ),
        name=name,
        **options,
    )(*args)


def shaped(shape, dtype):
    return jax.ShapeDtypeStruct(shape, dtype)


SCALAR = pl.BlockSpec(memory_space=pltpu.SMEM)


def plane(operand, block=None, index=None):
    array, at = operand if isinstance(operand, tuple) else (operand, ())
    shape = array.shape[len(at) :] if block is None else block
    place = (lambda *i: (0,) * len(shape)) if index is None else index
    return array, pl.BlockSpec((None,) * len(at) + tuple(shape), lambda *i: at + place(*i))


def normalise(stream):
    row_mean = jnp.mean(stream, axis=-1, keepdims=True)
    centred = stream - row_mean
    variance = jnp.mean(centred * centred, axis=-1, keepdims=True)
    inv_std = lax.rsqrt(variance + EPSILON)
    return centred * inv_std, inv_std


def norm_back(grad_normed, normed, inv_std, norm_gain):
    scaled_grad = grad_normed * norm_gain
    return inv_std * (
        scaled_grad
        - jnp.mean(scaled_grad, axis=-1, keepdims=True)
        - normed * jnp.mean(scaled_grad * normed, axis=-1, keepdims=True)
    )


def first_head(shape):
    return lax.broadcasted_iota(jnp.int32, shape, 1) % PAIR < HEAD_DIM


def swap_halves(values):
    half = HEAD_DIM // 2
    lane = lax.broadcasted_iota(jnp.int32, values.shape, 1)
    ahead = pltpu.roll(values, PAIR - half, 1)
    behind = pltpu.roll(values, half, 1)
    return jnp.where(lane % HEAD_DIM < half, ahead, behind)


def project_kernel(blocks, norms_ref, w_ref, cos_ref, sin_ref, *refs):
    x_refs = refs[:blocks]
    normed_ref, q_ref, kv_ref = refs[blocks:]
    cols = q_ref.shape[2]
    gain, bias = norms_ref[0:1, :], norms_ref[1:2, :]
    at_row = 0
    for x_ref in x_refs:
        rows = slice(at_row, at_row + x_ref.shape[1])
        at_row += x_ref.shape[1]
        normed = (normalise(x_ref[0].astype(F32))[0] * gain + bias).astype(BF16)
        normed_ref[0, rows, :] = normed
        cosine, sine = cos_ref[rows, :], sin_ref[rows, :]
        query = dot_nn(normed, w_ref[:, :cols])
        key = dot_nn(normed, w_ref[:, cols : 2 * cols])
        for at in range(0, cols, PAIR):
            part = slice(at, at + PAIR)
            one = query[:, part]
            q_ref[0, rows, part] = (one * cosine + swap_halves(one) * sine).astype(BF16)
            one = key[:, part]
            kv_ref[0, 0, rows, part] = (one * cosine + swap_halves(one) * sine).astype(BF16)
        kv_ref[0, 1, rows, :] = dot_nn(normed, w_ref[:, 2 * cols : 3 * cols]).astype(BF16)


def project(x_blocks, norms, w_att, cosine, sine):
    windows = x_blocks[0].shape[0]
    width, cols = w_att.shape[0], w_att.shape[1] // 4
    rows = sum(block.shape[1] for block in x_blocks)
    args = [norms, w_att, cosine, sine, *x_blocks]
    return run(
        functools.partial(project_kernel, len(x_blocks)),
        "project",
        [
            shaped((windows, rows, width), BF16),
            shaped((windows, rows, cols), BF16),
            shaped((windows, 2, rows, cols), BF16),
        ],
        6 * windows * rows * width * cols,
        args,
        grid=(windows,),
        in_specs=[pl.BlockSpec(array.shape, lambda i: (0, 0)) for array in args[:4]]
        + [pl.BlockSpec((1,) + block.shape[1:], lambda i: (i, 0, 0)) for block in x_blocks],
        out_specs=[
            pl.BlockSpec((1, rows, width), lambda i: (i, 0, 0)),
            pl.BlockSpec((1, rows, cols), lambda i: (i, 0, 0)),
            pl.BlockSpec((1, 2, rows, cols), lambda i: (i, 0, 0, 0)),
        ],
    )


def flipped(index, mask):
    bit = 1
    while bit <= mask:
        if mask & bit:
            index = index + bit - 2 * bit * ((index // bit) % 2)
        bit *= 2
    return index


def greet(peers):
    barrier = pltpu.get_barrier_semaphore()
    for peer in peers:
        pl.semaphore_signal(barrier, inc=1, device_id=peer, device_id_type=MESH)
    pl.semaphore_wait(barrier, len(peers))


def send(source, target, send_sem, recv_sem, peer):
    return pltpu.make_async_remote_copy(
        src_ref=source,
        dst_ref=target,
        send_sem=send_sem,
        recv_sem=recv_sem,
        device_id=peer,
        device_id_type=MESH,
    )


def half_chip_peers():
    seq, depth = lax.axis_index("seq"), lax.axis_index("dp")
    size = lax.axis_size("dp")
    return {
        "far": {"seq": flipped(seq, 2)},
        "up": {"dp": (depth + 1) % size},
        "down": {"dp": (depth + size - 1) % size},
        "core": {"seq": flipped(seq, 1)},
    }


class Route:
    PARTS = ((0, 0), (3, 0), (1, 0), (2, 0), (0, 1), (3, 1), (1, 1), (2, 1))

    def __init__(self, whole, rows, send_sem, recv_sem, own):
        self.whole, self.rows, self.own = whole, rows, own
        self.send_sem, self.recv_sem = send_sem, recv_sem
        self.seq, self.depth = lax.axis_index("seq"), lax.axis_index("dp")
        self.peers = half_chip_peers()

    def part(self, place):
        turn, other = place
        seq = flipped(self.seq, 2) if other else self.seq
        at = (((self.depth + turn) % lax.axis_size("dp")) * lax.axis_size("seq") + seq) * self.rows
        return self.whole.at[pl.ds(pl.multiple_of(at, self.rows), self.rows), :]

    def message(self, number):
        if number >= 7:
            place, peer = self.PARTS[number - 7], "core"
        else:
            place, peer = (
                ((0, 0), "up"),
                ((0, 0), "down"),
                ((3, 0), "up"),
                ((0, 0), "far"),
                ((3, 0), "far"),
                ((1, 0), "far"),
                ((2, 0), "far"),
            )[number]
        target = self.part(place)
        return send(
            self.own if place == (0, 0) else target,
            target,
            self.send_sem.at[number],
            self.recv_sem.at[number],
            self.peers[peer],
        )

    def start(self, *numbers):
        for number in numbers:
            self.message(number).start()

    def arrived(self, *numbers):
        for number in numbers:
            self.message(number).wait_recv()

    def sent(self, *numbers):
        for number in numbers:
            self.message(number).wait_send()


MESSAGES = 15


def gather_kernel(trades, att_ref, tile_ref, tokens_ref, *refs):
    att_all, norms_ref, tokens_all = refs[:3]
    tiles, pair_of_tiles = refs[3:5]
    att_send, att_recv, tile_send, tile_recv = refs[5:9]
    own_sem, tokens_send, tokens_recv, pair_send, pair_recv = refs[9:]
    tensor = lax.axis_index("tensor")
    others = [{"tensor": flipped(tensor, other + 1)} for other in range(trades)]
    att = Route(att_all, att_ref.shape[0], att_send, att_recv, att_ref)
    tile_rows = tile_ref.shape[0]
    small = Route(tiles, pair_of_tiles.shape[0], tile_send, tile_recv, pair_of_tiles)

    def tokens_trade(other):
        return send(
            tokens_ref,
            tokens_all.at[other],
            tokens_send.at[other],
            tokens_recv.at[other],
            others[other],
        )

    own_rows = pl.ds(pl.multiple_of(tensor * tile_rows, tile_rows), tile_rows)

    def pair_trade(other):
        return send(
            tile_ref,
            pair_of_tiles.at[own_rows, :],
            pair_send.at[other],
            pair_recv.at[other],
            others[other],
        )

    own_copies = [
        pltpu.make_async_copy(att_ref, att.part((0, 0)), own_sem.at[0]),
        pltpu.make_async_copy(tile_ref, pair_of_tiles.at[own_rows, :], own_sem.at[1]),
        pltpu.make_async_copy(pair_of_tiles, small.part((0, 0)), own_sem.at[2]),
    ]

    greet(list(att.peers.values()) + others)
    for other in range(trades):
        pair_trade(other).start()
    own_copies[1].start()
    att.start(0, 1, 3, 7)
    own_copies[1].wait()
    for other in range(trades):
        pair_trade(other).wait_recv()
    small.start(0, 1, 3, 7)
    own_copies[0].start()
    own_copies[2].start()
    for other in range(trades):
        tokens_trade(other).start()
    for route in (small, att):
        route.arrived(0)
        route.start(2, 4, 8)
    for route in (small, att):
        route.arrived(3)
        route.start(11)
    for route in (small, att):
        route.arrived(1)
        route.start(5, 9)
    for route in (small, att):
        route.arrived(2)
        route.start(6, 10)
    for route in (small, att):
        route.arrived(4)
        route.start(12)
        route.arrived(5)
        route.start(13)
        route.arrived(6)
        route.start(14)
    for route in (small, att):
        route.arrived(*range(7, MESSAGES))
    own_copies[2].wait()
    shard = norms_ref.shape[1] // (tiles.shape[0] // tile_rows)
    total = None
    for device in range(tiles.shape[0] // tile_rows):
        tile = tiles[device * tile_rows : (device + 1) * tile_rows, :]
        norms_ref[:, device * shard : (device + 1) * shard] = tile[:, :shard]
    for depth in range(lax.axis_size("dp")):
        at = depth * (tiles.shape[0] // lax.axis_size("dp"))
        one = tiles[at + 4 : at + 5, :]
        total = one if total is None else total + one
    norms_ref[4:5, : total.shape[1]] = total
    for route in (att, small):
        route.sent(*range(MESSAGES))
    own_copies[0].wait()
    for other in range(trades):
        pair_trade(other).wait_send()
        tokens_trade(other).wait_recv()
        tokens_trade(other).wait_send()


def gather(att, tile, tokens, trades):
    count = lax.axis_size("dp") * lax.axis_size("seq")
    rows = att.shape[0]
    group = tile.shape[0] * (trades + 1)
    anywhere = pl.BlockSpec(memory_space=pl.ANY)
    vmem = pl.BlockSpec(memory_space=pltpu.VMEM)
    dma = pltpu.SemaphoreType.DMA
    return run(
        functools.partial(gather_kernel, trades),
        "gather",
        [
            shaped((count * rows, att.shape[1]), BF16),
            shaped((tile.shape[0], count * rows), F32),
            shaped((trades,) + tokens.shape, BF16),
        ],
        0,
        [att, tile, tokens],
        collective_id=1,
        in_specs=[vmem, vmem, anywhere],
        out_specs=[anywhere, vmem, anywhere],
        scratch_shapes=[pltpu.VMEM((count * group, 128), F32), pltpu.VMEM((group, 128), F32)]
        + [dma((MESSAGES,))] * 4
        + [dma((3,)), dma((trades,)), dma((trades,)), dma((trades,)), dma((trades,))],
    )


def attend_kernel(windows, pairs, trades, exp_scale, *refs):
    stages = (trades + 1).bit_length() - 1
    q_ref, w_ref, kv_ref, cot_ref, x_ref, norms_ref = refs[:6]
    low_ref, wide_ref, log_ref, kept_ref, sent_ref, slots_ref, cots_ref = refs[6:13]
    middle_ref, normed_ref, others_ref = refs[13:16]
    slots, acc_all, top_all, total_all, mixed_rows = refs[16:21]
    own_sem, send_sem, recv_sem, save_sem, cot_send, cot_recv = refs[21:27]
    early_kept, early_normed, early_sem, early_recv, normed_sem, normed_recv = refs[27:33]
    early_sent, early_arrived = refs[33 : 33 + stages], refs[33 + stages :]
    step = pl.program_id(0)
    near_steps = windows * pairs
    steps = 2 * near_steps
    turn = step % (2 * pairs)
    is_far = turn >= pairs
    number = step // (2 * pairs) * pairs + turn % pairs
    seq, tensor = lax.axis_index("seq"), lax.axis_index("tensor")
    core_peer = {"seq": flipped(seq, 1)}
    far_peer = {"seq": flipped(seq, 2)}
    cot_peers = [{"tensor": flipped(tensor, other + 1)} for other in range(trades)]

    def piece(number):
        columns = pl.ds(pl.multiple_of((number % pairs) * PAIR, PAIR), PAIR)
        return kv_ref.at[number // pairs, :, :, columns]

    def own_copy(number):
        return pltpu.make_async_copy(piece(number), slots.at[number, 0], own_sem.at[number])

    def trade(number, slot):
        peer = far_peer if slot == 2 else core_peer
        source = slots.at[number, 2] if slot == 3 else piece(number)
        return send(
            source,
            slots.at[number, slot],
            send_sem.at[number, slot - 1],
            recv_sem.at[number, slot - 1],
            peer,
        )

    def cot_trade(other):
        return send(
            cot_ref, cots_ref.at[other], cot_send.at[other], cot_recv.at[other], cot_peers[other]
        )

    def early_trade(stage):
        return send(
            early_sent[stage],
            early_arrived[stage],
            early_sem.at[stage],
            early_recv.at[stage],
            {"tensor": flipped(tensor, (trades + 1) >> (stage + 1))},
        )

    def normed_trade(other):
        return send(
            early_normed,
            others_ref.at[other],
            normed_sem.at[other],
            normed_recv.at[other],
            cot_peers[other],
        )

    def save(number, slot):
        return pltpu.make_async_copy(
            slots.at[number, slot], slots_ref.at[number, slot], save_sem.at[number, slot]
        )

    @pl.when(step == 0)
    def _():
        greet([core_peer, far_peer] + cot_peers)

        @pl.loop(0, near_steps)
        def _(number):
            own_copy(number).start()
            trade(number, 1).start()
            trade(number, 2).start()

        for other in range(trades):
            cot_trade(other).start()

    @pl.when(step == 2 * pairs)
    def _():
        early_trade(0).start()

    @pl.when(step == min(3 * pairs + 1, steps - 2))
    def _():
        kept = early_kept[...]
        for stage in range(stages):
            early_trade(stage).wait_recv()
            kept = kept + early_arrived[stage][...].astype(F32)
            if stage + 1 < stages:
                half = kept.shape[0] // 2
                early_sent[stage + 1][...] = kept[half:].astype(BF16)
                early_trade(stage + 1).start()
                kept = kept[:half]
        middle = x_ref[...].astype(F32) + kept
        middle_ref[...] = middle
        normed = (normalise(middle)[0] * norms_ref[2:3, :] + norms_ref[3:4, :]).astype(BF16)
        normed_ref[...] = normed
        early_normed[...] = normed

    @pl.when(step == min(3 * pairs + 2, steps - 1))
    def _():
        for other in range(trades):
            normed_trade(other).start()

    relayed = step // (2 * pairs) * pairs + turn - (pairs - 1)

    @pl.when(jnp.logical_and(turn >= pairs - 1, turn < 2 * pairs - 1))
    def _():
        trade(relayed, 2).wait_recv()
        trade(relayed, 3).start()
        save(relayed, 2).start()

    @pl.when(jnp.logical_not(is_far))
    def _():
        own_copy(number).wait()
        trade(number, 1).wait_recv()
        save(number, 0).start()
        save(number, 1).start()
        acc_all[number] = jnp.zeros(acc_all.shape[1:], F32)
        total_all[number] = jnp.zeros(acc_all.shape[1:], F32)
        top_all[number] = jnp.full(acc_all.shape[1:], -1e30, F32)

    @pl.when(is_far)
    def _():
        trade(number, 3).wait_recv()
        save(number, 3).start()

    query = q_ref[0]
    is_first = first_head(query.shape)
    base = jnp.where(is_far, 2, 0)
    carried_top = top_all[number]
    outs, tops = [], []
    for head in range(2):
        mine = is_first if head == 0 else jnp.logical_not(is_first)
        own_query = jnp.where(mine, query, jnp.zeros_like(query))
        scores = [dot_nt(own_query, slots[number, base + slot, 0]) for slot in range(2)]
        at = head * HEAD_DIM
        top = carried_top[:, at : at + 1]
        for one in scores:
            top = jnp.maximum(top, one.max(axis=1, keepdims=True))
        shift = top * exp_scale
        mixed = None
        for slot, one in enumerate(scores):
            weight = jnp.exp2(one * exp_scale - shift).astype(BF16)
            value = slots[number, base + slot, 1]
            lane_first = first_head(value.shape)
            lane_mine = lane_first if head == 0 else jnp.logical_not(lane_first)
            term = dot_nn(weight, jnp.where(lane_mine, value, jnp.ones_like(value)))
            mixed = term if mixed is None else mixed + term
        outs.append(mixed)
        tops.append(jnp.broadcast_to(top, mixed.shape))
    top = jnp.where(is_first, tops[0], tops[1])
    fade = jnp.exp2((carried_top - top) * exp_scale)
    acc = jnp.where(is_first, outs[0], outs[1]) + acc_all[number] * fade
    total = pltpu.roll(jnp.where(is_first, outs[1], outs[0]), HEAD_DIM, 1) + total_all[number] * fade

    @pl.when(jnp.logical_not(is_far))
    def _():
        acc_all[number] = acc
        top_all[number] = top
        total_all[number] = total

    @pl.when(is_far)
    def _():
        attended = acc / total
        low = attended.astype(BF16)
        low_ref[0] = low
        wide_ref[0] = attended
        log_ref[0] = (top * exp_scale + jnp.log2(total)).T
        term = dot_nt(low, w_ref[...])
        pair = number % pairs

        @pl.when(pair == 0)
        def _():
            mixed_rows[...] = term

        @pl.when(pair > 0)
        def _():
            mixed_rows[...] += term

        @pl.when(jnp.logical_and(pair == pairs - 1, number >= pairs))
        def _():
            half = kept_ref.shape[1]
            kept_ref[0] = mixed_rows[:half]
            sent_ref[0] = mixed_rows[half:].astype(BF16)

        @pl.when(number == pairs - 1)
        def _():
            half = kept_ref.shape[1]
            early_kept[...] = mixed_rows[:half]
            early_sent[0][...] = mixed_rows[half:].astype(BF16)

    @pl.when(step == steps - 1)
    def _():
        @pl.loop(0, near_steps)
        def _(number):
            for slot in range(1, 4):
                trade(number, slot).wait_send()
            for slot in range(4):
                save(number, slot).wait()

        for stage in range(stages):
            early_trade(stage).wait_send()
        for other in range(trades):
            cot_trade(other).wait_send()
            cot_trade(other).wait_recv()
            normed_trade(other).wait_send()
            normed_trade(other).wait_recv()


def attend(queries, own_kv, w_att, cotangent, tokens, norms, trades):
    windows, rows, cols = queries.shape
    width = w_att.shape[0]
    pairs = cols // PAIR
    near = windows * pairs
    out_at = 3 * pairs

    def far(i):
        turn = i % (2 * pairs)
        done = i // (2 * pairs) * pairs
        return jnp.where(turn >= pairs, done + turn - pairs, jnp.maximum(done - 1, 0))

    anywhere = pl.BlockSpec(memory_space=pl.ANY)
    wide = pl.BlockSpec((1, rows, PAIR), lambda i: (far(i) // pairs, 0, far(i) % pairs))
    half = pl.BlockSpec(
        (1, rows // 2, width), lambda i: (jnp.maximum(far(i) // pairs, 1) - 1, 0, 0)
    )
    own_rows = tokens.shape[1]
    own = pl.BlockSpec((own_rows, width), lambda i: (0, 0))
    stages = [rows >> (stage + 1) for stage in range((trades + 1).bit_length() - 1)]
    state = pltpu.VMEM((near, rows, PAIR), F32)
    dma = pltpu.SemaphoreType.DMA
    return run(
        functools.partial(attend_kernel, windows, pairs, trades, LOG2E / math.sqrt(HEAD_DIM)),
        "attend",
        [
            shaped((windows, rows, cols), BF16),
            shaped((windows, rows, cols), F32),
            shaped((windows, cols, rows), F32),
            shaped((windows - 1, rows // 2, width), F32),
            shaped((windows - 1, rows // 2, width), BF16),
            shaped((near, 4, 2, rows, PAIR), BF16),
            shaped((trades,) + cotangent.shape, BF16),
            shaped((own_rows, width), F32),
            shaped((own_rows, width), BF16),
            shaped((trades, own_rows, width), BF16),
        ],
        64 * windows * rows * rows * cols,
        [queries, w_att, own_kv, cotangent, tokens, norms],
        collective_id=0,
        grid=(2 * near,),
        in_specs=[
            pl.BlockSpec((1, rows, PAIR), lambda i: (i // (2 * pairs), 0, i % pairs)),
            pl.BlockSpec((width, PAIR), lambda i: (0, out_at + far(i) % pairs)),
            anywhere,
            anywhere,
            pl.BlockSpec((None, own_rows, width), lambda i: (0, 0, 0)),
            pl.BlockSpec(norms.shape, lambda i: (0, 0)),
        ],
        out_specs=[
            wide,
            wide,
            pl.BlockSpec((1, PAIR, rows), lambda i: (far(i) // pairs, far(i) % pairs, 0)),
            half,
            half,
            anywhere,
            anywhere,
            own,
            own,
            anywhere,
        ],
        scratch_shapes=[
            pltpu.VMEM((near, 4, 2, rows, PAIR), BF16),
            state,
            state,
            state,
            pltpu.VMEM((rows, width), F32),
            dma((near,)),
            dma((near, 3)),
            dma((near, 3)),
            dma((near, 4)),
            dma((trades,)),
            dma((trades,)),
            pltpu.VMEM((rows // 2, width), F32),
            pltpu.VMEM((own_rows, width), BF16),
            dma((len(stages),)),
            dma((len(stages),)),
            dma((trades,)),
            dma((trades,)),
        ]
        + [pltpu.VMEM((count, width), BF16) for count in stages] * 2,
    )


def attend_back_kernel(windows, pairs, blocks, exp_scale, score_scale, *refs):
    q_ref, wide_ref, log_ref, slots_ref, w_ref, cos_ref, sin_ref, last_ref = refs[:8]
    trades = blocks - 1
    known = (windows - 1) * blocks + 1
    grad_refs = list(refs[8 : 8 + known])
    refs = refs[8 + known :]
    sent_refs, refs = refs[:windows], refs[windows:]
    gq_ref, gk_ref, gv_ref, rows_ref = refs[:4]
    arrived_refs, refs = refs[4 : 4 + windows], refs[4 + windows :]
    dq_all, do_all, far_kept, far_sent, far_core, far_x, near_kept, near_sent, near_core = refs[:9]
    send_sem, recv_sem, result_send, result_recv, last_send, last_recv, last_others = refs[9:]
    grad_refs += [last_others.at[other] for other in range(trades)]
    step = pl.program_id(0)
    count = windows * pairs
    seq, tensor = lax.axis_index("seq"), lax.axis_index("tensor")
    core_peer = {"seq": flipped(seq, 1)}
    far_peer = {"seq": flipped(seq, 2)}
    result_peer = {"tensor": flipped(tensor, lax.axis_size("tensor") // 2)}

    def trade(kind, number):
        source, target, peer = (
            (far_sent, far_core, core_peer),
            (far_kept, far_x, far_peer),
            (near_sent, near_core, core_peer),
        )[kind]
        return send(
            source.at[number],
            target.at[number],
            send_sem.at[kind, number],
            recv_sem.at[kind, number],
            peer,
        )

    def result_trade(w):
        return send(
            sent_refs[w], arrived_refs[w], result_send.at[w], result_recv.at[w], result_peer
        )

    others = [{"tensor": flipped(tensor, other + 1)} for other in range(trades)]

    def last_trade(other):
        return send(
            last_ref, last_others.at[other], last_send.at[other], last_recv.at[other], others[other]
        )

    @pl.when(step == 0)
    def _():
        greet([core_peer, far_peer] + others)
        for other in range(trades):
            last_trade(other).start()
        for w in range(windows):
            result_trade(w).start()

    def at_step(first, body):
        number = step - first

        @pl.when(jnp.logical_and(number >= 0, number < count))
        def _():
            body(number)

    def send_far(number):
        trade(0, number).start()

    def add_far(number):
        trade(0, number).wait_recv()
        far_kept[number] = (
            far_kept[number].astype(F32) + far_core[number].astype(F32)
        ).astype(BF16)

    def send_x(number):
        trade(1, number).start()

    def send_near(number):
        trade(2, number).start()

    def finish(number):
        trade(2, number).wait_recv()
        trade(1, number).wait_recv()
        total = (
            near_kept[number].astype(F32)
            + near_core[number].astype(F32)
            + far_x[number].astype(F32)
        )
        key = total[0]
        gk_ref[0] = (key * cos_ref[...] - swap_halves(key) * sin_ref[...]).astype(BF16)
        gv_ref[0] = total[1].astype(BF16)

    at_step(1, send_far)
    at_step(3, send_x)
    at_step(count + 1, send_near)
    at_step(2, add_far)
    at_step(count + 2, finish)

    for w in range(windows):

        @pl.when(step == w * pairs)
        def _(w=w):
            if w == windows - 1:
                for other in range(trades):
                    last_trade(other).wait_recv()
            at_row = 0
            for grad_ref in grad_refs[w * blocks : (w + 1) * blocks]:
                rows_ref[0, at_row : at_row + grad_ref.shape[0], :] = grad_ref[...]
                at_row += grad_ref.shape[0]

    def gradients(number, grad_out, kept, sent):
        query = q_ref[0]
        is_first = first_head(query.shape)
        overlap = (grad_out.astype(F32) * wide_ref[0]).T
        logs = log_ref[0]
        zero = jnp.zeros_like(query)
        own_q, own_do, row_log, row_sum = [], [], [], []
        for head in range(2):
            mine = is_first if head == 0 else jnp.logical_not(is_first)
            own_q.append(jnp.where(mine, query, zero))
            own_do.append(jnp.where(mine, grad_out, zero))
            at = head * HEAD_DIM
            row_log.append(logs[at : at + 1, :])
            row_sum.append(jnp.sum(overlap[at : at + HEAD_DIM, :], axis=0, keepdims=True))
        dq_parts = [None, None]
        for slot, target in enumerate((kept, sent)):
            key, value = slots_ref[0, slot, 0], slots_ref[0, slot, 1]
            key_turned = key.T
            grad_key, grad_value = None, None
            for head in range(2):
                scores = dot_nt(key, own_q[head])
                probs = jnp.exp2(scores * exp_scale - row_log[head])
                grad_probs = dot_nt(value, own_do[head])
                grad_scores = (probs * (grad_probs - row_sum[head])).astype(BF16)
                term_v = dot_nn(probs.astype(BF16), own_do[head])
                term_k = dot_nn(grad_scores, own_q[head])
                at = head * HEAD_DIM
                term_q = dot_nn(key_turned[at : at + HEAD_DIM, :], grad_scores)
                grad_value = term_v if grad_value is None else grad_value + term_v
                grad_key = term_k if grad_key is None else grad_key + term_k
                dq_parts[head] = term_q if dq_parts[head] is None else dq_parts[head] + term_q
            target[number, 0] = (grad_key * score_scale).astype(BF16)
            target[number, 1] = grad_value.astype(BF16)
        return jnp.concatenate(dq_parts, axis=0).T * score_scale

    @pl.when(step < count)
    def _():
        grad_out = dot_nn(rows_ref[0], w_ref[...]).astype(BF16)
        do_all[step] = grad_out
        dq_all[step] = gradients(step, grad_out, far_kept, far_sent)

    @pl.when(jnp.logical_and(step >= count, step < 2 * count))
    def _():
        number = step - count
        grad_query = dq_all[number] + gradients(number, do_all[number], near_kept, near_sent)
        gq_ref[0] = (grad_query * cos_ref[...] - swap_halves(grad_query) * sin_ref[...]).astype(
            BF16
        )

    @pl.when(step == pl.num_programs(0) - 1)
    def _():
        @pl.loop(0, count)
        def _(number):
            for kind in range(3):
                trade(kind, number).wait_send()

        for other in range(trades):
            last_trade(other).wait_send()
        for w in range(windows):
            result_trade(w).wait_send()
            result_trade(w).wait_recv()


def attend_back(queries, wide, logs, slots_all, grad_blocks, w_att, tables, sent):
    windows, rows, cols = queries.shape
    width = w_att.shape[0]
    pairs = cols // PAIR
    count = windows * pairs
    out_at = 3 * pairs
    score_scale = 1.0 / math.sqrt(HEAD_DIM)
    blocks = lax.axis_size("tensor")
    grads = [block for one in grad_blocks for block in one]
    last = grads[-1]

    def spot(lag, last=None):
        def index(i):
            number = jnp.clip(i - lag, 0, count - 1)
            return (number // pairs, 0, number % pairs)

        return pl.BlockSpec((1, rows, PAIR), index)

    def both(i):
        return jnp.minimum(i, 2 * count - 1) % count

    dma = pltpu.SemaphoreType.DMA
    piece = pltpu.VMEM((count, 2, rows, PAIR), BF16)
    anywhere = pl.BlockSpec(memory_space=pl.ANY)
    return run(
        functools.partial(
            attend_back_kernel, windows, pairs, blocks, score_scale * LOG2E, score_scale
        ),
        "attend_back",
        [shaped((windows, rows, cols), BF16)] * 3
        + [shaped((windows, rows, width), BF16)]
        + [shaped(one.shape, BF16) for one in sent],
        160 * windows * rows * rows * cols,
        [queries, wide, logs, slots_all, w_att, *tables, last, *grads, *sent],
        collective_id=2,
        grid=(2 * count + 2,),
        in_specs=[
            pl.BlockSpec((1, rows, PAIR), lambda i: (both(i) // pairs, 0, both(i) % pairs)),
            pl.BlockSpec((1, rows, PAIR), lambda i: (both(i) // pairs, 0, both(i) % pairs)),
            pl.BlockSpec((1, PAIR, rows), lambda i: (both(i) // pairs, both(i) % pairs, 0)),
            pl.BlockSpec(
                (1, 2, 2, rows, PAIR),
                lambda i: (both(i), jnp.where(i < count, 1, 0), 0, 0, 0),
            ),
            pl.BlockSpec((width, PAIR), lambda i: (0, out_at + jnp.minimum(i, count - 1) % pairs)),
            pl.BlockSpec((rows, PAIR), lambda i: (0, 0)),
            pl.BlockSpec((rows, PAIR), lambda i: (0, 0)),
            anywhere,
        ]
        + [pl.BlockSpec(block.shape, lambda i: (0, 0)) for block in grads]
        + [anywhere] * windows,
        out_specs=[
            spot(count),
            spot(count + 2),
            spot(count + 2),
            pl.BlockSpec((1, rows, width), lambda i: (jnp.minimum(i // pairs, windows - 1), 0, 0)),
        ]
        + [anywhere] * windows,
        scratch_shapes=[pltpu.VMEM((count, rows, PAIR), F32), pltpu.VMEM((count, rows, PAIR), BF16)]
        + [piece] * 7
        + [dma((3, count)), dma((3, count)), dma((windows,)), dma((windows,))]
        + [dma((blocks - 1,)), dma((blocks - 1,)), pltpu.VMEM((blocks - 1,) + last.shape, BF16)],
    )


def middle_kernel(x_ref, kept_ref, arrived_ref, norms_ref, middle_ref, normed_ref):
    middle = x_ref[...].astype(F32) + (kept_ref[...] + arrived_ref[...].astype(F32))
    middle_ref[...] = middle
    normed_ref[...] = (
        normalise(middle)[0] * norms_ref[2:3, :] + norms_ref[3:4, :]
    ).astype(BF16)


def second_norm(x_rows, kept, arrived, norms):
    args, in_specs = zip(*[plane(one) for one in (x_rows, kept, arrived, norms)])
    rows, width = in_specs[1].block_shape[-2:]
    full = pl.BlockSpec((rows, width), lambda i: (0, 0))
    return run(
        middle_kernel,
        "second_norm",
        [shaped((rows, width), F32), shaped((rows, width), BF16)],
        20 * rows * width,
        args,
        grid=(1,),
        in_specs=list(in_specs),
        out_specs=[full, full],
    )


def feed_step(x_rows, gy_rows, w_refs, out_refs):
    gate_w_ref, up_w_ref, down_w_ref = w_refs
    hidden_ref, grad_gate_ref, grad_up_ref = out_refs
    gate = dot_nn(x_rows, gate_w_ref[...])
    up = dot_nn(x_rows, up_w_ref[...])
    grad_hidden = dot_nn(gy_rows, down_w_ref[...])
    sig = jax.nn.sigmoid(gate)
    swish = gate * sig
    hidden = (swish * up).astype(BF16)
    grad_gate = (grad_hidden * up * sig * (1.0 + gate * (1.0 - sig))).astype(BF16)
    grad_up = (grad_hidden * swish).astype(BF16)
    hidden_ref[...] = hidden
    grad_gate_ref[...] = grad_gate
    grad_up_ref[...] = grad_up
    grad_term = dot_nt(grad_gate, gate_w_ref[...]) + dot_nt(grad_up, up_w_ref[...])
    return dot_nt(hidden, down_w_ref[...]), grad_term


def feed_first_kernel(blocks, factor_ref, *refs):
    w_refs, refs = refs[:3], refs[3:]
    x_refs, cot_refs = refs[:blocks], refs[blocks : 2 * blocks]
    x_all, gy_all = refs[2 * blocks : 2 * blocks + 2]
    total, grad_total = refs[2 * blocks + 5 :]
    step = pl.program_id(0)

    @pl.when(step == 0)
    def _():
        at_row = 0
        for x_ref, cot_ref in zip(x_refs, cot_refs):
            rows = slice(at_row, at_row + x_ref.shape[0])
            at_row += x_ref.shape[0]
            x_all[rows, :] = x_ref[...]
            gy_all[rows, :] = (cot_ref[...].astype(F32) * factor_ref[0, 0]).astype(BF16)

    term, grad_term = feed_step(
        x_all[...], gy_all[...], w_refs, refs[2 * blocks + 2 : 2 * blocks + 5]
    )

    @pl.when(step == 0)
    def _():
        total[...] = term
        grad_total[...] = grad_term

    @pl.when(step > 0)
    def _():
        total[...] += term
        grad_total[...] += grad_term


def feed_last_kernel(*refs):
    w_refs = refs[:3]
    x_ref, gy_ref, total_in, grad_in = refs[3:7]
    kept_ref, sent_ref, grad_kept_ref, grad_sent_ref, total, grad_total = refs[13:]
    step = pl.program_id(0)
    term, grad_term = feed_step(x_ref[...], gy_ref[...], w_refs, refs[10:13])

    @pl.when(step == 0)
    def _():
        total[...] = total_in[...] + term
        grad_total[...] = grad_in[...] + grad_term

    @pl.when(step > 0)
    def _():
        total[...] += term
        grad_total[...] += grad_term

    @pl.when(step == pl.num_programs(0) - 1)
    def _():
        half = kept_ref.shape[0]
        kept_ref[...] = total[:half]
        sent_ref[...] = total[half:].astype(BF16)
        grad_kept_ref[...] = grad_total[:half]
        grad_sent_ref[...] = grad_total[half:].astype(BF16)


def feed_specs(weights):
    width, part_cols = weights.shape[0], weights.shape[1] // 3
    step = min(512, part_cols)
    steps = part_cols // step
    specs = [
        pl.BlockSpec((width, step), functools.partial(lambda at, i: (0, at + i), k * steps))
        for k in range(3)
    ]
    return step, steps, specs


def feed_first(x_blocks, cot_blocks, factor, weights):
    blocks, block_specs = zip(*[plane(block) for block in (*x_blocks, *cot_blocks)])
    width = x_blocks[0].shape[1]
    rows = sum(block.shape[0] for block in x_blocks)
    step, steps, w_specs = feed_specs(weights)
    hidden_cols = 2 * step * steps
    full = pl.BlockSpec((rows, width), lambda i: (0, 0))
    return run(
        functools.partial(feed_first_kernel, len(x_blocks)),
        "feed_first",
        [shaped((rows, width), BF16)] * 2
        + [shaped((rows, hidden_cols), BF16)] * 3
        + [shaped((rows, width), F32)] * 2,
        6 * rows * width * hidden_cols,
        [factor, weights, weights, weights, *blocks],
        grid=(steps,),
        in_specs=[SCALAR] + w_specs + list(block_specs),
        out_specs=[full] * 2 + [pl.BlockSpec((rows, step), lambda i: (0, i))] * 3 + [full] * 2,
    )


def feed_last(x_rows, gy_rows, totals, earlier, weights):
    rows, width = x_rows.shape
    step, steps, w_specs = feed_specs(weights)
    hidden_cols = 2 * step * steps
    full = pl.BlockSpec((rows, width), lambda i: (0, 0))
    half = pl.BlockSpec((rows // 2, width), lambda i: (0, 0))
    return run(
        feed_last_kernel,
        "feed_last",
        [shaped((rows, hidden_cols), BF16)] * 3
        + [shaped((rows // 2, width), F32), shaped((rows // 2, width), BF16)] * 2,
        6 * rows * width * hidden_cols,
        [weights, weights, weights, x_rows, gy_rows, *totals, *earlier],
        grid=(steps,),
        in_specs=w_specs + [full] * 4 + [pl.BlockSpec(memory_space=pl.ANY)] * 3,
        out_specs=[pl.BlockSpec((rows, step), lambda i: (0, steps + i))] * 3 + [half] * 4,
        scratch_shapes=[pltpu.VMEM((rows, width), F32)] * 2,
        input_output_aliases={7: 0, 8: 1, 9: 2},
    )


def weights_kernel(windows, starts, masks, *refs):
    inputs = 2 * windows * len(starts)
    sources = refs[inputs : inputs + len(masks)]
    out_ref = refs[inputs + len(masks)]
    targets = refs[inputs + len(masks) + 1 : inputs + 2 * len(masks) + 1]
    at = pl.program_id(0)
    trades = []
    if masks:
        send_sem, recv_sem = refs[inputs + 2 * len(masks) + 1 :]
        tensor = lax.axis_index("tensor")
        for source, target, kinds in zip(sources, targets, masks):
            for number, mask in enumerate(kinds):
                sems = (send_sem.at[len(trades)], recv_sem.at[len(trades)])
                peer = {"tensor": flipped(tensor, mask)}
                trades.append(send(source, target.at[number], *sems, peer))

        @pl.when(at == 0)
        def _():
            greet(
                [
                    {"tensor": flipped(tensor, mask)}
                    for mask in sorted({mask for kinds in masks for mask in kinds})
                ]
            )
            for trade in trades:
                trade.start()

    for group, (start, stop) in enumerate(starts):
        pairs = refs[2 * windows * group : 2 * windows * (group + 1)]

        @pl.when(jnp.logical_and(at >= start, at < stop))
        def _(pairs=pairs):
            total = None
            for left, right in zip(pairs[:windows], pairs[windows:]):
                term = dot_tn(left[...], right[...])
                total = term if total is None else total + term
            out_ref[...] = total.astype(BF16)

    if masks:

        @pl.when(at == pl.num_programs(0) - 1)
        def _():
            for trade in trades:
                trade.wait()


def weight_grads(groups, step, name, first=0, parts=1, swaps=(), collective_id=None):
    windows = len(groups[0][0])
    args, in_specs, starts = [], [], []
    at = 0
    for lefts, rights in groups:
        for left in lefts:
            array, spec = plane(left)
            rows, width = array.shape[-2:]
            args.append(array)
            in_specs.append(spec)
        for right in rights:
            cols = plane(right)[0].shape[-1]
            count = cols // (step * parts)
            place = functools.partial(
                lambda at, count, i: (0, first * count + jnp.clip(i - at, 0, count - 1)), at, count
            )
            array, spec = plane(right, (rows, step), place)
            args.append(array)
            in_specs.append(spec)
        starts.append((at, at + count))
        at += count
    masks = [kinds for _, kinds in swaps]
    anywhere = pl.BlockSpec(memory_space=pl.ANY)
    out_shape = [shaped((width, at * step), BF16)]
    out_shape += [shaped((len(kinds),) + array.shape, BF16) for array, kinds in swaps]
    total = sum(len(kinds) for kinds in masks)
    outs = run(
        functools.partial(weights_kernel, windows, starts, masks),
        name,
        out_shape,
        2 * windows * rows * width * at * step,
        args + [array for array, _ in swaps],
        collective_id=collective_id,
        grid=(at,),
        in_specs=in_specs + [anywhere] * len(swaps),
        out_specs=[pl.BlockSpec((width, step), lambda i: (0, i))] + [anywhere] * len(swaps),
        scratch_shapes=[pltpu.SemaphoreType.DMA((total,))] * 2 if total else [],
    )
    return outs if swaps else outs[0]


def norm_grad(kept_ref, arrived_ref, stream, gain, sums_ref):
    grad_normed = kept_ref[...] + arrived_ref[...].astype(F32)
    normed, inv_std = normalise(stream)
    sums_ref[0:1, :] = jnp.sum(grad_normed * normed, axis=0, keepdims=True)
    sums_ref[1:2, :] = jnp.sum(grad_normed, axis=0, keepdims=True)
    return norm_back(grad_normed, normed, inv_std, gain)


def middle_back_kernel(
    factor_ref, kept_ref, arrived_ref, middle_ref, cot_ref, norms_ref, grad_ref, low_ref, sums_ref
):
    grad_y = cot_ref[...].astype(F32) * factor_ref[0, 0]
    grad = grad_y + norm_grad(
        kept_ref, arrived_ref, middle_ref[...], norms_ref[2:3, :], sums_ref
    )
    grad_ref[...] = grad
    low_ref[...] = grad.astype(BF16)


def second_norm_back(factor, kept, arrived, middle, cot_rows, norms):
    args, in_specs = zip(*[plane(one) for one in (kept, arrived, middle, cot_rows, norms)])
    full = pl.BlockSpec(kept.shape, lambda i: (0, 0))
    return run(
        middle_back_kernel,
        "second_norm_back",
        [
            shaped(kept.shape, F32),
            shaped(kept.shape, BF16),
            shaped((2, kept.shape[1]), F32),
        ],
        40 * kept.size,
        [factor, *args],
        grid=(1,),
        in_specs=[SCALAR, *in_specs],
        out_specs=[full, full, pl.BlockSpec((2, kept.shape[1]), lambda i: (0, 0))],
    )


class SumRoute:
    def __init__(self, part, rows, core_in, mine, x_in, z_in, send_sem, recv_sem):
        self.read, self.rows = part, rows
        self.core_in, self.mine, self.x_in, self.z_in = core_in, mine, x_in, z_in
        self.send_sem, self.recv_sem = send_sem, recv_sem
        self.seq, self.depth = lax.axis_index("seq"), lax.axis_index("dp")
        self.peers = half_chip_peers()

    def place(self, number, other_core):
        seq = flipped(self.seq, 2) if number >= 4 else self.seq
        seq = flipped(seq, 1) if other_core else seq
        turn = (self.depth + number % 4) % lax.axis_size("dp")
        return pl.ds(
            pl.multiple_of((turn * lax.axis_size("seq") + seq) * self.rows, self.rows), self.rows
        )

    def message(self, number):
        if number < 8:
            source, target, peer = self.read.at[self.place(number, True), :], self.core_in, "core"
            target = target.at[number]
        elif number < 12:
            source, target, peer = self.mine.at[number - 4], self.x_in.at[number - 8], "far"
        else:
            turn, peer = ((2, "up"), (1, "up"), (3, "down"))[number - 12]
            source, target = self.mine.at[turn], self.z_in.at[number - 12]
        return send(
            source, target, self.send_sem.at[number], self.recv_sem.at[number], self.peers[peer]
        )

    def start(self, *numbers):
        for number in numbers:
            self.message(number).start()

    def add_core(self, number):
        self.message(number).wait_recv()
        own = self.read[self.place(number, False), :].astype(F32)
        self.mine[number] = (own + self.core_in[number].astype(F32)).astype(self.mine.dtype)

    def add_x(self, number):
        self.message(8 + number).wait_recv()
        total = self.mine[number].astype(F32) + self.x_in[number].astype(F32)
        self.mine[number] = total.astype(self.mine.dtype)

    def add_up(self):
        self.message(12).wait_recv()
        total = self.mine[1].astype(F32) + self.z_in[0].astype(F32)
        self.mine[1] = total.astype(self.mine.dtype)

    def total(self):
        self.message(13).wait_recv()
        self.message(14).wait_recv()
        return (
            self.mine[0].astype(F32) + self.z_in[1].astype(F32) + self.z_in[2].astype(F32)
        )

    def sent(self):
        for number in range(SUM_MESSAGES):
            self.message(number).wait_send()


SUM_MESSAGES = 15


def finish_kernel(windows, trades, score_cols, *refs):
    stages = (trades + 1).bit_length() - 1
    refs = list(refs)

    def take(count):
        taken = refs[:count]
        del refs[:count]
        return taken

    far_inputs = take(8)
    norms_ref = take(1)[0]
    second_refs = take(windows)
    grad_refs = take(windows)
    part_refs = take(3 * windows)
    weights_ref, vectors_ref, input_ref, output_ref = take(4)
    loads = take(8)
    grad_loads = take(windows)
    part_loads = take(3 * windows)
    part, core_in, mine, x_in, z_in = take(5)
    tiles, own_tiles, arrived_tiles = take(3)
    small_core, small_mine, small_x, small_z = take(4)
    kept_all = take(windows)
    stage_sent = [take(stages) for _ in range(windows)]
    stage_arrived = [take(stages) for _ in range(windows)]
    load_sem, big_send, big_recv, small_send, small_recv = take(5)
    y_send, y_recv, tile_send, tile_recv = take(4)
    assert not refs
    (grad_q, grad_k, grad_v, normed, grad_mid, attended, w_qkv, tokens) = loads[:8]
    tensor = lax.axis_index("tensor")
    others = [{"tensor": flipped(tensor, other + 1)} for other in range(trades)]
    shards = lax.axis_size("dp") * lax.axis_size("seq")
    devices = shards * (trades + 1)
    group = tiles.shape[0] // shards
    width = part.shape[1]
    cols = score_cols
    rows = width // shards

    w_source = far_inputs[6].at[:, pl.ds(0, 3 * cols)]
    sources = [*far_inputs[:6], w_source, far_inputs[7]]
    sources += [*grad_refs, *part_refs]
    targets = [*loads, *grad_loads, *part_loads]
    copies = [
        pltpu.make_async_copy(source, target, load_sem.at[at])
        for at, (source, target) in enumerate(zip(sources, targets))
    ]
    order = [4, 5, 6, 0, 1, 2, 3, 7] + list(range(8, len(copies)))
    for at in order:
        copies[at].start()

    def block_route(block):
        return SumRoute(
            part.at[block],
            rows,
            core_in.at[block],
            mine.at[block],
            x_in.at[block],
            z_in.at[block],
            big_send.at[block],
            big_recv.at[block],
        )

    routes = [block_route(block) for block in range(4)]
    small = SumRoute(
        tiles, group, small_core, small_mine, small_x, small_z, small_send, small_recv
    )
    greet(list(small.peers.values()) + others)
    everything = (6, 7, 5, 4, 2, 3, 1, 0)

    def product(block, left, right):
        total = None
        for w in range(windows):
            term = dot_tn(left[w], right[w])
            total = term if total is None else total + term
        part[block] = total.astype(BF16)

    def y_trade(w, stage):
        return send(
            stage_sent[w][stage],
            stage_arrived[w][stage],
            y_send.at[w, stage],
            y_recv.at[w, stage],
            {"tensor": flipped(tensor, (trades + 1) >> (stage + 1))},
        )

    def turn_back(w):
        total = None
        for at, grad in enumerate((grad_q, grad_k, grad_v)):
            term = dot_nt(grad[w], w_qkv[:, at * cols : (at + 1) * cols])
            total = term if total is None else total + term
        half = total.shape[0] // 2
        kept_all[w][...] = total[:half]
        stage_sent[w][0][...] = total[half:].astype(BF16)

    def add_cores(route):
        for number in everything:
            route.add_core(number)

    def across(route):
        route.start(10, 11, 9, 8)

    def add_across(route):
        for number in (2, 3, 1, 0):
            route.add_x(number)

    copies[4].wait()
    copies[5].wait()
    product(3, grad_mid, attended)
    for at in (6, 0, 1, 2):
        copies[at].wait()
    routes[3].start(*everything)
    turn_back(0)
    add_cores(routes[3])
    y_trade(0, 0).start()
    across(routes[3])
    for w in range(1, windows):
        turn_back(w)
    copies[3].wait()
    product(0, normed, grad_q)
    for w in range(1, windows):
        y_trade(w, 0).start()
    routes[0].start(*everything)
    product(1, normed, grad_k)
    add_cores(routes[0])
    routes[1].start(*everything)
    across(routes[0])
    product(2, normed, grad_v)
    add_cores(routes[1])
    routes[2].start(*everything)
    across(routes[1])
    add_across(routes[3])
    add_cores(routes[2])
    routes[3].start(12, 14)
    across(routes[2])
    for at in range(8 + windows, len(copies)):
        copies[at].wait()
    for w in range(windows):
        middle_ref, kept_ref, arrived_ref = part_loads[3 * w : 3 * w + 3]
        output_ref[w] = (
            middle_ref[...] + (kept_ref[...] + arrived_ref[...].astype(F32))
        ).astype(BF16)
    routes[3].add_up()
    for at in range(7, 8 + windows):
        copies[at].wait()
    sums = [None, None]

    def first_norm(w):
        kept = kept_all[w][...]
        for stage in range(stages):
            y_trade(w, stage).wait_recv()
            kept = kept + stage_arrived[w][stage][...].astype(F32)
            if stage + 1 < stages:
                half = kept.shape[0] // 2
                stage_sent[w][stage + 1][...] = kept[half:].astype(BF16)
                y_trade(w, stage + 1).start()
                kept = kept[:half]
        normed_rows, inv_std = normalise(tokens[w].astype(F32))
        for at, one in enumerate((kept * normed_rows, kept)):
            one = jnp.sum(one, axis=0, keepdims=True)
            sums[at] = one if sums[at] is None else sums[at] + one
        input_ref[w] = grad_loads[w][...] + norm_back(
            kept, normed_rows, inv_std, norms_ref[0:1, :]
        )

    first_norm(0)
    routes[3].start(13)
    add_across(routes[0])
    for w in range(1, windows):
        first_norm(w)
    routes[0].start(12, 14)
    first = jnp.concatenate(sums, axis=0)
    second = sum(ref[...] for ref in second_refs)
    span = width // devices
    tiles[...] = jnp.zeros_like(tiles)
    for device in range(devices):
        at = device * 8
        columns = slice(device * span, (device + 1) * span)
        tiles[at : at + 2, :span] = first[:, columns]
        tiles[at + 2 : at + 4, :span] = second[:, columns]
    add_across(routes[1])
    small.start(*everything)
    routes[0].add_up()
    routes[1].start(12, 14)
    add_cores(small)
    routes[0].start(13)
    across(small)
    add_across(routes[2])
    routes[1].add_up()
    routes[2].start(12, 14)
    add_across(small)
    routes[1].start(13)
    small.start(12, 14)
    for block in (3, 0):
        weights_ref[:, block * cols : (block + 1) * cols] = routes[block].total()
    small.add_up()
    routes[2].add_up()
    small.start(13)
    weights_ref[:, cols : 2 * cols] = routes[1].total()
    routes[2].start(13)
    own_tiles[...] = small.total()

    def tile_trade(other):
        place = pl.ds(pl.multiple_of(flipped(tensor, other + 1) * 8, 8), 8)
        return send(
            own_tiles.at[place, :],
            arrived_tiles.at[other],
            tile_send.at[other],
            tile_recv.at[other],
            others[other],
        )

    weights_ref[:, 2 * cols : 3 * cols] = routes[2].total()
    for other in range(trades):
        tile_trade(other).start()
    vectors = own_tiles[pl.ds(pl.multiple_of(tensor * 8, 8), 8), :]
    for other in range(trades):
        tile_trade(other).wait_recv()
        vectors = vectors + arrived_tiles[other]
    vectors_ref[...] = vectors
    for route in (*routes, small):
        route.sent()
    for w in range(windows):
        for stage in range(stages):
            y_trade(w, stage).wait_send()
    for other in range(trades):
        tile_trade(other).wait_send()


def finish(
    grads, normed, grad_mid, attended, w_att, tokens, norms, second_sums, grad_middles, parts, trades
):
    windows, rows, cols = grads[0].shape
    width = w_att.shape[0]
    own_rows = tokens.shape[1]
    shards = lax.axis_size("dp") * lax.axis_size("seq")
    shard = width // shards
    group = 8 * (trades + 1)
    stages = [rows >> (stage + 1) for stage in range((trades + 1).bit_length() - 1)]
    dma = pltpu.SemaphoreType.DMA
    anywhere = pl.BlockSpec(memory_space=pl.ANY)
    vmem = pl.BlockSpec(memory_space=pltpu.VMEM)
    far_inputs = [*grads, normed, grad_mid, attended, w_att, tokens]
    flat = [array for one in parts for array in one]
    kinds = (8, 8, 4, 3)

    def like(array):
        return pltpu.VMEM(array.shape, array.dtype)

    loads = [like(array) for array in far_inputs]
    loads[6] = pltpu.VMEM((width, 3 * cols), BF16)
    return run(
        functools.partial(finish_kernel, windows, trades, cols),
        "finish",
        [
            shaped((shard, 4 * cols), F32),
            shaped((8, 128), F32),
            shaped((windows, own_rows, width), F32),
            shaped((windows, own_rows, width), BF16),
        ],
        8 * windows * rows * width * cols + 6 * windows * rows * width * cols,
        [*far_inputs, norms, *second_sums, *grad_middles, *flat],
        collective_id=3,
        in_specs=[anywhere] * 8
        + [vmem] * (1 + windows)
        + [anywhere] * (windows + len(flat)),
        out_specs=[vmem] * 4,
        scratch_shapes=loads
        + [like(array) for array in grad_middles]
        + [like(array) for array in flat]
        + [pltpu.VMEM((4, width, cols), BF16)]
        + [pltpu.VMEM((4, count, shard, cols), BF16) for count in kinds]
        + [
            pltpu.VMEM((shards * group, 128), F32),
            pltpu.VMEM((group, 128), F32),
            pltpu.VMEM((trades, 8, 128), F32),
        ]
        + [pltpu.VMEM((count, group, 128), F32) for count in kinds]
        + [pltpu.VMEM((rows // 2, width), F32)] * windows
        + [pltpu.VMEM((count, width), BF16) for count in stages] * (2 * windows)
        + [
            dma((8 + windows + len(flat),)),
            dma((4, SUM_MESSAGES)),
            dma((4, SUM_MESSAGES)),
            dma((SUM_MESSAGES,)),
            dma((SUM_MESSAGES,)),
            dma((windows, len(stages))),
            dma((windows, len(stages))),
            dma((trades,)),
            dma((trades,)),
        ],
    )


def local(
    tokens,
    cotangent,
    species,
    counts,
    species_scale,
    norm1_gain,
    norm1_bias,
    w_query,
    w_key,
    w_value,
    w_out,
    norm2_gain,
    norm2_bias,
    w_gate,
    w_up,
    w_down,
):
    windows_here, own_rows, model_width = tokens.shape
    tensor_size = lax.axis_size("tensor")
    seq_size = lax.axis_size("seq")
    block_rows = own_rows * tensor_size
    head_cols = w_query.shape[1]
    hidden_cols = w_gate.shape[1]
    shards = ("dp", "seq")

    own_at = lax.axis_index("tensor")
    starts = jnp.concatenate(
        [
            lax.iota(jnp.int32, own_rows) + (own_at ^ other) * own_rows
            for other in range(tensor_size)
        ]
    )
    positions = (lax.axis_index("seq") * block_rows + starts).astype(F32)
    cos_half, sin_half = angles(positions, HEAD_DIM)
    cosine = jnp.concatenate([cos_half] * 4, axis=1)
    sine = jnp.concatenate([-sin_half, sin_half] * 2, axis=1)

    labels = lax.broadcasted_iota(jnp.int32, (windows_here, species_scale.shape[0]), 1)
    chosen = jnp.sum(jnp.where(species[:, None] == labels, species_scale[None, :], 0.0), axis=1)
    weighted = counts.astype(F32) * chosen

    lanes = jnp.zeros((8, 128), F32)
    vectors = jnp.stack([norm1_gain, norm1_bias, norm2_gain, norm2_bias])
    tile = lanes.at[:4, : vectors.shape[1]].set(vectors).at[4, :].set(jnp.sum(weighted))
    part = hidden_cols // 2
    turned = w_down.T
    first_ffn = jnp.concatenate([w_gate[:, :part], w_up[:, :part], turned[:, :part]], axis=1)
    last_ffn = jnp.concatenate([w_gate[:, part:], w_up[:, part:], turned[:, part:]], axis=1)
    first_ffn = lax.all_gather(first_ffn, shards, axis=0, tiled=True)
    w_att, norms, arrived_tokens = gather(
        jnp.concatenate([w_query, w_key, w_value, w_out.T], axis=1),
        tile,
        tokens,
        tensor_size - 1,
    )
    factor = weighted * float(windows_here * lax.axis_size("dp")) / norms[4, 0]

    windows = range(windows_here)
    factors = [factor[w].reshape(1, 1) for w in windows]
    top_bit = seq_size // 2

    token_blocks = [tokens] + [arrived_tokens[other] for other in range(tensor_size - 1)]
    normed_rows, queries, own_kv = project(token_blocks, norms, w_att, cosine, sine)
    (
        attended,
        wide_attended,
        logs,
        kept_all,
        sent_all,
        slots_all,
        cots,
        first_middle,
        first_normed,
        first_others,
    ) = attend(queries, own_kv, w_att, cotangent, tokens, norms, tensor_size - 1)
    last_ffn = lax.all_gather(hold(last_ffn, kept_all), shards, axis=0, tiled=True)
    others = range(tensor_size - 1)
    cot_blocks = [
        [(cotangent, (w,))] + [(cots, (other, w)) for other in others] for w in windows
    ]
    middles = [first_middle]

    begun = [
        feed_first(
            [first_normed] + [first_others[other] for other in others],
            cot_blocks[0],
            factors[0],
            first_ffn,
        )
    ]
    for w in windows[1:]:
        kept, arrived = scatter_pair(kept_all[w - 1], sent_all[w - 1], "tensor")
        middle, normed_mid = second_norm(
            (tokens, (w,)), hold(kept, begun[-1]), arrived, norms
        )
        middles.append(middle)
        begun.append(
            feed_first(spread(normed_mid, "tensor"), cot_blocks[w], factors[w], first_ffn)
        )
    step = min(512, part)

    def feed_weights(done, half, swaps, collective_id):
        return weight_grads(
            [
                ([one[0] for one in done], [one[3] for one in done]),
                ([one[0] for one in done], [one[4] for one in done]),
                ([one[1] for one in done], [one[2] for one in done]),
            ],
            step,
            "feed_weights",
            half,
            2,
            swaps,
            collective_id,
        )

    g_first_part = feed_weights(begun, 0, (), None)
    g_first = lax.psum_scatter(g_first_part, shards, scatter_dimension=0, tiled=True)
    fed = []
    for w in windows:
        x_rows, gy_rows, *parts = hold(begun[w], fed[-1] if fed else g_first_part)
        ended = feed_last(x_rows, gy_rows, parts[3:], parts[:3], last_ffn)
        fed.append((x_rows, gy_rows, *ended))
    grad_middles, second_sums = [], []

    def through_second_norm(w, kept, arrived):
        grad_middle, low, sums = second_norm_back(
            factors[w], kept, arrived, middles[w], (cotangent, (w,)), norms
        )
        grad_middles.append(grad_middle)
        second_sums.append(sums)
        return low

    lows = []
    for w in windows[:-1]:
        kept, arrived = scatter_pair(fed[w][7], fed[w][8], "tensor")
        lows.append(through_second_norm(w, hold(kept, fed[w + 1]), arrived))
    masks = [other + 1 for other in others]
    g_last_part, arrived, *arrived_lows = feed_weights(
        hold(fed, grad_middles),
        1,
        [(fed[-1][8], [tensor_size // 2])] + [(low, masks) for low in lows],
        4,
    )
    g_last = lax.psum_scatter(g_last_part, shards, scatter_dimension=0, tiled=True)
    kept, arrived = later_pair(fed[-1][7], arrived[0], "tensor")
    last_low = through_second_norm(windows[-1], hold(kept, g_last_part), arrived)
    grad_mid_blocks = [
        [low] + [arrived[other] for other in others] for low, arrived in zip(lows, arrived_lows)
    ] + [[last_low]]

    grad_q, grad_k, grad_v, grad_mid_rows, *arrived_results = attend_back(
        hold(queries, g_last_part),
        wide_attended,
        logs,
        slots_all,
        grad_mid_blocks,
        w_att,
        (cosine, sine),
        [fed[w][6] for w in windows],
    )
    parts = [
        (middles[w], *later_pair(fed[w][5], arrived_results[w], "tensor")) for w in windows
    ]

    g_att, vectors, input_grad, output = finish(
        (grad_q, grad_k, grad_v),
        normed_rows,
        grad_mid_rows,
        attended,
        w_att,
        tokens,
        norms,
        second_sums,
        grad_middles,
        parts,
        tensor_size - 1,
    )
    norm_sums = vectors[:4, : norm1_gain.shape[0]]
    ffn_grads = [
        jnp.concatenate(
            [g_first[:, at * part : (at + 1) * part], g_last[:, at * part : (at + 1) * part]],
            axis=1,
        ).astype(F32)
        for at in range(3)
    ]

    return (
        output,
        input_grad,
        norm_sums[0],
        norm_sums[1],
        g_att[:, :head_cols],
        g_att[:, head_cols : 2 * head_cols],
        g_att[:, 2 * head_cols : 3 * head_cols],
        g_att[:, 3 * head_cols :].T,
        norm_sums[2],
        norm_sums[3],
        ffn_grads[0],
        ffn_grads[1],
        ffn_grads[2].T,
    )


def solution(mesh):
    rows = P("dp", ("seq", "tensor"), None)
    vector = P(("dp", "seq", "tensor"))
    tall = P(("dp", "seq"), "tensor")
    flat = P("tensor", ("dp", "seq"))
    return jax.shard_map(
        local,
        mesh=mesh,
        in_specs=(
            rows, rows, P("dp"), P("dp"), P(), vector, vector,
            tall, tall, tall, flat, vector, vector, tall, tall, flat,
        ),
        out_specs=(
            rows, rows, vector, vector, tall, tall, tall, flat,
            vector, vector, tall, tall, flat,
        ),
        check_vma=False,
    )
```

```python
import functools
import math

import jax
import jax.numpy as jnp
from jax import lax
from jax.experimental import pallas as pl
from jax.experimental.pallas import tpu as pltpu
from jax.sharding import PartitionSpec as P

HEAD_DIM = 64
EPSILON = 1e-05
ROPE_BASE = 10000.0
PAIR = 2 * HEAD_DIM
LOG2E = math.log2(math.e)
BF16 = jnp.bfloat16
F32 = jnp.float32
VMEM_BYTES = 56 * 1024 * 1024
MESH = pl.DeviceIdType.MESH


def angles(positions, head_dim):
    half_dim = head_dim // 2
    inverse = jnp.exp(
        -(math.log(ROPE_BASE) * 2.0 / head_dim) * jnp.arange(half_dim, dtype=F32)
    )
    phase_angle = positions[:, None] * inverse[None, :]
    return (jnp.cos(phase_angle), jnp.sin(phase_angle))


def dot_nn(left, right):
    return lax.dot_general(left, right, (((1,), (0,)), ((), ())), preferred_element_type=F32)


def dot_nt(left, right):
    return lax.dot_general(left, right, (((1,), (1,)), ((), ())), preferred_element_type=F32)


def dot_tn(left, right):
    return lax.dot_general(left, right, (((0,), (0,)), ((), ())), preferred_element_type=F32)


def swap(array, axis, bit):
    size = lax.axis_size(axis)
    return lax.ppermute(array, axis, [(i, i ^ bit) for i in range(size)])


def spread(array, axis):
    blocks = [array]
    bit = 1
    while bit < lax.axis_size(axis):
        blocks = blocks + [swap(block, axis, bit) for block in blocks]
        bit *= 2
    return blocks


def scatter_pair(kept, sent, axis):
    return later_pair(kept, swap(sent, axis, lax.axis_size(axis) // 2), axis)


def later_pair(kept, arrived, axis):
    bit = lax.axis_size(axis) // 2
    while bit > 1:
        partial = kept + arrived.astype(F32)
        bit //= 2
        rows = partial.shape[0] // 2
        kept, arrived = partial[:rows], swap(partial[rows:].astype(BF16), axis, bit)
    return kept, arrived


def seq_size():
    return lax.axis_size("x") * lax.axis_size("core")


def seq_index():
    return lax.axis_index("x") * lax.axis_size("core") + lax.axis_index("core")


def hold(values, *others):
    return lax.optimization_barrier((values, others))[0]


def run(kernel, name, out_shape, flops, args, collective_id=None, **options):
    trading = {} if collective_id is None else dict(collective_id=collective_id, has_side_effects=True)
    moved = sum(math.prod(array.shape) * array.dtype.itemsize for array in args)
    outs = out_shape if isinstance(out_shape, list) else [out_shape]
    moved += sum(math.prod(array.shape) * array.dtype.itemsize for array in outs)
    return pl.pallas_call(
        kernel,
        out_shape=out_shape,
        compiler_params=pltpu.CompilerParams(vmem_limit_bytes=VMEM_BYTES, **trading),
        cost_estimate=pl.CostEstimate(
            flops=int(flops), bytes_accessed=int(moved), transcendentals=0
        ),
        name=name,
        **options,
    )(*args)


def shaped(shape, dtype):
    return jax.ShapeDtypeStruct(shape, dtype)


SCALAR = pl.BlockSpec(memory_space=pltpu.SMEM)


def plane(operand, block=None, index=None):
    array, at = operand if isinstance(operand, tuple) else (operand, ())
    shape = array.shape[len(at) :] if block is None else block
    place = (lambda *i: (0,) * len(shape)) if index is None else index
    return array, pl.BlockSpec((None,) * len(at) + tuple(shape), lambda *i: at + place(*i))


def normalise(stream):
    row_mean = jnp.mean(stream, axis=-1, keepdims=True)
    centred = stream - row_mean
    variance = jnp.mean(centred * centred, axis=-1, keepdims=True)
    inv_std = lax.rsqrt(variance + EPSILON)
    return centred * inv_std, inv_std


def norm_back(grad_normed, normed, inv_std, norm_gain):
    scaled_grad = grad_normed * norm_gain
    return inv_std * (
        scaled_grad
        - jnp.mean(scaled_grad, axis=-1, keepdims=True)
        - normed * jnp.mean(scaled_grad * normed, axis=-1, keepdims=True)
    )


def first_head(shape):
    return lax.broadcasted_iota(jnp.int32, shape, 1) % PAIR < HEAD_DIM


def swap_halves(values):
    half = HEAD_DIM // 2
    lane = lax.broadcasted_iota(jnp.int32, values.shape, 1)
    ahead = pltpu.roll(values, PAIR - half, 1)
    behind = pltpu.roll(values, half, 1)
    return jnp.where(lane % HEAD_DIM < half, ahead, behind)


def project_kernel(blocks, norms_ref, w_ref, cos_ref, sin_ref, *refs):
    x_refs = refs[:blocks]
    normed_ref, q_ref, kv_ref = refs[blocks:]
    cols = q_ref.shape[2]
    gain, bias = norms_ref[0:1, :], norms_ref[1:2, :]
    at_row = 0
    for x_ref in x_refs:
        rows = slice(at_row, at_row + x_ref.shape[1])
        at_row += x_ref.shape[1]
        normed = (normalise(x_ref[0].astype(F32))[0] * gain + bias).astype(BF16)
        normed_ref[0, rows, :] = normed
        cosine, sine = cos_ref[rows, :], sin_ref[rows, :]
        query = dot_nn(normed, w_ref[:, :cols])
        key = dot_nn(normed, w_ref[:, cols : 2 * cols])
        for at in range(0, cols, PAIR):
            part = slice(at, at + PAIR)
            one = query[:, part]
            q_ref[0, rows, part] = (one * cosine + swap_halves(one) * sine).astype(BF16)
            one = key[:, part]
            kv_ref[0, 0, rows, part] = (one * cosine + swap_halves(one) * sine).astype(BF16)
        kv_ref[0, 1, rows, :] = dot_nn(normed, w_ref[:, 2 * cols : 3 * cols]).astype(BF16)


def project(x_blocks, norms, w_att, cosine, sine):
    windows = x_blocks[0].shape[0]
    width, cols = w_att.shape[0], w_att.shape[1] // 4
    rows = sum(block.shape[1] for block in x_blocks)
    args = [norms, w_att, cosine, sine, *x_blocks]
    return run(
        functools.partial(project_kernel, len(x_blocks)),
        "project",
        [
            shaped((windows, rows, width), BF16),
            shaped((windows, rows, cols), BF16),
            shaped((windows, 2, rows, cols), BF16),
        ],
        6 * windows * rows * width * cols,
        args,
        grid=(windows,),
        in_specs=[pl.BlockSpec(array.shape, lambda i: (0, 0)) for array in args[:4]]
        + [pl.BlockSpec((1,) + block.shape[1:], lambda i: (i, 0, 0)) for block in x_blocks],
        out_specs=[
            pl.BlockSpec((1, rows, width), lambda i: (i, 0, 0)),
            pl.BlockSpec((1, rows, cols), lambda i: (i, 0, 0)),
            pl.BlockSpec((1, 2, rows, cols), lambda i: (i, 0, 0, 0)),
        ],
    )


def flipped(index, mask):
    bit = 1
    while bit <= mask:
        if mask & bit:
            index = index + bit - 2 * bit * ((index // bit) % 2)
        bit *= 2
    return index


def greet(peers):
    barrier = pltpu.get_barrier_semaphore()
    for peer in peers:
        pl.semaphore_signal(barrier, inc=1, device_id=peer, device_id_type=MESH)
    pl.semaphore_wait(barrier, len(peers))


def send(source, target, send_sem, recv_sem, peer):
    return pltpu.make_async_remote_copy(
        src_ref=source,
        dst_ref=target,
        send_sem=send_sem,
        recv_sem=recv_sem,
        device_id=peer,
        device_id_type=MESH,
    )


def half_chip_peers():
    depth = lax.axis_index("dp")
    size = lax.axis_size("dp")
    return {
        "far": {"x": 1 - lax.axis_index("x")},
        "up": {"dp": (depth + 1) % size},
        "down": {"dp": (depth + size - 1) % size},
        "core": {"core": 1 - lax.axis_index("core")},
    }


class Route:
    PARTS = ((0, 0), (3, 0), (1, 0), (2, 0), (0, 1), (3, 1), (1, 1), (2, 1))

    def __init__(self, whole, rows, send_sem, recv_sem, own):
        self.whole, self.rows, self.own = whole, rows, own
        self.send_sem, self.recv_sem = send_sem, recv_sem
        self.seq, self.depth = seq_index(), lax.axis_index("dp")
        self.peers = half_chip_peers()

    def part(self, place):
        turn, other = place
        seq = flipped(self.seq, 2) if other else self.seq
        at = (((self.depth + turn) % lax.axis_size("dp")) * seq_size() + seq) * self.rows
        return self.whole.at[pl.ds(pl.multiple_of(at, self.rows), self.rows), :]

    def message(self, number):
        if number >= 7:
            place, peer = self.PARTS[number - 7], "core"
        else:
            place, peer = (
                ((0, 0), "up"),
                ((0, 0), "down"),
                ((3, 0), "up"),
                ((0, 0), "far"),
                ((3, 0), "far"),
                ((1, 0), "far"),
                ((2, 0), "far"),
            )[number]
        target = self.part(place)
        return send(
            self.own if place == (0, 0) else target,
            target,
            self.send_sem.at[number],
            self.recv_sem.at[number],
            self.peers[peer],
        )

    def start(self, *numbers):
        for number in numbers:
            self.message(number).start()

    def arrived(self, *numbers):
        for number in numbers:
            self.message(number).wait_recv()

    def sent(self, *numbers):
        for number in numbers:
            self.message(number).wait_send()


MESSAGES = 15


def gather_kernel(trades, att_ref, tile_ref, tokens_ref, *refs):
    att_all, norms_ref, tokens_all = refs[:3]
    tiles, pair_of_tiles = refs[3:5]
    att_send, att_recv, tile_send, tile_recv = refs[5:9]
    own_sem, tokens_send, tokens_recv, pair_send, pair_recv = refs[9:]
    tensor = lax.axis_index("tensor")
    others = [{"tensor": flipped(tensor, other + 1)} for other in range(trades)]
    att = Route(att_all, att_ref.shape[0], att_send, att_recv, att_ref)
    tile_rows = tile_ref.shape[0]
    small = Route(tiles, pair_of_tiles.shape[0], tile_send, tile_recv, pair_of_tiles)

    def tokens_trade(other):
        return send(
            tokens_ref,
            tokens_all.at[other],
            tokens_send.at[other],
            tokens_recv.at[other],
            others[other],
        )

    own_rows = pl.ds(pl.multiple_of(tensor * tile_rows, tile_rows), tile_rows)

    def pair_trade(other):
        return send(
            tile_ref,
            pair_of_tiles.at[own_rows, :],
            pair_send.at[other],
            pair_recv.at[other],
            others[other],
        )

    own_copies = [
        pltpu.make_async_copy(att_ref, att.part((0, 0)), own_sem.at[0]),
        pltpu.make_async_copy(tile_ref, pair_of_tiles.at[own_rows, :], own_sem.at[1]),
        pltpu.make_async_copy(pair_of_tiles, small.part((0, 0)), own_sem.at[2]),
    ]

    greet(list(att.peers.values()) + others)
    for other in range(trades):
        pair_trade(other).start()
    own_copies[1].start()
    att.start(0, 1, 3, 7)
    own_copies[1].wait()
    for other in range(trades):
        pair_trade(other).wait_recv()
    small.start(0, 1, 3, 7)
    own_copies[0].start()
    own_copies[2].start()
    for other in range(trades):
        tokens_trade(other).start()
    for route in (small, att):
        route.arrived(0)
        route.start(2, 4, 8)
    for route in (small, att):
        route.arrived(3)
        route.start(11)
    for route in (small, att):
        route.arrived(1)
        route.start(5, 9)
    for route in (small, att):
        route.arrived(2)
        route.start(6, 10)
    for route in (small, att):
        route.arrived(4)
        route.start(12)
        route.arrived(5)
        route.start(13)
        route.arrived(6)
        route.start(14)
    for route in (small, att):
        route.arrived(*range(7, MESSAGES))
    own_copies[2].wait()
    shard = norms_ref.shape[1] // (tiles.shape[0] // tile_rows)
    total = None
    for device in range(tiles.shape[0] // tile_rows):
        tile = tiles[device * tile_rows : (device + 1) * tile_rows, :]
        norms_ref[:, device * shard : (device + 1) * shard] = tile[:, :shard]
    for depth in range(lax.axis_size("dp")):
        at = depth * (tiles.shape[0] // lax.axis_size("dp"))
        one = tiles[at + 4 : at + 5, :]
        total = one if total is None else total + one
    norms_ref[4:5, : total.shape[1]] = total
    for route in (att, small):
        route.sent(*range(MESSAGES))
    own_copies[0].wait()
    for other in range(trades):
        pair_trade(other).wait_send()
        tokens_trade(other).wait_recv()
        tokens_trade(other).wait_send()


def gather(att, tile, tokens, trades):
    count = lax.axis_size("dp") * seq_size()
    rows = att.shape[0]
    group = tile.shape[0] * (trades + 1)
    anywhere = pl.BlockSpec(memory_space=pl.ANY)
    vmem = pl.BlockSpec(memory_space=pltpu.VMEM)
    dma = pltpu.SemaphoreType.DMA
    return run(
        functools.partial(gather_kernel, trades),
        "gather",
        [
            shaped((count * rows, att.shape[1]), BF16),
            shaped((tile.shape[0], count * rows), F32),
            shaped((trades,) + tokens.shape, BF16),
        ],
        0,
        [att, tile, tokens],
        collective_id=1,
        in_specs=[vmem, vmem, anywhere],
        out_specs=[anywhere, vmem, anywhere],
        scratch_shapes=[pltpu.VMEM((count * group, 128), F32), pltpu.VMEM((group, 128), F32)]
        + [dma((MESSAGES,))] * 4
        + [dma((3,)), dma((trades,)), dma((trades,)), dma((trades,)), dma((trades,))],
    )


def attend_kernel(windows, pairs, trades, exp_scale, *refs):
    stages = (trades + 1).bit_length() - 1
    q_ref, w_ref, kv_ref, cot_ref, x_ref, norms_ref = refs[:6]
    low_ref, wide_ref, log_ref, kept_ref, sent_ref, slots_ref, cots_ref = refs[6:13]
    middle_ref, normed_ref, others_ref = refs[13:16]
    slots, acc_all, top_all, total_all, mixed_rows = refs[16:21]
    own_sem, send_sem, recv_sem, save_sem, cot_send, cot_recv = refs[21:27]
    early_kept, early_normed, early_sem, early_recv, normed_sem, normed_recv = refs[27:33]
    early_sent, early_arrived = refs[33 : 33 + stages], refs[33 + stages :]
    step = pl.program_id(0)
    near_steps = windows * pairs
    steps = 2 * near_steps
    turn = step % (2 * pairs)
    is_far = turn >= pairs
    number = step // (2 * pairs) * pairs + turn % pairs
    tensor = lax.axis_index("tensor")
    core_peer = {"core": 1 - lax.axis_index("core")}
    far_peer = {"x": 1 - lax.axis_index("x")}
    cot_peers = [{"tensor": flipped(tensor, other + 1)} for other in range(trades)]

    def piece(number):
        columns = pl.ds(pl.multiple_of((number % pairs) * PAIR, PAIR), PAIR)
        return kv_ref.at[number // pairs, :, :, columns]

    def own_copy(number):
        return pltpu.make_async_copy(piece(number), slots.at[number, 0], own_sem.at[number])

    def trade(number, slot):
        peer = far_peer if slot == 2 else core_peer
        source = slots.at[number, 2] if slot == 3 else piece(number)
        return send(
            source,
            slots.at[number, slot],
            send_sem.at[number, slot - 1],
            recv_sem.at[number, slot - 1],
            peer,
        )

    def cot_trade(other):
        return send(
            cot_ref, cots_ref.at[other], cot_send.at[other], cot_recv.at[other], cot_peers[other]
        )

    def early_trade(stage):
        return send(
            early_sent[stage],
            early_arrived[stage],
            early_sem.at[stage],
            early_recv.at[stage],
            {"tensor": flipped(tensor, (trades + 1) >> (stage + 1))},
        )

    def normed_trade(other):
        return send(
            early_normed,
            others_ref.at[other],
            normed_sem.at[other],
            normed_recv.at[other],
            cot_peers[other],
        )

    def save(number, slot):
        return pltpu.make_async_copy(
            slots.at[number, slot], slots_ref.at[number, slot], save_sem.at[number, slot]
        )

    @pl.when(step == 0)
    def _():
        greet([core_peer, far_peer] + cot_peers)

        @pl.loop(0, near_steps)
        def _(number):
            own_copy(number).start()
            trade(number, 1).start()
            trade(number, 2).start()

        for other in range(trades):
            cot_trade(other).start()

    @pl.when(step == 2 * pairs)
    def _():
        early_trade(0).start()

    @pl.when(step == min(3 * pairs + 1, steps - 2))
    def _():
        kept = early_kept[...]
        for stage in range(stages):
            early_trade(stage).wait_recv()
            kept = kept + early_arrived[stage][...].astype(F32)
            if stage + 1 < stages:
                half = kept.shape[0] // 2
                early_sent[stage + 1][...] = kept[half:].astype(BF16)
                early_trade(stage + 1).start()
                kept = kept[:half]
        middle = x_ref[...].astype(F32) + kept
        middle_ref[...] = middle
        normed = (normalise(middle)[0] * norms_ref[2:3, :] + norms_ref[3:4, :]).astype(BF16)
        normed_ref[...] = normed
        early_normed[...] = normed

    @pl.when(step == min(3 * pairs + 2, steps - 1))
    def _():
        for other in range(trades):
            normed_trade(other).start()

    relayed = step // (2 * pairs) * pairs + turn - (pairs - 1)

    @pl.when(jnp.logical_and(turn >= pairs - 1, turn < 2 * pairs - 1))
    def _():
        trade(relayed, 2).wait_recv()
        trade(relayed, 3).start()
        save(relayed, 2).start()

    @pl.when(jnp.logical_not(is_far))
    def _():
        own_copy(number).wait()
        trade(number, 1).wait_recv()
        save(number, 0).start()
        save(number, 1).start()
        acc_all[number] = jnp.zeros(acc_all.shape[1:], F32)
        total_all[number] = jnp.zeros(acc_all.shape[1:], F32)
        top_all[number] = jnp.full(acc_all.shape[1:], -1e30, F32)

    @pl.when(is_far)
    def _():
        trade(number, 3).wait_recv()
        save(number, 3).start()

    query = q_ref[0]
    is_first = first_head(query.shape)
    base = jnp.where(is_far, 2, 0)
    carried_top = top_all[number]
    outs, tops = [], []
    for head in range(2):
        mine = is_first if head == 0 else jnp.logical_not(is_first)
        own_query = jnp.where(mine, query, jnp.zeros_like(query))
        scores = [dot_nt(own_query, slots[number, base + slot, 0]) for slot in range(2)]
        at = head * HEAD_DIM
        top = carried_top[:, at : at + 1]
        for one in scores:
            top = jnp.maximum(top, one.max(axis=1, keepdims=True))
        shift = top * exp_scale
        mixed = None
        for slot, one in enumerate(scores):
            weight = jnp.exp2(one * exp_scale - shift).astype(BF16)
            value = slots[number, base + slot, 1]
            lane_first = first_head(value.shape)
            lane_mine = lane_first if head == 0 else jnp.logical_not(lane_first)
            term = dot_nn(weight, jnp.where(lane_mine, value, jnp.ones_like(value)))
            mixed = term if mixed is None else mixed + term
        outs.append(mixed)
        tops.append(jnp.broadcast_to(top, mixed.shape))
    top = jnp.where(is_first, tops[0], tops[1])
    fade = jnp.exp2((carried_top - top) * exp_scale)
    acc = jnp.where(is_first, outs[0], outs[1]) + acc_all[number] * fade
    total = pltpu.roll(jnp.where(is_first, outs[1], outs[0]), HEAD_DIM, 1) + total_all[number] * fade

    @pl.when(jnp.logical_not(is_far))
    def _():
        acc_all[number] = acc
        top_all[number] = top
        total_all[number] = total

    @pl.when(is_far)
    def _():
        attended = acc / total
        low = attended.astype(BF16)
        low_ref[0] = low
        wide_ref[0] = attended
        log_ref[0] = (top * exp_scale + jnp.log2(total)).T
        term = dot_nt(low, w_ref[...])
        pair = number % pairs

        @pl.when(pair == 0)
        def _():
            mixed_rows[...] = term

        @pl.when(pair > 0)
        def _():
            mixed_rows[...] += term

        @pl.when(jnp.logical_and(pair == pairs - 1, number >= pairs))
        def _():
            half = kept_ref.shape[1]
            kept_ref[0] = mixed_rows[:half]
            sent_ref[0] = mixed_rows[half:].astype(BF16)

        @pl.when(number == pairs - 1)
        def _():
            half = kept_ref.shape[1]
            early_kept[...] = mixed_rows[:half]
            early_sent[0][...] = mixed_rows[half:].astype(BF16)

    @pl.when(step == steps - 1)
    def _():
        @pl.loop(0, near_steps)
        def _(number):
            for slot in range(1, 4):
                trade(number, slot).wait_send()
            for slot in range(4):
                save(number, slot).wait()

        for stage in range(stages):
            early_trade(stage).wait_send()
        for other in range(trades):
            cot_trade(other).wait_send()
            cot_trade(other).wait_recv()
            normed_trade(other).wait_send()
            normed_trade(other).wait_recv()


def attend(queries, own_kv, w_att, cotangent, tokens, norms, trades):
    windows, rows, cols = queries.shape
    width = w_att.shape[0]
    pairs = cols // PAIR
    near = windows * pairs
    out_at = 3 * pairs

    def far(i):
        turn = i % (2 * pairs)
        done = i // (2 * pairs) * pairs
        return jnp.where(turn >= pairs, done + turn - pairs, jnp.maximum(done - 1, 0))

    anywhere = pl.BlockSpec(memory_space=pl.ANY)
    wide = pl.BlockSpec((1, rows, PAIR), lambda i: (far(i) // pairs, 0, far(i) % pairs))
    half = pl.BlockSpec(
        (1, rows // 2, width), lambda i: (jnp.maximum(far(i) // pairs, 1) - 1, 0, 0)
    )
    own_rows = tokens.shape[1]
    own = pl.BlockSpec((own_rows, width), lambda i: (0, 0))
    stages = [rows >> (stage + 1) for stage in range((trades + 1).bit_length() - 1)]
    state = pltpu.VMEM((near, rows, PAIR), F32)
    dma = pltpu.SemaphoreType.DMA
    return run(
        functools.partial(attend_kernel, windows, pairs, trades, LOG2E / math.sqrt(HEAD_DIM)),
        "attend",
        [
            shaped((windows, rows, cols), BF16),
            shaped((windows, rows, cols), F32),
            shaped((windows, cols, rows), F32),
            shaped((windows - 1, rows // 2, width), F32),
            shaped((windows - 1, rows // 2, width), BF16),
            shaped((near, 4, 2, rows, PAIR), BF16),
            shaped((trades,) + cotangent.shape, BF16),
            shaped((own_rows, width), F32),
            shaped((own_rows, width), BF16),
            shaped((trades, own_rows, width), BF16),
        ],
        64 * windows * rows * rows * cols,
        [queries, w_att, own_kv, cotangent, tokens, norms],
        collective_id=0,
        grid=(2 * near,),
        in_specs=[
            pl.BlockSpec((1, rows, PAIR), lambda i: (i // (2 * pairs), 0, i % pairs)),
            pl.BlockSpec((width, PAIR), lambda i: (0, out_at + far(i) % pairs)),
            anywhere,
            anywhere,
            pl.BlockSpec((None, own_rows, width), lambda i: (0, 0, 0)),
            pl.BlockSpec(norms.shape, lambda i: (0, 0)),
        ],
        out_specs=[
            wide,
            wide,
            pl.BlockSpec((1, PAIR, rows), lambda i: (far(i) // pairs, far(i) % pairs, 0)),
            half,
            half,
            anywhere,
            anywhere,
            own,
            own,
            anywhere,
        ],
        scratch_shapes=[
            pltpu.VMEM((near, 4, 2, rows, PAIR), BF16),
            state,
            state,
            state,
            pltpu.VMEM((rows, width), F32),
            dma((near,)),
            dma((near, 3)),
            dma((near, 3)),
            dma((near, 4)),
            dma((trades,)),
            dma((trades,)),
            pltpu.VMEM((rows // 2, width), F32),
            pltpu.VMEM((own_rows, width), BF16),
            dma((len(stages),)),
            dma((len(stages),)),
            dma((trades,)),
            dma((trades,)),
        ]
        + [pltpu.VMEM((count, width), BF16) for count in stages] * 2,
    )


def attend_back_kernel(windows, pairs, blocks, exp_scale, score_scale, *refs):
    q_ref, wide_ref, log_ref, slots_ref, w_ref, cos_ref, sin_ref, last_ref = refs[:8]
    trades = blocks - 1
    known = (windows - 1) * blocks + 1
    grad_refs = list(refs[8 : 8 + known])
    refs = refs[8 + known :]
    sent_refs, shard_ref, refs = refs[:windows], refs[windows], refs[windows + 1 :]
    gq_ref, gk_ref, gv_ref, rows_ref = refs[:4]
    arrived_refs, shard_arrived = refs[4 : 4 + windows], refs[4 + windows]
    refs = refs[5 + windows :]
    dq_all, do_all, far_kept, far_sent, far_core, far_x, near_kept, near_sent, near_core = refs[:9]
    send_sem, recv_sem, result_send, result_recv, last_send, last_recv, last_others, shard_sem = refs[9:]
    grad_refs += [last_others.at[other] for other in range(trades)]
    step = pl.program_id(0)
    count = windows * pairs
    tensor = lax.axis_index("tensor")
    core_peer = {"core": 1 - lax.axis_index("core")}
    far_peer = {"x": 1 - lax.axis_index("x")}
    result_peer = {"tensor": flipped(tensor, lax.axis_size("tensor") // 2)}

    def trade(kind, number):
        source, target, peer = (
            (far_sent, far_core, core_peer),
            (far_kept, far_x, far_peer),
            (near_sent, near_core, core_peer),
        )[kind]
        return send(
            source.at[number],
            target.at[number],
            send_sem.at[kind, number],
            recv_sem.at[kind, number],
            peer,
        )

    def result_trade(w):
        return send(
            sent_refs[w], arrived_refs[w], result_send.at[w], result_recv.at[w], result_peer
        )

    others = [{"tensor": flipped(tensor, other + 1)} for other in range(trades)]

    def last_trade(other):
        return send(
            last_ref, last_others.at[other], last_send.at[other], last_recv.at[other], others[other]
        )

    def shard_trade():
        return send(shard_ref, shard_arrived, shard_sem.at[0], shard_sem.at[1], far_peer)

    @pl.when(step == 0)
    def _():
        greet([core_peer, far_peer] + others)
        shard_trade().start()
        for other in range(trades):
            last_trade(other).start()
        for w in range(windows):
            result_trade(w).start()

    def at_step(first, body):
        number = step - first

        @pl.when(jnp.logical_and(number >= 0, number < count))
        def _():
            body(number)

    def send_far(number):
        trade(0, number).start()

    def add_far(number):
        trade(0, number).wait_recv()
        far_kept[number] = (
            far_kept[number].astype(F32) + far_core[number].astype(F32)
        ).astype(BF16)

    def send_x(number):
        trade(1, number).start()

    def send_near(number):
        trade(2, number).start()

    def finish(number):
        trade(2, number).wait_recv()
        trade(1, number).wait_recv()
        total = (
            near_kept[number].astype(F32)
            + near_core[number].astype(F32)
            + far_x[number].astype(F32)
        )
        key = total[0]
        gk_ref[0] = (key * cos_ref[...] - swap_halves(key) * sin_ref[...]).astype(BF16)
        gv_ref[0] = total[1].astype(BF16)

    at_step(1, send_far)
    at_step(3, send_x)
    at_step(count + 1, send_near)
    at_step(2, add_far)
    at_step(count + 2, finish)

    for w in range(windows):

        @pl.when(step == w * pairs)
        def _(w=w):
            if w == windows - 1:
                for other in range(trades):
                    last_trade(other).wait_recv()
            at_row = 0
            for grad_ref in grad_refs[w * blocks : (w + 1) * blocks]:
                rows_ref[0, at_row : at_row + grad_ref.shape[0], :] = grad_ref[...]
                at_row += grad_ref.shape[0]

    def gradients(number, grad_out, kept, sent):
        query = q_ref[0]
        is_first = first_head(query.shape)
        overlap = (grad_out.astype(F32) * wide_ref[0]).T
        logs = log_ref[0]
        zero = jnp.zeros_like(query)
        own_q, own_do, row_log, row_sum = [], [], [], []
        for head in range(2):
            mine = is_first if head == 0 else jnp.logical_not(is_first)
            own_q.append(jnp.where(mine, query, zero))
            own_do.append(jnp.where(mine, grad_out, zero))
            at = head * HEAD_DIM
            row_log.append(logs[at : at + 1, :])
            row_sum.append(jnp.sum(overlap[at : at + HEAD_DIM, :], axis=0, keepdims=True))
        dq_parts = [None, None]
        for slot, target in enumerate((kept, sent)):
            key, value = slots_ref[0, slot, 0], slots_ref[0, slot, 1]
            key_turned = key.T
            grad_key, grad_value = None, None
            for head in range(2):
                scores = dot_nt(key, own_q[head])
                probs = jnp.exp2(scores * exp_scale - row_log[head])
                grad_probs = dot_nt(value, own_do[head])
                grad_scores = (probs * (grad_probs - row_sum[head])).astype(BF16)
                term_v = dot_nn(probs.astype(BF16), own_do[head])
                term_k = dot_nn(grad_scores, own_q[head])
                at = head * HEAD_DIM
                term_q = dot_nn(key_turned[at : at + HEAD_DIM, :], grad_scores)
                grad_value = term_v if grad_value is None else grad_value + term_v
                grad_key = term_k if grad_key is None else grad_key + term_k
                dq_parts[head] = term_q if dq_parts[head] is None else dq_parts[head] + term_q
            target[number, 0] = (grad_key * score_scale).astype(BF16)
            target[number, 1] = grad_value.astype(BF16)
        return jnp.concatenate(dq_parts, axis=0).T * score_scale

    @pl.when(step < count)
    def _():
        grad_out = dot_nn(rows_ref[0], w_ref[...]).astype(BF16)
        do_all[step] = grad_out
        dq_all[step] = gradients(step, grad_out, far_kept, far_sent)

    @pl.when(jnp.logical_and(step >= count, step < 2 * count))
    def _():
        number = step - count
        grad_query = dq_all[number] + gradients(number, do_all[number], near_kept, near_sent)
        gq_ref[0] = (grad_query * cos_ref[...] - swap_halves(grad_query) * sin_ref[...]).astype(
            BF16
        )

    @pl.when(step == pl.num_programs(0) - 1)
    def _():
        @pl.loop(0, count)
        def _(number):
            for kind in range(3):
                trade(kind, number).wait_send()

        shard_trade().wait()
        for other in range(trades):
            last_trade(other).wait_send()
        for w in range(windows):
            result_trade(w).wait_send()
            result_trade(w).wait_recv()


def attend_back(queries, wide, logs, slots_all, grad_blocks, w_att, tables, sent, shard):
    windows, rows, cols = queries.shape
    width = w_att.shape[0]
    pairs = cols // PAIR
    count = windows * pairs
    out_at = 3 * pairs
    score_scale = 1.0 / math.sqrt(HEAD_DIM)
    blocks = lax.axis_size("tensor")
    grads = [block for one in grad_blocks for block in one]
    last = grads[-1]

    def spot(lag, last=None):
        def index(i):
            number = jnp.clip(i - lag, 0, count - 1)
            return (number // pairs, 0, number % pairs)

        return pl.BlockSpec((1, rows, PAIR), index)

    def both(i):
        return jnp.minimum(i, 2 * count - 1) % count

    dma = pltpu.SemaphoreType.DMA
    piece = pltpu.VMEM((count, 2, rows, PAIR), BF16)
    anywhere = pl.BlockSpec(memory_space=pl.ANY)
    return run(
        functools.partial(
            attend_back_kernel, windows, pairs, blocks, score_scale * LOG2E, score_scale
        ),
        "attend_back",
        [shaped((windows, rows, cols), BF16)] * 3
        + [shaped((windows, rows, width), BF16)]
        + [shaped(one.shape, BF16) for one in (*sent, shard)],
        160 * windows * rows * rows * cols,
        [queries, wide, logs, slots_all, w_att, *tables, last, *grads, *sent, shard],
        collective_id=2,
        grid=(2 * count + 2,),
        in_specs=[
            pl.BlockSpec((1, rows, PAIR), lambda i: (both(i) // pairs, 0, both(i) % pairs)),
            pl.BlockSpec((1, rows, PAIR), lambda i: (both(i) // pairs, 0, both(i) % pairs)),
            pl.BlockSpec((1, PAIR, rows), lambda i: (both(i) // pairs, both(i) % pairs, 0)),
            pl.BlockSpec(
                (1, 2, 2, rows, PAIR),
                lambda i: (both(i), jnp.where(i < count, 1, 0), 0, 0, 0),
            ),
            pl.BlockSpec((width, PAIR), lambda i: (0, out_at + jnp.minimum(i, count - 1) % pairs)),
            pl.BlockSpec((rows, PAIR), lambda i: (0, 0)),
            pl.BlockSpec((rows, PAIR), lambda i: (0, 0)),
            anywhere,
        ]
        + [pl.BlockSpec(block.shape, lambda i: (0, 0)) for block in grads]
        + [anywhere] * (windows + 1),
        out_specs=[
            spot(count),
            spot(count + 2),
            spot(count + 2),
            pl.BlockSpec((1, rows, width), lambda i: (jnp.minimum(i // pairs, windows - 1), 0, 0)),
        ]
        + [anywhere] * (windows + 1),
        scratch_shapes=[pltpu.VMEM((count, rows, PAIR), F32), pltpu.VMEM((count, rows, PAIR), BF16)]
        + [piece] * 7
        + [dma((3, count)), dma((3, count)), dma((windows,)), dma((windows,))]
        + [dma((blocks - 1,)), dma((blocks - 1,)), pltpu.VMEM((blocks - 1,) + last.shape, BF16)]
        + [dma((2,))],
    )


def feed_kernel(blocks, trades, chained, *refs):
    stages = (trades + 1).bit_length() - 1
    refs = list(refs)

    def take(count):
        taken = refs[:count]
        del refs[:count]
        return taken

    first = blocks > 0
    w_refs = take(3)
    if first:
        factor_ref = take(1)[0]
        x_refs, cot_refs = take(blocks), take(blocks)
    else:
        both_ref, total_in, grad_in, _ = take(4)
    if chained:
        next_kept, next_sent, next_x, norms_ref = take(4)
    if first:
        both_ref, wide_ref, total, grad_total = take(4)
    else:
        wide_ref, kept_ref, sent_ref, grad_kept_ref, grad_sent_ref = take(5)
    if chained:
        middle_ref, normed_ref, others_ref = take(3)
    if not first:
        total, grad_total = take(2)
    step, steps = pl.program_id(0), pl.num_programs(0)

    gate_w, up_w, down_w = [ref[...] for ref in w_refs]
    if chained:
        normed, sum_send, sum_recv, normed_send, normed_recv = take(5)
        later_sent, arrived = take(stages - 1), take(stages)
        tensor = lax.axis_index("tensor")
        others = [{"tensor": flipped(tensor, other + 1)} for other in range(trades)]

        def sum_trade(stage):
            return send(
                next_sent if stage == 0 else later_sent[stage - 1],
                arrived[stage],
                sum_send.at[stage],
                sum_recv.at[stage],
                {"tensor": flipped(tensor, (trades + 1) >> (stage + 1))},
            )

        def normed_trade(other):
            return send(
                normed,
                others_ref.at[other],
                normed_send.at[other],
                normed_recv.at[other],
                others[other],
            )

    @pl.when(step == 0)
    def _():
        if chained:
            greet(others)
            sum_trade(0).start()
        if first:
            at_row = 0
            for x_ref, cot_ref in zip(x_refs, cot_refs):
                rows = slice(at_row, at_row + x_ref.shape[0])
                at_row += x_ref.shape[0]
                both_ref[0, rows, :] = x_ref[...]
                both_ref[1, rows, :] = (cot_ref[...].astype(F32) * factor_ref[0, 0]).astype(BF16)

    x_rows = both_ref[0]
    gate = dot_nn(x_rows, gate_w)
    up = dot_nn(x_rows, up_w)
    grad_hidden = dot_nn(both_ref[1], down_w)
    sig = jax.nn.sigmoid(gate)
    swish = gate * sig
    hidden = (swish * up).astype(BF16)
    grad_gate = (grad_hidden * up * sig * (1.0 + gate * (1.0 - sig))).astype(BF16)
    grad_up = (grad_hidden * swish).astype(BF16)
    wide_ref[0] = grad_gate
    wide_ref[1] = grad_up
    wide_ref[2] = hidden
    grad_term = dot_nt(grad_gate, gate_w) + dot_nt(grad_up, up_w)
    term = dot_nt(hidden, down_w)

    @pl.when(step == 0)
    def _():
        total[...] = term if first else total_in[...] + term
        grad_total[...] = grad_term if first else grad_in[...] + grad_term

    @pl.when(step > 0)
    def _():
        total[...] += term
        grad_total[...] += grad_term

    if chained:

        @pl.when(step == steps - 1)
        def _():
            kept = next_kept[...]
            for stage in range(stages):
                sum_trade(stage).wait_recv()
                kept = kept + arrived[stage][...].astype(F32)
                if stage + 1 < stages:
                    half = kept.shape[0] // 2
                    later_sent[stage][...] = kept[half:].astype(BF16)
                    sum_trade(stage + 1).start()
                    kept = kept[:half]
            middle = next_x[...].astype(F32) + kept
            low = (normalise(middle)[0] * norms_ref[2:3, :] + norms_ref[3:4, :]).astype(BF16)
            normed[...] = low
            normed_ref[...] = low
            middle_ref[...] = middle

    @pl.when(step == steps - 1)
    def _():
        if not first:
            half = kept_ref.shape[0]
            kept_ref[...] = total[:half]
            sent_ref[...] = total[half:].astype(BF16)
            grad_kept_ref[...] = grad_total[:half]
            grad_sent_ref[...] = grad_total[half:].astype(BF16)
        if chained:
            for other in range(trades):
                normed_trade(other).start()
            for stage in range(stages):
                sum_trade(stage).wait_send()
            for other in range(trades):
                normed_trade(other).wait_recv()
                normed_trade(other).wait_send()


def feed_specs(weights):
    lead = weights.shape[:-1]
    part_cols = weights.shape[-1] // 3
    step = min(512, part_cols)
    steps = part_cols // step
    zeros = (0,) * len(lead)
    specs = [
        pl.BlockSpec(
            lead + (step,), functools.partial(lambda at, i: zeros + (at + i,), k * steps)
        )
        for k in range(3)
    ]
    return step, steps, specs


def full(*shape):
    return pl.BlockSpec(shape, lambda i: (0,) * len(shape))


def feed_first(x_blocks, cot_blocks, factor, weights, trades, chain=None):
    blocks, block_specs = zip(*[plane(block) for block in (*x_blocks, *cot_blocks)])
    width = weights.shape[0]
    rows = sum(spec.block_shape[-2] for spec in block_specs[: len(x_blocks)])
    step, steps, w_specs = feed_specs(weights)
    hidden_cols = 2 * step * steps
    anywhere = pl.BlockSpec(memory_space=pl.ANY)
    args = [weights, weights, weights, factor, *blocks]
    in_specs = w_specs + [SCALAR] + list(block_specs)
    out_shape = [shaped((2, rows, width), BF16), shaped((3, rows, hidden_cols), BF16)]
    out_shape += [shaped((rows, width), F32)] * 2
    out_specs = [full(2, rows, width), pl.BlockSpec((3, rows, step), lambda i: (0, 0, i))]
    out_specs += [full(rows, width)] * 2
    scratch = []
    if chain is not None:
        kept, sent, x_rows, norms = chain
        for one in (kept, None, x_rows, norms):
            array, spec = (sent, anywhere) if one is None else plane(one)
            args.append(array)
            in_specs.append(spec)
        own = in_specs[-2].block_shape[-2]
        out_shape += [
            shaped((own, width), F32),
            shaped((own, width), BF16),
            shaped((trades, own, width), BF16),
        ]
        out_specs += [full(own, width), full(own, width), anywhere]
        dma = pltpu.SemaphoreType.DMA
        stages = [rows >> (stage + 1) for stage in range((trades + 1).bit_length() - 1)]
        scratch += [pltpu.VMEM((own, width), BF16)]
        scratch += [dma((len(stages),))] * 2 + [dma((trades,))] * 2
        scratch += [pltpu.VMEM((count, width), BF16) for count in stages[1:] + stages]
    return run(
        functools.partial(feed_kernel, len(x_blocks), trades, chain is not None),
        "feed_first",
        out_shape,
        6 * rows * width * hidden_cols,
        args,
        collective_id=None if chain is None else 5,
        grid=(steps,),
        in_specs=in_specs,
        out_specs=out_specs,
        scratch_shapes=scratch,
    )


def feed_last(both, wide, totals, weights):
    rows, width = both.shape[1:]
    step, steps, w_specs = feed_specs(weights)
    hidden_cols = 2 * step * steps
    half = full(rows // 2, width)
    return run(
        functools.partial(feed_kernel, 0, 0, False),
        "feed_last",
        [shaped((3, rows, hidden_cols), BF16)]
        + [shaped((rows // 2, width), F32), shaped((rows // 2, width), BF16)] * 2,
        6 * rows * width * hidden_cols,
        [weights, weights, weights, both, *totals, wide],
        grid=(steps,),
        in_specs=w_specs
        + [full(2, rows, width), full(rows, width), full(rows, width)]
        + [pl.BlockSpec(memory_space=pl.ANY)],
        out_specs=[pl.BlockSpec((3, rows, step), lambda i: (0, 0, steps + i))] + [half] * 4,
        scratch_shapes=[pltpu.VMEM((rows, width), F32)] * 2,
        input_output_aliases={6: 0},
    )


def weights_kernel(windows, masks, *refs):
    lefts, rights = refs[:windows], refs[windows : 2 * windows]
    refs = refs[2 * windows :]
    sources, out_ref, targets = refs[: len(masks)], refs[len(masks)], refs[len(masks) + 1 :]
    at = pl.program_id(0)
    tensor = lax.axis_index("tensor")
    trades = []
    if masks:
        targets, (send_sem, recv_sem) = targets[: len(masks)], targets[len(masks) :]
    for source, target, kinds in zip(sources, targets, masks):
        for number, mask in enumerate(kinds):
            sems = (send_sem.at[len(trades)], recv_sem.at[len(trades)])
            peer = {"tensor": flipped(tensor, mask)}
            trades.append(send(source, target.at[number], *sems, peer))

    if masks:

        @pl.when(at == 0)
        def _():
            peers = sorted({mask for kinds in masks for mask in kinds})
            greet([{"tensor": flipped(tensor, mask)} for mask in peers])
            for trade in trades:
                trade.start()

    total = None
    for left, right in zip(lefts, rights):
        term = dot_tn(left[...], right[...])
        total = term if total is None else total + term
    total = total.astype(BF16)
    depths, cores, halves, shard = out_ref.shape[:4]
    for depth in range(depths):
        for half in range(halves):
            for core in range(cores):
                start = ((depth * halves + half) * cores + core) * shard
                out_ref[depth, core, half] = total[start : start + shard]

    if masks:

        @pl.when(at == pl.num_programs(0) - 1)
        def _():
            for trade in trades:
                trade.wait()


def feed_weights(boths, wides, part, swaps):
    windows = len(boths)
    rows, width = boths[0].shape[1:]
    hidden_cols = wides[0].shape[2] // 2
    step = min(512, hidden_cols)
    steps = hidden_cols // step
    lead = (lax.axis_size("dp"), lax.axis_size("core"), lax.axis_size("x"))
    lead += (width // math.prod(lead),)
    masks = [kinds for _, kinds in swaps]
    anywhere = pl.BlockSpec(memory_space=pl.ANY)
    left = pl.BlockSpec((None, rows, width), lambda i: (i // (2 * steps), 0, 0))
    right = pl.BlockSpec((None, rows, step), lambda i: (i // steps, 0, part * steps + i % steps))
    total = sum(len(kinds) for kinds in masks)
    return run(
        functools.partial(weights_kernel, windows, masks),
        "feed_weights",
        [shaped(lead + (3 * hidden_cols,), BF16)]
        + [shaped((len(kinds),) + array.shape, BF16) for array, kinds in swaps],
        6 * windows * rows * width * hidden_cols,
        [*boths, *wides] + [array for array, _ in swaps],
        collective_id=4 if swaps else None,
        grid=(3 * steps,),
        in_specs=[left] * windows + [right] * windows + [anywhere] * len(swaps),
        out_specs=[pl.BlockSpec(lead + (step,), lambda i: (0, 0, 0, 0, i))]
        + [anywhere] * len(swaps),
        scratch_shapes=[pltpu.SemaphoreType.DMA((total,))] * 2 if swaps else [],
    )


def norm_grad(kept_ref, arrived_ref, stream, gain, sums_ref):
    grad_normed = kept_ref[...] + arrived_ref[...].astype(F32)
    normed, inv_std = normalise(stream)
    sums_ref[0:1, :] = jnp.sum(grad_normed * normed, axis=0, keepdims=True)
    sums_ref[1:2, :] = jnp.sum(grad_normed, axis=0, keepdims=True)
    return norm_back(grad_normed, normed, inv_std, gain)


def middle_back_kernel(
    factor_ref, kept_ref, arrived_ref, middle_ref, cot_ref, norms_ref, grad_ref, low_ref, sums_ref
):
    grad_y = cot_ref[...].astype(F32) * factor_ref[0, 0]
    grad = grad_y + norm_grad(
        kept_ref, arrived_ref, middle_ref[...], norms_ref[2:3, :], sums_ref
    )
    grad_ref[...] = grad
    low_ref[...] = grad.astype(BF16)


def second_norm_back(factor, kept, arrived, middle, cot_rows, norms):
    args, in_specs = zip(*[plane(one) for one in (kept, arrived, middle, cot_rows, norms)])
    full = pl.BlockSpec(kept.shape, lambda i: (0, 0))
    return run(
        middle_back_kernel,
        "second_norm_back",
        [
            shaped(kept.shape, F32),
            shaped(kept.shape, BF16),
            shaped((2, kept.shape[1]), F32),
        ],
        40 * kept.size,
        [factor, *args],
        grid=(1,),
        in_specs=[SCALAR, *in_specs],
        out_specs=[full, full, pl.BlockSpec((2, kept.shape[1]), lambda i: (0, 0))],
    )


class SumRoute:
    def __init__(self, part, rows, core_in, mine, x_in, z_in, send_sem, recv_sem):
        self.read, self.rows = part, rows
        self.core_in, self.mine, self.x_in, self.z_in = core_in, mine, x_in, z_in
        self.send_sem, self.recv_sem = send_sem, recv_sem
        self.seq, self.depth = seq_index(), lax.axis_index("dp")
        self.peers = half_chip_peers()

    def place(self, number, other_core):
        seq = flipped(self.seq, 2) if number >= 4 else self.seq
        seq = flipped(seq, 1) if other_core else seq
        turn = (self.depth + number % 4) % lax.axis_size("dp")
        return pl.ds(
            pl.multiple_of((turn * seq_size() + seq) * self.rows, self.rows), self.rows
        )

    def message(self, number):
        if number < 8:
            source, target, peer = self.read.at[self.place(number, True), :], self.core_in, "core"
            target = target.at[number]
        elif number < 12:
            source, target, peer = self.mine.at[number - 4], self.x_in.at[number - 8], "far"
        else:
            turn, peer = ((2, "up"), (1, "up"), (3, "down"))[number - 12]
            source, target = self.mine.at[turn], self.z_in.at[number - 12]
        return send(
            source, target, self.send_sem.at[number], self.recv_sem.at[number], self.peers[peer]
        )

    def start(self, *numbers):
        for number in numbers:
            self.message(number).start()

    def add_core(self, number):
        self.message(number).wait_recv()
        own = self.read[self.place(number, False), :].astype(F32)
        self.mine[number] = (own + self.core_in[number].astype(F32)).astype(self.mine.dtype)

    def add_x(self, number):
        self.message(8 + number).wait_recv()
        total = self.mine[number].astype(F32) + self.x_in[number].astype(F32)
        self.mine[number] = total.astype(self.mine.dtype)

    def add_up(self):
        self.message(12).wait_recv()
        total = self.mine[1].astype(F32) + self.z_in[0].astype(F32)
        self.mine[1] = total.astype(self.mine.dtype)

    def total(self):
        self.message(13).wait_recv()
        self.message(14).wait_recv()
        return (
            self.mine[0].astype(F32) + self.z_in[1].astype(F32) + self.z_in[2].astype(F32)
        )

    def sent(self):
        for number in range(SUM_MESSAGES):
            self.message(number).wait_send()


SUM_MESSAGES = 15


def finish_kernel(windows, trades, score_cols, *refs):
    stages = (trades + 1).bit_length() - 1
    refs = list(refs)

    def take(count):
        taken = refs[:count]
        del refs[:count]
        return taken

    far_inputs = take(8)
    shard_ref = take(1)[0]
    norms_ref = take(1)[0]
    second_refs = take(windows)
    grad_refs = take(windows)
    part_refs = take(3 * windows)
    weights_ref, vectors_ref, input_ref, output_ref, shard_arrived = take(5)
    loads = take(8)
    grad_loads = take(windows)
    part_loads = take(3 * windows)
    part, core_in, mine, x_in, z_in = take(5)
    tiles, own_tiles, arrived_tiles = take(3)
    small_core, small_mine, small_x, small_z = take(4)
    kept_all = take(windows)
    stage_sent = [take(stages) for _ in range(windows)]
    stage_arrived = [take(stages) for _ in range(windows)]
    load_sem, big_send, big_recv, small_send, small_recv = take(5)
    y_send, y_recv, tile_send, tile_recv, shard_sem = take(5)
    assert not refs
    (grad_q, grad_k, grad_v, normed, grad_mid, attended, w_qkv, tokens) = loads[:8]
    tensor = lax.axis_index("tensor")
    others = [{"tensor": flipped(tensor, other + 1)} for other in range(trades)]
    shards = lax.axis_size("dp") * seq_size()
    devices = shards * (trades + 1)
    group = tiles.shape[0] // shards
    width = part.shape[1]
    cols = score_cols
    rows = width // shards

    w_source = far_inputs[6].at[:, pl.ds(0, 3 * cols)]
    sources = [*far_inputs[:6], w_source, far_inputs[7]]
    sources += [*grad_refs, *part_refs]
    targets = [*loads, *grad_loads, *part_loads]
    copies = [
        pltpu.make_async_copy(source, target, load_sem.at[at])
        for at, (source, target) in enumerate(zip(sources, targets))
    ]
    order = [4, 5, 6, 0, 1, 2, 3, 7] + list(range(8, len(copies)))
    for at in order:
        copies[at].start()

    def block_route(block):
        return SumRoute(
            part.at[block],
            rows,
            core_in.at[block],
            mine.at[block],
            x_in.at[block],
            z_in.at[block],
            big_send.at[block],
            big_recv.at[block],
        )

    routes = [block_route(block) for block in range(4)]
    small = SumRoute(
        tiles, group, small_core, small_mine, small_x, small_z, small_send, small_recv
    )
    greet(list(small.peers.values()) + others)
    everything = (6, 7, 5, 4, 2, 3, 1, 0)

    def product(block, left, right):
        total = None
        for w in range(windows):
            term = dot_tn(left[w], right[w])
            total = term if total is None else total + term
        part[block] = total.astype(BF16)

    def y_trade(w, stage):
        return send(
            stage_sent[w][stage],
            stage_arrived[w][stage],
            y_send.at[w, stage],
            y_recv.at[w, stage],
            {"tensor": flipped(tensor, (trades + 1) >> (stage + 1))},
        )

    def turn_back(w):
        total = None
        for at, grad in enumerate((grad_q, grad_k, grad_v)):
            term = dot_nt(grad[w], w_qkv[:, at * cols : (at + 1) * cols])
            total = term if total is None else total + term
        half = total.shape[0] // 2
        kept_all[w][...] = total[:half]
        stage_sent[w][0][...] = total[half:].astype(BF16)

    def add_cores(route):
        for number in everything:
            route.add_core(number)

    def across(route):
        route.start(10, 11, 9, 8)

    def add_across(route):
        for number in (2, 3, 1, 0):
            route.add_x(number)

    shard_trade = send(
        shard_ref, shard_arrived, shard_sem.at[0], shard_sem.at[1], small.peers["far"]
    )
    shard_trade.start()
    copies[4].wait()
    copies[5].wait()
    product(3, grad_mid, attended)
    for at in (6, 0, 1, 2):
        copies[at].wait()
    routes[3].start(*everything)
    turn_back(0)
    add_cores(routes[3])
    y_trade(0, 0).start()
    across(routes[3])
    for w in range(1, windows):
        turn_back(w)
    copies[3].wait()
    product(0, normed, grad_q)
    for w in range(1, windows):
        y_trade(w, 0).start()
    routes[0].start(*everything)
    product(1, normed, grad_k)
    add_cores(routes[0])
    routes[1].start(*everything)
    across(routes[0])
    product(2, normed, grad_v)
    add_cores(routes[1])
    routes[2].start(*everything)
    across(routes[1])
    add_across(routes[3])
    add_cores(routes[2])
    routes[3].start(12, 14)
    across(routes[2])
    for at in range(8 + windows, len(copies)):
        copies[at].wait()
    for w in range(windows):
        middle_ref, kept_ref, arrived_ref = part_loads[3 * w : 3 * w + 3]
        output_ref[w] = (
            middle_ref[...] + (kept_ref[...] + arrived_ref[...].astype(F32))
        ).astype(BF16)
    routes[3].add_up()
    for at in range(7, 8 + windows):
        copies[at].wait()
    sums = [None, None]

    def first_norm(w):
        kept = kept_all[w][...]
        for stage in range(stages):
            y_trade(w, stage).wait_recv()
            kept = kept + stage_arrived[w][stage][...].astype(F32)
            if stage + 1 < stages:
                half = kept.shape[0] // 2
                stage_sent[w][stage + 1][...] = kept[half:].astype(BF16)
                y_trade(w, stage + 1).start()
                kept = kept[:half]
        normed_rows, inv_std = normalise(tokens[w].astype(F32))
        for at, one in enumerate((kept * normed_rows, kept)):
            one = jnp.sum(one, axis=0, keepdims=True)
            sums[at] = one if sums[at] is None else sums[at] + one
        input_ref[w] = grad_loads[w][...] + norm_back(
            kept, normed_rows, inv_std, norms_ref[0:1, :]
        )

    first_norm(0)
    routes[3].start(13)
    add_across(routes[0])
    for w in range(1, windows):
        first_norm(w)
    routes[0].start(12, 14)
    first = jnp.concatenate(sums, axis=0)
    second = sum(ref[...] for ref in second_refs)
    span = width // devices
    tiles[...] = jnp.zeros_like(tiles)
    for device in range(devices):
        at = device * 8
        columns = slice(device * span, (device + 1) * span)
        tiles[at : at + 2, :span] = first[:, columns]
        tiles[at + 2 : at + 4, :span] = second[:, columns]
    add_across(routes[1])
    small.start(*everything)
    routes[0].add_up()
    routes[1].start(12, 14)
    add_cores(small)
    routes[0].start(13)
    across(small)
    add_across(routes[2])
    routes[1].add_up()
    routes[2].start(12, 14)
    add_across(small)
    routes[1].start(13)
    small.start(12, 14)
    for block in (3, 0):
        weights_ref[:, block * cols : (block + 1) * cols] = routes[block].total()
    small.add_up()
    routes[2].add_up()
    small.start(13)
    weights_ref[:, cols : 2 * cols] = routes[1].total()
    routes[2].start(13)
    own_tiles[...] = small.total()

    def tile_trade(other):
        place = pl.ds(pl.multiple_of(flipped(tensor, other + 1) * 8, 8), 8)
        return send(
            own_tiles.at[place, :],
            arrived_tiles.at[other],
            tile_send.at[other],
            tile_recv.at[other],
            others[other],
        )

    weights_ref[:, 2 * cols : 3 * cols] = routes[2].total()
    for other in range(trades):
        tile_trade(other).start()
    vectors = own_tiles[pl.ds(pl.multiple_of(tensor * 8, 8), 8), :]
    for other in range(trades):
        tile_trade(other).wait_recv()
        vectors = vectors + arrived_tiles[other]
    vectors_ref[...] = vectors
    shard_trade.wait()
    for route in (*routes, small):
        route.sent()
    for w in range(windows):
        for stage in range(stages):
            y_trade(w, stage).wait_send()
    for other in range(trades):
        tile_trade(other).wait_send()


def finish(
    grads,
    normed,
    grad_mid,
    attended,
    w_att,
    tokens,
    ffn_shard,
    norms,
    second_sums,
    grad_middles,
    parts,
    trades,
):
    windows, rows, cols = grads[0].shape
    width = w_att.shape[0]
    own_rows = tokens.shape[1]
    shards = lax.axis_size("dp") * seq_size()
    shard = width // shards
    group = 8 * (trades + 1)
    stages = [rows >> (stage + 1) for stage in range((trades + 1).bit_length() - 1)]
    dma = pltpu.SemaphoreType.DMA
    anywhere = pl.BlockSpec(memory_space=pl.ANY)
    vmem = pl.BlockSpec(memory_space=pltpu.VMEM)
    far_inputs = [*grads, normed, grad_mid, attended, w_att, tokens]
    flat = [array for one in parts for array in one]
    kinds = (8, 8, 4, 3)

    def like(array):
        return pltpu.VMEM(array.shape, array.dtype)

    loads = [like(array) for array in far_inputs]
    loads[6] = pltpu.VMEM((width, 3 * cols), BF16)
    return run(
        functools.partial(finish_kernel, windows, trades, cols),
        "finish",
        [
            shaped((shard, 4 * cols), F32),
            shaped((8, 128), F32),
            shaped((windows, own_rows, width), F32),
            shaped((windows, own_rows, width), BF16),
            shaped(ffn_shard.shape, BF16),
        ],
        8 * windows * rows * width * cols + 6 * windows * rows * width * cols,
        [*far_inputs, ffn_shard, norms, *second_sums, *grad_middles, *flat],
        collective_id=3,
        in_specs=[anywhere] * 9
        + [vmem] * (1 + windows)
        + [anywhere] * (windows + len(flat)),
        out_specs=[vmem] * 4 + [anywhere],
        scratch_shapes=loads
        + [like(array) for array in grad_middles]
        + [like(array) for array in flat]
        + [pltpu.VMEM((4, width, cols), BF16)]
        + [pltpu.VMEM((4, count, shard, cols), BF16) for count in kinds]
        + [
            pltpu.VMEM((shards * group, 128), F32),
            pltpu.VMEM((group, 128), F32),
            pltpu.VMEM((trades, 8, 128), F32),
        ]
        + [pltpu.VMEM((count, group, 128), F32) for count in kinds]
        + [pltpu.VMEM((rows // 2, width), F32)] * windows
        + [pltpu.VMEM((count, width), BF16) for count in stages] * (2 * windows)
        + [
            dma((8 + windows + len(flat),)),
            dma((4, SUM_MESSAGES)),
            dma((4, SUM_MESSAGES)),
            dma((SUM_MESSAGES,)),
            dma((SUM_MESSAGES,)),
            dma((windows, len(stages))),
            dma((windows, len(stages))),
            dma((trades,)),
            dma((trades,)),
            dma((2,)),
        ],
    )


def local(
    tokens,
    cotangent,
    species,
    counts,
    species_scale,
    norm1_gain,
    norm1_bias,
    w_query,
    w_key,
    w_value,
    w_out,
    norm2_gain,
    norm2_bias,
    w_gate,
    w_up,
    w_down,
):
    windows_here, own_rows, model_width = tokens.shape
    tensor_size = lax.axis_size("tensor")
    block_rows = own_rows * tensor_size
    head_cols = w_query.shape[1]
    hidden_cols = w_gate.shape[1]
    shards = ("dp", "x", "core")

    own_at = lax.axis_index("tensor")
    starts = jnp.concatenate(
        [
            lax.iota(jnp.int32, own_rows) + (own_at ^ other) * own_rows
            for other in range(tensor_size)
        ]
    )
    positions = (seq_index() * block_rows + starts).astype(F32)
    cos_half, sin_half = angles(positions, HEAD_DIM)
    cosine = jnp.concatenate([cos_half] * 4, axis=1)
    sine = jnp.concatenate([-sin_half, sin_half] * 2, axis=1)

    labels = lax.broadcasted_iota(jnp.int32, (windows_here, species_scale.shape[0]), 1)
    chosen = jnp.sum(jnp.where(species[:, None] == labels, species_scale[None, :], 0.0), axis=1)
    weighted = counts.astype(F32) * chosen

    lanes = jnp.zeros((8, 128), F32)
    vectors = jnp.stack([norm1_gain, norm1_bias, norm2_gain, norm2_bias])
    tile = lanes.at[:4, : vectors.shape[1]].set(vectors).at[4, :].set(jnp.sum(weighted))
    part = hidden_cols // 2
    turned = w_down.T
    first_ffn = jnp.concatenate([w_gate[:, :part], w_up[:, :part], turned[:, :part]], axis=1)
    last_ffn = jnp.concatenate([w_gate[:, part:], w_up[:, part:], turned[:, part:]], axis=1)
    first_ffn = lax.all_gather(first_ffn, shards, axis=0, tiled=True)
    upper = lax.axis_index("x") == 1
    w_att, norms, arrived_tokens = gather(
        jnp.concatenate([w_query, w_key, w_value, w_out.T], axis=1),
        tile,
        tokens,
        tensor_size - 1,
    )
    factor = weighted * float(windows_here * lax.axis_size("dp")) / norms[4, 0]

    windows = range(windows_here)
    factors = [factor[w].reshape(1, 1) for w in windows]

    token_blocks = [tokens] + [arrived_tokens[other] for other in range(tensor_size - 1)]
    normed_rows, queries, own_kv = project(token_blocks, norms, w_att, cosine, sine)
    (
        attended,
        wide_attended,
        logs,
        kept_all,
        sent_all,
        slots_all,
        cots,
        first_middle,
        first_normed,
        first_others,
    ) = attend(queries, own_kv, w_att, cotangent, tokens, norms, tensor_size - 1)
    last_ffn = lax.all_gather(hold(last_ffn, kept_all), shards, axis=0, tiled=True)
    others = range(tensor_size - 1)
    cot_blocks = [
        [(cotangent, (w,))] + [(cots, (other, w)) for other in others] for w in windows
    ]
    middles = [first_middle]

    begun = []
    blocks = [first_normed] + [first_others[other] for other in others]
    for w in windows:
        chain = None
        if w + 1 < windows_here:
            chain = ((kept_all, (w,)), sent_all[w], (tokens, (w + 1,)), norms)
        begun.append(
            feed_first(blocks, cot_blocks[w], factors[w], first_ffn, tensor_size - 1, chain)
        )
        if chain is not None:
            middle, normed_mid, arrived = begun[-1][4:]
            middles.append(middle)
            blocks = [normed_mid] + [arrived[other] for other in others]

    def reduce_ffn(partial):
        partial = partial.reshape(-1, partial.shape[-1])
        mine = lax.psum_scatter(partial, ("dp", "core"), scatter_dimension=0, tiled=True)
        count = mine.shape[0] // 2
        kept = jnp.where(upper, mine[count:], mine[:count])
        sent = jnp.where(upper, mine[:count], mine[count:])
        return kept, sent

    boths = [one[0] for one in begun]
    g_first_part = feed_weights(boths, [one[1] for one in begun], 0, ())[0]
    first_kept, first_sent = reduce_ffn(g_first_part)
    fed = []
    for w in windows:
        both, wide, *totals = hold(begun[w][:4], fed[-1] if fed else g_first_part)
        fed.append(feed_last(both, wide, totals, last_ffn))
    grad_middles, second_sums = [], []

    def through_second_norm(w, kept, arrived):
        grad_middle, low, sums = second_norm_back(
            factors[w], kept, arrived, middles[w], (cotangent, (w,)), norms
        )
        grad_middles.append(grad_middle)
        second_sums.append(sums)
        return low

    lows = []
    for w in windows[:-1]:
        kept, arrived = scatter_pair(fed[w][3], fed[w][4], "tensor")
        lows.append(through_second_norm(w, hold(kept, fed[w + 1]), arrived))
    masks = [other + 1 for other in others]
    g_ffn_part, arrived, *arrived_lows = feed_weights(
        boths,
        [one[0] for one in hold(fed, grad_middles)],
        1,
        [(fed[-1][4], [tensor_size // 2])] + [(low, masks) for low in lows],
    )
    last_kept, last_sent = reduce_ffn(g_ffn_part)
    kept, arrived = later_pair(fed[-1][3], arrived[0], "tensor")
    last_low = through_second_norm(windows[-1], hold(kept, g_ffn_part), arrived)
    grad_mid_blocks = [
        [low] + [arrived[other] for other in others] for low, arrived in zip(lows, arrived_lows)
    ] + [[last_low]]

    grad_q, grad_k, grad_v, grad_mid_rows, *arrived_results, first_arrived = attend_back(
        hold(queries, g_ffn_part),
        wide_attended,
        logs,
        slots_all,
        grad_mid_blocks,
        w_att,
        (cosine, sine),
        [fed[w][2] for w in windows],
        first_sent,
    )
    parts = [
        (middles[w], *later_pair(fed[w][1], arrived_results[w], "tensor")) for w in windows
    ]

    g_att, vectors, input_grad, output, last_arrived = finish(
        (grad_q, grad_k, grad_v),
        normed_rows,
        grad_mid_rows,
        attended,
        w_att,
        tokens,
        last_sent,
        norms,
        second_sums,
        grad_middles,
        parts,
        tensor_size - 1,
    )
    g_first = first_kept.astype(F32) + first_arrived.astype(F32)
    g_last = last_kept.astype(F32) + last_arrived.astype(F32)
    norm_sums = vectors[:4, : norm1_gain.shape[0]]
    ffn_grads = [
        jnp.concatenate(
            [g_first[:, at * part : (at + 1) * part], g_last[:, at * part : (at + 1) * part]],
            axis=1,
        )
        for at in range(3)
    ]

    return (
        output,
        input_grad,
        norm_sums[0],
        norm_sums[1],
        g_att[:, :head_cols],
        g_att[:, head_cols : 2 * head_cols],
        g_att[:, 2 * head_cols : 3 * head_cols],
        g_att[:, 3 * head_cols :].T,
        norm_sums[2],
        norm_sums[3],
        ffn_grads[0],
        ffn_grads[1],
        ffn_grads[2].T,
    )


def solution(mesh):
    depth, seq, tensor = mesh.devices.shape
    finer = jax.sharding.Mesh(
        mesh.devices.reshape(depth, seq // 2, 2, tensor), ("dp", "x", "core", "tensor")
    )
    rows = P("dp", ("x", "core", "tensor"), None)
    vector = P(("dp", "x", "core", "tensor"))
    tall = P(("dp", "x", "core"), "tensor")
    flat = P("tensor", ("dp", "x", "core"))
    return jax.shard_map(
        local,
        mesh=finer,
        in_specs=(
            rows, rows, P("dp"), P("dp"), P(), vector, vector,
            tall, tall, tall, flat, vector, vector, tall, tall, flat,
        ),
        out_specs=(
            rows, rows, vector, vector, tall, tall, tall, flat,
            vector, vector, tall, tall, flat,
        ),
        check_vma=False,
    )
```

```python
import functools
import math

import jax
import jax.numpy as jnp
from jax import lax
from jax.experimental import pallas as pl
from jax.experimental.pallas import tpu as pltpu
from jax.sharding import PartitionSpec as P

HEAD_DIM = 64
EPSILON = 1e-05
ROPE_BASE = 10000.0
PAIR = 2 * HEAD_DIM
LOG2E = math.log2(math.e)
BF16 = jnp.bfloat16
F32 = jnp.float32
VMEM_BYTES = 56 * 1024 * 1024
MESH = pl.DeviceIdType.MESH


def angles(positions, head_dim):
    half_dim = head_dim // 2
    inverse = jnp.exp(
        -(math.log(ROPE_BASE) * 2.0 / head_dim) * jnp.arange(half_dim, dtype=F32)
    )
    phase_angle = positions[:, None] * inverse[None, :]
    return (jnp.cos(phase_angle), jnp.sin(phase_angle))


def dot_nn(left, right):
    return lax.dot_general(left, right, (((1,), (0,)), ((), ())), preferred_element_type=F32)


def dot_nt(left, right):
    return lax.dot_general(left, right, (((1,), (1,)), ((), ())), preferred_element_type=F32)


def dot_tn(left, right):
    return lax.dot_general(left, right, (((0,), (0,)), ((), ())), preferred_element_type=F32)


def swap(array, axis, bit):
    size = lax.axis_size(axis)
    return lax.ppermute(array, axis, [(i, i ^ bit) for i in range(size)])


def spread(array, axis):
    blocks = [array]
    bit = 1
    while bit < lax.axis_size(axis):
        blocks = blocks + [swap(block, axis, bit) for block in blocks]
        bit *= 2
    return blocks


def scatter_pair(kept, sent, axis):
    return later_pair(kept, swap(sent, axis, lax.axis_size(axis) // 2), axis)


def later_pair(kept, arrived, axis):
    bit = lax.axis_size(axis) // 2
    while bit > 1:
        partial = kept + arrived.astype(F32)
        bit //= 2
        rows = partial.shape[0] // 2
        kept, arrived = partial[:rows], swap(partial[rows:].astype(BF16), axis, bit)
    return kept, arrived


def seq_size():
    return lax.axis_size("x") * lax.axis_size("core")


def seq_index():
    return lax.axis_index("x") * lax.axis_size("core") + lax.axis_index("core")


def hold(values, *others):
    return lax.optimization_barrier((values, others))[0]


def run(kernel, name, out_shape, flops, args, collective_id=None, **options):
    trading = {} if collective_id is None else dict(collective_id=collective_id, has_side_effects=True)
    moved = sum(math.prod(array.shape) * array.dtype.itemsize for array in args)
    outs = out_shape if isinstance(out_shape, list) else [out_shape]
    moved += sum(math.prod(array.shape) * array.dtype.itemsize for array in outs)
    return pl.pallas_call(
        kernel,
        out_shape=out_shape,
        compiler_params=pltpu.CompilerParams(vmem_limit_bytes=VMEM_BYTES, **trading),
        cost_estimate=pl.CostEstimate(
            flops=int(flops), bytes_accessed=int(moved), transcendentals=0
        ),
        name=name,
        **options,
    )(*args)


def shaped(shape, dtype):
    return jax.ShapeDtypeStruct(shape, dtype)


SCALAR = pl.BlockSpec(memory_space=pltpu.SMEM)


def plane(operand, block=None, index=None):
    array, at = operand if isinstance(operand, tuple) else (operand, ())
    shape = array.shape[len(at) :] if block is None else block
    place = (lambda *i: (0,) * len(shape)) if index is None else index
    return array, pl.BlockSpec((None,) * len(at) + tuple(shape), lambda *i: at + place(*i))


def normalise(stream):
    row_mean = jnp.mean(stream, axis=-1, keepdims=True)
    centred = stream - row_mean
    variance = jnp.mean(centred * centred, axis=-1, keepdims=True)
    inv_std = lax.rsqrt(variance + EPSILON)
    return centred * inv_std, inv_std


def norm_back(grad_normed, normed, inv_std, norm_gain):
    scaled_grad = grad_normed * norm_gain
    return inv_std * (
        scaled_grad
        - jnp.mean(scaled_grad, axis=-1, keepdims=True)
        - normed * jnp.mean(scaled_grad * normed, axis=-1, keepdims=True)
    )


def first_head(shape):
    return lax.broadcasted_iota(jnp.int32, shape, 1) % PAIR < HEAD_DIM


def swap_halves(values):
    half = HEAD_DIM // 2
    lane = lax.broadcasted_iota(jnp.int32, values.shape, 1)
    ahead = pltpu.roll(values, PAIR - half, 1)
    behind = pltpu.roll(values, half, 1)
    return jnp.where(lane % HEAD_DIM < half, ahead, behind)


def project_kernel(blocks, norms_ref, w_ref, cos_ref, sin_ref, *refs):
    x_refs = refs[:blocks]
    normed_ref, q_ref, kv_ref = refs[blocks:]
    cols = q_ref.shape[2]
    gain, bias = norms_ref[0:1, :], norms_ref[1:2, :]
    at_row = 0
    for x_ref in x_refs:
        rows = slice(at_row, at_row + x_ref.shape[1])
        at_row += x_ref.shape[1]
        normed = (normalise(x_ref[0].astype(F32))[0] * gain + bias).astype(BF16)
        normed_ref[0, rows, :] = normed
        cosine, sine = cos_ref[rows, :], sin_ref[rows, :]
        query = dot_nn(normed, w_ref[:, :cols])
        key = dot_nn(normed, w_ref[:, cols : 2 * cols])
        value = dot_nn(normed, w_ref[:, 2 * cols : 3 * cols]).astype(BF16)
        for at in range(0, cols, PAIR):
            part, pair = slice(at, at + PAIR), at // PAIR
            one = query[:, part]
            q_ref[0, rows, part] = (one * cosine + swap_halves(one) * sine).astype(BF16)
            one = key[:, part]
            kv_ref[0, pair, 0, rows, :] = (one * cosine + swap_halves(one) * sine).astype(BF16)
            kv_ref[0, pair, 1, rows, :] = value[:, part]


def project(x_blocks, norms, w_att, cosine, sine):
    windows = x_blocks[0].shape[0]
    width, cols = w_att.shape[0], w_att.shape[1] // 4
    rows = sum(block.shape[1] for block in x_blocks)
    pieces = (cols // PAIR, 2, rows, PAIR)
    args = [norms, w_att, cosine, sine, *x_blocks]
    return run(
        functools.partial(project_kernel, len(x_blocks)),
        "project",
        [
            shaped((windows, rows, width), BF16),
            shaped((windows, rows, cols), BF16),
            shaped((windows,) + pieces, BF16),
        ],
        6 * windows * rows * width * cols,
        args,
        grid=(windows,),
        in_specs=[pl.BlockSpec(array.shape, lambda i: (0, 0)) for array in args[:4]]
        + [pl.BlockSpec((1,) + block.shape[1:], lambda i: (i, 0, 0)) for block in x_blocks],
        out_specs=[
            pl.BlockSpec((1, rows, width), lambda i: (i, 0, 0)),
            pl.BlockSpec((1, rows, cols), lambda i: (i, 0, 0)),
            pl.BlockSpec((1,) + pieces, lambda i: (i, 0, 0, 0, 0)),
        ],
    )


def flipped(index, mask):
    bit = 1
    while bit <= mask:
        if mask & bit:
            index = index + bit - 2 * bit * ((index // bit) % 2)
        bit *= 2
    return index


def greet(peers):
    barrier = pltpu.get_barrier_semaphore()
    for peer in peers:
        pl.semaphore_signal(barrier, inc=1, device_id=peer, device_id_type=MESH)
    pl.semaphore_wait(barrier, len(peers))


def send(source, target, send_sem, recv_sem, peer):
    return pltpu.make_async_remote_copy(
        src_ref=source,
        dst_ref=target,
        send_sem=send_sem,
        recv_sem=recv_sem,
        device_id=peer,
        device_id_type=MESH,
    )


def half_chip_peers():
    depth = lax.axis_index("dp")
    size = lax.axis_size("dp")
    return {
        "far": {"x": 1 - lax.axis_index("x")},
        "up": {"dp": (depth + 1) % size},
        "down": {"dp": (depth + size - 1) % size},
        "core": {"core": 1 - lax.axis_index("core")},
    }


class Route:
    PARTS = ((0, 0), (3, 0), (1, 0), (2, 0), (0, 1), (3, 1), (1, 1), (2, 1))

    def __init__(self, whole, rows, send_sem, recv_sem, own):
        self.whole, self.rows, self.own = whole, rows, own
        self.send_sem, self.recv_sem = send_sem, recv_sem
        self.seq, self.depth = seq_index(), lax.axis_index("dp")
        self.peers = half_chip_peers()

    def part(self, place):
        turn, other = place
        seq = flipped(self.seq, 2) if other else self.seq
        at = (((self.depth + turn) % lax.axis_size("dp")) * seq_size() + seq) * self.rows
        return self.whole.at[pl.ds(pl.multiple_of(at, self.rows), self.rows), :]

    def message(self, number):
        if number >= 7:
            place, peer = self.PARTS[number - 7], "core"
        else:
            place, peer = (
                ((0, 0), "up"),
                ((0, 0), "down"),
                ((3, 0), "up"),
                ((0, 0), "far"),
                ((3, 0), "far"),
                ((1, 0), "far"),
                ((2, 0), "far"),
            )[number]
        target = self.part(place)
        return send(
            self.own if place == (0, 0) else target,
            target,
            self.send_sem.at[number],
            self.recv_sem.at[number],
            self.peers[peer],
        )

    def start(self, *numbers):
        for number in numbers:
            self.message(number).start()

    def arrived(self, *numbers):
        for number in numbers:
            self.message(number).wait_recv()

    def sent(self, *numbers):
        for number in numbers:
            self.message(number).wait_send()


MESSAGES = 15


def gather_kernel(trades, att_ref, tile_ref, tokens_ref, *refs):
    att_all, norms_ref, tokens_all = refs[:3]
    tiles, pair_of_tiles = refs[3:5]
    att_send, att_recv, tile_send, tile_recv = refs[5:9]
    own_sem, tokens_send, tokens_recv, pair_send, pair_recv = refs[9:]
    tensor = lax.axis_index("tensor")
    others = [{"tensor": flipped(tensor, other + 1)} for other in range(trades)]
    att = Route(att_all, att_ref.shape[0], att_send, att_recv, att_ref)
    tile_rows = tile_ref.shape[0]
    small = Route(tiles, pair_of_tiles.shape[0], tile_send, tile_recv, pair_of_tiles)

    def tokens_trade(other):
        return send(
            tokens_ref,
            tokens_all.at[other],
            tokens_send.at[other],
            tokens_recv.at[other],
            others[other],
        )

    own_rows = pl.ds(pl.multiple_of(tensor * tile_rows, tile_rows), tile_rows)

    def pair_trade(other):
        return send(
            tile_ref,
            pair_of_tiles.at[own_rows, :],
            pair_send.at[other],
            pair_recv.at[other],
            others[other],
        )

    own_copies = [
        pltpu.make_async_copy(att_ref, att.part((0, 0)), own_sem.at[0]),
        pltpu.make_async_copy(tile_ref, pair_of_tiles.at[own_rows, :], own_sem.at[1]),
        pltpu.make_async_copy(pair_of_tiles, small.part((0, 0)), own_sem.at[2]),
    ]

    greet(list(att.peers.values()) + others)
    for other in range(trades):
        pair_trade(other).start()
    own_copies[1].start()
    att.start(0, 1, 3, 7)
    own_copies[1].wait()
    for other in range(trades):
        pair_trade(other).wait_recv()
    small.start(0, 1, 3, 7)
    own_copies[0].start()
    own_copies[2].start()
    for other in range(trades):
        tokens_trade(other).start()
    for route in (small, att):
        route.arrived(0)
        route.start(2, 4, 8)
    for route in (small, att):
        route.arrived(3)
        route.start(11)
    for route in (small, att):
        route.arrived(1)
        route.start(5, 9)
    for route in (small, att):
        route.arrived(2)
        route.start(6, 10)
    for route in (small, att):
        route.arrived(4)
        route.start(12)
        route.arrived(5)
        route.start(13)
        route.arrived(6)
        route.start(14)
    for route in (small, att):
        route.arrived(*range(7, MESSAGES))
    own_copies[2].wait()
    shard = norms_ref.shape[1] // (tiles.shape[0] // tile_rows)
    total = None
    for device in range(tiles.shape[0] // tile_rows):
        tile = tiles[device * tile_rows : (device + 1) * tile_rows, :]
        norms_ref[:, device * shard : (device + 1) * shard] = tile[:, :shard]
    for depth in range(lax.axis_size("dp")):
        at = depth * (tiles.shape[0] // lax.axis_size("dp"))
        one = tiles[at + 4 : at + 5, :]
        total = one if total is None else total + one
    norms_ref[4:5, : total.shape[1]] = total
    for route in (att, small):
        route.sent(*range(MESSAGES))
    own_copies[0].wait()
    for other in range(trades):
        pair_trade(other).wait_send()
        tokens_trade(other).wait_recv()
        tokens_trade(other).wait_send()


def gather(att, tile, tokens, trades):
    count = lax.axis_size("dp") * seq_size()
    rows = att.shape[0]
    group = tile.shape[0] * (trades + 1)
    anywhere = pl.BlockSpec(memory_space=pl.ANY)
    vmem = pl.BlockSpec(memory_space=pltpu.VMEM)
    dma = pltpu.SemaphoreType.DMA
    return run(
        functools.partial(gather_kernel, trades),
        "gather",
        [
            shaped((count * rows, att.shape[1]), BF16),
            shaped((tile.shape[0], count * rows), F32),
            shaped((trades,) + tokens.shape, BF16),
        ],
        0,
        [att, tile, tokens],
        collective_id=1,
        in_specs=[vmem, vmem, anywhere],
        out_specs=[anywhere, vmem, anywhere],
        scratch_shapes=[pltpu.VMEM((count * group, 128), F32), pltpu.VMEM((group, 128), F32)]
        + [dma((MESSAGES,))] * 4
        + [dma((3,)), dma((trades,)), dma((trades,)), dma((trades,)), dma((trades,))],
    )


def attend_kernel(windows, pairs, trades, exp_scale, *refs):
    stages = (trades + 1).bit_length() - 1
    q_ref, w_ref, kv_ref, cot_ref, x_ref, norms_ref = refs[:6]
    low_ref, wide_ref, log_ref, kept_ref, sent_ref, slots_ref, cots_ref = refs[6:13]
    middle_ref, normed_ref, others_ref = refs[13:16]
    slots, acc_all, top_all, total_all, mixed_rows = refs[16:21]
    own_sem, send_sem, recv_sem, save_sem, cot_send, cot_recv = refs[21:27]
    early_kept, early_normed, early_sem, early_recv, normed_sem, normed_recv = refs[27:33]
    early_sent, early_arrived = refs[33 : 33 + stages], refs[33 + stages :]
    step = pl.program_id(0)
    near_steps = windows * pairs
    steps = 2 * near_steps
    turn = step % (2 * pairs)
    is_far = turn >= pairs
    number = step // (2 * pairs) * pairs + turn % pairs
    tensor = lax.axis_index("tensor")
    core_peer = {"core": 1 - lax.axis_index("core")}
    far_peer = {"x": 1 - lax.axis_index("x")}
    cot_peers = [{"tensor": flipped(tensor, other + 1)} for other in range(trades)]

    def piece(number):
        return kv_ref.at[number // pairs, number % pairs]

    def own_copy(number):
        return pltpu.make_async_copy(piece(number), slots.at[number, 0], own_sem.at[number])

    def trade(number, slot):
        peer = far_peer if slot == 2 else core_peer
        source = slots.at[number, 2] if slot == 3 else piece(number)
        return send(
            source,
            slots.at[number, slot],
            send_sem.at[number, slot - 1],
            recv_sem.at[number, slot - 1],
            peer,
        )

    def cot_trade(other):
        return send(
            cot_ref, cots_ref.at[other], cot_send.at[other], cot_recv.at[other], cot_peers[other]
        )

    def early_trade(stage):
        return send(
            early_sent[stage],
            early_arrived[stage],
            early_sem.at[stage],
            early_recv.at[stage],
            {"tensor": flipped(tensor, (trades + 1) >> (stage + 1))},
        )

    def normed_trade(other):
        return send(
            early_normed,
            others_ref.at[other],
            normed_sem.at[other],
            normed_recv.at[other],
            cot_peers[other],
        )

    def save(number, slot):
        return pltpu.make_async_copy(
            slots.at[number, slot], slots_ref.at[number, slot], save_sem.at[number, slot]
        )

    @pl.when(step == 0)
    def _():
        greet([core_peer, far_peer] + cot_peers)

        @pl.loop(0, near_steps)
        def _(number):
            own_copy(number).start()
            trade(number, 1).start()
            trade(number, 2).start()

        for other in range(trades):
            cot_trade(other).start()

    @pl.when(step == 2 * pairs)
    def _():
        early_trade(0).start()

    @pl.when(step == min(3 * pairs + 1, steps - 2))
    def _():
        kept = early_kept[...]
        for stage in range(stages):
            early_trade(stage).wait_recv()
            kept = kept + early_arrived[stage][...].astype(F32)
            if stage + 1 < stages:
                half = kept.shape[0] // 2
                early_sent[stage + 1][...] = kept[half:].astype(BF16)
                early_trade(stage + 1).start()
                kept = kept[:half]
        middle = x_ref[...].astype(F32) + kept
        middle_ref[...] = middle
        normed = (normalise(middle)[0] * norms_ref[2:3, :] + norms_ref[3:4, :]).astype(BF16)
        normed_ref[...] = normed
        early_normed[...] = normed

    @pl.when(step == min(3 * pairs + 2, steps - 1))
    def _():
        for other in range(trades):
            normed_trade(other).start()

    relayed = step // (2 * pairs) * pairs + turn - (pairs - 1)

    @pl.when(jnp.logical_and(turn >= pairs - 1, turn < 2 * pairs - 1))
    def _():
        trade(relayed, 2).wait_recv()
        trade(relayed, 3).start()
        save(relayed, 2).start()

    @pl.when(jnp.logical_not(is_far))
    def _():
        own_copy(number).wait()
        trade(number, 1).wait_recv()
        save(number, 0).start()
        save(number, 1).start()
        acc_all[number] = jnp.zeros(acc_all.shape[1:], F32)
        total_all[number] = jnp.zeros(acc_all.shape[1:], F32)
        top_all[number] = jnp.full(acc_all.shape[1:], -1e30, F32)

    @pl.when(is_far)
    def _():
        trade(number, 3).wait_recv()
        save(number, 3).start()

    query = q_ref[0]
    is_first = first_head(query.shape)
    base = jnp.where(is_far, 2, 0)
    carried_top = top_all[number]
    outs, tops = [], []
    for head in range(2):
        mine = is_first if head == 0 else jnp.logical_not(is_first)
        own_query = jnp.where(mine, query, jnp.zeros_like(query))
        scores = [dot_nt(own_query, slots[number, base + slot, 0]) for slot in range(2)]
        at = head * HEAD_DIM
        top = carried_top[:, at : at + 1]
        for one in scores:
            top = jnp.maximum(top, one.max(axis=1, keepdims=True))
        shift = top * exp_scale
        mixed = None
        for slot, one in enumerate(scores):
            weight = jnp.exp2(one * exp_scale - shift).astype(BF16)
            value = slots[number, base + slot, 1]
            lane_first = first_head(value.shape)
            lane_mine = lane_first if head == 0 else jnp.logical_not(lane_first)
            term = dot_nn(weight, jnp.where(lane_mine, value, jnp.ones_like(value)))
            mixed = term if mixed is None else mixed + term
        outs.append(mixed)
        tops.append(jnp.broadcast_to(top, mixed.shape))
    top = jnp.where(is_first, tops[0], tops[1])
    fade = jnp.exp2((carried_top - top) * exp_scale)
    acc = jnp.where(is_first, outs[0], outs[1]) + acc_all[number] * fade
    total = pltpu.roll(jnp.where(is_first, outs[1], outs[0]), HEAD_DIM, 1) + total_all[number] * fade

    @pl.when(jnp.logical_not(is_far))
    def _():
        acc_all[number] = acc
        top_all[number] = top
        total_all[number] = total

    @pl.when(is_far)
    def _():
        attended = acc / total
        low = attended.astype(BF16)
        low_ref[0] = low
        wide_ref[0] = attended
        log_ref[0] = (top * exp_scale + jnp.log2(total)).T
        term = dot_nt(low, w_ref[...])
        pair = number % pairs

        @pl.when(pair == 0)
        def _():
            mixed_rows[...] = term

        @pl.when(pair > 0)
        def _():
            mixed_rows[...] += term

        @pl.when(jnp.logical_and(pair == pairs - 1, number >= pairs))
        def _():
            half = kept_ref.shape[1]
            kept_ref[0] = mixed_rows[:half]
            sent_ref[0] = mixed_rows[half:].astype(BF16)

        @pl.when(number == pairs - 1)
        def _():
            half = kept_ref.shape[1]
            early_kept[...] = mixed_rows[:half]
            early_sent[0][...] = mixed_rows[half:].astype(BF16)

    @pl.when(step == steps - 1)
    def _():
        @pl.loop(0, near_steps)
        def _(number):
            for slot in range(1, 4):
                trade(number, slot).wait_send()
            for slot in range(4):
                save(number, slot).wait()

        for stage in range(stages):
            early_trade(stage).wait_send()
        for other in range(trades):
            cot_trade(other).wait_send()
            cot_trade(other).wait_recv()
            normed_trade(other).wait_send()
            normed_trade(other).wait_recv()


def attend(queries, own_kv, w_att, cotangent, tokens, norms, trades):
    windows, rows, cols = queries.shape
    width = w_att.shape[0]
    pairs = cols // PAIR
    near = windows * pairs
    out_at = 3 * pairs

    def far(i):
        turn = i % (2 * pairs)
        done = i // (2 * pairs) * pairs
        return jnp.where(turn >= pairs, done + turn - pairs, jnp.maximum(done - 1, 0))

    anywhere = pl.BlockSpec(memory_space=pl.ANY)
    wide = pl.BlockSpec((1, rows, PAIR), lambda i: (far(i) // pairs, 0, far(i) % pairs))
    half = pl.BlockSpec(
        (1, rows // 2, width), lambda i: (jnp.maximum(far(i) // pairs, 1) - 1, 0, 0)
    )
    own_rows = tokens.shape[1]
    own = pl.BlockSpec((own_rows, width), lambda i: (0, 0))
    stages = [rows >> (stage + 1) for stage in range((trades + 1).bit_length() - 1)]
    state = pltpu.VMEM((near, rows, PAIR), F32)
    dma = pltpu.SemaphoreType.DMA
    return run(
        functools.partial(attend_kernel, windows, pairs, trades, LOG2E / math.sqrt(HEAD_DIM)),
        "attend",
        [
            shaped((windows, rows, cols), BF16),
            shaped((windows, rows, cols), F32),
            shaped((windows, cols, rows), F32),
            shaped((windows - 1, rows // 2, width), F32),
            shaped((windows - 1, rows // 2, width), BF16),
            shaped((near, 4, 2, rows, PAIR), BF16),
            shaped((trades,) + cotangent.shape, BF16),
            shaped((own_rows, width), F32),
            shaped((own_rows, width), BF16),
            shaped((trades, own_rows, width), BF16),
        ],
        64 * windows * rows * rows * cols,
        [queries, w_att, own_kv, cotangent, tokens, norms],
        collective_id=0,
        grid=(2 * near,),
        in_specs=[
            pl.BlockSpec((1, rows, PAIR), lambda i: (i // (2 * pairs), 0, i % pairs)),
            pl.BlockSpec((width, PAIR), lambda i: (0, out_at + far(i) % pairs)),
            anywhere,
            anywhere,
            pl.BlockSpec((None, own_rows, width), lambda i: (0, 0, 0)),
            pl.BlockSpec(norms.shape, lambda i: (0, 0)),
        ],
        out_specs=[
            wide,
            wide,
            pl.BlockSpec((1, PAIR, rows), lambda i: (far(i) // pairs, far(i) % pairs, 0)),
            half,
            half,
            anywhere,
            anywhere,
            own,
            own,
            anywhere,
        ],
        scratch_shapes=[
            pltpu.VMEM((near, 4, 2, rows, PAIR), BF16),
            state,
            state,
            state,
            pltpu.VMEM((rows, width), F32),
            dma((near,)),
            dma((near, 3)),
            dma((near, 3)),
            dma((near, 4)),
            dma((trades,)),
            dma((trades,)),
            pltpu.VMEM((rows // 2, width), F32),
            pltpu.VMEM((own_rows, width), BF16),
            dma((len(stages),)),
            dma((len(stages),)),
            dma((trades,)),
            dma((trades,)),
        ]
        + [pltpu.VMEM((count, width), BF16) for count in stages] * 2,
    )


def attend_back_kernel(windows, pairs, blocks, exp_scale, score_scale, *refs):
    q_ref, wide_ref, log_ref, slots_ref, w_ref, cos_ref, sin_ref, last_ref = refs[:8]
    trades = blocks - 1
    known = (windows - 1) * blocks + 1
    grad_refs = list(refs[8 : 8 + known])
    refs = refs[8 + known :]
    sent_refs, refs = refs[:windows], refs[windows:]
    gq_ref, gk_ref, gv_ref, rows_ref = refs[:4]
    arrived_refs, refs = refs[4 : 4 + windows], refs[4 + windows :]
    dq_all, do_all, far_kept, far_sent, far_core, far_x, near_kept, near_sent, near_core = refs[:9]
    send_sem, recv_sem, result_send, result_recv, last_send, last_recv, last_others = refs[9:]
    grad_refs += [last_others.at[other] for other in range(trades)]
    step = pl.program_id(0)
    count = windows * pairs
    tensor = lax.axis_index("tensor")
    core_peer = {"core": 1 - lax.axis_index("core")}
    far_peer = {"x": 1 - lax.axis_index("x")}
    result_peer = {"tensor": flipped(tensor, lax.axis_size("tensor") // 2)}

    def trade(kind, number):
        source, target, peer = (
            (far_sent, far_core, core_peer),
            (far_kept, far_x, far_peer),
            (near_sent, near_core, core_peer),
        )[kind]
        return send(
            source.at[number],
            target.at[number],
            send_sem.at[kind, number],
            recv_sem.at[kind, number],
            peer,
        )

    def result_trade(w):
        return send(
            sent_refs[w], arrived_refs[w], result_send.at[w], result_recv.at[w], result_peer
        )

    others = [{"tensor": flipped(tensor, other + 1)} for other in range(trades)]

    def last_trade(other):
        return send(
            last_ref, last_others.at[other], last_send.at[other], last_recv.at[other], others[other]
        )

    @pl.when(step == 0)
    def _():
        greet([core_peer, far_peer] + others)
        for other in range(trades):
            last_trade(other).start()
        for w in range(windows):
            result_trade(w).start()

    def at_step(first, body):
        number = step - first

        @pl.when(jnp.logical_and(number >= 0, number < count))
        def _():
            body(number)

    def send_far(number):
        trade(0, number).start()

    def add_far(number):
        trade(0, number).wait_recv()
        far_kept[number] = (
            far_kept[number].astype(F32) + far_core[number].astype(F32)
        ).astype(BF16)

    def send_x(number):
        trade(1, number).start()

    def send_near(number):
        trade(2, number).start()

    def finish(number):
        trade(2, number).wait_recv()
        trade(1, number).wait_recv()
        total = (
            near_kept[number].astype(F32)
            + near_core[number].astype(F32)
            + far_x[number].astype(F32)
        )
        key = total[0]
        gk_ref[0] = (key * cos_ref[...] - swap_halves(key) * sin_ref[...]).astype(BF16)
        gv_ref[0] = total[1].astype(BF16)

    at_step(1, send_far)
    at_step(3, send_x)
    at_step(count + 1, send_near)
    at_step(2, add_far)
    at_step(count + 2, finish)

    for w in range(windows):

        @pl.when(step == w * pairs)
        def _(w=w):
            if w == windows - 1:
                for other in range(trades):
                    last_trade(other).wait_recv()
            at_row = 0
            for grad_ref in grad_refs[w * blocks : (w + 1) * blocks]:
                rows_ref[0, at_row : at_row + grad_ref.shape[0], :] = grad_ref[...]
                at_row += grad_ref.shape[0]

    def gradients(number, grad_out, kept, sent):
        query = q_ref[0]
        is_first = first_head(query.shape)
        overlap = (grad_out.astype(F32) * wide_ref[0]).T
        logs = log_ref[0]
        zero = jnp.zeros_like(query)
        own_q, own_do, row_log, row_sum = [], [], [], []
        for head in range(2):
            mine = is_first if head == 0 else jnp.logical_not(is_first)
            own_q.append(jnp.where(mine, query, zero))
            own_do.append(jnp.where(mine, grad_out, zero))
            at = head * HEAD_DIM
            row_log.append(logs[at : at + 1, :])
            row_sum.append(jnp.sum(overlap[at : at + HEAD_DIM, :], axis=0, keepdims=True))
        dq_parts = [None, None]
        for slot, target in enumerate((kept, sent)):
            key, value = slots_ref[0, slot, 0], slots_ref[0, slot, 1]
            key_turned = key.T
            grad_key, grad_value = None, None
            for head in range(2):
                scores = dot_nt(key, own_q[head])
                probs = jnp.exp2(scores * exp_scale - row_log[head])
                grad_probs = dot_nt(value, own_do[head])
                grad_scores = (probs * (grad_probs - row_sum[head])).astype(BF16)
                term_v = dot_nn(probs.astype(BF16), own_do[head])
                term_k = dot_nn(grad_scores, own_q[head])
                at = head * HEAD_DIM
                term_q = dot_nn(key_turned[at : at + HEAD_DIM, :], grad_scores)
                grad_value = term_v if grad_value is None else grad_value + term_v
                grad_key = term_k if grad_key is None else grad_key + term_k
                dq_parts[head] = term_q if dq_parts[head] is None else dq_parts[head] + term_q
            target[number, 0] = (grad_key * score_scale).astype(BF16)
            target[number, 1] = grad_value.astype(BF16)
        return jnp.concatenate(dq_parts, axis=0).T * score_scale

    @pl.when(step < count)
    def _():
        grad_out = dot_nn(rows_ref[0], w_ref[...]).astype(BF16)
        do_all[step] = grad_out
        dq_all[step] = gradients(step, grad_out, far_kept, far_sent)

    @pl.when(jnp.logical_and(step >= count, step < 2 * count))
    def _():
        number = step - count
        grad_query = dq_all[number] + gradients(number, do_all[number], near_kept, near_sent)
        gq_ref[0] = (grad_query * cos_ref[...] - swap_halves(grad_query) * sin_ref[...]).astype(
            BF16
        )

    @pl.when(step == pl.num_programs(0) - 1)
    def _():
        @pl.loop(0, count)
        def _(number):
            for kind in range(3):
                trade(kind, number).wait_send()

        for other in range(trades):
            last_trade(other).wait_send()
        for w in range(windows):
            result_trade(w).wait_send()
            result_trade(w).wait_recv()


def attend_back(queries, wide, logs, slots_all, grad_blocks, w_att, tables, sent):
    windows, rows, cols = queries.shape
    width = w_att.shape[0]
    pairs = cols // PAIR
    count = windows * pairs
    out_at = 3 * pairs
    score_scale = 1.0 / math.sqrt(HEAD_DIM)
    blocks = lax.axis_size("tensor")
    grads = [block for one in grad_blocks for block in one]
    last = grads[-1]

    def spot(lag, last=None):
        def index(i):
            number = jnp.clip(i - lag, 0, count - 1)
            return (number // pairs, 0, number % pairs)

        return pl.BlockSpec((1, rows, PAIR), index)

    def both(i):
        return jnp.minimum(i, 2 * count - 1) % count

    dma = pltpu.SemaphoreType.DMA
    piece = pltpu.VMEM((count, 2, rows, PAIR), BF16)
    anywhere = pl.BlockSpec(memory_space=pl.ANY)
    return run(
        functools.partial(
            attend_back_kernel, windows, pairs, blocks, score_scale * LOG2E, score_scale
        ),
        "attend_back",
        [shaped((windows, rows, cols), BF16)] * 3
        + [shaped((windows, rows, width), BF16)]
        + [shaped(one.shape, BF16) for one in sent],
        160 * windows * rows * rows * cols,
        [queries, wide, logs, slots_all, w_att, *tables, last, *grads, *sent],
        collective_id=2,
        grid=(2 * count + 2,),
        in_specs=[
            pl.BlockSpec((1, rows, PAIR), lambda i: (both(i) // pairs, 0, both(i) % pairs)),
            pl.BlockSpec((1, rows, PAIR), lambda i: (both(i) // pairs, 0, both(i) % pairs)),
            pl.BlockSpec((1, PAIR, rows), lambda i: (both(i) // pairs, both(i) % pairs, 0)),
            pl.BlockSpec(
                (1, 2, 2, rows, PAIR),
                lambda i: (both(i), jnp.where(i < count, 1, 0), 0, 0, 0),
            ),
            pl.BlockSpec((width, PAIR), lambda i: (0, out_at + jnp.minimum(i, count - 1) % pairs)),
            pl.BlockSpec((rows, PAIR), lambda i: (0, 0)),
            pl.BlockSpec((rows, PAIR), lambda i: (0, 0)),
            anywhere,
        ]
        + [pl.BlockSpec(block.shape, lambda i: (0, 0)) for block in grads]
        + [anywhere] * windows,
        out_specs=[
            spot(count),
            spot(count + 2),
            spot(count + 2),
            pl.BlockSpec((1, rows, width), lambda i: (jnp.minimum(i // pairs, windows - 1), 0, 0)),
        ]
        + [anywhere] * windows,
        scratch_shapes=[pltpu.VMEM((count, rows, PAIR), F32), pltpu.VMEM((count, rows, PAIR), BF16)]
        + [piece] * 7
        + [dma((3, count)), dma((3, count)), dma((windows,)), dma((windows,))]
        + [dma((blocks - 1,)), dma((blocks - 1,)), pltpu.VMEM((blocks - 1,) + last.shape, BF16)],
    )


def middle_kernel(x_ref, kept_ref, arrived_ref, norms_ref, middle_ref, normed_ref):
    middle = x_ref[...].astype(F32) + (kept_ref[...] + arrived_ref[...].astype(F32))
    middle_ref[...] = middle
    normed_ref[...] = (
        normalise(middle)[0] * norms_ref[2:3, :] + norms_ref[3:4, :]
    ).astype(BF16)


def second_norm(x_rows, kept, arrived, norms):
    args, in_specs = zip(*[plane(one) for one in (x_rows, kept, arrived, norms)])
    rows, width = in_specs[1].block_shape[-2:]
    full = pl.BlockSpec((rows, width), lambda i: (0, 0))
    return run(
        middle_kernel,
        "second_norm",
        [shaped((rows, width), F32), shaped((rows, width), BF16)],
        20 * rows * width,
        args,
        grid=(1,),
        in_specs=list(in_specs),
        out_specs=[full, full],
    )


def feed_kernel(blocks, swaps, first, *refs):
    refs = list(refs)

    def take(count):
        taken = refs[:count]
        del refs[:count]
        return taken

    w_refs = take(3)
    if first:
        factor_ref = take(1)[0]
        x_refs, cot_refs = take(blocks), take(blocks)
        sources = take(len(swaps))
        both_ref, wide_ref, total_ref, grad_ref = take(4)
    else:
        both_ref, total_in, grad_in, _ = take(4)
        sources = take(len(swaps))
        wide_ref, kept_ref, sent_ref, grad_kept_ref, grad_sent_ref = take(5)
    trades = tensor_trades(sources, take(len(swaps)), swaps, *take(2 if swaps else 0))
    block = pl.program_id(0)

    def weights_of(ref):
        if len(ref.shape) == 2:
            return ref[...]
        depths, cores, halves = ref.shape[:3]
        return jnp.concatenate(
            [
                ref[depth, core, half]
                for depth in range(depths)
                for half in range(halves)
                for core in range(cores)
            ],
            axis=0,
        )

    gate_w, up_w, down_w = [weights_of(ref) for ref in w_refs]

    @pl.when(block == 0)
    def _():
        start_trades(trades, swaps)

    if first:
        for at in range(blocks):

            @pl.when(block == at)
            def _(at=at):
                both_ref[0] = x_refs[at][...]
                both_ref[1] = (cot_refs[at][...].astype(F32) * factor_ref[0, 0]).astype(BF16)

    x_rows = both_ref[0]
    gate = dot_nn(x_rows, gate_w)
    up = dot_nn(x_rows, up_w)
    grad_hidden = dot_nn(both_ref[1], down_w)
    sig = jax.nn.sigmoid(gate)
    swish = gate * sig
    hidden = (swish * up).astype(BF16)
    grad_gate = (grad_hidden * up * sig * (1.0 + gate * (1.0 - sig))).astype(BF16)
    grad_up = (grad_hidden * swish).astype(BF16)
    wide_ref[0] = grad_gate
    wide_ref[1] = grad_up
    wide_ref[2] = hidden
    grad_total = dot_nt(grad_gate, gate_w) + dot_nt(grad_up, up_w)
    total = dot_nt(hidden, down_w)
    if first:
        total_ref[...] = total
        grad_ref[...] = grad_total
    else:
        total = total + total_in[...]
        grad_total = grad_total + grad_in[...]
        rows = total.shape[0]
        for at in range(blocks):

            @pl.when(block == at)
            def _(at=at):
                start = (at % (blocks // 2)) * rows
                if at < blocks // 2:
                    kept_ref[start : start + rows] = total
                    grad_kept_ref[start : start + rows] = grad_total
                else:
                    sent_ref[start : start + rows] = total.astype(BF16)
                    grad_sent_ref[start : start + rows] = grad_total.astype(BF16)

    @pl.when(block == blocks - 1)
    def _():
        for trade in trades:
            trade.wait()


def tensor_trades(sources, targets, masks, send_sem=None, recv_sem=None):
    tensor = lax.axis_index("tensor")
    trades = []
    for source, target, kinds in zip(sources, targets, masks):
        for number, mask in enumerate(kinds):
            sems = (send_sem.at[len(trades)], recv_sem.at[len(trades)])
            peer = {"tensor": flipped(tensor, mask)}
            trades.append(send(source, target.at[number], *sems, peer))
    return trades


def start_trades(trades, masks):
    if trades:
        tensor = lax.axis_index("tensor")
        peers = sorted({mask for kinds in masks for mask in kinds})
        greet([{"tensor": flipped(tensor, mask)} for mask in peers])
        for trade in trades:
            trade.start()


def feed_specs(weights):
    lead = weights.shape[:-1]
    part_cols = weights.shape[-1] // 3
    zeros = (0,) * len(lead)
    return part_cols, [
        pl.BlockSpec(lead + (part_cols,), functools.partial(lambda at, i: zeros + (at,), k))
        for k in range(3)
    ]


def full(*shape):
    return pl.BlockSpec(shape, lambda i: (0,) * len(shape))


def feed_call(name, collective_id, blocks, rows, width, part_cols, out, args, swaps, **options):
    masks = [kinds for _, kinds in swaps]
    anywhere = pl.BlockSpec(memory_space=pl.ANY)
    total = sum(len(kinds) for kinds in masks)
    out_shape, out_specs = out
    return run(
        functools.partial(feed_kernel, blocks, masks, name == "feed_first"),
        name,
        out_shape + [shaped((len(kinds),) + array.shape, BF16) for array, kinds in swaps],
        12 * rows * width * part_cols,
        args + [array for array, _ in swaps],
        collective_id=collective_id if swaps else None,
        grid=(blocks,),
        in_specs=options.pop("in_specs") + [anywhere] * len(swaps),
        out_specs=out_specs + [anywhere] * len(swaps),
        scratch_shapes=[pltpu.SemaphoreType.DMA((total,))] * 2 if swaps else [],
        **options,
    )


def feed_first(x_blocks, cot_blocks, factor, weights, swaps=()):
    operands, specs = zip(*[plane(block) for block in (*x_blocks, *cot_blocks)])
    width = math.prod(weights.shape[:-1])
    blocks, own = len(x_blocks), specs[0].block_shape[-2]
    rows = blocks * own
    part_cols, w_specs = feed_specs(weights)
    row_block = pl.BlockSpec((own, width), lambda i: (i, 0))
    out_shape = [shaped((2, rows, width), BF16), shaped((3, rows, 2 * part_cols), BF16)]
    out_shape += [shaped((rows, width), F32)] * 2
    out_specs = [
        pl.BlockSpec((2, own, width), lambda i: (0, i, 0)),
        pl.BlockSpec((3, own, part_cols), lambda i: (0, i, 0)),
        row_block,
        row_block,
    ]
    return feed_call(
        "feed_first",
        6,
        blocks,
        rows,
        width,
        part_cols,
        (out_shape, out_specs),
        [weights, weights, weights, factor, *operands],
        swaps,
        in_specs=w_specs + [SCALAR] + list(specs),
    )


def feed_last(both, wide, totals, weights, blocks, swaps=()):
    rows, width = both.shape[1:]
    own = rows // blocks
    part_cols, w_specs = feed_specs(weights)
    half = full(rows // 2, width)
    row_block = pl.BlockSpec((own, width), lambda i: (i, 0))
    out_shape = [shaped(wide.shape, BF16)]
    out_shape += [shaped((rows // 2, width), F32), shaped((rows // 2, width), BF16)] * 2
    return feed_call(
        "feed_last",
        5,
        blocks,
        rows,
        width,
        part_cols,
        (out_shape, [pl.BlockSpec((3, own, part_cols), lambda i: (0, i, 1))] + [half] * 4),
        [weights, weights, weights, both, *totals, wide],
        swaps,
        in_specs=w_specs
        + [pl.BlockSpec((2, own, width), lambda i: (0, i, 0)), row_block, row_block]
        + [pl.BlockSpec(memory_space=pl.ANY)],
        input_output_aliases={6: 0},
    )


def weights_kernel(windows, masks, *refs):
    lefts, rights = refs[:windows], refs[windows : 2 * windows]
    refs = refs[2 * windows :]
    sources, out_ref, targets = refs[: len(masks)], refs[len(masks)], refs[len(masks) + 1 :]
    at = pl.program_id(0)
    trades = tensor_trades(refs[: len(masks)], targets[: len(masks)], masks, *targets[len(masks) :])

    @pl.when(at == 0)
    def _():
        start_trades(trades, masks)

    total = None
    for left, right in zip(lefts, rights):
        term = dot_tn(left[...], right[...])
        total = term if total is None else total + term
    total = total.astype(BF16)
    depths, cores, halves, shard = out_ref.shape[:4]
    for depth in range(depths):
        for half in range(halves):
            for core in range(cores):
                start = ((depth * halves + half) * cores + core) * shard
                out_ref[depth, core, half] = total[start : start + shard]

    if masks:

        @pl.when(at == pl.num_programs(0) - 1)
        def _():
            for trade in trades:
                trade.wait()


def feed_weights(boths, wides, part, swaps):
    windows = len(boths)
    rows, width = boths[0].shape[1:]
    hidden_cols = wides[0].shape[2] // 2
    step = min(512, hidden_cols)
    steps = hidden_cols // step
    lead = (lax.axis_size("dp"), lax.axis_size("core"), lax.axis_size("x"))
    lead += (width // math.prod(lead),)
    masks = [kinds for _, kinds in swaps]
    anywhere = pl.BlockSpec(memory_space=pl.ANY)
    left = pl.BlockSpec((None, rows, width), lambda i: (i // (2 * steps), 0, 0))
    right = pl.BlockSpec((None, rows, step), lambda i: (i // steps, 0, part * steps + i % steps))
    total = sum(len(kinds) for kinds in masks)
    return run(
        functools.partial(weights_kernel, windows, masks),
        "feed_weights",
        [shaped(lead + (3 * hidden_cols,), BF16)]
        + [shaped((len(kinds),) + array.shape, BF16) for array, kinds in swaps],
        6 * windows * rows * width * hidden_cols,
        [*boths, *wides] + [array for array, _ in swaps],
        collective_id=4 if swaps else None,
        grid=(3 * steps,),
        in_specs=[left] * windows + [right] * windows + [anywhere] * len(swaps),
        out_specs=[pl.BlockSpec(lead + (step,), lambda i: (0, 0, 0, 0, i))]
        + [anywhere] * len(swaps),
        scratch_shapes=[pltpu.SemaphoreType.DMA((total,))] * 2 if swaps else [],
    )


def norm_grad(kept_ref, arrived_ref, stream, gain, sums_ref):
    grad_normed = kept_ref[...] + arrived_ref[...].astype(F32)
    normed, inv_std = normalise(stream)
    sums_ref[0:1, :] = jnp.sum(grad_normed * normed, axis=0, keepdims=True)
    sums_ref[1:2, :] = jnp.sum(grad_normed, axis=0, keepdims=True)
    return norm_back(grad_normed, normed, inv_std, gain)


def middle_back_kernel(
    factor_ref, kept_ref, arrived_ref, middle_ref, cot_ref, norms_ref, grad_ref, low_ref, sums_ref
):
    grad_y = cot_ref[...].astype(F32) * factor_ref[0, 0]
    grad = grad_y + norm_grad(
        kept_ref, arrived_ref, middle_ref[...], norms_ref[2:3, :], sums_ref
    )
    grad_ref[...] = grad
    low_ref[...] = grad.astype(BF16)


def second_norm_back(factor, kept, arrived, middle, cot_rows, norms):
    args, in_specs = zip(*[plane(one) for one in (kept, arrived, middle, cot_rows, norms)])
    full = pl.BlockSpec(kept.shape, lambda i: (0, 0))
    return run(
        middle_back_kernel,
        "second_norm_back",
        [
            shaped(kept.shape, F32),
            shaped(kept.shape, BF16),
            shaped((2, kept.shape[1]), F32),
        ],
        40 * kept.size,
        [factor, *args],
        grid=(1,),
        in_specs=[SCALAR, *in_specs],
        out_specs=[full, full, pl.BlockSpec((2, kept.shape[1]), lambda i: (0, 0))],
    )


class SumRoute:
    def __init__(self, part, rows, core_in, mine, x_in, z_in, send_sem, recv_sem):
        self.read, self.rows = part, rows
        self.core_in, self.mine, self.x_in, self.z_in = core_in, mine, x_in, z_in
        self.send_sem, self.recv_sem = send_sem, recv_sem
        self.seq, self.depth = seq_index(), lax.axis_index("dp")
        self.peers = half_chip_peers()

    def place(self, number, other_core):
        seq = flipped(self.seq, 2) if number >= 4 else self.seq
        seq = flipped(seq, 1) if other_core else seq
        turn = (self.depth + number % 4) % lax.axis_size("dp")
        return pl.ds(
            pl.multiple_of((turn * seq_size() + seq) * self.rows, self.rows), self.rows
        )

    def message(self, number):
        if number < 8:
            source, target, peer = self.read.at[self.place(number, True), :], self.core_in, "core"
            target = target.at[number]
        elif number < 12:
            source, target, peer = self.mine.at[number - 4], self.x_in.at[number - 8], "far"
        else:
            turn, peer = ((2, "up"), (1, "up"), (3, "down"))[number - 12]
            source, target = self.mine.at[turn], self.z_in.at[number - 12]
        return send(
            source, target, self.send_sem.at[number], self.recv_sem.at[number], self.peers[peer]
        )

    def start(self, *numbers):
        for number in numbers:
            self.message(number).start()

    def add_core(self, number):
        self.message(number).wait_recv()
        own = self.read[self.place(number, False), :].astype(F32)
        self.mine[number] = (own + self.core_in[number].astype(F32)).astype(self.mine.dtype)

    def add_x(self, number):
        self.message(8 + number).wait_recv()
        total = self.mine[number].astype(F32) + self.x_in[number].astype(F32)
        self.mine[number] = total.astype(self.mine.dtype)

    def add_up(self):
        self.message(12).wait_recv()
        total = self.mine[1].astype(F32) + self.z_in[0].astype(F32)
        self.mine[1] = total.astype(self.mine.dtype)

    def total(self):
        self.message(13).wait_recv()
        self.message(14).wait_recv()
        return (
            self.mine[0].astype(F32) + self.z_in[1].astype(F32) + self.z_in[2].astype(F32)
        )

    def sent(self):
        for number in range(SUM_MESSAGES):
            self.message(number).wait_send()


SUM_MESSAGES = 15


def finish_kernel(windows, trades, score_cols, *refs):
    stages = (trades + 1).bit_length() - 1
    refs = list(refs)

    def take(count):
        taken = refs[:count]
        del refs[:count]
        return taken

    far_inputs = take(8)
    shard_ref = take(1)[0]
    norms_ref = take(1)[0]
    second_refs = take(windows)
    grad_refs = take(windows)
    part_refs = take(3 * windows)
    weights_ref, vectors_ref, input_ref, output_ref, shard_arrived = take(5)
    loads = take(8)
    grad_loads = take(windows)
    part_loads = take(3 * windows)
    part, core_in, mine, x_in, z_in = take(5)
    tiles, own_tiles, arrived_tiles = take(3)
    small_core, small_mine, small_x, small_z = take(4)
    kept_all = take(windows)
    stage_sent = [take(stages) for _ in range(windows)]
    stage_arrived = [take(stages) for _ in range(windows)]
    load_sem, big_send, big_recv, small_send, small_recv = take(5)
    y_send, y_recv, tile_send, tile_recv, shard_sem = take(5)
    assert not refs
    (grad_q, grad_k, grad_v, normed, grad_mid, attended, w_qkv, tokens) = loads[:8]
    tensor = lax.axis_index("tensor")
    others = [{"tensor": flipped(tensor, other + 1)} for other in range(trades)]
    shards = lax.axis_size("dp") * seq_size()
    devices = shards * (trades + 1)
    group = tiles.shape[0] // shards
    width = part.shape[1]
    cols = score_cols
    rows = width // shards

    w_source = far_inputs[6].at[:, pl.ds(0, 3 * cols)]
    sources = [*far_inputs[:6], w_source, far_inputs[7]]
    sources += [*grad_refs, *part_refs]
    targets = [*loads, *grad_loads, *part_loads]
    copies = [
        pltpu.make_async_copy(source, target, load_sem.at[at])
        for at, (source, target) in enumerate(zip(sources, targets))
    ]
    order = [4, 5, 6, 0, 1, 2, 3, 7] + list(range(8, len(copies)))
    for at in order:
        copies[at].start()

    def block_route(block):
        return SumRoute(
            part.at[block],
            rows,
            core_in.at[block],
            mine.at[block],
            x_in.at[block],
            z_in.at[block],
            big_send.at[block],
            big_recv.at[block],
        )

    routes = [block_route(block) for block in range(4)]
    small = SumRoute(
        tiles, group, small_core, small_mine, small_x, small_z, small_send, small_recv
    )
    greet(list(small.peers.values()) + others)
    everything = (6, 7, 5, 4, 2, 3, 1, 0)

    def product(block, left, right):
        total = None
        for w in range(windows):
            term = dot_tn(left[w], right[w])
            total = term if total is None else total + term
        part[block] = total.astype(BF16)

    def y_trade(w, stage):
        return send(
            stage_sent[w][stage],
            stage_arrived[w][stage],
            y_send.at[w, stage],
            y_recv.at[w, stage],
            {"tensor": flipped(tensor, (trades + 1) >> (stage + 1))},
        )

    def turn_back(w):
        total = None
        for at, grad in enumerate((grad_q, grad_k, grad_v)):
            term = dot_nt(grad[w], w_qkv[:, at * cols : (at + 1) * cols])
            total = term if total is None else total + term
        half = total.shape[0] // 2
        kept_all[w][...] = total[:half]
        stage_sent[w][0][...] = total[half:].astype(BF16)

    def add_cores(route):
        for number in everything:
            route.add_core(number)

    def across(route):
        route.start(10, 11, 9, 8)

    def add_across(route):
        for number in (2, 3, 1, 0):
            route.add_x(number)

    count = shard_ref.shape[0] // 2
    far_rows = pl.ds(pl.multiple_of((1 - lax.axis_index("x")) * count, count), count)
    shard_trade = send(
        shard_ref.at[far_rows, :],
        shard_arrived,
        shard_sem.at[0],
        shard_sem.at[1],
        small.peers["far"],
    )
    shard_trade.start()
    copies[4].wait()
    copies[5].wait()
    product(3, grad_mid, attended)
    for at in (6, 0, 1, 2):
        copies[at].wait()
    routes[3].start(*everything)
    turn_back(0)
    add_cores(routes[3])
    y_trade(0, 0).start()
    across(routes[3])
    for w in range(1, windows):
        turn_back(w)
    copies[3].wait()
    product(0, normed, grad_q)
    for w in range(1, windows):
        y_trade(w, 0).start()
    routes[0].start(*everything)
    product(1, normed, grad_k)
    add_cores(routes[0])
    routes[1].start(*everything)
    across(routes[0])
    product(2, normed, grad_v)
    add_cores(routes[1])
    routes[2].start(*everything)
    across(routes[1])
    add_across(routes[3])
    add_cores(routes[2])
    routes[3].start(12, 14)
    across(routes[2])
    for at in range(8 + windows, len(copies)):
        copies[at].wait()
    for w in range(windows):
        middle_ref, kept_ref, arrived_ref = part_loads[3 * w : 3 * w + 3]
        output_ref[w] = (
            middle_ref[...] + (kept_ref[...] + arrived_ref[...].astype(F32))
        ).astype(BF16)
    routes[3].add_up()
    for at in range(7, 8 + windows):
        copies[at].wait()
    sums = [None, None]

    def first_norm(w):
        kept = kept_all[w][...]
        for stage in range(stages):
            y_trade(w, stage).wait_recv()
            kept = kept + stage_arrived[w][stage][...].astype(F32)
            if stage + 1 < stages:
                half = kept.shape[0] // 2
                stage_sent[w][stage + 1][...] = kept[half:].astype(BF16)
                y_trade(w, stage + 1).start()
                kept = kept[:half]
        normed_rows, inv_std = normalise(tokens[w].astype(F32))
        for at, one in enumerate((kept * normed_rows, kept)):
            one = jnp.sum(one, axis=0, keepdims=True)
            sums[at] = one if sums[at] is None else sums[at] + one
        input_ref[w] = grad_loads[w][...] + norm_back(
            kept, normed_rows, inv_std, norms_ref[0:1, :]
        )

    first_norm(0)
    routes[3].start(13)
    add_across(routes[0])
    for w in range(1, windows):
        first_norm(w)
    routes[0].start(12, 14)
    first = jnp.concatenate(sums, axis=0)
    second = sum(ref[...] for ref in second_refs)
    span = width // devices
    tiles[...] = jnp.zeros_like(tiles)
    for device in range(devices):
        at = device * 8
        columns = slice(device * span, (device + 1) * span)
        tiles[at : at + 2, :span] = first[:, columns]
        tiles[at + 2 : at + 4, :span] = second[:, columns]
    add_across(routes[1])
    small.start(*everything)
    routes[0].add_up()
    routes[1].start(12, 14)
    add_cores(small)
    routes[0].start(13)
    across(small)
    add_across(routes[2])
    routes[1].add_up()
    routes[2].start(12, 14)
    add_across(small)
    routes[1].start(13)
    small.start(12, 14)
    for block in (3, 0):
        weights_ref[:, block * cols : (block + 1) * cols] = routes[block].total()
    small.add_up()
    routes[2].add_up()
    small.start(13)
    weights_ref[:, cols : 2 * cols] = routes[1].total()
    routes[2].start(13)
    own_tiles[...] = small.total()

    def tile_trade(other):
        place = pl.ds(pl.multiple_of(flipped(tensor, other + 1) * 8, 8), 8)
        return send(
            own_tiles.at[place, :],
            arrived_tiles.at[other],
            tile_send.at[other],
            tile_recv.at[other],
            others[other],
        )

    weights_ref[:, 2 * cols : 3 * cols] = routes[2].total()
    for other in range(trades):
        tile_trade(other).start()
    vectors = own_tiles[pl.ds(pl.multiple_of(tensor * 8, 8), 8), :]
    for other in range(trades):
        tile_trade(other).wait_recv()
        vectors = vectors + arrived_tiles[other]
    vectors_ref[...] = vectors
    shard_trade.wait()
    for route in (*routes, small):
        route.sent()
    for w in range(windows):
        for stage in range(stages):
            y_trade(w, stage).wait_send()
    for other in range(trades):
        tile_trade(other).wait_send()


def finish(
    grads,
    normed,
    grad_mid,
    attended,
    w_att,
    tokens,
    ffn_shard,
    norms,
    second_sums,
    grad_middles,
    parts,
    trades,
):
    windows, rows, cols = grads[0].shape
    width = w_att.shape[0]
    own_rows = tokens.shape[1]
    shards = lax.axis_size("dp") * seq_size()
    shard = width // shards
    group = 8 * (trades + 1)
    stages = [rows >> (stage + 1) for stage in range((trades + 1).bit_length() - 1)]
    dma = pltpu.SemaphoreType.DMA
    anywhere = pl.BlockSpec(memory_space=pl.ANY)
    vmem = pl.BlockSpec(memory_space=pltpu.VMEM)
    far_inputs = [*grads, normed, grad_mid, attended, w_att, tokens]
    flat = [array for one in parts for array in one]
    kinds = (8, 8, 4, 3)

    def like(array):
        return pltpu.VMEM(array.shape, array.dtype)

    loads = [like(array) for array in far_inputs]
    loads[6] = pltpu.VMEM((width, 3 * cols), BF16)
    return run(
        functools.partial(finish_kernel, windows, trades, cols),
        "finish",
        [
            shaped((shard, 4 * cols), F32),
            shaped((8, 128), F32),
            shaped((windows, own_rows, width), F32),
            shaped((windows, own_rows, width), BF16),
            shaped((ffn_shard.shape[0] // 2, ffn_shard.shape[1]), BF16),
        ],
        8 * windows * rows * width * cols + 6 * windows * rows * width * cols,
        [*far_inputs, ffn_shard, norms, *second_sums, *grad_middles, *flat],
        collective_id=3,
        in_specs=[anywhere] * 9
        + [vmem] * (1 + windows)
        + [anywhere] * (windows + len(flat)),
        out_specs=[vmem] * 4 + [anywhere],
        scratch_shapes=loads
        + [like(array) for array in grad_middles]
        + [like(array) for array in flat]
        + [pltpu.VMEM((4, width, cols), BF16)]
        + [pltpu.VMEM((4, count, shard, cols), BF16) for count in kinds]
        + [
            pltpu.VMEM((shards * group, 128), F32),
            pltpu.VMEM((group, 128), F32),
            pltpu.VMEM((trades, 8, 128), F32),
        ]
        + [pltpu.VMEM((count, group, 128), F32) for count in kinds]
        + [pltpu.VMEM((rows // 2, width), F32)] * windows
        + [pltpu.VMEM((count, width), BF16) for count in stages] * (2 * windows)
        + [
            dma((8 + windows + len(flat),)),
            dma((4, SUM_MESSAGES)),
            dma((4, SUM_MESSAGES)),
            dma((SUM_MESSAGES,)),
            dma((SUM_MESSAGES,)),
            dma((windows, len(stages))),
            dma((windows, len(stages))),
            dma((trades,)),
            dma((trades,)),
            dma((2,)),
        ],
    )


def local(
    tokens,
    cotangent,
    species,
    counts,
    species_scale,
    norm1_gain,
    norm1_bias,
    w_query,
    w_key,
    w_value,
    w_out,
    norm2_gain,
    norm2_bias,
    w_gate,
    w_up,
    w_down,
):
    windows_here, own_rows, model_width = tokens.shape
    tensor_size = lax.axis_size("tensor")
    block_rows = own_rows * tensor_size
    head_cols = w_query.shape[1]
    hidden_cols = w_gate.shape[1]
    shards = ("dp", "x", "core")

    own_at = lax.axis_index("tensor")
    starts = jnp.concatenate(
        [
            lax.iota(jnp.int32, own_rows) + (own_at ^ other) * own_rows
            for other in range(tensor_size)
        ]
    )
    positions = (seq_index() * block_rows + starts).astype(F32)
    cos_half, sin_half = angles(positions, HEAD_DIM)
    cosine = jnp.concatenate([cos_half] * 4, axis=1)
    sine = jnp.concatenate([-sin_half, sin_half] * 2, axis=1)

    labels = lax.broadcasted_iota(jnp.int32, (windows_here, species_scale.shape[0]), 1)
    chosen = jnp.sum(jnp.where(species[:, None] == labels, species_scale[None, :], 0.0), axis=1)
    weighted = counts.astype(F32) * chosen

    lanes = jnp.zeros((8, 128), F32)
    vectors = jnp.stack([norm1_gain, norm1_bias, norm2_gain, norm2_bias])
    tile = lanes.at[:4, : vectors.shape[1]].set(vectors).at[4, :].set(jnp.sum(weighted))
    part = hidden_cols // 2
    turned = w_down.T
    first_ffn = jnp.concatenate([w_gate[:, :part], w_up[:, :part], turned[:, :part]], axis=1)
    last_ffn = jnp.concatenate([w_gate[:, part:], w_up[:, part:], turned[:, part:]], axis=1)
    upper = lax.axis_index("x") == 1

    def gather_ffn(own, across):
        pair = jnp.where(
            upper,
            jnp.concatenate([across, own], axis=0),
            jnp.concatenate([own, across], axis=0),
        )
        whole = lax.all_gather(pair, ("dp", "core"), axis=0, tiled=True)
        return whole.reshape(
            lax.axis_size("dp"), lax.axis_size("core"), lax.axis_size("x"), -1, whole.shape[1]
        )

    first_ffn = lax.all_gather(first_ffn, shards, axis=0, tiled=True)
    last_across = swap(last_ffn, "x", 1)
    w_att, norms, arrived_tokens = gather(
        jnp.concatenate([w_query, w_key, w_value, w_out.T], axis=1),
        tile,
        tokens,
        tensor_size - 1,
    )
    factor = weighted * float(windows_here * lax.axis_size("dp")) / norms[4, 0]

    windows = range(windows_here)
    factors = [factor[w].reshape(1, 1) for w in windows]

    token_blocks = [tokens] + [arrived_tokens[other] for other in range(tensor_size - 1)]
    normed_rows, queries, own_kv = project(token_blocks, norms, w_att, cosine, sine)
    last_ffn = gather_ffn(last_ffn, hold(last_across, w_att))
    (
        attended,
        wide_attended,
        logs,
        kept_all,
        sent_all,
        slots_all,
        cots,
        first_middle,
        first_normed,
        first_others,
    ) = attend(queries, own_kv, w_att, cotangent, tokens, norms, tensor_size - 1)
    others = range(tensor_size - 1)
    cot_blocks = [
        [(cotangent, (w,))] + [(cots, (other, w)) for other in others] for w in windows
    ]
    middles = [first_middle]

    def reduce_ffn(partial):
        partial = partial.reshape(-1, partial.shape[-1])
        mine = lax.psum_scatter(partial, ("dp", "core"), scatter_dimension=0, tiled=True)
        count = mine.shape[0] // 2
        kept = jnp.where(upper, mine[count:], mine[:count])
        return kept, mine

    blocks = [first_normed] + [first_others[other] for other in others]
    begun, fed, lows, arrived_lows = [], [], [], []
    grad_middles, second_sums = [], []
    masks = [other + 1 for other in others]

    def through_second_norm(w, kept, arrived):
        grad_middle, low, sums = second_norm_back(
            factors[w], kept, arrived, middles[w], (cotangent, (w,)), norms
        )
        grad_middles.append(grad_middle)
        second_sums.append(sums)
        return low

    for w in windows:
        swaps = [(fed[-1][4], [tensor_size // 2])] if fed else []
        started = feed_first(blocks, cot_blocks[w], factors[w], first_ffn, swaps)
        begun.append(started[:4])
        if w + 1 < windows_here:
            kept, arrived = scatter_pair(kept_all[w], sent_all[w], "tensor")
            middle, normed_mid = second_norm(
                (tokens, (w + 1,)), hold(kept, begun[-1]), arrived, norms
            )
            middles.append(middle)
            blocks = hold(spread(normed_mid, "tensor"), fed)
            after = normed_mid
        else:
            g_first_part = feed_weights(
                [one[0] for one in begun],
                [one[0] for one in fed] + [one[1] for one in begun[len(fed) :]],
                0,
                (),
            )[0]
            first_kept, first_sent = reduce_ffn(g_first_part)
            after = g_first_part
        swaps = ()
        if w > 0:
            kept, arrived = later_pair(fed[-1][3], started[4][0], "tensor")
            low = through_second_norm(w - 1, hold(kept, g_first_part), arrived)
            lows.append(low)
            swaps = [(low, masks)]
            after = low
        both, wide, *totals = hold(begun[w], after)
        ended = feed_last(both, wide, totals, last_ffn, tensor_size, swaps)
        fed.append(ended[:5])
        arrived_lows += ended[5:]
        if w + 1 < windows_here:
            blocks = hold(blocks, ended[3])
    g_ffn_part, arrived = feed_weights(
        [one[0] for one in begun],
        [one[0] for one in fed],
        1,
        [(fed[-1][4], [tensor_size // 2])],
    )
    last_kept, last_sent = reduce_ffn(g_ffn_part)
    kept, arrived = later_pair(fed[-1][3], arrived[0], "tensor")
    last_low = through_second_norm(windows[-1], hold(kept, g_ffn_part), arrived)
    grad_mid_blocks = [
        [low] + [arrived[other] for other in others] for low, arrived in zip(lows, arrived_lows)
    ] + [[last_low]]

    grad_q, grad_k, grad_v, grad_mid_rows, *arrived_results = attend_back(
        hold(queries, g_ffn_part),
        wide_attended,
        logs,
        slots_all,
        grad_mid_blocks,
        w_att,
        (cosine, sine),
        [fed[w][2] for w in windows],
    )
    parts = [
        (middles[w], *later_pair(fed[w][1], arrived_results[w], "tensor")) for w in windows
    ]

    g_att, vectors, input_grad, output, first_arrived = finish(
        (grad_q, grad_k, grad_v),
        normed_rows,
        grad_mid_rows,
        attended,
        w_att,
        tokens,
        first_sent,
        norms,
        second_sums,
        grad_middles,
        parts,
        tensor_size - 1,
    )
    g_first = first_kept.astype(F32) + first_arrived.astype(F32)
    last_sent = hold(last_sent, output)
    count = last_sent.shape[0] // 2
    last_sent = jnp.where(upper, last_sent[:count], last_sent[count:])
    last_arrived = swap(last_sent, "x", 1)
    g_last = last_kept.astype(F32) + last_arrived.astype(F32)
    norm_sums = vectors[:4, : norm1_gain.shape[0]]
    ffn_grads = [
        jnp.concatenate(
            [g_first[:, at * part : (at + 1) * part], g_last[:, at * part : (at + 1) * part]],
            axis=1,
        )
        for at in range(3)
    ]

    return (
        output,
        input_grad,
        norm_sums[0],
        norm_sums[1],
        g_att[:, :head_cols],
        g_att[:, head_cols : 2 * head_cols],
        g_att[:, 2 * head_cols : 3 * head_cols],
        g_att[:, 3 * head_cols :].T,
        norm_sums[2],
        norm_sums[3],
        ffn_grads[0],
        ffn_grads[1],
        ffn_grads[2].T,
    )


def solution(mesh):
    depth, seq, tensor = mesh.devices.shape
    finer = jax.sharding.Mesh(
        mesh.devices.reshape(depth, seq // 2, 2, tensor), ("dp", "x", "core", "tensor")
    )
    rows = P("dp", ("x", "core", "tensor"), None)
    vector = P(("dp", "x", "core", "tensor"))
    tall = P(("dp", "x", "core"), "tensor")
    flat = P("tensor", ("dp", "x", "core"))
    return jax.shard_map(
        local,
        mesh=finer,
        in_specs=(
            rows, rows, P("dp"), P("dp"), P(), vector, vector,
            tall, tall, tall, flat, vector, vector, tall, tall, flat,
        ),
        out_specs=(
            rows, rows, vector, vector, tall, tall, tall, flat,
            vector, vector, tall, tall, flat,
        ),
        check_vma=False,
    )
```

```python
import functools
import math

import jax
import jax.numpy as jnp
from jax import lax
from jax.experimental import pallas as pl
from jax.experimental.pallas import tpu as pltpu
from jax.sharding import PartitionSpec as P

HEAD_DIM = 64
EPSILON = 1e-05
ROPE_BASE = 10000.0
PAIR = 2 * HEAD_DIM
LOG2E = math.log2(math.e)
BF16 = jnp.bfloat16
F32 = jnp.float32
VMEM_BYTES = 56 * 1024 * 1024
MESH = pl.DeviceIdType.MESH


def dot_nn(left, right):
    return lax.dot_general(left, right, (((1,), (0,)), ((), ())), preferred_element_type=F32)


def dot_nt(left, right):
    return lax.dot_general(left, right, (((1,), (1,)), ((), ())), preferred_element_type=F32)


def dot_tn(left, right):
    return lax.dot_general(left, right, (((0,), (0,)), ((), ())), preferred_element_type=F32)


def swap(array, axis, bit):
    size = lax.axis_size(axis)
    return lax.ppermute(array, axis, [(i, i ^ bit) for i in range(size)])


def spread(array, axis):
    blocks = [array]
    bit = 1
    while bit < lax.axis_size(axis):
        blocks = blocks + [swap(block, axis, bit) for block in blocks]
        bit *= 2
    return blocks


def scatter_pair(kept, sent, axis):
    return later_pair(kept, swap(sent, axis, lax.axis_size(axis) // 2), axis)


def later_pair(kept, arrived, axis):
    bit = lax.axis_size(axis) // 2
    while bit > 1:
        partial = kept + arrived.astype(F32)
        bit //= 2
        rows = partial.shape[0] // 2
        kept, arrived = partial[:rows], swap(partial[rows:].astype(BF16), axis, bit)
    return kept, arrived


def seq_size():
    return lax.axis_size("x") * lax.axis_size("core")


def seq_index():
    return lax.axis_index("x") * lax.axis_size("core") + lax.axis_index("core")


def hold(values, *others):
    return lax.optimization_barrier((values, others))[0]


def run(kernel, name, out_shape, flops, args, collective_id=None, **options):
    trading = {} if collective_id is None else dict(collective_id=collective_id, has_side_effects=True)
    moved = sum(math.prod(array.shape) * array.dtype.itemsize for array in args)
    outs = out_shape if isinstance(out_shape, list) else [out_shape]
    moved += sum(math.prod(array.shape) * array.dtype.itemsize for array in outs)
    return pl.pallas_call(
        kernel,
        out_shape=out_shape,
        compiler_params=pltpu.CompilerParams(vmem_limit_bytes=VMEM_BYTES, **trading),
        cost_estimate=pl.CostEstimate(
            flops=int(flops), bytes_accessed=int(moved), transcendentals=0
        ),
        name=name,
        **options,
    )(*args)


def shaped(shape, dtype):
    return jax.ShapeDtypeStruct(shape, dtype)


SCALAR = pl.BlockSpec(memory_space=pltpu.SMEM)


def plane(operand, block=None, index=None):
    array, at = operand if isinstance(operand, tuple) else (operand, ())
    shape = array.shape[len(at) :] if block is None else block
    place = (lambda *i: (0,) * len(shape)) if index is None else index
    return array, pl.BlockSpec((None,) * len(at) + tuple(shape), lambda *i: at + place(*i))


def normalise(stream):
    row_mean = jnp.mean(stream, axis=-1, keepdims=True)
    centred = stream - row_mean
    variance = jnp.mean(centred * centred, axis=-1, keepdims=True)
    inv_std = lax.rsqrt(variance + EPSILON)
    return centred * inv_std, inv_std


def norm_back(grad_normed, normed, inv_std, norm_gain):
    scaled_grad = grad_normed * norm_gain
    return inv_std * (
        scaled_grad
        - jnp.mean(scaled_grad, axis=-1, keepdims=True)
        - normed * jnp.mean(scaled_grad * normed, axis=-1, keepdims=True)
    )


def factor_of(weight_ref, norms_ref, slots):
    return weight_ref[0, 0] * slots / norms_ref[4:5, 0:1]


def first_head(shape):
    return lax.broadcasted_iota(jnp.int32, shape, 1) % PAIR < HEAD_DIM


def swap_halves(values):
    half = HEAD_DIM // 2
    lane = lax.broadcasted_iota(jnp.int32, values.shape, 1)
    ahead = pltpu.roll(values, PAIR - half, 1)
    behind = pltpu.roll(values, half, 1)
    return jnp.where(lane % HEAD_DIM < half, ahead, behind)


def project_kernel(blocks, norms_ref, w_ref, cos_ref, sin_ref, *refs):
    x_refs = refs[:blocks]
    normed_ref, q_ref, kv_ref = refs[blocks:]
    cols = q_ref.shape[2]
    gain, bias = norms_ref[0:1, :], norms_ref[1:2, :]
    at_row = 0
    for x_ref in x_refs:
        rows = slice(at_row, at_row + x_ref.shape[1])
        at_row += x_ref.shape[1]
        normed = (normalise(x_ref[0].astype(F32))[0] * gain + bias).astype(BF16)
        normed_ref[0, rows, :] = normed
        cosine, sine = cos_ref[rows, :], sin_ref[rows, :]
        query = dot_nn(normed, w_ref[:, :cols])
        key = dot_nn(normed, w_ref[:, cols : 2 * cols])
        value = dot_nn(normed, w_ref[:, 2 * cols : 3 * cols]).astype(BF16)
        for at in range(0, cols, PAIR):
            part, pair = slice(at, at + PAIR), at // PAIR
            one = query[:, part]
            q_ref[0, rows, part] = (one * cosine + swap_halves(one) * sine).astype(BF16)
            one = key[:, part]
            kv_ref[0, pair, 0, rows, :] = (one * cosine + swap_halves(one) * sine).astype(BF16)
            kv_ref[0, pair, 1, rows, :] = value[:, part]


def project(x_blocks, norms, w_att, cosine, sine):
    windows = x_blocks[0].shape[0]
    width, cols = w_att.shape[0], w_att.shape[1] // 4
    rows = sum(block.shape[1] for block in x_blocks)
    pieces = (cols // PAIR, 2, rows, PAIR)
    args = [norms, w_att, cosine, sine, *x_blocks]
    return run(
        functools.partial(project_kernel, len(x_blocks)),
        "project",
        [
            shaped((windows, rows, width), BF16),
            shaped((windows, rows, cols), BF16),
            shaped((windows,) + pieces, BF16),
        ],
        6 * windows * rows * width * cols,
        args,
        grid=(windows,),
        in_specs=[pl.BlockSpec(array.shape, lambda i: (0, 0)) for array in args[:4]]
        + [pl.BlockSpec((1,) + block.shape[1:], lambda i: (i, 0, 0)) for block in x_blocks],
        out_specs=[
            pl.BlockSpec((1, rows, width), lambda i: (i, 0, 0)),
            pl.BlockSpec((1, rows, cols), lambda i: (i, 0, 0)),
            pl.BlockSpec((1,) + pieces, lambda i: (i, 0, 0, 0, 0)),
        ],
    )


def flipped(index, mask):
    bit = 1
    while bit <= mask:
        if mask & bit:
            index = index + bit - 2 * bit * ((index // bit) % 2)
        bit *= 2
    return index


def greet(peers):
    barrier = pltpu.get_barrier_semaphore()
    for peer in peers:
        pl.semaphore_signal(barrier, inc=1, device_id=peer, device_id_type=MESH)
    pl.semaphore_wait(barrier, len(peers))


def send(source, target, send_sem, recv_sem, peer):
    return pltpu.make_async_remote_copy(
        src_ref=source,
        dst_ref=target,
        send_sem=send_sem,
        recv_sem=recv_sem,
        device_id=peer,
        device_id_type=MESH,
    )


def half_chip_peers():
    depth = lax.axis_index("dp")
    size = lax.axis_size("dp")
    return {
        "far": {"x": 1 - lax.axis_index("x")},
        "up": {"dp": (depth + 1) % size},
        "down": {"dp": (depth + size - 1) % size},
        "core": {"core": 1 - lax.axis_index("core")},
    }


class Route:
    PARTS = ((0, 0), (3, 0), (1, 0), (2, 0), (0, 1), (3, 1), (1, 1), (2, 1))

    def __init__(self, whole, rows, send_sem, recv_sem, own):
        self.whole, self.rows, self.own = whole, rows, own
        self.send_sem, self.recv_sem = send_sem, recv_sem
        self.seq, self.depth = seq_index(), lax.axis_index("dp")
        self.peers = half_chip_peers()

    def part(self, place):
        turn, other = place
        seq = flipped(self.seq, 2) if other else self.seq
        at = (((self.depth + turn) % lax.axis_size("dp")) * seq_size() + seq) * self.rows
        return self.whole.at[pl.ds(pl.multiple_of(at, self.rows), self.rows), :]

    def message(self, number):
        if number >= 7:
            place, peer = self.PARTS[number - 7], "core"
        else:
            place, peer = (
                ((0, 0), "up"),
                ((0, 0), "down"),
                ((3, 0), "up"),
                ((0, 0), "far"),
                ((3, 0), "far"),
                ((1, 0), "far"),
                ((2, 0), "far"),
            )[number]
        target = self.part(place)
        return send(
            self.own if place == (0, 0) else target,
            target,
            self.send_sem.at[number],
            self.recv_sem.at[number],
            self.peers[peer],
        )

    def start(self, *numbers):
        for number in numbers:
            self.message(number).start()

    def arrived(self, *numbers):
        for number in numbers:
            self.message(number).wait_recv()

    def sent(self, *numbers):
        for number in numbers:
            self.message(number).wait_send()


MESSAGES = 15


def tables(cos_ref, sin_ref, trades):
    own_rows = cos_ref.shape[0] // (trades + 1)
    tensor = lax.axis_index("tensor")
    half = HEAD_DIM // 2
    shape = (own_rows, PAIR)
    lane = lax.broadcasted_iota(jnp.int32, shape, 1)
    exponent = -(math.log(ROPE_BASE) * 2.0 / HEAD_DIM) * (lane % half).astype(F32)
    inverse = jnp.exp(exponent)
    row = lax.broadcasted_iota(jnp.int32, shape, 0)
    for other in range(trades + 1):
        start = (seq_index() * (trades + 1) + flipped(tensor, other)) * own_rows
        phase = (row + start).astype(F32) * inverse
        rows = slice(other * own_rows, (other + 1) * own_rows)
        cos_ref[rows, :] = jnp.cos(phase)
        sine = jnp.sin(phase)
        sin_ref[rows, :] = jnp.where(lane % HEAD_DIM < half, -sine, sine)


def gather_kernel(trades, att_ref, tile_ref, tokens_ref, *refs):
    att_all, norms_ref, tokens_all, cos_ref, sin_ref = refs[:5]
    tiles, pair_of_tiles = refs[5:7]
    att_send, att_recv, tile_send, tile_recv = refs[7:11]
    own_sem, tokens_send, tokens_recv, pair_send, pair_recv = refs[11:]
    tensor = lax.axis_index("tensor")
    others = [{"tensor": flipped(tensor, other + 1)} for other in range(trades)]
    att = Route(att_all, att_ref.shape[0], att_send, att_recv, att_ref)
    tile_rows = tile_ref.shape[0]
    small = Route(tiles, pair_of_tiles.shape[0], tile_send, tile_recv, pair_of_tiles)

    def tokens_trade(other):
        return send(
            tokens_ref,
            tokens_all.at[other],
            tokens_send.at[other],
            tokens_recv.at[other],
            others[other],
        )

    own_rows = pl.ds(pl.multiple_of(tensor * tile_rows, tile_rows), tile_rows)

    def pair_trade(other):
        return send(
            tile_ref,
            pair_of_tiles.at[own_rows, :],
            pair_send.at[other],
            pair_recv.at[other],
            others[other],
        )

    own_copies = [
        pltpu.make_async_copy(att_ref, att.part((0, 0)), own_sem.at[0]),
        pltpu.make_async_copy(tile_ref, pair_of_tiles.at[own_rows, :], own_sem.at[1]),
        pltpu.make_async_copy(pair_of_tiles, small.part((0, 0)), own_sem.at[2]),
    ]

    greet(list(att.peers.values()) + others)
    for other in range(trades):
        pair_trade(other).start()
    own_copies[1].start()
    att.start(0, 1, 3, 7)
    own_copies[1].wait()
    for other in range(trades):
        pair_trade(other).wait_recv()
    small.start(0, 1, 3, 7)
    own_copies[0].start()
    own_copies[2].start()
    for other in range(trades):
        tokens_trade(other).start()
    tables(cos_ref, sin_ref, trades)
    for route in (small, att):
        route.arrived(0)
        route.start(2, 4, 8)
    for route in (small, att):
        route.arrived(3)
        route.start(11)
    for route in (small, att):
        route.arrived(1)
        route.start(5, 9)
    for route in (small, att):
        route.arrived(2)
        route.start(6, 10)
    for route in (small, att):
        route.arrived(4)
        route.start(12)
        route.arrived(5)
        route.start(13)
        route.arrived(6)
        route.start(14)
    for route in (small, att):
        route.arrived(*range(7, MESSAGES))
    own_copies[2].wait()
    shard = norms_ref.shape[1] // (tiles.shape[0] // tile_rows)
    total = None
    for device in range(tiles.shape[0] // tile_rows):
        tile = tiles[device * tile_rows : (device + 1) * tile_rows, :]
        norms_ref[:, device * shard : (device + 1) * shard] = tile[:, :shard]
    for depth in range(lax.axis_size("dp")):
        at = depth * (tiles.shape[0] // lax.axis_size("dp"))
        one = tiles[at + 4 : at + 5, :]
        total = one if total is None else total + one
    norms_ref[4:5, : total.shape[1]] = total
    for route in (att, small):
        route.sent(*range(MESSAGES))
    own_copies[0].wait()
    for other in range(trades):
        pair_trade(other).wait_send()
        tokens_trade(other).wait_recv()
        tokens_trade(other).wait_send()


def gather(att, tile, tokens, trades):
    count = lax.axis_size("dp") * seq_size()
    rows = att.shape[0]
    group = tile.shape[0] * (trades + 1)
    anywhere = pl.BlockSpec(memory_space=pl.ANY)
    vmem = pl.BlockSpec(memory_space=pltpu.VMEM)
    dma = pltpu.SemaphoreType.DMA
    return run(
        functools.partial(gather_kernel, trades),
        "gather",
        [
            shaped((count * rows, att.shape[1]), BF16),
            shaped((tile.shape[0], count * rows), F32),
            shaped((trades,) + tokens.shape, BF16),
        ]
        + [shaped((tokens.shape[1] * (trades + 1), PAIR), F32)] * 2,
        0,
        [att, tile, tokens],
        collective_id=1,
        in_specs=[vmem, vmem, anywhere],
        out_specs=[anywhere, vmem, anywhere, vmem, vmem],
        scratch_shapes=[pltpu.VMEM((count * group, 128), F32), pltpu.VMEM((group, 128), F32)]
        + [dma((MESSAGES,))] * 4
        + [dma((3,)), dma((trades,)), dma((trades,)), dma((trades,)), dma((trades,))],
    )


def attend_kernel(windows, pairs, trades, exp_scale, *refs):
    stages = (trades + 1).bit_length() - 1
    q_ref, w_ref, kv_ref, cot_ref, x_ref, norms_ref = refs[:6]
    low_ref, wide_ref, log_ref, kept_ref, sent_ref, slots_ref, cots_ref = refs[6:13]
    middle_ref, normed_ref, others_ref = refs[13:16]
    slots, acc_all, top_all, total_all, mixed_rows = refs[16:21]
    own_sem, send_sem, recv_sem, save_sem, cot_send, cot_recv = refs[21:27]
    early_kept, early_normed, early_sem, early_recv, normed_sem, normed_recv = refs[27:33]
    early_sent, early_arrived = refs[33 : 33 + stages], refs[33 + stages :]
    step = pl.program_id(0)
    near_steps = windows * pairs
    steps = 2 * near_steps
    turn = step % (2 * pairs)
    is_far = turn >= pairs
    number = step // (2 * pairs) * pairs + turn % pairs
    tensor = lax.axis_index("tensor")
    core_peer = {"core": 1 - lax.axis_index("core")}
    far_peer = {"x": 1 - lax.axis_index("x")}
    cot_peers = [{"tensor": flipped(tensor, other + 1)} for other in range(trades)]

    def piece(number):
        return kv_ref.at[number // pairs, number % pairs]

    def own_copy(number):
        return pltpu.make_async_copy(piece(number), slots.at[number, 0], own_sem.at[number])

    def trade(number, slot):
        peer = far_peer if slot == 2 else core_peer
        source = slots.at[number, 2] if slot == 3 else piece(number)
        return send(
            source,
            slots.at[number, slot],
            send_sem.at[number, slot - 1],
            recv_sem.at[number, slot - 1],
            peer,
        )

    def cot_trade(other):
        return send(
            cot_ref, cots_ref.at[other], cot_send.at[other], cot_recv.at[other], cot_peers[other]
        )

    def early_trade(stage):
        return send(
            early_sent[stage],
            early_arrived[stage],
            early_sem.at[stage],
            early_recv.at[stage],
            {"tensor": flipped(tensor, (trades + 1) >> (stage + 1))},
        )

    def normed_trade(other):
        return send(
            early_normed,
            others_ref.at[other],
            normed_sem.at[other],
            normed_recv.at[other],
            cot_peers[other],
        )

    def save(number, slot):
        return pltpu.make_async_copy(
            slots.at[number, slot], slots_ref.at[number, slot], save_sem.at[number, slot]
        )

    @pl.when(step == 0)
    def _():
        greet([core_peer, far_peer] + cot_peers)

        @pl.loop(0, near_steps)
        def _(number):
            own_copy(number).start()
            trade(number, 1).start()
            trade(number, 2).start()

        for other in range(trades):
            cot_trade(other).start()

    @pl.when(step == 2 * pairs)
    def _():
        early_trade(0).start()

    @pl.when(step == 3 * pairs)
    def _():
        kept = early_kept[...]
        for stage in range(stages):
            early_trade(stage).wait_recv()
            kept = kept + early_arrived[stage][...].astype(F32)
            if stage + 1 < stages:
                half = kept.shape[0] // 2
                early_sent[stage + 1][...] = kept[half:].astype(BF16)
                early_trade(stage + 1).start()
                kept = kept[:half]
        middle = x_ref[...].astype(F32) + kept
        middle_ref[...] = middle
        normed = (normalise(middle)[0] * norms_ref[2:3, :] + norms_ref[3:4, :]).astype(BF16)
        normed_ref[...] = normed
        early_normed[...] = normed

    @pl.when(step == 3 * pairs + 1)
    def _():
        for other in range(trades):
            normed_trade(other).start()

    relayed = step // (2 * pairs) * pairs + turn - (pairs - 1)

    @pl.when(jnp.logical_and(turn >= pairs - 1, turn < 2 * pairs - 1))
    def _():
        trade(relayed, 2).wait_recv()
        trade(relayed, 3).start()
        save(relayed, 2).start()

    @pl.when(jnp.logical_not(is_far))
    def _():
        own_copy(number).wait()
        trade(number, 1).wait_recv()
        save(number, 0).start()
        save(number, 1).start()
        acc_all[number] = jnp.zeros(acc_all.shape[1:], F32)
        total_all[number] = jnp.zeros(acc_all.shape[1:], F32)
        top_all[number] = jnp.full(acc_all.shape[1:], -1e30, F32)

    @pl.when(is_far)
    def _():
        trade(number, 3).wait_recv()
        save(number, 3).start()

    query = q_ref[0]
    is_first = first_head(query.shape)
    base = jnp.where(is_far, 2, 0)
    carried_top = top_all[number]
    outs, tops = [], []
    for head in range(2):
        mine = is_first if head == 0 else jnp.logical_not(is_first)
        own_query = jnp.where(mine, query, jnp.zeros_like(query))
        scores = [dot_nt(own_query, slots[number, base + slot, 0]) for slot in range(2)]
        at = head * HEAD_DIM
        top = carried_top[:, at : at + 1]
        for one in scores:
            top = jnp.maximum(top, one.max(axis=1, keepdims=True))
        shift = top * exp_scale
        mixed = None
        for slot, one in enumerate(scores):
            weight = jnp.exp2(one * exp_scale - shift).astype(BF16)
            value = slots[number, base + slot, 1]
            lane_first = first_head(value.shape)
            lane_mine = lane_first if head == 0 else jnp.logical_not(lane_first)
            term = dot_nn(weight, jnp.where(lane_mine, value, jnp.ones_like(value)))
            mixed = term if mixed is None else mixed + term
        outs.append(mixed)
        tops.append(jnp.broadcast_to(top, mixed.shape))
    top = jnp.where(is_first, tops[0], tops[1])
    fade = jnp.exp2((carried_top - top) * exp_scale)
    acc = jnp.where(is_first, outs[0], outs[1]) + acc_all[number] * fade
    total = pltpu.roll(jnp.where(is_first, outs[1], outs[0]), HEAD_DIM, 1) + total_all[number] * fade

    @pl.when(jnp.logical_not(is_far))
    def _():
        acc_all[number] = acc
        top_all[number] = top
        total_all[number] = total

    @pl.when(is_far)
    def _():
        attended = acc / total
        low = attended.astype(BF16)
        low_ref[0] = low
        wide_ref[0] = attended
        log_ref[0] = (top * exp_scale + jnp.log2(total)).T
        term = dot_nt(low, w_ref[...])
        pair = number % pairs

        @pl.when(pair == 0)
        def _():
            mixed_rows[...] = term

        @pl.when(pair > 0)
        def _():
            mixed_rows[...] += term

        @pl.when(jnp.logical_and(pair == pairs - 1, number >= pairs))
        def _():
            half = kept_ref.shape[1]
            kept_ref[0] = mixed_rows[:half]
            sent_ref[0] = mixed_rows[half:].astype(BF16)

        @pl.when(number == pairs - 1)
        def _():
            half = kept_ref.shape[1]
            early_kept[...] = mixed_rows[:half]
            early_sent[0][...] = mixed_rows[half:].astype(BF16)

    @pl.when(step == steps - 1)
    def _():
        @pl.loop(0, near_steps)
        def _(number):
            for slot in range(1, 4):
                trade(number, slot).wait_send()
            for slot in range(4):
                save(number, slot).wait()

        for stage in range(stages):
            early_trade(stage).wait_send()
        for other in range(trades):
            cot_trade(other).wait_send()
            cot_trade(other).wait_recv()
            normed_trade(other).wait_send()
            normed_trade(other).wait_recv()


def attend(queries, own_kv, w_att, cotangent, tokens, norms, trades):
    windows, rows, cols = queries.shape
    width = w_att.shape[0]
    pairs = cols // PAIR
    near = windows * pairs
    out_at = 3 * pairs

    def far(i):
        turn = i % (2 * pairs)
        done = i // (2 * pairs) * pairs
        return jnp.where(turn >= pairs, done + turn - pairs, jnp.maximum(done - 1, 0))

    anywhere = pl.BlockSpec(memory_space=pl.ANY)
    wide = pl.BlockSpec((1, rows, PAIR), lambda i: (far(i) // pairs, 0, far(i) % pairs))
    half = pl.BlockSpec(
        (1, rows // 2, width), lambda i: (jnp.maximum(far(i) // pairs, 1) - 1, 0, 0)
    )
    own_rows = tokens.shape[1]
    own = pl.BlockSpec((own_rows, width), lambda i: (0, 0))
    stages = [rows >> (stage + 1) for stage in range((trades + 1).bit_length() - 1)]
    state = pltpu.VMEM((near, rows, PAIR), F32)
    dma = pltpu.SemaphoreType.DMA
    return run(
        functools.partial(attend_kernel, windows, pairs, trades, LOG2E / math.sqrt(HEAD_DIM)),
        "attend",
        [
            shaped((windows, rows, cols), BF16),
            shaped((windows, rows, cols), F32),
            shaped((windows, cols, rows), F32),
            shaped((windows - 1, rows // 2, width), F32),
            shaped((windows - 1, rows // 2, width), BF16),
            shaped((near, 4, 2, rows, PAIR), BF16),
            shaped((trades,) + cotangent.shape, BF16),
            shaped((own_rows, width), F32),
            shaped((own_rows, width), BF16),
            shaped((trades, own_rows, width), BF16),
        ],
        64 * windows * rows * rows * cols,
        [queries, w_att, own_kv, cotangent, tokens, norms],
        collective_id=0,
        grid=(2 * near,),
        in_specs=[
            pl.BlockSpec((1, rows, PAIR), lambda i: (i // (2 * pairs), 0, i % pairs)),
            pl.BlockSpec((width, PAIR), lambda i: (0, out_at + far(i) % pairs)),
            anywhere,
            anywhere,
            pl.BlockSpec((None, own_rows, width), lambda i: (0, 0, 0)),
            pl.BlockSpec(norms.shape, lambda i: (0, 0)),
        ],
        out_specs=[
            wide,
            wide,
            pl.BlockSpec((1, PAIR, rows), lambda i: (far(i) // pairs, far(i) % pairs, 0)),
            half,
            half,
            anywhere,
            anywhere,
            own,
            own,
            anywhere,
        ],
        scratch_shapes=[
            pltpu.VMEM((near, 4, 2, rows, PAIR), BF16),
            state,
            state,
            state,
            pltpu.VMEM((rows, width), F32),
            dma((near,)),
            dma((near, 3)),
            dma((near, 3)),
            dma((near, 4)),
            dma((trades,)),
            dma((trades,)),
            pltpu.VMEM((rows // 2, width), F32),
            pltpu.VMEM((own_rows, width), BF16),
            dma((len(stages),)),
            dma((len(stages),)),
            dma((trades,)),
            dma((trades,)),
        ]
        + [pltpu.VMEM((count, width), BF16) for count in stages] * 2,
    )


def attend_back_kernel(windows, pairs, blocks, exp_scale, score_scale, *refs):
    q_ref, wide_ref, log_ref, slots_ref, w_ref, cos_ref, sin_ref, last_ref = refs[:8]
    trades = blocks - 1
    known = (windows - 1) * blocks + 1
    grad_refs = list(refs[8 : 8 + known])
    refs = refs[8 + known :]
    sent_refs, refs = refs[:windows], refs[windows:]
    gq_ref, gk_ref, gv_ref, rows_ref = refs[:4]
    arrived_refs, refs = refs[4 : 4 + windows], refs[4 + windows :]
    dq_all, do_all, far_kept, far_sent, far_core, far_x, near_kept, near_sent, near_core = refs[:9]
    send_sem, recv_sem, result_send, result_recv, last_send, last_recv, last_others = refs[9:]
    grad_refs += [last_others.at[other] for other in range(trades)]
    step = pl.program_id(0)
    count = windows * pairs
    tensor = lax.axis_index("tensor")
    core_peer = {"core": 1 - lax.axis_index("core")}
    far_peer = {"x": 1 - lax.axis_index("x")}
    result_peer = {"tensor": flipped(tensor, lax.axis_size("tensor") // 2)}

    def trade(kind, number):
        source, target, peer = (
            (far_sent, far_core, core_peer),
            (far_kept, far_x, far_peer),
            (near_sent, near_core, core_peer),
        )[kind]
        return send(
            source.at[number],
            target.at[number],
            send_sem.at[kind, number],
            recv_sem.at[kind, number],
            peer,
        )

    def result_trade(w):
        return send(
            sent_refs[w], arrived_refs[w], result_send.at[w], result_recv.at[w], result_peer
        )

    others = [{"tensor": flipped(tensor, other + 1)} for other in range(trades)]

    def last_trade(other):
        return send(
            last_ref, last_others.at[other], last_send.at[other], last_recv.at[other], others[other]
        )

    @pl.when(step == 0)
    def _():
        greet([core_peer, far_peer] + others)
        for other in range(trades):
            last_trade(other).start()
        for w in range(windows):
            result_trade(w).start()

    def at_step(first, body):
        number = step - first

        @pl.when(jnp.logical_and(number >= 0, number < count))
        def _():
            body(number)

    def send_far(number):
        trade(0, number).start()

    def add_far(number):
        trade(0, number).wait_recv()
        far_kept[number] = (
            far_kept[number].astype(F32) + far_core[number].astype(F32)
        ).astype(BF16)

    def send_x(number):
        trade(1, number).start()

    def send_near(number):
        trade(2, number).start()

    def finish(number):
        trade(2, number).wait_recv()
        trade(1, number).wait_recv()
        total = (
            near_kept[number].astype(F32)
            + near_core[number].astype(F32)
            + far_x[number].astype(F32)
        )
        key = total[0]
        gk_ref[0] = (key * cos_ref[...] - swap_halves(key) * sin_ref[...]).astype(BF16)
        gv_ref[0] = total[1].astype(BF16)

    at_step(1, send_far)
    at_step(3, send_x)
    at_step(count + 1, send_near)
    at_step(2, add_far)
    at_step(count + 2, finish)

    for w in range(windows):

        @pl.when(step == w * pairs)
        def _(w=w):
            if w == windows - 1:
                for other in range(trades):
                    last_trade(other).wait_recv()
            at_row = 0
            for grad_ref in grad_refs[w * blocks : (w + 1) * blocks]:
                rows_ref[0, at_row : at_row + grad_ref.shape[0], :] = grad_ref[...]
                at_row += grad_ref.shape[0]

    def gradients(number, grad_out, kept, sent):
        query = q_ref[0]
        is_first = first_head(query.shape)
        overlap = (grad_out.astype(F32) * wide_ref[0]).T
        logs = log_ref[0]
        zero = jnp.zeros_like(query)
        own_q, own_do, row_log, row_sum = [], [], [], []
        for head in range(2):
            mine = is_first if head == 0 else jnp.logical_not(is_first)
            own_q.append(jnp.where(mine, query, zero))
            own_do.append(jnp.where(mine, grad_out, zero))
            at = head * HEAD_DIM
            row_log.append(logs[at : at + 1, :])
            row_sum.append(jnp.sum(overlap[at : at + HEAD_DIM, :], axis=0, keepdims=True))
        dq_parts = [None, None]
        for slot, target in enumerate((kept, sent)):
            key, value = slots_ref[0, slot, 0], slots_ref[0, slot, 1]
            key_turned = key.T
            grad_key, grad_value = None, None
            for head in range(2):
                scores = dot_nt(key, own_q[head])
                probs = jnp.exp2(scores * exp_scale - row_log[head])
                grad_probs = dot_nt(value, own_do[head])
                grad_scores = (probs * (grad_probs - row_sum[head])).astype(BF16)
                term_v = dot_nn(probs.astype(BF16), own_do[head])
                term_k = dot_nn(grad_scores, own_q[head])
                at = head * HEAD_DIM
                term_q = dot_nn(key_turned[at : at + HEAD_DIM, :], grad_scores)
                grad_value = term_v if grad_value is None else grad_value + term_v
                grad_key = term_k if grad_key is None else grad_key + term_k
                dq_parts[head] = term_q if dq_parts[head] is None else dq_parts[head] + term_q
            target[number, 0] = (grad_key * score_scale).astype(BF16)
            target[number, 1] = grad_value.astype(BF16)
        return jnp.concatenate(dq_parts, axis=0).T * score_scale

    @pl.when(step < count)
    def _():
        grad_out = dot_nn(rows_ref[0], w_ref[...]).astype(BF16)
        do_all[step] = grad_out
        dq_all[step] = gradients(step, grad_out, far_kept, far_sent)

    @pl.when(jnp.logical_and(step >= count, step < 2 * count))
    def _():
        number = step - count
        grad_query = dq_all[number] + gradients(number, do_all[number], near_kept, near_sent)
        gq_ref[0] = (grad_query * cos_ref[...] - swap_halves(grad_query) * sin_ref[...]).astype(
            BF16
        )

    @pl.when(step == pl.num_programs(0) - 1)
    def _():
        @pl.loop(0, count)
        def _(number):
            for kind in range(3):
                trade(kind, number).wait_send()

        for other in range(trades):
            last_trade(other).wait_send()
        for w in range(windows):
            result_trade(w).wait_send()
            result_trade(w).wait_recv()


def attend_back(queries, wide, logs, slots_all, grad_blocks, w_att, tables, sent):
    windows, rows, cols = queries.shape
    width = w_att.shape[0]
    pairs = cols // PAIR
    count = windows * pairs
    out_at = 3 * pairs
    score_scale = 1.0 / math.sqrt(HEAD_DIM)
    blocks = lax.axis_size("tensor")
    grads = [block for one in grad_blocks for block in one]
    last = grads[-1]

    def spot(lag, last=None):
        def index(i):
            number = jnp.clip(i - lag, 0, count - 1)
            return (number // pairs, 0, number % pairs)

        return pl.BlockSpec((1, rows, PAIR), index)

    def both(i):
        return jnp.minimum(i, 2 * count - 1) % count

    dma = pltpu.SemaphoreType.DMA
    piece = pltpu.VMEM((count, 2, rows, PAIR), BF16)
    anywhere = pl.BlockSpec(memory_space=pl.ANY)
    return run(
        functools.partial(
            attend_back_kernel, windows, pairs, blocks, score_scale * LOG2E, score_scale
        ),
        "attend_back",
        [shaped((windows, rows, cols), BF16)] * 3
        + [shaped((windows, rows, width), BF16)]
        + [shaped(one.shape, BF16) for one in sent],
        160 * windows * rows * rows * cols,
        [queries, wide, logs, slots_all, w_att, *tables, last, *grads, *sent],
        collective_id=2,
        grid=(2 * count + 2,),
        in_specs=[
            pl.BlockSpec((1, rows, PAIR), lambda i: (both(i) // pairs, 0, both(i) % pairs)),
            pl.BlockSpec((1, rows, PAIR), lambda i: (both(i) // pairs, 0, both(i) % pairs)),
            pl.BlockSpec((1, PAIR, rows), lambda i: (both(i) // pairs, both(i) % pairs, 0)),
            pl.BlockSpec(
                (1, 2, 2, rows, PAIR),
                lambda i: (both(i), jnp.where(i < count, 1, 0), 0, 0, 0),
            ),
            pl.BlockSpec((width, PAIR), lambda i: (0, out_at + jnp.minimum(i, count - 1) % pairs)),
            pl.BlockSpec((rows, PAIR), lambda i: (0, 0)),
            pl.BlockSpec((rows, PAIR), lambda i: (0, 0)),
            anywhere,
        ]
        + [pl.BlockSpec(block.shape, lambda i: (0, 0)) for block in grads]
        + [anywhere] * windows,
        out_specs=[
            spot(count),
            spot(count + 2),
            spot(count + 2),
            pl.BlockSpec((1, rows, width), lambda i: (jnp.minimum(i // pairs, windows - 1), 0, 0)),
        ]
        + [anywhere] * windows,
        scratch_shapes=[pltpu.VMEM((count, rows, PAIR), F32), pltpu.VMEM((count, rows, PAIR), BF16)]
        + [piece] * 7
        + [dma((3, count)), dma((3, count)), dma((windows,)), dma((windows,))]
        + [dma((blocks - 1,)), dma((blocks - 1,)), pltpu.VMEM((blocks - 1,) + last.shape, BF16)],
    )


def middle_kernel(x_ref, kept_ref, arrived_ref, norms_ref, middle_ref, normed_ref):
    middle = x_ref[...].astype(F32) + (kept_ref[...] + arrived_ref[...].astype(F32))
    middle_ref[...] = middle
    normed_ref[...] = (
        normalise(middle)[0] * norms_ref[2:3, :] + norms_ref[3:4, :]
    ).astype(BF16)


def second_norm(x_rows, kept, arrived, norms):
    args, in_specs = row_planes((x_rows, kept, arrived))
    rows, width = arrived.shape
    block = pl.BlockSpec((rows // NORM_BLOCKS, width), lambda i: (i, 0))
    return run(
        middle_kernel,
        "second_norm",
        [shaped((rows, width), F32), shaped((rows, width), BF16)],
        20 * rows * width,
        [*args, norms],
        grid=(NORM_BLOCKS,),
        in_specs=[*in_specs, full(*norms.shape)],
        out_specs=[block, block],
    )


def feed_kernel(blocks, swaps, first, slots, *refs):
    refs = list(refs)

    def take(count):
        taken = refs[:count]
        del refs[:count]
        return taken

    w_refs = take(3)
    if first:
        weight_ref, norms_ref = take(2)
        x_refs, cot_refs = take(blocks), take(blocks)
        sources = take(len(swaps))
        both_ref, wide_ref, total_ref, grad_ref = take(4)
    else:
        both_ref, total_in, grad_in, _ = take(4)
        sources = take(len(swaps))
        wide_ref, kept_ref, sent_ref, grad_kept_ref, grad_sent_ref = take(5)
    trades = tensor_trades(sources, take(len(swaps)), swaps, *take(2 if swaps else 0))
    block = pl.program_id(0)

    def weights_of(ref):
        if len(ref.shape) == 2:
            return ref[...]
        depths, cores, halves = ref.shape[:3]
        return jnp.concatenate(
            [
                ref[depth, core, half]
                for depth in range(depths)
                for half in range(halves)
                for core in range(cores)
            ],
            axis=0,
        )

    gate_w, up_w, down_w = [weights_of(ref) for ref in w_refs]

    @pl.when(block == 0)
    def _():
        start_trades(trades, swaps)

    if first:
        factor = factor_of(weight_ref, norms_ref, slots)
        for at in range(blocks):

            @pl.when(block == at)
            def _(at=at):
                both_ref[0] = x_refs[at][...]
                both_ref[1] = (cot_refs[at][...].astype(F32) * factor).astype(BF16)

    x_rows = both_ref[0]
    gate = dot_nn(x_rows, gate_w)
    up = dot_nn(x_rows, up_w)
    grad_hidden = dot_nn(both_ref[1], down_w)
    sig = jax.nn.sigmoid(gate)
    swish = gate * sig
    hidden = (swish * up).astype(BF16)
    grad_gate = (grad_hidden * up * sig * (1.0 + gate * (1.0 - sig))).astype(BF16)
    grad_up = (grad_hidden * swish).astype(BF16)
    wide_ref[0] = grad_gate
    wide_ref[1] = grad_up
    wide_ref[2] = hidden
    grad_total = dot_nt(grad_gate, gate_w) + dot_nt(grad_up, up_w)
    total = dot_nt(hidden, down_w)
    if first:
        total_ref[...] = total
        grad_ref[...] = grad_total
    else:
        total = total + total_in[...]
        grad_total = grad_total + grad_in[...]
        rows = total.shape[0]
        for at in range(blocks):

            @pl.when(block == at)
            def _(at=at):
                start = (at % (blocks // 2)) * rows
                if at < blocks // 2:
                    kept_ref[start : start + rows] = total
                    grad_kept_ref[start : start + rows] = grad_total
                else:
                    sent_ref[start : start + rows] = total.astype(BF16)
                    grad_sent_ref[start : start + rows] = grad_total.astype(BF16)

    @pl.when(block == blocks - 1)
    def _():
        for trade in trades:
            trade.wait()


def tensor_trades(sources, targets, masks, send_sem=None, recv_sem=None):
    tensor = lax.axis_index("tensor")
    trades = []
    for source, target, kinds in zip(sources, targets, masks):
        for number, mask in enumerate(kinds):
            sems = (send_sem.at[len(trades)], recv_sem.at[len(trades)])
            peer = {"tensor": flipped(tensor, mask)}
            trades.append(send(source, target.at[number], *sems, peer))
    return trades


def start_trades(trades, masks):
    if trades:
        tensor = lax.axis_index("tensor")
        peers = sorted({mask for kinds in masks for mask in kinds})
        greet([{"tensor": flipped(tensor, mask)} for mask in peers])
        for trade in trades:
            trade.start()


def feed_specs(weights):
    lead = weights.shape[:-1]
    part_cols = weights.shape[-1] // 3
    zeros = (0,) * len(lead)
    return part_cols, [
        pl.BlockSpec(lead + (part_cols,), functools.partial(lambda at, i: zeros + (at,), k))
        for k in range(3)
    ]


def full(*shape):
    return pl.BlockSpec(shape, lambda i: (0,) * len(shape))


def feed_call(name, collective_id, blocks, rows, width, part_cols, out, args, swaps, **options):
    masks = [kinds for _, kinds in swaps]
    anywhere = pl.BlockSpec(memory_space=pl.ANY)
    total = sum(len(kinds) for kinds in masks)
    out_shape, out_specs = out
    return run(
        functools.partial(
            feed_kernel, blocks, masks, name == "feed_first", options.pop("slots", None)
        ),
        name,
        out_shape + [shaped((len(kinds),) + array.shape, BF16) for array, kinds in swaps],
        12 * rows * width * part_cols,
        args + [array for array, _ in swaps],
        collective_id=collective_id if swaps else None,
        grid=(blocks,),
        in_specs=options.pop("in_specs") + [anywhere] * len(swaps),
        out_specs=out_specs + [anywhere] * len(swaps),
        scratch_shapes=[pltpu.SemaphoreType.DMA((total,))] * 2 if swaps else [],
        **options,
    )


def feed_first(x_blocks, cot_blocks, weight, norms, slots, weights, swaps=()):
    operands, specs = zip(*[plane(block) for block in (*x_blocks, *cot_blocks)])
    width = math.prod(weights.shape[:-1])
    blocks, own = len(x_blocks), specs[0].block_shape[-2]
    rows = blocks * own
    part_cols, w_specs = feed_specs(weights)
    row_block = pl.BlockSpec((own, width), lambda i: (i, 0))
    out_shape = [shaped((2, rows, width), BF16), shaped((3, rows, 2 * part_cols), BF16)]
    out_shape += [shaped((rows, width), F32)] * 2
    out_specs = [
        pl.BlockSpec((2, own, width), lambda i: (0, i, 0)),
        pl.BlockSpec((3, own, part_cols), lambda i: (0, i, 0)),
        row_block,
        row_block,
    ]
    return feed_call(
        "feed_first",
        6,
        blocks,
        rows,
        width,
        part_cols,
        (out_shape, out_specs),
        [weights, weights, weights, weight, norms, *operands],
        swaps,
        in_specs=w_specs + [SCALAR, full(*norms.shape)] + list(specs),
        slots=slots,
    )


def feed_last(both, wide, totals, weights, blocks, swaps=()):
    rows, width = both.shape[1:]
    own = rows // blocks
    part_cols, w_specs = feed_specs(weights)
    half = full(rows // 2, width)
    row_block = pl.BlockSpec((own, width), lambda i: (i, 0))
    out_shape = [shaped(wide.shape, BF16)]
    out_shape += [shaped((rows // 2, width), F32), shaped((rows // 2, width), BF16)] * 2
    return feed_call(
        "feed_last",
        5,
        blocks,
        rows,
        width,
        part_cols,
        (out_shape, [pl.BlockSpec((3, own, part_cols), lambda i: (0, i, 1))] + [half] * 4),
        [weights, weights, weights, both, *totals, wide],
        swaps,
        in_specs=w_specs
        + [pl.BlockSpec((2, own, width), lambda i: (0, i, 0)), row_block, row_block]
        + [pl.BlockSpec(memory_space=pl.ANY)],
        input_output_aliases={6: 0},
    )


def weights_kernel(windows, masks, *refs):
    lefts, rights = refs[:windows], refs[windows : 2 * windows]
    refs = refs[2 * windows :]
    sources, out_ref, targets = refs[: len(masks)], refs[len(masks)], refs[len(masks) + 1 :]
    at = pl.program_id(0)
    trades = tensor_trades(refs[: len(masks)], targets[: len(masks)], masks, *targets[len(masks) :])

    @pl.when(at == 0)
    def _():
        start_trades(trades, masks)

    total = None
    for left, right in zip(lefts, rights):
        term = dot_tn(left[...], right[...])
        total = term if total is None else total + term
    total = total.astype(BF16)
    depths, cores, halves, shard = out_ref.shape[:4]
    for depth in range(depths):
        for half in range(halves):
            for core in range(cores):
                start = ((depth * halves + half) * cores + core) * shard
                out_ref[depth, core, half] = total[start : start + shard]

    if masks:

        @pl.when(at == pl.num_programs(0) - 1)
        def _():
            for trade in trades:
                trade.wait()


def feed_weights(boths, wides, part, swaps):
    windows = len(boths)
    rows, width = boths[0].shape[1:]
    hidden_cols = wides[0].shape[2] // 2
    step = min(512, hidden_cols)
    steps = hidden_cols // step
    lead = (lax.axis_size("dp"), lax.axis_size("core"), lax.axis_size("x"))
    lead += (width // math.prod(lead),)
    masks = [kinds for _, kinds in swaps]
    anywhere = pl.BlockSpec(memory_space=pl.ANY)
    left = pl.BlockSpec((None, rows, width), lambda i: (i // (2 * steps), 0, 0))
    right = pl.BlockSpec((None, rows, step), lambda i: (i // steps, 0, part * steps + i % steps))
    total = sum(len(kinds) for kinds in masks)
    return run(
        functools.partial(weights_kernel, windows, masks),
        "feed_weights",
        [shaped(lead + (3 * hidden_cols,), BF16)]
        + [shaped((len(kinds),) + array.shape, BF16) for array, kinds in swaps],
        6 * windows * rows * width * hidden_cols,
        [*boths, *wides] + [array for array, _ in swaps],
        collective_id=(6 if part else 4) if swaps else None,
        grid=(3 * steps,),
        in_specs=[left] * windows + [right] * windows + [anywhere] * len(swaps),
        out_specs=[pl.BlockSpec(lead + (step,), lambda i: (0, 0, 0, 0, i))]
        + [anywhere] * len(swaps),
        scratch_shapes=[pltpu.SemaphoreType.DMA((total,))] * 2 if swaps else [],
    )


def norm_grad(kept_ref, arrived_ref, stream, gain, sums_ref):
    grad_normed = kept_ref[...] + arrived_ref[...].astype(F32)
    normed, inv_std = normalise(stream)
    sums = [
        jnp.sum(one, axis=0, keepdims=True) for one in (grad_normed * normed, grad_normed)
    ]

    @pl.when(pl.program_id(0) == 0)
    def _():
        for at, one in enumerate(sums):
            sums_ref[at : at + 1, :] = one

    @pl.when(pl.program_id(0) > 0)
    def _():
        for at, one in enumerate(sums):
            sums_ref[at : at + 1, :] += one

    return norm_back(grad_normed, normed, inv_std, gain)


def middle_back_kernel(
    slots, weight_ref, kept_ref, arrived_ref, middle_ref, cot_ref, norms_ref, grad_ref, low_ref, sums_ref
):
    grad_y = cot_ref[...].astype(F32) * factor_of(weight_ref, norms_ref, slots)
    grad = grad_y + norm_grad(
        kept_ref, arrived_ref, middle_ref[...], norms_ref[2:3, :], sums_ref
    )
    grad_ref[...] = grad
    low_ref[...] = grad.astype(BF16)


NORM_BLOCKS = 1


def row_planes(operands):
    pairs = []
    for one in operands:
        array, at = one if isinstance(one, tuple) else (one, ())
        rows, width = array.shape[len(at) :]
        pairs.append(plane(one, (rows // NORM_BLOCKS, width), lambda i: (i, 0)))
    return [list(part) for part in zip(*pairs)]


def second_norm_back(weight, slots, kept, arrived, middle, cot_rows, norms):
    args, in_specs = row_planes((kept, arrived, middle, cot_rows))
    rows, width = kept.shape
    block = pl.BlockSpec((rows // NORM_BLOCKS, width), lambda i: (i, 0))
    return run(
        functools.partial(middle_back_kernel, slots),
        "second_norm_back",
        [shaped(kept.shape, F32), shaped(kept.shape, BF16), shaped((2, width), F32)],
        40 * kept.size,
        [weight, *args, norms],
        grid=(NORM_BLOCKS,),
        in_specs=[SCALAR, *in_specs, full(*norms.shape)],
        out_specs=[block, block, full(2, width)],
    )


class SumRoute:
    def __init__(self, part, rows, core_in, mine, x_in, z_in, send_sem, recv_sem):
        self.read, self.rows = part, rows
        self.core_in, self.mine, self.x_in, self.z_in = core_in, mine, x_in, z_in
        self.send_sem, self.recv_sem = send_sem, recv_sem
        self.seq, self.depth = seq_index(), lax.axis_index("dp")
        self.peers = half_chip_peers()

    def place(self, number, other_core):
        seq = flipped(self.seq, 2) if number >= 4 else self.seq
        seq = flipped(seq, 1) if other_core else seq
        turn = (self.depth + number % 4) % lax.axis_size("dp")
        return pl.ds(
            pl.multiple_of((turn * seq_size() + seq) * self.rows, self.rows), self.rows
        )

    def message(self, number):
        if number < 8:
            source, target, peer = self.read.at[self.place(number, True), :], self.core_in, "core"
            target = target.at[number]
        elif number < 12:
            source, target, peer = self.mine.at[number - 4], self.x_in.at[number - 8], "far"
        else:
            turn, peer = ((2, "up"), (1, "up"), (3, "down"))[number - 12]
            source, target = self.mine.at[turn], self.z_in.at[number - 12]
        return send(
            source, target, self.send_sem.at[number], self.recv_sem.at[number], self.peers[peer]
        )

    def start(self, *numbers):
        for number in numbers:
            self.message(number).start()

    def add_core(self, number):
        self.message(number).wait_recv()
        own = self.read[self.place(number, False), :].astype(F32)
        self.mine[number] = (own + self.core_in[number].astype(F32)).astype(self.mine.dtype)

    def add_x(self, number):
        self.message(8 + number).wait_recv()
        total = self.mine[number].astype(F32) + self.x_in[number].astype(F32)
        self.mine[number] = total.astype(self.mine.dtype)

    def add_up(self):
        self.message(12).wait_recv()
        total = self.mine[1].astype(F32) + self.z_in[0].astype(F32)
        self.mine[1] = total.astype(self.mine.dtype)

    def total(self):
        self.message(13).wait_recv()
        self.message(14).wait_recv()
        return (
            self.mine[0].astype(F32) + self.z_in[1].astype(F32) + self.z_in[2].astype(F32)
        )

    def sent(self):
        for number in range(SUM_MESSAGES):
            self.message(number).wait_send()


SUM_MESSAGES = 15


def finish_kernel(windows, trades, score_cols, *refs):
    stages = (trades + 1).bit_length() - 1
    refs = list(refs)

    def take(count):
        taken = refs[:count]
        del refs[:count]
        return taken

    far_inputs = take(8)
    shard_ref = take(1)[0]
    norms_ref = take(1)[0]
    second_refs = take(windows)
    grad_refs = take(windows)
    weights_ref, vectors_ref, input_ref, shard_arrived = take(4)
    loads = take(8)
    grad_loads = take(windows)
    part, core_in, mine, x_in, z_in = take(5)
    tiles, own_tiles, arrived_tiles = take(3)
    small_core, small_mine, small_x, small_z = take(4)
    kept_all = take(windows)
    stage_sent = [take(stages) for _ in range(windows)]
    stage_arrived = [take(stages) for _ in range(windows)]
    load_sem, big_send, big_recv, small_send, small_recv = take(5)
    y_send, y_recv, tile_send, tile_recv, shard_sem = take(5)
    assert not refs
    (grad_q, grad_k, grad_v, normed, grad_mid, attended, w_qkv, tokens) = loads[:8]
    tensor = lax.axis_index("tensor")
    others = [{"tensor": flipped(tensor, other + 1)} for other in range(trades)]
    shards = lax.axis_size("dp") * seq_size()
    devices = shards * (trades + 1)
    group = tiles.shape[0] // shards
    width = part.shape[1]
    cols = score_cols
    rows = width // shards

    w_source = far_inputs[6].at[:, pl.ds(0, 3 * cols)]
    sources = [*far_inputs[:6], w_source, far_inputs[7]]
    sources += [*grad_refs]
    targets = [*loads, *grad_loads]
    copies = [
        pltpu.make_async_copy(source, target, load_sem.at[at])
        for at, (source, target) in enumerate(zip(sources, targets))
    ]
    order = [4, 5, 6, 0, 1, 2, 3, 7] + list(range(8, len(copies)))
    for at in order:
        copies[at].start()

    def block_route(block):
        return SumRoute(
            part.at[block],
            rows,
            core_in.at[block],
            mine.at[block],
            x_in.at[block],
            z_in.at[block],
            big_send.at[block],
            big_recv.at[block],
        )

    routes = [block_route(block) for block in range(4)]
    small = SumRoute(
        tiles, group, small_core, small_mine, small_x, small_z, small_send, small_recv
    )
    greet(list(small.peers.values()) + others)
    everything = (6, 7, 5, 4, 2, 3, 1, 0)

    def product(block, left, right):
        total = None
        for w in range(windows):
            term = dot_tn(left[w], right[w])
            total = term if total is None else total + term
        part[block] = total.astype(BF16)

    def y_trade(w, stage):
        return send(
            stage_sent[w][stage],
            stage_arrived[w][stage],
            y_send.at[w, stage],
            y_recv.at[w, stage],
            {"tensor": flipped(tensor, (trades + 1) >> (stage + 1))},
        )

    def turn_back(w):
        total = None
        for at, grad in enumerate((grad_q, grad_k, grad_v)):
            term = dot_nt(grad[w], w_qkv[:, at * cols : (at + 1) * cols])
            total = term if total is None else total + term
        half = total.shape[0] // 2
        kept_all[w][...] = total[:half]
        stage_sent[w][0][...] = total[half:].astype(BF16)

    def add_cores(route):
        for number in everything:
            route.add_core(number)

    def across(route):
        route.start(10, 11, 9, 8)

    def add_across(route):
        for number in (2, 3, 1, 0):
            route.add_x(number)

    count = shard_ref.shape[0] // 2
    far_rows = pl.ds(pl.multiple_of((1 - lax.axis_index("x")) * count, count), count)
    shard_trade = send(
        shard_ref.at[far_rows, :],
        shard_arrived,
        shard_sem.at[0],
        shard_sem.at[1],
        small.peers["far"],
    )
    shard_trade.start()
    copies[4].wait()
    copies[5].wait()
    product(3, grad_mid, attended)
    for at in (6, 0, 1, 2):
        copies[at].wait()
    routes[3].start(*everything)
    turn_back(0)
    add_cores(routes[3])
    y_trade(0, 0).start()
    across(routes[3])
    for w in range(1, windows):
        turn_back(w)
    copies[3].wait()
    product(0, normed, grad_q)
    for w in range(1, windows):
        y_trade(w, 0).start()
    routes[0].start(*everything)
    product(1, normed, grad_k)
    add_cores(routes[0])
    routes[1].start(*everything)
    across(routes[0])
    product(2, normed, grad_v)
    add_cores(routes[1])
    routes[2].start(*everything)
    across(routes[1])
    add_across(routes[3])
    add_cores(routes[2])
    routes[3].start(12, 14)
    across(routes[2])
    routes[3].add_up()
    for at in range(7, 8 + windows):
        copies[at].wait()
    sums = [None, None]

    def first_norm(w):
        kept = kept_all[w][...]
        for stage in range(stages):
            y_trade(w, stage).wait_recv()
            kept = kept + stage_arrived[w][stage][...].astype(F32)
            if stage + 1 < stages:
                half = kept.shape[0] // 2
                stage_sent[w][stage + 1][...] = kept[half:].astype(BF16)
                y_trade(w, stage + 1).start()
                kept = kept[:half]
        normed_rows, inv_std = normalise(tokens[w].astype(F32))
        for at, one in enumerate((kept * normed_rows, kept)):
            one = jnp.sum(one, axis=0, keepdims=True)
            sums[at] = one if sums[at] is None else sums[at] + one
        input_ref[w] = grad_loads[w][...] + norm_back(
            kept, normed_rows, inv_std, norms_ref[0:1, :]
        )

    first_norm(0)
    routes[3].start(13)
    add_across(routes[0])
    for w in range(1, windows):
        first_norm(w)
    routes[0].start(12, 14)
    first = jnp.concatenate(sums, axis=0)
    second = sum(ref[...] for ref in second_refs)
    span = width // devices
    tiles[...] = jnp.zeros_like(tiles)
    for device in range(devices):
        at = device * 8
        columns = slice(device * span, (device + 1) * span)
        tiles[at : at + 2, :span] = first[:, columns]
        tiles[at + 2 : at + 4, :span] = second[:, columns]
    add_across(routes[1])
    small.start(*everything)
    routes[0].add_up()
    routes[1].start(12, 14)
    add_cores(small)
    routes[0].start(13)
    across(small)
    add_across(routes[2])
    routes[1].add_up()
    routes[2].start(12, 14)
    add_across(small)
    routes[1].start(13)
    small.start(12, 14)
    for block in (3, 0):
        weights_ref[:, block * cols : (block + 1) * cols] = routes[block].total()
    small.add_up()
    routes[2].add_up()
    small.start(13)
    weights_ref[:, cols : 2 * cols] = routes[1].total()
    routes[2].start(13)
    own_tiles[...] = small.total()

    def tile_trade(other):
        place = pl.ds(pl.multiple_of(flipped(tensor, other + 1) * 8, 8), 8)
        return send(
            own_tiles.at[place, :],
            arrived_tiles.at[other],
            tile_send.at[other],
            tile_recv.at[other],
            others[other],
        )

    weights_ref[:, 2 * cols : 3 * cols] = routes[2].total()
    for other in range(trades):
        tile_trade(other).start()
    vectors = own_tiles[pl.ds(pl.multiple_of(tensor * 8, 8), 8), :]
    for other in range(trades):
        tile_trade(other).wait_recv()
        vectors = vectors + arrived_tiles[other]
    vectors_ref[...] = vectors
    shard_trade.wait()
    for route in (*routes, small):
        route.sent()
    for w in range(windows):
        for stage in range(stages):
            y_trade(w, stage).wait_send()
    for other in range(trades):
        tile_trade(other).wait_send()


def finish(
    grads,
    normed,
    grad_mid,
    attended,
    w_att,
    tokens,
    ffn_shard,
    norms,
    second_sums,
    grad_middles,
    trades,
):
    windows, rows, cols = grads[0].shape
    width = w_att.shape[0]
    own_rows = tokens.shape[1]
    shards = lax.axis_size("dp") * seq_size()
    shard = width // shards
    group = 8 * (trades + 1)
    stages = [rows >> (stage + 1) for stage in range((trades + 1).bit_length() - 1)]
    dma = pltpu.SemaphoreType.DMA
    anywhere = pl.BlockSpec(memory_space=pl.ANY)
    vmem = pl.BlockSpec(memory_space=pltpu.VMEM)
    far_inputs = [*grads, normed, grad_mid, attended, w_att, tokens]
    kinds = (8, 8, 4, 3)

    def like(array):
        return pltpu.VMEM(array.shape, array.dtype)

    loads = [like(array) for array in far_inputs]
    loads[6] = pltpu.VMEM((width, 3 * cols), BF16)
    return run(
        functools.partial(finish_kernel, windows, trades, cols),
        "finish",
        [
            shaped((shard, 4 * cols), F32),
            shaped((8, 128), F32),
            shaped((windows, own_rows, width), F32),
            shaped((ffn_shard.shape[0] // 2, ffn_shard.shape[1]), BF16),
        ],
        8 * windows * rows * width * cols + 6 * windows * rows * width * cols,
        [*far_inputs, ffn_shard, norms, *second_sums, *grad_middles],
        collective_id=3,
        in_specs=[anywhere] * 9
        + [vmem] * (1 + windows)
        + [anywhere] * windows,
        out_specs=[vmem] * 3 + [anywhere],
        scratch_shapes=loads
        + [like(array) for array in grad_middles]
        + [pltpu.VMEM((4, width, cols), BF16)]
        + [pltpu.VMEM((4, count, shard, cols), BF16) for count in kinds]
        + [
            pltpu.VMEM((shards * group, 128), F32),
            pltpu.VMEM((group, 128), F32),
            pltpu.VMEM((trades, 8, 128), F32),
        ]
        + [pltpu.VMEM((count, group, 128), F32) for count in kinds]
        + [pltpu.VMEM((rows // 2, width), F32)] * windows
        + [pltpu.VMEM((count, width), BF16) for count in stages] * (2 * windows)
        + [
            dma((8 + windows,)),
            dma((4, SUM_MESSAGES)),
            dma((4, SUM_MESSAGES)),
            dma((SUM_MESSAGES,)),
            dma((SUM_MESSAGES,)),
            dma((windows, len(stages))),
            dma((windows, len(stages))),
            dma((trades,)),
            dma((trades,)),
            dma((2,)),
        ],
    )


def result_kernel(windows, *refs):
    out_ref = refs[-1]
    for w in range(windows):
        middle_ref, kept_ref, arrived_ref = refs[3 * w : 3 * w + 3]
        out_ref[w] = (
            middle_ref[...] + (kept_ref[...] + arrived_ref[...].astype(F32))
        ).astype(BF16)


def results(parts):
    rows, width = parts[0][0].shape
    return run(
        functools.partial(result_kernel, len(parts)),
        "results",
        shaped((len(parts), rows, width), BF16),
        2 * len(parts) * rows * width,
        [array for part in parts for array in part],
    )


def local(
    tokens,
    cotangent,
    species,
    counts,
    species_scale,
    norm1_gain,
    norm1_bias,
    w_query,
    w_key,
    w_value,
    w_out,
    norm2_gain,
    norm2_bias,
    w_gate,
    w_up,
    w_down,
):
    windows_here, own_rows, model_width = tokens.shape
    tensor_size = lax.axis_size("tensor")
    block_rows = own_rows * tensor_size
    head_cols = w_query.shape[1]
    hidden_cols = w_gate.shape[1]
    shards = ("dp", "x", "core")

    labels = lax.broadcasted_iota(jnp.int32, (windows_here, species_scale.shape[0]), 1)
    chosen = jnp.sum(jnp.where(species[:, None] == labels, species_scale[None, :], 0.0), axis=1)
    weighted = counts.astype(F32) * chosen

    lanes = jnp.zeros((8, 128), F32)
    vectors = jnp.stack([norm1_gain, norm1_bias, norm2_gain, norm2_bias])
    tile = lanes.at[:4, : vectors.shape[1]].set(vectors).at[4, :].set(jnp.sum(weighted))
    part = hidden_cols // 2
    turned = w_down.T
    first_ffn = jnp.concatenate([w_gate[:, :part], w_up[:, :part], turned[:, :part]], axis=1)
    last_ffn = jnp.concatenate([w_gate[:, part:], w_up[:, part:], turned[:, part:]], axis=1)
    upper = lax.axis_index("x") == 1

    def gather_ffn(own, across):
        pair = jnp.where(
            upper,
            jnp.concatenate([across, own], axis=0),
            jnp.concatenate([own, across], axis=0),
        )
        whole = lax.all_gather(pair, ("dp", "core"), axis=0, tiled=True)
        return whole.reshape(
            lax.axis_size("dp"), lax.axis_size("core"), lax.axis_size("x"), -1, whole.shape[1]
        )

    first_ffn = lax.all_gather(first_ffn, shards, axis=0, tiled=True)
    last_across = swap(last_ffn, "x", 1)
    w_att, norms, arrived_tokens, cosine, sine = gather(
        jnp.concatenate([w_query, w_key, w_value, w_out.T], axis=1),
        tile,
        tokens,
        tensor_size - 1,
    )
    slots = float(windows_here * lax.axis_size("dp"))

    windows = range(windows_here)
    weights = [weighted[w].reshape(1, 1) for w in windows]

    token_blocks = [tokens] + [arrived_tokens[other] for other in range(tensor_size - 1)]
    normed_rows, queries, own_kv = project(token_blocks, norms, w_att, cosine, sine)
    last_ffn = gather_ffn(last_ffn, hold(last_across, w_att))
    (
        attended,
        wide_attended,
        logs,
        kept_all,
        sent_all,
        slots_all,
        cots,
        first_middle,
        first_normed,
        first_others,
    ) = attend(queries, own_kv, w_att, cotangent, tokens, norms, tensor_size - 1)
    others = range(tensor_size - 1)
    cot_blocks = [
        [(cotangent, (w,))] + [(cots, (other, w)) for other in others] for w in windows
    ]
    middles = [first_middle]

    def reduce_ffn(partial):
        partial = partial.reshape(-1, partial.shape[-1])
        mine = lax.psum_scatter(partial, ("dp", "core"), scatter_dimension=0, tiled=True)
        count = mine.shape[0] // 2
        kept = jnp.where(upper, mine[count:], mine[:count])
        return kept, mine

    blocks = [first_normed] + [first_others[other] for other in others]
    begun, fed, lows, arrived_lows = [], [], [], []
    grad_middles, second_sums = [], []
    masks = [other + 1 for other in others]

    def through_second_norm(w, kept, arrived):
        grad_middle, low, sums = second_norm_back(
            weights[w], slots, kept, arrived, middles[w], (cotangent, (w,)), norms
        )
        grad_middles.append(grad_middle)
        second_sums.append(sums)
        return low

    for w in windows:
        begun.append(
            feed_first(blocks, cot_blocks[w], weights[w], norms, slots, first_ffn)
        )
        if w + 1 < windows_here:
            kept, arrived = scatter_pair(kept_all[w], sent_all[w], "tensor")
            middle, normed_mid = second_norm(
                (tokens, (w + 1,)), hold(kept, begun[-1]), arrived, norms
            )
            middles.append(middle)
            blocks = hold(spread(normed_mid, "tensor"), fed)
            after = normed_mid
        else:
            g_first_part, *arrived = feed_weights(
                [one[0] for one in begun],
                [one[0] for one in fed] + [one[1] for one in begun[len(fed) :]],
                0,
                [(one[4], [tensor_size // 2]) for one in fed],
            )
            first_kept, first_sent = reduce_ffn(g_first_part)
            after = g_first_part
        swaps = ()
        if w > 0:
            kept, arrived = later_pair(fed[-1][3], arrived[-1][0], "tensor")
            low = through_second_norm(w - 1, hold(kept, g_first_part), arrived)
            lows.append(low)
            swaps = [(low, masks)]
            after = low
        both, wide, *totals = hold(begun[w], after)
        ended = feed_last(both, wide, totals, last_ffn, tensor_size, swaps)
        fed.append(ended[:5])
        arrived_lows += ended[5:]
        if w + 1 < windows_here:
            blocks = hold(blocks, ended[3])
    g_ffn_part, arrived = feed_weights(
        [one[0] for one in begun],
        [one[0] for one in fed],
        1,
        [(fed[-1][4], [tensor_size // 2])],
    )
    last_kept, last_sent = reduce_ffn(g_ffn_part)
    kept, arrived = later_pair(fed[-1][3], arrived[0], "tensor")
    last_low = through_second_norm(windows[-1], hold(kept, g_ffn_part), arrived)
    grad_mid_blocks = [
        [low] + [arrived[other] for other in others] for low, arrived in zip(lows, arrived_lows)
    ] + [[last_low]]

    grad_q, grad_k, grad_v, grad_mid_rows, *arrived_results = attend_back(
        hold(queries, g_ffn_part),
        wide_attended,
        logs,
        slots_all,
        grad_mid_blocks,
        w_att,
        (cosine, sine),
        [fed[w][2] for w in windows],
    )
    parts = [
        (middles[w], *later_pair(fed[w][1], arrived_results[w], "tensor")) for w in windows
    ]

    g_att, vectors, input_grad, first_arrived = finish(
        (grad_q, grad_k, grad_v),
        normed_rows,
        grad_mid_rows,
        attended,
        w_att,
        tokens,
        first_sent,
        norms,
        second_sums,
        grad_middles,
        tensor_size - 1,
    )
    output = results(hold(parts, input_grad))
    g_first = first_kept.astype(F32) + first_arrived.astype(F32)
    last_sent = hold(last_sent, input_grad)
    count = last_sent.shape[0] // 2
    last_sent = jnp.where(upper, last_sent[:count], last_sent[count:])
    last_arrived = swap(last_sent, "x", 1)
    g_last = last_kept.astype(F32) + last_arrived.astype(F32)
    norm_sums = vectors[:4, : norm1_gain.shape[0]]
    ffn_grads = [
        jnp.concatenate(
            [g_first[:, at * part : (at + 1) * part], g_last[:, at * part : (at + 1) * part]],
            axis=1,
        )
        for at in range(3)
    ]

    return (
        output,
        input_grad,
        norm_sums[0],
        norm_sums[1],
        g_att[:, :head_cols],
        g_att[:, head_cols : 2 * head_cols],
        g_att[:, 2 * head_cols : 3 * head_cols],
        g_att[:, 3 * head_cols :].T,
        norm_sums[2],
        norm_sums[3],
        ffn_grads[0],
        ffn_grads[1],
        ffn_grads[2].T,
    )


def solution(mesh):
    depth, seq, tensor = mesh.devices.shape
    finer = jax.sharding.Mesh(
        mesh.devices.reshape(depth, seq // 2, 2, tensor), ("dp", "x", "core", "tensor")
    )
    rows = P("dp", ("x", "core", "tensor"), None)
    vector = P(("dp", "x", "core", "tensor"))
    tall = P(("dp", "x", "core"), "tensor")
    flat = P("tensor", ("dp", "x", "core"))
    return jax.shard_map(
        local,
        mesh=finer,
        in_specs=(
            rows, rows, P("dp"), P("dp"), P(), vector, vector,
            tall, tall, tall, flat, vector, vector, tall, tall, flat,
        ),
        out_specs=(
            rows, rows, vector, vector, tall, tall, tall, flat,
            vector, vector, tall, tall, flat,
        ),
        check_vma=False,
    )
```

```python
import functools
import math

import jax
import jax.numpy as jnp
from jax import lax
from jax.experimental import pallas as pl
from jax.experimental.pallas import tpu as pltpu
from jax.sharding import PartitionSpec as P

HEAD_DIM = 64
EPSILON = 1e-05
ROPE_BASE = 10000.0
PAIR = 2 * HEAD_DIM
LOG2E = math.log2(math.e)
BF16 = jnp.bfloat16
F32 = jnp.float32
VMEM_BYTES = 56 * 1024 * 1024
MESH = pl.DeviceIdType.MESH


def dot_nn(left, right):
    return lax.dot_general(left, right, (((1,), (0,)), ((), ())), preferred_element_type=F32)


def dot_nt(left, right):
    return lax.dot_general(left, right, (((1,), (1,)), ((), ())), preferred_element_type=F32)


def dot_tn(left, right):
    return lax.dot_general(left, right, (((0,), (0,)), ((), ())), preferred_element_type=F32)


def swap(array, axis, bit):
    size = lax.axis_size(axis)
    return lax.ppermute(array, axis, [(i, i ^ bit) for i in range(size)])


def spread(array, axis):
    blocks = [array]
    bit = 1
    while bit < lax.axis_size(axis):
        blocks = blocks + [swap(block, axis, bit) for block in blocks]
        bit *= 2
    return blocks


def scatter_pair(kept, sent, axis):
    return later_pair(kept, swap(sent, axis, lax.axis_size(axis) // 2), axis)


def later_pair(kept, arrived, axis):
    bit = lax.axis_size(axis) // 2
    while bit > 1:
        partial = kept + arrived.astype(F32)
        bit //= 2
        rows = partial.shape[0] // 2
        kept, arrived = partial[:rows], swap(partial[rows:].astype(BF16), axis, bit)
    return kept, arrived


def seq_size():
    return lax.axis_size("x") * lax.axis_size("core")


def seq_index():
    return lax.axis_index("x") * lax.axis_size("core") + lax.axis_index("core")


def hold(values, *others):
    return lax.optimization_barrier((values, others))[0]


def run(kernel, name, out_shape, flops, args, collective_id=None, **options):
    trading = {} if collective_id is None else dict(collective_id=collective_id, has_side_effects=True)
    moved = sum(math.prod(array.shape) * array.dtype.itemsize for array in args)
    outs = out_shape if isinstance(out_shape, list) else [out_shape]
    moved += sum(math.prod(array.shape) * array.dtype.itemsize for array in outs)
    return pl.pallas_call(
        kernel,
        out_shape=out_shape,
        compiler_params=pltpu.CompilerParams(vmem_limit_bytes=VMEM_BYTES, **trading),
        cost_estimate=pl.CostEstimate(
            flops=int(flops), bytes_accessed=int(moved), transcendentals=0
        ),
        name=name,
        **options,
    )(*args)


def shaped(shape, dtype):
    return jax.ShapeDtypeStruct(shape, dtype)


SCALAR = pl.BlockSpec(memory_space=pltpu.SMEM)


def plane(operand, block=None, index=None):
    array, at = operand if isinstance(operand, tuple) else (operand, ())
    shape = array.shape[len(at) :] if block is None else block
    place = (lambda *i: (0,) * len(shape)) if index is None else index
    return array, pl.BlockSpec((None,) * len(at) + tuple(shape), lambda *i: at + place(*i))


def normalise(stream):
    row_mean = jnp.mean(stream, axis=-1, keepdims=True)
    centred = stream - row_mean
    variance = jnp.mean(centred * centred, axis=-1, keepdims=True)
    inv_std = lax.rsqrt(variance + EPSILON)
    return centred * inv_std, inv_std


def norm_back(grad_normed, normed, inv_std, norm_gain):
    scaled_grad = grad_normed * norm_gain
    return inv_std * (
        scaled_grad
        - jnp.mean(scaled_grad, axis=-1, keepdims=True)
        - normed * jnp.mean(scaled_grad * normed, axis=-1, keepdims=True)
    )


def factor_of(weight_ref, norms_ref, slots):
    return weight_ref[0, 0] * slots / norms_ref[4:5, 0:1]


def first_head(shape):
    return lax.broadcasted_iota(jnp.int32, shape, 1) % PAIR < HEAD_DIM


def swap_halves(values):
    half = HEAD_DIM // 2
    lane = lax.broadcasted_iota(jnp.int32, values.shape, 1)
    ahead = pltpu.roll(values, PAIR - half, 1)
    behind = pltpu.roll(values, half, 1)
    return jnp.where(lane % HEAD_DIM < half, ahead, behind)


def project_kernel(blocks, norms_ref, w_ref, cos_ref, sin_ref, *refs):
    x_refs = refs[:blocks]
    normed_ref, q_ref, kv_ref = refs[blocks:]
    cols = q_ref.shape[2]
    gain, bias = norms_ref[0:1, :], norms_ref[1:2, :]
    at_row = 0
    for x_ref in x_refs:
        rows = slice(at_row, at_row + x_ref.shape[1])
        at_row += x_ref.shape[1]
        normed = (normalise(x_ref[0].astype(F32))[0] * gain + bias).astype(BF16)
        normed_ref[0, rows, :] = normed
        cosine, sine = cos_ref[rows, :], sin_ref[rows, :]
        query = dot_nn(normed, w_ref[:, :cols])
        key = dot_nn(normed, w_ref[:, cols : 2 * cols])
        value = dot_nn(normed, w_ref[:, 2 * cols : 3 * cols]).astype(BF16)
        for at in range(0, cols, PAIR):
            part, pair = slice(at, at + PAIR), at // PAIR
            one = query[:, part]
            q_ref[0, rows, part] = (one * cosine + swap_halves(one) * sine).astype(BF16)
            one = key[:, part]
            kv_ref[0, pair, 0, rows, :] = (one * cosine + swap_halves(one) * sine).astype(BF16)
            kv_ref[0, pair, 1, rows, :] = value[:, part]


def project(x_blocks, norms, w_att, cosine, sine):
    windows = x_blocks[0].shape[0]
    width, cols = w_att.shape[0], w_att.shape[1] // 4
    rows = sum(block.shape[1] for block in x_blocks)
    pieces = (cols // PAIR, 2, rows, PAIR)
    args = [norms, w_att, cosine, sine, *x_blocks]
    return run(
        functools.partial(project_kernel, len(x_blocks)),
        "project",
        [
            shaped((windows, rows, width), BF16),
            shaped((windows, rows, cols), BF16),
            shaped((windows,) + pieces, BF16),
        ],
        6 * windows * rows * width * cols,
        args,
        grid=(windows,),
        in_specs=[pl.BlockSpec(array.shape, lambda i: (0, 0)) for array in args[:4]]
        + [pl.BlockSpec((1,) + block.shape[1:], lambda i: (i, 0, 0)) for block in x_blocks],
        out_specs=[
            pl.BlockSpec((1, rows, width), lambda i: (i, 0, 0)),
            pl.BlockSpec((1, rows, cols), lambda i: (i, 0, 0)),
            pl.BlockSpec((1,) + pieces, lambda i: (i, 0, 0, 0, 0)),
        ],
    )


def flipped(index, mask):
    bit = 1
    while bit <= mask:
        if mask & bit:
            index = index + bit - 2 * bit * ((index // bit) % 2)
        bit *= 2
    return index


def greet(peers):
    barrier = pltpu.get_barrier_semaphore()
    for peer in peers:
        pl.semaphore_signal(barrier, inc=1, device_id=peer, device_id_type=MESH)
    pl.semaphore_wait(barrier, len(peers))


def send(source, target, send_sem, recv_sem, peer):
    return pltpu.make_async_remote_copy(
        src_ref=source,
        dst_ref=target,
        send_sem=send_sem,
        recv_sem=recv_sem,
        device_id=peer,
        device_id_type=MESH,
    )


def half_chip_peers():
    depth = lax.axis_index("dp")
    size = lax.axis_size("dp")
    return {
        "far": {"x": 1 - lax.axis_index("x")},
        "up": {"dp": (depth + 1) % size},
        "down": {"dp": (depth + size - 1) % size},
        "core": {"core": 1 - lax.axis_index("core")},
    }


class Route:
    PARTS = ((0, 0), (3, 0), (1, 0), (2, 0), (0, 1), (3, 1), (1, 1), (2, 1))

    def __init__(self, whole, rows, send_sem, recv_sem, own):
        self.whole, self.rows, self.own = whole, rows, own
        self.send_sem, self.recv_sem = send_sem, recv_sem
        self.seq, self.depth = seq_index(), lax.axis_index("dp")
        self.peers = half_chip_peers()

    def part(self, place):
        turn, other = place
        seq = flipped(self.seq, 2) if other else self.seq
        at = (((self.depth + turn) % lax.axis_size("dp")) * seq_size() + seq) * self.rows
        return self.whole.at[pl.ds(pl.multiple_of(at, self.rows), self.rows), :]

    def message(self, number):
        if number >= 7:
            place, peer = self.PARTS[number - 7], "core"
        else:
            place, peer = (
                ((0, 0), "up"),
                ((0, 0), "down"),
                ((3, 0), "up"),
                ((0, 0), "far"),
                ((3, 0), "far"),
                ((1, 0), "far"),
                ((2, 0), "far"),
            )[number]
        target = self.part(place)
        return send(
            self.own if place == (0, 0) else target,
            target,
            self.send_sem.at[number],
            self.recv_sem.at[number],
            self.peers[peer],
        )

    def start(self, *numbers):
        for number in numbers:
            self.message(number).start()

    def arrived(self, *numbers):
        for number in numbers:
            self.message(number).wait_recv()

    def sent(self, *numbers):
        for number in numbers:
            self.message(number).wait_send()


MESSAGES = 15


def tables(cos_ref, sin_ref, trades):
    own_rows = cos_ref.shape[0] // (trades + 1)
    tensor = lax.axis_index("tensor")
    half = HEAD_DIM // 2
    shape = (own_rows, PAIR)
    lane = lax.broadcasted_iota(jnp.int32, shape, 1)
    exponent = -(math.log(ROPE_BASE) * 2.0 / HEAD_DIM) * (lane % half).astype(F32)
    inverse = jnp.exp(exponent)
    row = lax.broadcasted_iota(jnp.int32, shape, 0)
    for other in range(trades + 1):
        start = (seq_index() * (trades + 1) + flipped(tensor, other)) * own_rows
        phase = (row + start).astype(F32) * inverse
        rows = slice(other * own_rows, (other + 1) * own_rows)
        cos_ref[rows, :] = jnp.cos(phase)
        sine = jnp.sin(phase)
        sin_ref[rows, :] = jnp.where(lane % HEAD_DIM < half, -sine, sine)


def gather_kernel(trades, att_ref, tile_ref, tokens_ref, *refs):
    att_all, norms_ref, tokens_all, cos_ref, sin_ref = refs[:5]
    tiles, pair_of_tiles = refs[5:7]
    att_send, att_recv, tile_send, tile_recv = refs[7:11]
    own_sem, tokens_send, tokens_recv, pair_send, pair_recv = refs[11:]
    tensor = lax.axis_index("tensor")
    others = [{"tensor": flipped(tensor, other + 1)} for other in range(trades)]
    att = Route(att_all, att_ref.shape[0], att_send, att_recv, att_ref)
    tile_rows = tile_ref.shape[0]
    small = Route(tiles, pair_of_tiles.shape[0], tile_send, tile_recv, pair_of_tiles)

    def tokens_trade(other):
        return send(
            tokens_ref,
            tokens_all.at[other],
            tokens_send.at[other],
            tokens_recv.at[other],
            others[other],
        )

    own_rows = pl.ds(pl.multiple_of(tensor * tile_rows, tile_rows), tile_rows)

    def pair_trade(other):
        return send(
            tile_ref,
            pair_of_tiles.at[own_rows, :],
            pair_send.at[other],
            pair_recv.at[other],
            others[other],
        )

    own_copies = [
        pltpu.make_async_copy(att_ref, att.part((0, 0)), own_sem.at[0]),
        pltpu.make_async_copy(tile_ref, pair_of_tiles.at[own_rows, :], own_sem.at[1]),
        pltpu.make_async_copy(pair_of_tiles, small.part((0, 0)), own_sem.at[2]),
    ]

    greet(list(att.peers.values()) + others)
    for other in range(trades):
        pair_trade(other).start()
    own_copies[1].start()
    att.start(0, 1, 3, 7)
    own_copies[1].wait()
    for other in range(trades):
        pair_trade(other).wait_recv()
    small.start(0, 1, 3, 7)
    own_copies[0].start()
    own_copies[2].start()
    for other in range(trades):
        tokens_trade(other).start()
    tables(cos_ref, sin_ref, trades)
    for route in (small, att):
        route.arrived(0)
        route.start(2, 4, 8)
    for route in (small, att):
        route.arrived(3)
        route.start(11)
    for route in (small, att):
        route.arrived(1)
        route.start(5, 9)
    for route in (small, att):
        route.arrived(2)
        route.start(6, 10)
    for route in (small, att):
        route.arrived(4)
        route.start(12)
        route.arrived(5)
        route.start(13)
        route.arrived(6)
        route.start(14)
    for route in (small, att):
        route.arrived(*range(7, MESSAGES))
    own_copies[2].wait()
    shard = norms_ref.shape[1] // (tiles.shape[0] // tile_rows)
    total = None
    for device in range(tiles.shape[0] // tile_rows):
        tile = tiles[device * tile_rows : (device + 1) * tile_rows, :]
        norms_ref[:, device * shard : (device + 1) * shard] = tile[:, :shard]
    for depth in range(lax.axis_size("dp")):
        at = depth * (tiles.shape[0] // lax.axis_size("dp"))
        one = tiles[at + 4 : at + 5, :]
        total = one if total is None else total + one
    norms_ref[4:5, : total.shape[1]] = total
    for route in (att, small):
        route.sent(*range(MESSAGES))
    own_copies[0].wait()
    for other in range(trades):
        pair_trade(other).wait_send()
        tokens_trade(other).wait_recv()
        tokens_trade(other).wait_send()


def gather(att, tile, tokens, trades):
    count = lax.axis_size("dp") * seq_size()
    rows = att.shape[0]
    group = tile.shape[0] * (trades + 1)
    anywhere = pl.BlockSpec(memory_space=pl.ANY)
    vmem = pl.BlockSpec(memory_space=pltpu.VMEM)
    dma = pltpu.SemaphoreType.DMA
    return run(
        functools.partial(gather_kernel, trades),
        "gather",
        [
            shaped((count * rows, att.shape[1]), BF16),
            shaped((tile.shape[0], count * rows), F32),
            shaped((trades,) + tokens.shape, BF16),
        ]
        + [shaped((tokens.shape[1] * (trades + 1), PAIR), F32)] * 2,
        0,
        [att, tile, tokens],
        collective_id=1,
        in_specs=[vmem, vmem, anywhere],
        out_specs=[anywhere, vmem, anywhere, vmem, vmem],
        scratch_shapes=[pltpu.VMEM((count * group, 128), F32), pltpu.VMEM((group, 128), F32)]
        + [dma((MESSAGES,))] * 4
        + [dma((3,)), dma((trades,)), dma((trades,)), dma((trades,)), dma((trades,))],
    )


def attend_kernel(windows, pairs, trades, exp_scale, *refs):
    stages = (trades + 1).bit_length() - 1
    q_ref, w_ref, kv_ref, cot_ref, x_ref, norms_ref = refs[:6]
    low_ref, wide_ref, log_ref, kept_ref, sent_ref, slots_ref, cots_ref = refs[6:13]
    middle_ref, normed_ref, others_ref = refs[13:16]
    slots, acc_all, top_all, total_all, mixed_rows = refs[16:21]
    own_sem, send_sem, recv_sem, save_sem, cot_send, cot_recv = refs[21:27]
    early_kept, early_normed, early_sem, early_recv, normed_sem, normed_recv = refs[27:33]
    early_sent, early_arrived = refs[33 : 33 + stages], refs[33 + stages :]
    step = pl.program_id(0)
    near_steps = windows * pairs
    steps = 2 * near_steps
    turn = step % (2 * pairs)
    is_far = turn >= pairs
    number = step // (2 * pairs) * pairs + turn % pairs
    tensor = lax.axis_index("tensor")
    core_peer = {"core": 1 - lax.axis_index("core")}
    far_peer = {"x": 1 - lax.axis_index("x")}
    cot_peers = [{"tensor": flipped(tensor, other + 1)} for other in range(trades)]

    def piece(number):
        return kv_ref.at[number // pairs, number % pairs]

    def own_copy(number):
        return pltpu.make_async_copy(piece(number), slots.at[number, 0], own_sem.at[number])

    def trade(number, slot):
        peer = far_peer if slot == 2 else core_peer
        source = slots.at[number, 2] if slot == 3 else piece(number)
        return send(
            source,
            slots.at[number, slot],
            send_sem.at[number, slot - 1],
            recv_sem.at[number, slot - 1],
            peer,
        )

    def cot_trade(other):
        return send(
            cot_ref, cots_ref.at[other], cot_send.at[other], cot_recv.at[other], cot_peers[other]
        )

    def early_trade(stage):
        return send(
            early_sent[stage],
            early_arrived[stage],
            early_sem.at[stage],
            early_recv.at[stage],
            {"tensor": flipped(tensor, (trades + 1) >> (stage + 1))},
        )

    def normed_trade(other):
        return send(
            early_normed,
            others_ref.at[other],
            normed_sem.at[other],
            normed_recv.at[other],
            cot_peers[other],
        )

    def save(number, slot):
        return pltpu.make_async_copy(
            slots.at[number, slot], slots_ref.at[number, slot], save_sem.at[number, slot]
        )

    @pl.when(step == 0)
    def _():
        greet([core_peer, far_peer] + cot_peers)

        @pl.loop(0, near_steps)
        def _(number):
            own_copy(number).start()
            trade(number, 1).start()
            trade(number, 2).start()

        for other in range(trades):
            cot_trade(other).start()

    @pl.when(step == 2 * pairs)
    def _():
        early_trade(0).start()

    @pl.when(step == 3 * pairs)
    def _():
        kept = early_kept[...]
        for stage in range(stages):
            early_trade(stage).wait_recv()
            kept = kept + early_arrived[stage][...].astype(F32)
            if stage + 1 < stages:
                half = kept.shape[0] // 2
                early_sent[stage + 1][...] = kept[half:].astype(BF16)
                early_trade(stage + 1).start()
                kept = kept[:half]
        middle = x_ref[...].astype(F32) + kept
        middle_ref[...] = middle
        normed = (normalise(middle)[0] * norms_ref[2:3, :] + norms_ref[3:4, :]).astype(BF16)
        normed_ref[...] = normed
        early_normed[...] = normed

    @pl.when(step == 3 * pairs + 1)
    def _():
        for other in range(trades):
            normed_trade(other).start()

    relayed = step // (2 * pairs) * pairs + turn - (pairs - 1)

    @pl.when(jnp.logical_and(turn >= pairs - 1, turn < 2 * pairs - 1))
    def _():
        trade(relayed, 2).wait_recv()
        trade(relayed, 3).start()
        save(relayed, 2).start()

    @pl.when(jnp.logical_not(is_far))
    def _():
        own_copy(number).wait()
        trade(number, 1).wait_recv()
        save(number, 0).start()
        save(number, 1).start()
        acc_all[number] = jnp.zeros(acc_all.shape[1:], F32)
        total_all[number] = jnp.zeros(acc_all.shape[1:], F32)
        top_all[number] = jnp.full(acc_all.shape[1:], -1e30, F32)

    @pl.when(is_far)
    def _():
        trade(number, 3).wait_recv()
        save(number, 3).start()

    query = q_ref[0]
    is_first = first_head(query.shape)
    base = jnp.where(is_far, 2, 0)
    carried_top = top_all[number]
    outs, tops = [], []
    for head in range(2):
        mine = is_first if head == 0 else jnp.logical_not(is_first)
        own_query = jnp.where(mine, query, jnp.zeros_like(query))
        scores = [dot_nt(own_query, slots[number, base + slot, 0]) for slot in range(2)]
        at = head * HEAD_DIM
        top = carried_top[:, at : at + 1]
        for one in scores:
            top = jnp.maximum(top, one.max(axis=1, keepdims=True))
        shift = top * exp_scale
        mixed = None
        for slot, one in enumerate(scores):
            weight = jnp.exp2(one * exp_scale - shift).astype(BF16)
            value = slots[number, base + slot, 1]
            lane_first = first_head(value.shape)
            lane_mine = lane_first if head == 0 else jnp.logical_not(lane_first)
            term = dot_nn(weight, jnp.where(lane_mine, value, jnp.ones_like(value)))
            mixed = term if mixed is None else mixed + term
        outs.append(mixed)
        tops.append(jnp.broadcast_to(top, mixed.shape))
    top = jnp.where(is_first, tops[0], tops[1])
    fade = jnp.exp2((carried_top - top) * exp_scale)
    acc = jnp.where(is_first, outs[0], outs[1]) + acc_all[number] * fade
    total = pltpu.roll(jnp.where(is_first, outs[1], outs[0]), HEAD_DIM, 1) + total_all[number] * fade

    @pl.when(jnp.logical_not(is_far))
    def _():
        acc_all[number] = acc
        top_all[number] = top
        total_all[number] = total

    @pl.when(is_far)
    def _():
        attended = acc / total
        low = attended.astype(BF16)
        low_ref[0] = low
        wide_ref[0] = attended
        log_ref[0] = (top * exp_scale + jnp.log2(total)).T
        term = dot_nt(low, w_ref[...])
        pair = number % pairs

        @pl.when(pair == 0)
        def _():
            mixed_rows[...] = term

        @pl.when(pair > 0)
        def _():
            mixed_rows[...] += term

        @pl.when(jnp.logical_and(pair == pairs - 1, number >= pairs))
        def _():
            half = kept_ref.shape[1]
            kept_ref[0] = mixed_rows[:half]
            sent_ref[0] = mixed_rows[half:].astype(BF16)

        @pl.when(number == pairs - 1)
        def _():
            half = kept_ref.shape[1]
            early_kept[...] = mixed_rows[:half]
            early_sent[0][...] = mixed_rows[half:].astype(BF16)

    @pl.when(step == steps - 1)
    def _():
        @pl.loop(0, near_steps)
        def _(number):
            for slot in range(1, 4):
                trade(number, slot).wait_send()
            for slot in range(4):
                save(number, slot).wait()

        for stage in range(stages):
            early_trade(stage).wait_send()
        for other in range(trades):
            cot_trade(other).wait_send()
            cot_trade(other).wait_recv()
            normed_trade(other).wait_send()
            normed_trade(other).wait_recv()


def attend(queries, own_kv, w_att, cotangent, tokens, norms, trades):
    windows, rows, cols = queries.shape
    width = w_att.shape[0]
    pairs = cols // PAIR
    near = windows * pairs
    out_at = 3 * pairs

    def far(i):
        turn = i % (2 * pairs)
        done = i // (2 * pairs) * pairs
        return jnp.where(turn >= pairs, done + turn - pairs, jnp.maximum(done - 1, 0))

    anywhere = pl.BlockSpec(memory_space=pl.ANY)
    wide = pl.BlockSpec((1, rows, PAIR), lambda i: (far(i) // pairs, 0, far(i) % pairs))
    half = pl.BlockSpec(
        (1, rows // 2, width), lambda i: (jnp.maximum(far(i) // pairs, 1) - 1, 0, 0)
    )
    own_rows = tokens.shape[1]
    own = pl.BlockSpec((own_rows, width), lambda i: (0, 0))
    stages = [rows >> (stage + 1) for stage in range((trades + 1).bit_length() - 1)]
    state = pltpu.VMEM((near, rows, PAIR), F32)
    dma = pltpu.SemaphoreType.DMA
    return run(
        functools.partial(attend_kernel, windows, pairs, trades, LOG2E / math.sqrt(HEAD_DIM)),
        "attend",
        [
            shaped((windows, rows, cols), BF16),
            shaped((windows, rows, cols), F32),
            shaped((windows, cols, rows), F32),
            shaped((windows - 1, rows // 2, width), F32),
            shaped((windows - 1, rows // 2, width), BF16),
            shaped((near, 4, 2, rows, PAIR), BF16),
            shaped((trades,) + cotangent.shape, BF16),
            shaped((own_rows, width), F32),
            shaped((own_rows, width), BF16),
            shaped((trades, own_rows, width), BF16),
        ],
        64 * windows * rows * rows * cols,
        [queries, w_att, own_kv, cotangent, tokens, norms],
        collective_id=0,
        grid=(2 * near,),
        in_specs=[
            pl.BlockSpec((1, rows, PAIR), lambda i: (i // (2 * pairs), 0, i % pairs)),
            pl.BlockSpec((width, PAIR), lambda i: (0, out_at + far(i) % pairs)),
            anywhere,
            anywhere,
            pl.BlockSpec((None, own_rows, width), lambda i: (0, 0, 0)),
            pl.BlockSpec(norms.shape, lambda i: (0, 0)),
        ],
        out_specs=[
            wide,
            wide,
            pl.BlockSpec((1, PAIR, rows), lambda i: (far(i) // pairs, far(i) % pairs, 0)),
            half,
            half,
            anywhere,
            anywhere,
            own,
            own,
            anywhere,
        ],
        scratch_shapes=[
            pltpu.VMEM((near, 4, 2, rows, PAIR), BF16),
            state,
            state,
            state,
            pltpu.VMEM((rows, width), F32),
            dma((near,)),
            dma((near, 3)),
            dma((near, 3)),
            dma((near, 4)),
            dma((trades,)),
            dma((trades,)),
            pltpu.VMEM((rows // 2, width), F32),
            pltpu.VMEM((own_rows, width), BF16),
            dma((len(stages),)),
            dma((len(stages),)),
            dma((trades,)),
            dma((trades,)),
        ]
        + [pltpu.VMEM((count, width), BF16) for count in stages] * 2,
    )


def attend_back_kernel(windows, pairs, blocks, exp_scale, score_scale, *refs):
    q_ref, wide_ref, log_ref, slots_ref, w_ref, cos_ref, sin_ref, last_ref = refs[:8]
    trades = blocks - 1
    known = (windows - 1) * blocks + 1
    grad_refs = list(refs[8 : 8 + known])
    refs = refs[8 + known :]
    sent_refs, refs = refs[:windows], refs[windows:]
    gq_ref, gk_ref, gv_ref, rows_ref = refs[:4]
    arrived_refs, refs = refs[4 : 4 + windows], refs[4 + windows :]
    dq_all, do_all, far_kept, far_sent, far_core, far_x, near_kept, near_sent, near_core = refs[:9]
    send_sem, recv_sem, result_send, result_recv, last_send, last_recv, last_others = refs[9:]
    grad_refs += [last_others.at[other] for other in range(trades)]
    step = pl.program_id(0)
    count = windows * pairs
    tensor = lax.axis_index("tensor")
    core_peer = {"core": 1 - lax.axis_index("core")}
    far_peer = {"x": 1 - lax.axis_index("x")}
    result_peer = {"tensor": flipped(tensor, lax.axis_size("tensor") // 2)}

    def trade(kind, number):
        source, target, peer = (
            (far_sent, far_core, core_peer),
            (far_kept, far_x, far_peer),
            (near_sent, near_core, core_peer),
        )[kind]
        return send(
            source.at[number],
            target.at[number],
            send_sem.at[kind, number],
            recv_sem.at[kind, number],
            peer,
        )

    def result_trade(w):
        return send(
            sent_refs[w], arrived_refs[w], result_send.at[w], result_recv.at[w], result_peer
        )

    others = [{"tensor": flipped(tensor, other + 1)} for other in range(trades)]

    def last_trade(other):
        return send(
            last_ref, last_others.at[other], last_send.at[other], last_recv.at[other], others[other]
        )

    @pl.when(step == 0)
    def _():
        greet([core_peer, far_peer] + others)
        for other in range(trades):
            last_trade(other).start()
        for w in range(windows):
            result_trade(w).start()

    def at_step(first, body):
        number = step - first

        @pl.when(jnp.logical_and(number >= 0, number < count))
        def _():
            body(number)

    def send_far(number):
        trade(0, number).start()

    def add_far(number):
        trade(0, number).wait_recv()
        far_kept[number] = (
            far_kept[number].astype(F32) + far_core[number].astype(F32)
        ).astype(BF16)

    def send_x(number):
        trade(1, number).start()

    def send_near(number):
        trade(2, number).start()

    def finish(number):
        trade(2, number).wait_recv()
        trade(1, number).wait_recv()
        total = (
            near_kept[number].astype(F32)
            + near_core[number].astype(F32)
            + far_x[number].astype(F32)
        )
        key = total[0]
        gk_ref[0] = (key * cos_ref[...] - swap_halves(key) * sin_ref[...]).astype(BF16)
        gv_ref[0] = total[1].astype(BF16)

    at_step(1, send_far)
    at_step(3, send_x)
    at_step(count + 1, send_near)
    at_step(2, add_far)
    at_step(count + 2, finish)

    for w in range(windows):

        @pl.when(step == w * pairs)
        def _(w=w):
            if w == windows - 1:
                for other in range(trades):
                    last_trade(other).wait_recv()
            at_row = 0
            for grad_ref in grad_refs[w * blocks : (w + 1) * blocks]:
                rows_ref[0, at_row : at_row + grad_ref.shape[0], :] = grad_ref[...]
                at_row += grad_ref.shape[0]

    def gradients(number, grad_out, kept, sent):
        query = q_ref[0]
        is_first = first_head(query.shape)
        overlap = (grad_out.astype(F32) * wide_ref[0]).T
        logs = log_ref[0]
        zero = jnp.zeros_like(query)
        own_q, own_do, row_log, row_sum = [], [], [], []
        for head in range(2):
            mine = is_first if head == 0 else jnp.logical_not(is_first)
            own_q.append(jnp.where(mine, query, zero))
            own_do.append(jnp.where(mine, grad_out, zero))
            at = head * HEAD_DIM
            row_log.append(logs[at : at + 1, :])
            row_sum.append(jnp.sum(overlap[at : at + HEAD_DIM, :], axis=0, keepdims=True))
        dq_parts = [None, None]
        for slot, target in enumerate((kept, sent)):
            key, value = slots_ref[0, slot, 0], slots_ref[0, slot, 1]
            key_turned = key.T
            grad_key, grad_value = None, None
            for head in range(2):
                scores = dot_nt(key, own_q[head])
                probs = jnp.exp2(scores * exp_scale - row_log[head])
                grad_probs = dot_nt(value, own_do[head])
                grad_scores = (probs * (grad_probs - row_sum[head])).astype(BF16)
                term_v = dot_nn(probs.astype(BF16), own_do[head])
                term_k = dot_nn(grad_scores, own_q[head])
                at = head * HEAD_DIM
                term_q = dot_nn(key_turned[at : at + HEAD_DIM, :], grad_scores)
                grad_value = term_v if grad_value is None else grad_value + term_v
                grad_key = term_k if grad_key is None else grad_key + term_k
                dq_parts[head] = term_q if dq_parts[head] is None else dq_parts[head] + term_q
            target[number, 0] = (grad_key * score_scale).astype(BF16)
            target[number, 1] = grad_value.astype(BF16)
        return jnp.concatenate(dq_parts, axis=0).T * score_scale

    @pl.when(step < count)
    def _():
        grad_out = dot_nn(rows_ref[0], w_ref[...]).astype(BF16)
        do_all[step] = grad_out
        dq_all[step] = gradients(step, grad_out, far_kept, far_sent)

    @pl.when(jnp.logical_and(step >= count, step < 2 * count))
    def _():
        number = step - count
        grad_query = dq_all[number] + gradients(number, do_all[number], near_kept, near_sent)
        gq_ref[0] = (grad_query * cos_ref[...] - swap_halves(grad_query) * sin_ref[...]).astype(
            BF16
        )

    @pl.when(step == pl.num_programs(0) - 1)
    def _():
        @pl.loop(0, count)
        def _(number):
            for kind in range(3):
                trade(kind, number).wait_send()

        for other in range(trades):
            last_trade(other).wait_send()
        for w in range(windows):
            result_trade(w).wait_send()
            result_trade(w).wait_recv()


def attend_back(queries, wide, logs, slots_all, grad_blocks, w_att, tables, sent):
    windows, rows, cols = queries.shape
    width = w_att.shape[0]
    pairs = cols // PAIR
    count = windows * pairs
    out_at = 3 * pairs
    score_scale = 1.0 / math.sqrt(HEAD_DIM)
    blocks = lax.axis_size("tensor")
    grads = [block for one in grad_blocks for block in one]
    last = grads[-1]

    def spot(lag, last=None):
        def index(i):
            number = jnp.clip(i - lag, 0, count - 1)
            return (number // pairs, 0, number % pairs)

        return pl.BlockSpec((1, rows, PAIR), index)

    def both(i):
        return jnp.minimum(i, 2 * count - 1) % count

    dma = pltpu.SemaphoreType.DMA
    piece = pltpu.VMEM((count, 2, rows, PAIR), BF16)
    anywhere = pl.BlockSpec(memory_space=pl.ANY)
    return run(
        functools.partial(
            attend_back_kernel, windows, pairs, blocks, score_scale * LOG2E, score_scale
        ),
        "attend_back",
        [shaped((windows, rows, cols), BF16)] * 3
        + [shaped((windows, rows, width), BF16)]
        + [shaped(one.shape, BF16) for one in sent],
        160 * windows * rows * rows * cols,
        [queries, wide, logs, slots_all, w_att, *tables, last, *grads, *sent],
        collective_id=2,
        grid=(2 * count + 2,),
        in_specs=[
            pl.BlockSpec((1, rows, PAIR), lambda i: (both(i) // pairs, 0, both(i) % pairs)),
            pl.BlockSpec((1, rows, PAIR), lambda i: (both(i) // pairs, 0, both(i) % pairs)),
            pl.BlockSpec((1, PAIR, rows), lambda i: (both(i) // pairs, both(i) % pairs, 0)),
            pl.BlockSpec(
                (1, 2, 2, rows, PAIR),
                lambda i: (both(i), jnp.where(i < count, 1, 0), 0, 0, 0),
            ),
            pl.BlockSpec((width, PAIR), lambda i: (0, out_at + jnp.minimum(i, count - 1) % pairs)),
            pl.BlockSpec((rows, PAIR), lambda i: (0, 0)),
            pl.BlockSpec((rows, PAIR), lambda i: (0, 0)),
            anywhere,
        ]
        + [pl.BlockSpec(block.shape, lambda i: (0, 0)) for block in grads]
        + [anywhere] * windows,
        out_specs=[
            spot(count),
            spot(count + 2),
            spot(count + 2),
            pl.BlockSpec((1, rows, width), lambda i: (jnp.minimum(i // pairs, windows - 1), 0, 0)),
        ]
        + [anywhere] * windows,
        scratch_shapes=[pltpu.VMEM((count, rows, PAIR), F32), pltpu.VMEM((count, rows, PAIR), BF16)]
        + [piece] * 7
        + [dma((3, count)), dma((3, count)), dma((windows,)), dma((windows,))]
        + [dma((blocks - 1,)), dma((blocks - 1,)), pltpu.VMEM((blocks - 1,) + last.shape, BF16)],
    )


def middle_kernel(x_ref, kept_ref, arrived_ref, norms_ref, middle_ref, normed_ref):
    middle = x_ref[...].astype(F32) + (kept_ref[...] + arrived_ref[...].astype(F32))
    middle_ref[...] = middle
    normed_ref[...] = (
        normalise(middle)[0] * norms_ref[2:3, :] + norms_ref[3:4, :]
    ).astype(BF16)


def second_norm(x_rows, kept, arrived, norms):
    args, in_specs = row_planes((x_rows, kept, arrived))
    rows, width = arrived.shape
    block = pl.BlockSpec((rows // NORM_BLOCKS, width), lambda i: (i, 0))
    return run(
        middle_kernel,
        "second_norm",
        [shaped((rows, width), F32), shaped((rows, width), BF16)],
        20 * rows * width,
        [*args, norms],
        grid=(NORM_BLOCKS,),
        in_specs=[*in_specs, full(*norms.shape)],
        out_specs=[block, block],
    )


def feed_kernel(blocks, swaps, first, slots, *refs):
    refs = list(refs)

    def take(count):
        taken = refs[:count]
        del refs[:count]
        return taken

    w_refs = take(3)
    if first:
        weight_ref, norms_ref = take(2)
        x_refs, cot_refs = take(blocks), take(blocks)
        sources = take(len(swaps))
        both_ref, wide_ref, total_ref, grad_ref = take(4)
    else:
        both_ref, total_in, grad_in, _ = take(4)
        sources = take(len(swaps))
        wide_ref, kept_ref, sent_ref, grad_kept_ref, grad_sent_ref = take(5)
    trades = tensor_trades(sources, take(len(swaps)), swaps, *take(2 if swaps else 0))
    block = pl.program_id(0)

    def weights_of(ref):
        if len(ref.shape) == 2:
            return ref[...]
        depths, cores, halves = ref.shape[:3]
        return jnp.concatenate(
            [
                ref[depth, core, half]
                for depth in range(depths)
                for half in range(halves)
                for core in range(cores)
            ],
            axis=0,
        )

    gate_w, up_w, down_w = [weights_of(ref) for ref in w_refs]

    @pl.when(block == 0)
    def _():
        start_trades(trades, swaps)

    if first:
        factor = factor_of(weight_ref, norms_ref, slots)
        for at in range(blocks):

            @pl.when(block == at)
            def _(at=at):
                both_ref[0] = x_refs[at][...]
                both_ref[1] = (cot_refs[at][...].astype(F32) * factor).astype(BF16)

    x_rows = both_ref[0]
    gate = dot_nn(x_rows, gate_w)
    up = dot_nn(x_rows, up_w)
    grad_hidden = dot_nn(both_ref[1], down_w)
    sig = jax.nn.sigmoid(gate)
    swish = gate * sig
    hidden = (swish * up).astype(BF16)
    grad_gate = (grad_hidden * up * sig * (1.0 + gate * (1.0 - sig))).astype(BF16)
    grad_up = (grad_hidden * swish).astype(BF16)
    wide_ref[0] = grad_gate
    wide_ref[1] = grad_up
    wide_ref[2] = hidden
    grad_total = dot_nt(grad_gate, gate_w) + dot_nt(grad_up, up_w)
    total = dot_nt(hidden, down_w)
    if first:
        total_ref[...] = total
        grad_ref[...] = grad_total
    else:
        total = total + total_in[...]
        grad_total = grad_total + grad_in[...]
        rows = total.shape[0]
        for at in range(blocks):

            @pl.when(block == at)
            def _(at=at):
                start = (at % (blocks // 2)) * rows
                if at < blocks // 2:
                    kept_ref[start : start + rows] = total
                    grad_kept_ref[start : start + rows] = grad_total
                else:
                    sent_ref[start : start + rows] = total.astype(BF16)
                    grad_sent_ref[start : start + rows] = grad_total.astype(BF16)

    @pl.when(block == blocks - 1)
    def _():
        for trade in trades:
            trade.wait()


def tensor_trades(sources, targets, masks, send_sem=None, recv_sem=None):
    tensor = lax.axis_index("tensor")
    trades = []
    for source, target, kinds in zip(sources, targets, masks):
        for number, mask in enumerate(kinds):
            sems = (send_sem.at[len(trades)], recv_sem.at[len(trades)])
            peer = {"tensor": flipped(tensor, mask)}
            trades.append(send(source, target.at[number], *sems, peer))
    return trades


def start_trades(trades, masks):
    if trades:
        tensor = lax.axis_index("tensor")
        peers = sorted({mask for kinds in masks for mask in kinds})
        greet([{"tensor": flipped(tensor, mask)} for mask in peers])
        for trade in trades:
            trade.start()


def feed_specs(weights):
    lead = weights.shape[:-1]
    part_cols = weights.shape[-1] // 3
    zeros = (0,) * len(lead)
    return part_cols, [
        pl.BlockSpec(lead + (part_cols,), functools.partial(lambda at, i: zeros + (at,), k))
        for k in range(3)
    ]


def full(*shape):
    return pl.BlockSpec(shape, lambda i: (0,) * len(shape))


def feed_call(name, collective_id, blocks, rows, width, part_cols, out, args, swaps, **options):
    masks = [kinds for _, kinds in swaps]
    anywhere = pl.BlockSpec(memory_space=pl.ANY)
    total = sum(len(kinds) for kinds in masks)
    out_shape, out_specs = out
    return run(
        functools.partial(
            feed_kernel, blocks, masks, name == "feed_first", options.pop("slots", None)
        ),
        name,
        out_shape + [shaped((len(kinds),) + array.shape, BF16) for array, kinds in swaps],
        12 * rows * width * part_cols,
        args + [array for array, _ in swaps],
        collective_id=collective_id if swaps else None,
        grid=(blocks,),
        in_specs=options.pop("in_specs") + [anywhere] * len(swaps),
        out_specs=out_specs + [anywhere] * len(swaps),
        scratch_shapes=[pltpu.SemaphoreType.DMA((total,))] * 2 if swaps else [],
        **options,
    )


def feed_first(x_blocks, cot_blocks, weight, norms, slots, weights, swaps=()):
    operands, specs = zip(*[plane(block) for block in (*x_blocks, *cot_blocks)])
    width = math.prod(weights.shape[:-1])
    blocks, own = len(x_blocks), specs[0].block_shape[-2]
    rows = blocks * own
    part_cols, w_specs = feed_specs(weights)
    row_block = pl.BlockSpec((own, width), lambda i: (i, 0))
    out_shape = [shaped((2, rows, width), BF16), shaped((3, rows, 2 * part_cols), BF16)]
    out_shape += [shaped((rows, width), F32)] * 2
    out_specs = [
        pl.BlockSpec((2, own, width), lambda i: (0, i, 0)),
        pl.BlockSpec((3, own, part_cols), lambda i: (0, i, 0)),
        row_block,
        row_block,
    ]
    return feed_call(
        "feed_first",
        6,
        blocks,
        rows,
        width,
        part_cols,
        (out_shape, out_specs),
        [weights, weights, weights, weight, norms, *operands],
        swaps,
        in_specs=w_specs + [SCALAR, full(*norms.shape)] + list(specs),
        slots=slots,
    )


def feed_last(both, wide, totals, weights, blocks, swaps=()):
    rows, width = both.shape[1:]
    own = rows // blocks
    part_cols, w_specs = feed_specs(weights)
    half = full(rows // 2, width)
    row_block = pl.BlockSpec((own, width), lambda i: (i, 0))
    out_shape = [shaped(wide.shape, BF16)]
    out_shape += [shaped((rows // 2, width), F32), shaped((rows // 2, width), BF16)] * 2
    return feed_call(
        "feed_last",
        5,
        blocks,
        rows,
        width,
        part_cols,
        (out_shape, [pl.BlockSpec((3, own, part_cols), lambda i: (0, i, 1))] + [half] * 4),
        [weights, weights, weights, both, *totals, wide],
        swaps,
        in_specs=w_specs
        + [pl.BlockSpec((2, own, width), lambda i: (0, i, 0)), row_block, row_block]
        + [pl.BlockSpec(memory_space=pl.ANY)],
        input_output_aliases={6: 0},
    )


def weights_kernel(windows, masks, *refs):
    lefts, rights = refs[:windows], refs[windows : 2 * windows]
    refs = refs[2 * windows :]
    sources, out_ref, targets = refs[: len(masks)], refs[len(masks)], refs[len(masks) + 1 :]
    at = pl.program_id(0)
    trades = tensor_trades(refs[: len(masks)], targets[: len(masks)], masks, *targets[len(masks) :])

    @pl.when(at == 0)
    def _():
        start_trades(trades, masks)

    total = None
    for left, right in zip(lefts, rights):
        term = dot_tn(left[...], right[...])
        total = term if total is None else total + term
    total = total.astype(BF16)
    depths, cores, halves, shard = out_ref.shape[:4]
    for depth in range(depths):
        for half in range(halves):
            for core in range(cores):
                start = ((depth * halves + half) * cores + core) * shard
                out_ref[depth, core, half] = total[start : start + shard]

    if masks:

        @pl.when(at == pl.num_programs(0) - 1)
        def _():
            for trade in trades:
                trade.wait()


def feed_weights(boths, wides, part, swaps):
    windows = len(boths)
    rows, width = boths[0].shape[1:]
    hidden_cols = wides[0].shape[2] // 2
    step = min(512, hidden_cols)
    steps = hidden_cols // step
    lead = (lax.axis_size("dp"), lax.axis_size("core"), lax.axis_size("x"))
    lead += (width // math.prod(lead),)
    masks = [kinds for _, kinds in swaps]
    anywhere = pl.BlockSpec(memory_space=pl.ANY)
    left = pl.BlockSpec((None, rows, width), lambda i: (i // (2 * steps), 0, 0))
    right = pl.BlockSpec((None, rows, step), lambda i: (i // steps, 0, part * steps + i % steps))
    total = sum(len(kinds) for kinds in masks)
    return run(
        functools.partial(weights_kernel, windows, masks),
        "feed_weights",
        [shaped(lead + (3 * hidden_cols,), BF16)]
        + [shaped((len(kinds),) + array.shape, BF16) for array, kinds in swaps],
        6 * windows * rows * width * hidden_cols,
        [*boths, *wides] + [array for array, _ in swaps],
        collective_id=(6 if part else 4) if swaps else None,
        grid=(3 * steps,),
        in_specs=[left] * windows + [right] * windows + [anywhere] * len(swaps),
        out_specs=[pl.BlockSpec(lead + (step,), lambda i: (0, 0, 0, 0, i))]
        + [anywhere] * len(swaps),
        scratch_shapes=[pltpu.SemaphoreType.DMA((total,))] * 2 if swaps else [],
    )


def norm_grad(kept_ref, arrived_ref, stream, gain, sums_ref):
    grad_normed = kept_ref[...] + arrived_ref[...].astype(F32)
    normed, inv_std = normalise(stream)
    sums = [
        jnp.sum(one, axis=0, keepdims=True) for one in (grad_normed * normed, grad_normed)
    ]

    @pl.when(pl.program_id(0) == 0)
    def _():
        for at, one in enumerate(sums):
            sums_ref[at : at + 1, :] = one

    @pl.when(pl.program_id(0) > 0)
    def _():
        for at, one in enumerate(sums):
            sums_ref[at : at + 1, :] += one

    return norm_back(grad_normed, normed, inv_std, gain)


def middle_back_kernel(
    slots, weight_ref, kept_ref, arrived_ref, middle_ref, cot_ref, norms_ref, grad_ref, low_ref, sums_ref
):
    grad_y = cot_ref[...].astype(F32) * factor_of(weight_ref, norms_ref, slots)
    grad = grad_y + norm_grad(
        kept_ref, arrived_ref, middle_ref[...], norms_ref[2:3, :], sums_ref
    )
    grad_ref[...] = grad
    low_ref[...] = grad.astype(BF16)


NORM_BLOCKS = 1


def row_planes(operands):
    pairs = []
    for one in operands:
        array, at = one if isinstance(one, tuple) else (one, ())
        rows, width = array.shape[len(at) :]
        pairs.append(plane(one, (rows // NORM_BLOCKS, width), lambda i: (i, 0)))
    return [list(part) for part in zip(*pairs)]


def second_norm_back(weight, slots, kept, arrived, middle, cot_rows, norms):
    args, in_specs = row_planes((kept, arrived, middle, cot_rows))
    rows, width = kept.shape
    block = pl.BlockSpec((rows // NORM_BLOCKS, width), lambda i: (i, 0))
    return run(
        functools.partial(middle_back_kernel, slots),
        "second_norm_back",
        [shaped(kept.shape, F32), shaped(kept.shape, BF16), shaped((2, width), F32)],
        40 * kept.size,
        [weight, *args, norms],
        grid=(NORM_BLOCKS,),
        in_specs=[SCALAR, *in_specs, full(*norms.shape)],
        out_specs=[block, block, full(2, width)],
    )


class SumRoute:
    def __init__(self, part, rows, core_in, mine, x_in, z_in, send_sem, recv_sem):
        self.read, self.rows = part, rows
        self.core_in, self.mine, self.x_in, self.z_in = core_in, mine, x_in, z_in
        self.send_sem, self.recv_sem = send_sem, recv_sem
        self.seq, self.depth = seq_index(), lax.axis_index("dp")
        self.peers = half_chip_peers()

    def place(self, number, other_core):
        seq = flipped(self.seq, 2) if number >= 4 else self.seq
        seq = flipped(seq, 1) if other_core else seq
        turn = (self.depth + number % 4) % lax.axis_size("dp")
        return pl.ds(
            pl.multiple_of((turn * seq_size() + seq) * self.rows, self.rows), self.rows
        )

    def message(self, number):
        if number < 8:
            source, target, peer = self.read.at[self.place(number, True), :], self.core_in, "core"
            target = target.at[number]
        elif number < 12:
            source, target, peer = self.mine.at[number - 4], self.x_in.at[number - 8], "far"
        else:
            turn, peer = ((2, "up"), (1, "up"), (3, "down"))[number - 12]
            source, target = self.mine.at[turn], self.z_in.at[number - 12]
        return send(
            source, target, self.send_sem.at[number], self.recv_sem.at[number], self.peers[peer]
        )

    def start(self, *numbers):
        for number in numbers:
            self.message(number).start()

    def add_core(self, number):
        self.message(number).wait_recv()
        own = self.read[self.place(number, False), :].astype(F32)
        self.mine[number] = (own + self.core_in[number].astype(F32)).astype(self.mine.dtype)

    def add_x(self, number):
        self.message(8 + number).wait_recv()
        total = self.mine[number].astype(F32) + self.x_in[number].astype(F32)
        self.mine[number] = total.astype(self.mine.dtype)

    def add_up(self):
        self.message(12).wait_recv()
        total = self.mine[1].astype(F32) + self.z_in[0].astype(F32)
        self.mine[1] = total.astype(self.mine.dtype)

    def total(self):
        self.message(13).wait_recv()
        self.message(14).wait_recv()
        return (
            self.mine[0].astype(F32) + self.z_in[1].astype(F32) + self.z_in[2].astype(F32)
        )

    def sent(self):
        for number in range(SUM_MESSAGES):
            self.message(number).wait_send()


SUM_MESSAGES = 15


def finish_kernel(windows, trades, score_cols, *refs):
    stages = (trades + 1).bit_length() - 1
    refs = list(refs)

    def take(count):
        taken = refs[:count]
        del refs[:count]
        return taken

    far_inputs = take(8)
    shard_ref = take(1)[0]
    norms_ref = take(1)[0]
    second_refs = take(windows)
    grad_refs = take(windows)
    weights_ref, vectors_ref, input_ref, shard_arrived = take(4)
    loads = take(8)
    grad_loads = take(windows)
    part, core_in, mine, x_in, z_in = take(5)
    tiles, own_tiles, arrived_tiles = take(3)
    small_core, small_mine, small_x, small_z = take(4)
    kept_all = take(windows)
    stage_sent = [take(stages) for _ in range(windows)]
    stage_arrived = [take(stages) for _ in range(windows)]
    load_sem, big_send, big_recv, small_send, small_recv = take(5)
    y_send, y_recv, tile_send, tile_recv, shard_sem = take(5)
    assert not refs
    (grad_q, grad_k, grad_v, normed, grad_mid, attended, w_qkv, tokens) = loads[:8]
    tensor = lax.axis_index("tensor")
    others = [{"tensor": flipped(tensor, other + 1)} for other in range(trades)]
    shards = lax.axis_size("dp") * seq_size()
    devices = shards * (trades + 1)
    group = tiles.shape[0] // shards
    width = part.shape[1]
    cols = score_cols
    rows = width // shards

    w_source = far_inputs[6].at[:, pl.ds(0, 3 * cols)]
    sources = [*far_inputs[:6], w_source, far_inputs[7]]
    sources += [*grad_refs]
    targets = [*loads, *grad_loads]
    copies = [
        pltpu.make_async_copy(source, target, load_sem.at[at])
        for at, (source, target) in enumerate(zip(sources, targets))
    ]
    order = [4, 5, 6, 0, 1, 2, 3, 7] + list(range(8, len(copies)))
    for at in order:
        copies[at].start()

    def block_route(block):
        return SumRoute(
            part.at[block],
            rows,
            core_in.at[block],
            mine.at[block],
            x_in.at[block],
            z_in.at[block],
            big_send.at[block],
            big_recv.at[block],
        )

    routes = [block_route(block) for block in range(4)]
    small = SumRoute(
        tiles, group, small_core, small_mine, small_x, small_z, small_send, small_recv
    )
    greet(list(small.peers.values()) + others)
    everything = (6, 7, 5, 4, 2, 3, 1, 0)

    def product(block, left, right):
        total = None
        for w in range(windows):
            term = dot_tn(left[w], right[w])
            total = term if total is None else total + term
        part[block] = total.astype(BF16)

    def y_trade(w, stage):
        return send(
            stage_sent[w][stage],
            stage_arrived[w][stage],
            y_send.at[w, stage],
            y_recv.at[w, stage],
            {"tensor": flipped(tensor, (trades + 1) >> (stage + 1))},
        )

    def turn_back(w):
        total = None
        for at, grad in enumerate((grad_q, grad_k, grad_v)):
            term = dot_nt(grad[w], w_qkv[:, at * cols : (at + 1) * cols])
            total = term if total is None else total + term
        half = total.shape[0] // 2
        kept_all[w][...] = total[:half]
        stage_sent[w][0][...] = total[half:].astype(BF16)

    def add_cores(route):
        for number in everything:
            route.add_core(number)

    def across(route):
        route.start(10, 11, 9, 8)

    def add_across(route):
        for number in (2, 3, 1, 0):
            route.add_x(number)

    count = shard_ref.shape[0] // 2
    far_rows = pl.ds(pl.multiple_of((1 - lax.axis_index("x")) * count, count), count)
    shard_trade = send(
        shard_ref.at[far_rows, :],
        shard_arrived,
        shard_sem.at[0],
        shard_sem.at[1],
        small.peers["far"],
    )
    shard_trade.start()
    for at in (6, 0, 1, 2):
        copies[at].wait()
    turn_back(0)
    copies[4].wait()
    copies[5].wait()
    product(3, grad_mid, attended)
    y_trade(0, 0).start()
    copies[3].wait()
    routes[3].start(*everything)
    product(0, normed, grad_q)
    add_cores(routes[3])
    routes[0].start(*everything)
    across(routes[3])
    for w in range(1, windows):
        turn_back(w)
    add_cores(routes[0])
    across(routes[0])
    for w in range(1, windows):
        y_trade(w, 0).start()
    product(1, normed, grad_k)
    add_across(routes[3])
    routes[1].start(*everything)
    product(2, normed, grad_v)
    routes[3].start(12, 14)
    add_cores(routes[1])
    across(routes[1])
    for at in range(7, 8 + windows):
        copies[at].wait()
    sums = [None, None]

    def first_norm(w):
        kept = kept_all[w][...]
        for stage in range(stages):
            y_trade(w, stage).wait_recv()
            kept = kept + stage_arrived[w][stage][...].astype(F32)
            if stage + 1 < stages:
                half = kept.shape[0] // 2
                stage_sent[w][stage + 1][...] = kept[half:].astype(BF16)
                y_trade(w, stage + 1).start()
                kept = kept[:half]
        normed_rows, inv_std = normalise(tokens[w].astype(F32))
        for at, one in enumerate((kept * normed_rows, kept)):
            one = jnp.sum(one, axis=0, keepdims=True)
            sums[at] = one if sums[at] is None else sums[at] + one
        input_ref[w] = grad_loads[w][...] + norm_back(
            kept, normed_rows, inv_std, norms_ref[0:1, :]
        )

    first_norm(0)
    routes[2].start(*everything)
    add_across(routes[0])
    add_cores(routes[2])
    across(routes[2])
    routes[3].add_up()
    routes[0].start(12, 14)
    routes[3].start(13)
    for w in range(1, windows):
        first_norm(w)
    first = jnp.concatenate(sums, axis=0)
    second = sum(ref[...] for ref in second_refs)
    span = width // devices
    tiles[...] = jnp.zeros_like(tiles)
    for device in range(devices):
        at = device * 8
        columns = slice(device * span, (device + 1) * span)
        tiles[at : at + 2, :span] = first[:, columns]
        tiles[at + 2 : at + 4, :span] = second[:, columns]
    add_across(routes[1])
    small.start(*everything)
    routes[0].add_up()
    routes[1].start(12, 14)
    add_cores(small)
    routes[0].start(13)
    across(small)
    add_across(routes[2])
    routes[1].add_up()
    routes[2].start(12, 14)
    add_across(small)
    routes[1].start(13)
    small.start(12, 14)
    for block in (3, 0):
        weights_ref[:, block * cols : (block + 1) * cols] = routes[block].total()
    small.add_up()
    routes[2].add_up()
    small.start(13)
    weights_ref[:, cols : 2 * cols] = routes[1].total()
    routes[2].start(13)
    own_tiles[...] = small.total()

    def tile_trade(other):
        place = pl.ds(pl.multiple_of(flipped(tensor, other + 1) * 8, 8), 8)
        return send(
            own_tiles.at[place, :],
            arrived_tiles.at[other],
            tile_send.at[other],
            tile_recv.at[other],
            others[other],
        )

    weights_ref[:, 2 * cols : 3 * cols] = routes[2].total()
    for other in range(trades):
        tile_trade(other).start()
    vectors = own_tiles[pl.ds(pl.multiple_of(tensor * 8, 8), 8), :]
    for other in range(trades):
        tile_trade(other).wait_recv()
        vectors = vectors + arrived_tiles[other]
    vectors_ref[...] = vectors
    shard_trade.wait()
    for route in (*routes, small):
        route.sent()
    for w in range(windows):
        for stage in range(stages):
            y_trade(w, stage).wait_send()
    for other in range(trades):
        tile_trade(other).wait_send()


def finish(
    grads,
    normed,
    grad_mid,
    attended,
    w_att,
    tokens,
    ffn_shard,
    norms,
    second_sums,
    grad_middles,
    trades,
):
    windows, rows, cols = grads[0].shape
    width = w_att.shape[0]
    own_rows = tokens.shape[1]
    shards = lax.axis_size("dp") * seq_size()
    shard = width // shards
    group = 8 * (trades + 1)
    stages = [rows >> (stage + 1) for stage in range((trades + 1).bit_length() - 1)]
    dma = pltpu.SemaphoreType.DMA
    anywhere = pl.BlockSpec(memory_space=pl.ANY)
    vmem = pl.BlockSpec(memory_space=pltpu.VMEM)
    far_inputs = [*grads, normed, grad_mid, attended, w_att, tokens]
    kinds = (8, 8, 4, 3)

    def like(array):
        return pltpu.VMEM(array.shape, array.dtype)

    loads = [like(array) for array in far_inputs]
    loads[6] = pltpu.VMEM((width, 3 * cols), BF16)
    return run(
        functools.partial(finish_kernel, windows, trades, cols),
        "finish",
        [
            shaped((shard, 4 * cols), F32),
            shaped((8, 128), F32),
            shaped((windows, own_rows, width), F32),
            shaped((ffn_shard.shape[0] // 2, ffn_shard.shape[1]), BF16),
        ],
        8 * windows * rows * width * cols + 6 * windows * rows * width * cols,
        [*far_inputs, ffn_shard, norms, *second_sums, *grad_middles],
        collective_id=3,
        in_specs=[anywhere] * 9
        + [vmem] * (1 + windows)
        + [anywhere] * windows,
        out_specs=[vmem] * 3 + [anywhere],
        scratch_shapes=loads
        + [like(array) for array in grad_middles]
        + [pltpu.VMEM((4, width, cols), BF16)]
        + [pltpu.VMEM((4, count, shard, cols), BF16) for count in kinds]
        + [
            pltpu.VMEM((shards * group, 128), F32),
            pltpu.VMEM((group, 128), F32),
            pltpu.VMEM((trades, 8, 128), F32),
        ]
        + [pltpu.VMEM((count, group, 128), F32) for count in kinds]
        + [pltpu.VMEM((rows // 2, width), F32)] * windows
        + [pltpu.VMEM((count, width), BF16) for count in stages] * (2 * windows)
        + [
            dma((8 + windows,)),
            dma((4, SUM_MESSAGES)),
            dma((4, SUM_MESSAGES)),
            dma((SUM_MESSAGES,)),
            dma((SUM_MESSAGES,)),
            dma((windows, len(stages))),
            dma((windows, len(stages))),
            dma((trades,)),
            dma((trades,)),
            dma((2,)),
        ],
    )


def result_kernel(windows, *refs):
    out_ref = refs[-1]
    for w in range(windows):
        middle_ref, kept_ref, arrived_ref = refs[3 * w : 3 * w + 3]
        out_ref[w] = (
            middle_ref[...] + (kept_ref[...] + arrived_ref[...].astype(F32))
        ).astype(BF16)


def results(parts):
    rows, width = parts[0][0].shape
    return run(
        functools.partial(result_kernel, len(parts)),
        "results",
        shaped((len(parts), rows, width), BF16),
        2 * len(parts) * rows * width,
        [array for part in parts for array in part],
    )


def local(
    tokens,
    cotangent,
    species,
    counts,
    species_scale,
    norm1_gain,
    norm1_bias,
    w_query,
    w_key,
    w_value,
    w_out,
    norm2_gain,
    norm2_bias,
    w_gate,
    w_up,
    w_down,
):
    windows_here, own_rows, model_width = tokens.shape
    tensor_size = lax.axis_size("tensor")
    block_rows = own_rows * tensor_size
    head_cols = w_query.shape[1]
    hidden_cols = w_gate.shape[1]
    shards = ("dp", "x", "core")

    labels = lax.broadcasted_iota(jnp.int32, (windows_here, species_scale.shape[0]), 1)
    chosen = jnp.sum(jnp.where(species[:, None] == labels, species_scale[None, :], 0.0), axis=1)
    weighted = counts.astype(F32) * chosen

    lanes = jnp.zeros((8, 128), F32)
    vectors = jnp.stack([norm1_gain, norm1_bias, norm2_gain, norm2_bias])
    tile = lanes.at[:4, : vectors.shape[1]].set(vectors).at[4, :].set(jnp.sum(weighted))
    part = hidden_cols // 2
    turned = w_down.T
    first_ffn = jnp.concatenate([w_gate[:, :part], w_up[:, :part], turned[:, :part]], axis=1)
    last_ffn = jnp.concatenate([w_gate[:, part:], w_up[:, part:], turned[:, part:]], axis=1)
    upper = lax.axis_index("x") == 1

    def gather_ffn(own, across):
        pair = jnp.where(
            upper,
            jnp.concatenate([across, own], axis=0),
            jnp.concatenate([own, across], axis=0),
        )
        whole = lax.all_gather(pair, ("dp", "core"), axis=0, tiled=True)
        return whole.reshape(
            lax.axis_size("dp"), lax.axis_size("core"), lax.axis_size("x"), -1, whole.shape[1]
        )

    first_ffn = lax.all_gather(first_ffn, shards, axis=0, tiled=True)
    last_across = swap(last_ffn, "x", 1)
    w_att, norms, arrived_tokens, cosine, sine = gather(
        jnp.concatenate([w_query, w_key, w_value, w_out.T], axis=1),
        tile,
        tokens,
        tensor_size - 1,
    )
    slots = float(windows_here * lax.axis_size("dp"))

    windows = range(windows_here)
    weights = [weighted[w].reshape(1, 1) for w in windows]

    token_blocks = [tokens] + [arrived_tokens[other] for other in range(tensor_size - 1)]
    normed_rows, queries, own_kv = project(token_blocks, norms, w_att, cosine, sine)
    last_ffn = gather_ffn(last_ffn, hold(last_across, w_att))
    (
        attended,
        wide_attended,
        logs,
        kept_all,
        sent_all,
        slots_all,
        cots,
        first_middle,
        first_normed,
        first_others,
    ) = attend(queries, own_kv, w_att, cotangent, tokens, norms, tensor_size - 1)
    others = range(tensor_size - 1)
    cot_blocks = [
        [(cotangent, (w,))] + [(cots, (other, w)) for other in others] for w in windows
    ]
    middles = [first_middle]

    def reduce_ffn(partial):
        partial = partial.reshape(-1, partial.shape[-1])
        mine = lax.psum_scatter(partial, ("dp", "core"), scatter_dimension=0, tiled=True)
        count = mine.shape[0] // 2
        kept = jnp.where(upper, mine[count:], mine[:count])
        return kept, mine

    blocks = [first_normed] + [first_others[other] for other in others]
    begun, fed, lows, arrived_lows = [], [], [], []
    grad_middles, second_sums = [], []
    masks = [other + 1 for other in others]

    def through_second_norm(w, kept, arrived):
        grad_middle, low, sums = second_norm_back(
            weights[w], slots, kept, arrived, middles[w], (cotangent, (w,)), norms
        )
        grad_middles.append(grad_middle)
        second_sums.append(sums)
        return low

    for w in windows:
        begun.append(
            feed_first(blocks, cot_blocks[w], weights[w], norms, slots, first_ffn)
        )
        if w + 1 < windows_here:
            kept, arrived = scatter_pair(kept_all[w], sent_all[w], "tensor")
            middle, normed_mid = second_norm(
                (tokens, (w + 1,)), hold(kept, begun[-1]), arrived, norms
            )
            middles.append(middle)
            blocks = hold(spread(normed_mid, "tensor"), fed)
            after = normed_mid
        else:
            g_first_part, *arrived = feed_weights(
                [one[0] for one in begun],
                [one[0] for one in fed] + [one[1] for one in begun[len(fed) :]],
                0,
                [(one[4], [tensor_size // 2]) for one in fed],
            )
            first_kept, first_sent = reduce_ffn(g_first_part)
            after = g_first_part
        swaps = ()
        if w > 0:
            kept, arrived = later_pair(fed[-1][3], arrived[-1][0], "tensor")
            low = through_second_norm(w - 1, hold(kept, g_first_part), arrived)
            lows.append(low)
            swaps = [(low, masks)]
            after = low
        both, wide, *totals = hold(begun[w], after)
        ended = feed_last(both, wide, totals, last_ffn, tensor_size, swaps)
        fed.append(ended[:5])
        arrived_lows += ended[5:]
        if w + 1 < windows_here:
            blocks = hold(blocks, ended[3])
    g_ffn_part, arrived = feed_weights(
        [one[0] for one in begun],
        [one[0] for one in fed],
        1,
        [(fed[-1][4], [tensor_size // 2])],
    )
    last_kept, last_sent = reduce_ffn(g_ffn_part)
    kept, arrived = later_pair(fed[-1][3], arrived[0], "tensor")
    last_low = through_second_norm(windows[-1], hold(kept, g_ffn_part), arrived)
    grad_mid_blocks = [
        [low] + [arrived[other] for other in others] for low, arrived in zip(lows, arrived_lows)
    ] + [[last_low]]

    grad_q, grad_k, grad_v, grad_mid_rows, *arrived_results = attend_back(
        hold(queries, g_ffn_part),
        wide_attended,
        logs,
        slots_all,
        grad_mid_blocks,
        w_att,
        (cosine, sine),
        [fed[w][2] for w in windows],
    )
    parts = [
        (middles[w], *later_pair(fed[w][1], arrived_results[w], "tensor")) for w in windows
    ]

    g_att, vectors, input_grad, first_arrived = finish(
        (grad_q, grad_k, grad_v),
        normed_rows,
        grad_mid_rows,
        attended,
        w_att,
        tokens,
        first_sent,
        norms,
        second_sums,
        grad_middles,
        tensor_size - 1,
    )
    output = results(hold(parts, input_grad))
    g_first = first_kept.astype(F32) + first_arrived.astype(F32)
    last_sent = hold(last_sent, input_grad)
    count = last_sent.shape[0] // 2
    last_sent = jnp.where(upper, last_sent[:count], last_sent[count:])
    last_arrived = swap(last_sent, "x", 1)
    g_last = last_kept.astype(F32) + last_arrived.astype(F32)
    norm_sums = vectors[:4, : norm1_gain.shape[0]]
    ffn_grads = [
        jnp.concatenate(
            [g_first[:, at * part : (at + 1) * part], g_last[:, at * part : (at + 1) * part]],
            axis=1,
        )
        for at in range(3)
    ]

    return (
        output,
        input_grad,
        norm_sums[0],
        norm_sums[1],
        g_att[:, :head_cols],
        g_att[:, head_cols : 2 * head_cols],
        g_att[:, 2 * head_cols : 3 * head_cols],
        g_att[:, 3 * head_cols :].T,
        norm_sums[2],
        norm_sums[3],
        ffn_grads[0],
        ffn_grads[1],
        ffn_grads[2].T,
    )


def solution(mesh):
    depth, seq, tensor = mesh.devices.shape
    finer = jax.sharding.Mesh(
        mesh.devices.reshape(depth, seq // 2, 2, tensor), ("dp", "x", "core", "tensor")
    )
    rows = P("dp", ("x", "core", "tensor"), None)
    vector = P(("dp", "x", "core", "tensor"))
    tall = P(("dp", "x", "core"), "tensor")
    flat = P("tensor", ("dp", "x", "core"))
    return jax.shard_map(
        local,
        mesh=finer,
        in_specs=(
            rows, rows, P("dp"), P("dp"), P(), vector, vector,
            tall, tall, tall, flat, vector, vector, tall, tall, flat,
        ),
        out_specs=(
            rows, rows, vector, vector, tall, tall, tall, flat,
            vector, vector, tall, tall, flat,
        ),
        check_vma=False,
    )
```

```python
import functools
import math

import jax
import jax.numpy as jnp
from jax import lax
from jax.experimental import pallas as pl
from jax.experimental.pallas import tpu as pltpu
from jax.sharding import PartitionSpec as P

HEAD_DIM = 64
EPSILON = 1e-05
ROPE_BASE = 10000.0
PAIR = 2 * HEAD_DIM
LOG2E = math.log2(math.e)
BF16 = jnp.bfloat16
F32 = jnp.float32
VMEM_BYTES = 56 * 1024 * 1024
MESH = pl.DeviceIdType.MESH


def dot_nn(left, right):
    return lax.dot_general(left, right, (((1,), (0,)), ((), ())), preferred_element_type=F32)


def dot_nt(left, right):
    return lax.dot_general(left, right, (((1,), (1,)), ((), ())), preferred_element_type=F32)


def dot_tn(left, right):
    return lax.dot_general(left, right, (((0,), (0,)), ((), ())), preferred_element_type=F32)


def swap(array, axis, bit):
    size = lax.axis_size(axis)
    return lax.ppermute(array, axis, [(i, i ^ bit) for i in range(size)])


def spread(array, axis):
    blocks = [array]
    bit = 1
    while bit < lax.axis_size(axis):
        blocks = blocks + [swap(block, axis, bit) for block in blocks]
        bit *= 2
    return blocks


def scatter_pair(kept, sent, axis):
    return later_pair(kept, swap(sent, axis, lax.axis_size(axis) // 2), axis)


def later_pair(kept, arrived, axis):
    bit = lax.axis_size(axis) // 2
    while bit > 1:
        partial = kept + arrived.astype(F32)
        bit //= 2
        rows = partial.shape[0] // 2
        kept, arrived = partial[:rows], swap(partial[rows:].astype(BF16), axis, bit)
    return kept, arrived


def seq_size():
    return lax.axis_size("x") * lax.axis_size("core")


def seq_index():
    return lax.axis_index("x") * lax.axis_size("core") + lax.axis_index("core")


def hold(values, *others):
    return lax.optimization_barrier((values, others))[0]


def run(kernel, name, out_shape, flops, args, collective_id=None, **options):
    trading = {} if collective_id is None else dict(collective_id=collective_id, has_side_effects=True)
    moved = sum(math.prod(array.shape) * array.dtype.itemsize for array in args)
    outs = out_shape if isinstance(out_shape, list) else [out_shape]
    moved += sum(math.prod(array.shape) * array.dtype.itemsize for array in outs)
    return pl.pallas_call(
        kernel,
        out_shape=out_shape,
        compiler_params=pltpu.CompilerParams(vmem_limit_bytes=VMEM_BYTES, **trading),
        cost_estimate=pl.CostEstimate(
            flops=int(flops), bytes_accessed=int(moved), transcendentals=0
        ),
        name=name,
        **options,
    )(*args)


def shaped(shape, dtype):
    return jax.ShapeDtypeStruct(shape, dtype)


SCALAR = pl.BlockSpec(memory_space=pltpu.SMEM)


def plane(operand, block=None, index=None):
    array, at = operand if isinstance(operand, tuple) else (operand, ())
    shape = array.shape[len(at) :] if block is None else block
    place = (lambda *i: (0,) * len(shape)) if index is None else index
    return array, pl.BlockSpec((None,) * len(at) + tuple(shape), lambda *i: at + place(*i))


def normalise(stream):
    row_mean = jnp.mean(stream, axis=-1, keepdims=True)
    centred = stream - row_mean
    variance = jnp.mean(centred * centred, axis=-1, keepdims=True)
    inv_std = lax.rsqrt(variance + EPSILON)
    return centred * inv_std, inv_std


def norm_back(grad_normed, normed, inv_std, norm_gain):
    scaled_grad = grad_normed * norm_gain
    return inv_std * (
        scaled_grad
        - jnp.mean(scaled_grad, axis=-1, keepdims=True)
        - normed * jnp.mean(scaled_grad * normed, axis=-1, keepdims=True)
    )


def factor_of(weight_ref, norms_ref, slots):
    return weight_ref[0, 0] * slots / norms_ref[4:5, 0:1]


def first_head(shape):
    return lax.broadcasted_iota(jnp.int32, shape, 1) % PAIR < HEAD_DIM


def swap_halves(values):
    half = HEAD_DIM // 2
    lane = lax.broadcasted_iota(jnp.int32, values.shape, 1)
    ahead = pltpu.roll(values, PAIR - half, 1)
    behind = pltpu.roll(values, half, 1)
    return jnp.where(lane % HEAD_DIM < half, ahead, behind)


def project_kernel(blocks, norms_ref, w_ref, cos_ref, sin_ref, *refs):
    x_refs = refs[:blocks]
    normed_ref, q_ref, kv_ref = refs[blocks:]
    cols = q_ref.shape[2]
    gain, bias = norms_ref[0:1, :], norms_ref[1:2, :]
    at_row = 0
    for x_ref in x_refs:
        rows = slice(at_row, at_row + x_ref.shape[1])
        at_row += x_ref.shape[1]
        normed = (normalise(x_ref[0].astype(F32))[0] * gain + bias).astype(BF16)
        normed_ref[0, rows, :] = normed
        cosine, sine = cos_ref[rows, :], sin_ref[rows, :]
        query = dot_nn(normed, w_ref[:, :cols])
        key = dot_nn(normed, w_ref[:, cols : 2 * cols])
        value = dot_nn(normed, w_ref[:, 2 * cols : 3 * cols]).astype(BF16)
        for at in range(0, cols, PAIR):
            part, pair = slice(at, at + PAIR), at // PAIR
            one = query[:, part]
            q_ref[0, rows, part] = (one * cosine + swap_halves(one) * sine).astype(BF16)
            one = key[:, part]
            kv_ref[0, pair, 0, rows, :] = (one * cosine + swap_halves(one) * sine).astype(BF16)
            kv_ref[0, pair, 1, rows, :] = value[:, part]


def project(x_blocks, norms, w_att, cosine, sine):
    windows = x_blocks[0].shape[0]
    width, cols = w_att.shape[0], w_att.shape[1] // 4
    rows = sum(block.shape[1] for block in x_blocks)
    pieces = (cols // PAIR, 2, rows, PAIR)
    args = [norms, w_att, cosine, sine, *x_blocks]
    return run(
        functools.partial(project_kernel, len(x_blocks)),
        "project",
        [
            shaped((windows, rows, width), BF16),
            shaped((windows, rows, cols), BF16),
            shaped((windows,) + pieces, BF16),
        ],
        6 * windows * rows * width * cols,
        args,
        grid=(windows,),
        in_specs=[pl.BlockSpec(array.shape, lambda i: (0, 0)) for array in args[:4]]
        + [pl.BlockSpec((1,) + block.shape[1:], lambda i: (i, 0, 0)) for block in x_blocks],
        out_specs=[
            pl.BlockSpec((1, rows, width), lambda i: (i, 0, 0)),
            pl.BlockSpec((1, rows, cols), lambda i: (i, 0, 0)),
            pl.BlockSpec((1,) + pieces, lambda i: (i, 0, 0, 0, 0)),
        ],
    )


def flipped(index, mask):
    bit = 1
    while bit <= mask:
        if mask & bit:
            index = index + bit - 2 * bit * ((index // bit) % 2)
        bit *= 2
    return index


def greet(peers):
    barrier = pltpu.get_barrier_semaphore()
    for peer in peers:
        pl.semaphore_signal(barrier, inc=1, device_id=peer, device_id_type=MESH)
    pl.semaphore_wait(barrier, len(peers))


def send(source, target, send_sem, recv_sem, peer):
    return pltpu.make_async_remote_copy(
        src_ref=source,
        dst_ref=target,
        send_sem=send_sem,
        recv_sem=recv_sem,
        device_id=peer,
        device_id_type=MESH,
    )


def half_chip_peers():
    depth = lax.axis_index("dp")
    size = lax.axis_size("dp")
    return {
        "far": {"x": 1 - lax.axis_index("x")},
        "up": {"dp": (depth + 1) % size},
        "down": {"dp": (depth + size - 1) % size},
        "core": {"core": 1 - lax.axis_index("core")},
    }


class Route:
    PARTS = ((0, 0), (3, 0), (1, 0), (2, 0), (0, 1), (3, 1), (1, 1), (2, 1))

    def __init__(self, whole, rows, send_sem, recv_sem, own):
        self.whole, self.rows, self.own = whole, rows, own
        self.send_sem, self.recv_sem = send_sem, recv_sem
        self.seq, self.depth = seq_index(), lax.axis_index("dp")
        self.peers = half_chip_peers()

    def part(self, place):
        turn, other = place
        seq = flipped(self.seq, 2) if other else self.seq
        at = (((self.depth + turn) % lax.axis_size("dp")) * seq_size() + seq) * self.rows
        return self.whole.at[pl.ds(pl.multiple_of(at, self.rows), self.rows), :]

    def message(self, number):
        if number >= 7:
            place, peer = self.PARTS[number - 7], "core"
        else:
            place, peer = (
                ((0, 0), "up"),
                ((0, 0), "down"),
                ((3, 0), "up"),
                ((0, 0), "far"),
                ((3, 0), "far"),
                ((1, 0), "far"),
                ((2, 0), "far"),
            )[number]
        target = self.part(place)
        return send(
            self.own if place == (0, 0) else target,
            target,
            self.send_sem.at[number],
            self.recv_sem.at[number],
            self.peers[peer],
        )

    def start(self, *numbers):
        for number in numbers:
            self.message(number).start()

    def arrived(self, *numbers):
        for number in numbers:
            self.message(number).wait_recv()

    def sent(self, *numbers):
        for number in numbers:
            self.message(number).wait_send()


MESSAGES = 15


def tables(cos_ref, sin_ref, trades):
    own_rows = cos_ref.shape[0] // (trades + 1)
    tensor = lax.axis_index("tensor")
    half = HEAD_DIM // 2
    shape = (own_rows, PAIR)
    lane = lax.broadcasted_iota(jnp.int32, shape, 1)
    exponent = -(math.log(ROPE_BASE) * 2.0 / HEAD_DIM) * (lane % half).astype(F32)
    inverse = jnp.exp(exponent)
    row = lax.broadcasted_iota(jnp.int32, shape, 0)
    for other in range(trades + 1):
        start = (seq_index() * (trades + 1) + flipped(tensor, other)) * own_rows
        phase = (row + start).astype(F32) * inverse
        rows = slice(other * own_rows, (other + 1) * own_rows)
        cos_ref[rows, :] = jnp.cos(phase)
        sine = jnp.sin(phase)
        sin_ref[rows, :] = jnp.where(lane % HEAD_DIM < half, -sine, sine)


def gather_kernel(trades, att_ref, tile_ref, tokens_ref, *refs):
    att_all, norms_ref, tokens_all, cos_ref, sin_ref = refs[:5]
    tiles, pair_of_tiles = refs[5:7]
    att_send, att_recv, tile_send, tile_recv = refs[7:11]
    own_sem, tokens_send, tokens_recv, pair_send, pair_recv = refs[11:]
    tensor = lax.axis_index("tensor")
    others = [{"tensor": flipped(tensor, other + 1)} for other in range(trades)]
    att = Route(att_all, att_ref.shape[0], att_send, att_recv, att_ref)
    tile_rows = tile_ref.shape[0]
    small = Route(tiles, pair_of_tiles.shape[0], tile_send, tile_recv, pair_of_tiles)

    def tokens_trade(other):
        return send(
            tokens_ref,
            tokens_all.at[other],
            tokens_send.at[other],
            tokens_recv.at[other],
            others[other],
        )

    own_rows = pl.ds(pl.multiple_of(tensor * tile_rows, tile_rows), tile_rows)

    def pair_trade(other):
        return send(
            tile_ref,
            pair_of_tiles.at[own_rows, :],
            pair_send.at[other],
            pair_recv.at[other],
            others[other],
        )

    own_copies = [
        pltpu.make_async_copy(att_ref, att.part((0, 0)), own_sem.at[0]),
        pltpu.make_async_copy(tile_ref, pair_of_tiles.at[own_rows, :], own_sem.at[1]),
        pltpu.make_async_copy(pair_of_tiles, small.part((0, 0)), own_sem.at[2]),
    ]

    greet(list(att.peers.values()) + others)
    for other in range(trades):
        pair_trade(other).start()
    own_copies[1].start()
    att.start(0, 1, 3, 7)
    own_copies[1].wait()
    for other in range(trades):
        pair_trade(other).wait_recv()
    small.start(0, 1, 3, 7)
    own_copies[0].start()
    own_copies[2].start()
    for other in range(trades):
        tokens_trade(other).start()
    tables(cos_ref, sin_ref, trades)
    for route in (small, att):
        route.arrived(0)
        route.start(2, 4, 8)
    for route in (small, att):
        route.arrived(3)
        route.start(11)
    for route in (small, att):
        route.arrived(1)
        route.start(5, 9)
    for route in (small, att):
        route.arrived(2)
        route.start(6, 10)
    for route in (small, att):
        route.arrived(4)
        route.start(12)
        route.arrived(5)
        route.start(13)
        route.arrived(6)
        route.start(14)
    for route in (small, att):
        route.arrived(*range(7, MESSAGES))
    own_copies[2].wait()
    shard = norms_ref.shape[1] // (tiles.shape[0] // tile_rows)
    total = None
    for device in range(tiles.shape[0] // tile_rows):
        tile = tiles[device * tile_rows : (device + 1) * tile_rows, :]
        norms_ref[:, device * shard : (device + 1) * shard] = tile[:, :shard]
    for depth in range(lax.axis_size("dp")):
        at = depth * (tiles.shape[0] // lax.axis_size("dp"))
        one = tiles[at + 4 : at + 5, :]
        total = one if total is None else total + one
    norms_ref[4:5, : total.shape[1]] = total
    for route in (att, small):
        route.sent(*range(MESSAGES))
    own_copies[0].wait()
    for other in range(trades):
        pair_trade(other).wait_send()
        tokens_trade(other).wait_recv()
        tokens_trade(other).wait_send()


def gather(att, tile, tokens, trades):
    count = lax.axis_size("dp") * seq_size()
    rows = att.shape[0]
    group = tile.shape[0] * (trades + 1)
    anywhere = pl.BlockSpec(memory_space=pl.ANY)
    vmem = pl.BlockSpec(memory_space=pltpu.VMEM)
    dma = pltpu.SemaphoreType.DMA
    return run(
        functools.partial(gather_kernel, trades),
        "gather",
        [
            shaped((count * rows, att.shape[1]), BF16),
            shaped((tile.shape[0], count * rows), F32),
            shaped((trades,) + tokens.shape, BF16),
        ]
        + [shaped((tokens.shape[1] * (trades + 1), PAIR), F32)] * 2,
        0,
        [att, tile, tokens],
        collective_id=1,
        in_specs=[vmem, vmem, anywhere],
        out_specs=[anywhere, vmem, anywhere, vmem, vmem],
        scratch_shapes=[pltpu.VMEM((count * group, 128), F32), pltpu.VMEM((group, 128), F32)]
        + [dma((MESSAGES,))] * 4
        + [dma((3,)), dma((trades,)), dma((trades,)), dma((trades,)), dma((trades,))],
    )


def attend_kernel(windows, pairs, trades, exp_scale, *refs):
    stages = (trades + 1).bit_length() - 1
    q_ref, w_ref, kv_ref, cot_ref, x_ref, norms_ref = refs[:6]
    low_ref, wide_ref, log_ref, kept_ref, sent_ref, slots_ref, cots_ref = refs[6:13]
    middle_ref, normed_ref, others_ref = refs[13:16]
    slots, acc_all, top_all, total_all, mixed_rows = refs[16:21]
    own_sem, send_sem, recv_sem, save_sem, cot_send, cot_recv = refs[21:27]
    early_kept, early_normed, early_sem, early_recv, normed_sem, normed_recv = refs[27:33]
    early_sent, early_arrived = refs[33 : 33 + stages], refs[33 + stages :]
    step = pl.program_id(0)
    near_steps = windows * pairs
    steps = 2 * near_steps
    turn = step % (2 * pairs)
    is_far = turn >= pairs
    number = step // (2 * pairs) * pairs + turn % pairs
    tensor = lax.axis_index("tensor")
    core_peer = {"core": 1 - lax.axis_index("core")}
    far_peer = {"x": 1 - lax.axis_index("x")}
    cot_peers = [{"tensor": flipped(tensor, other + 1)} for other in range(trades)]

    def piece(number):
        return kv_ref.at[number // pairs, number % pairs]

    def own_copy(number):
        return pltpu.make_async_copy(piece(number), slots.at[number, 0], own_sem.at[number])

    def trade(number, slot):
        peer = far_peer if slot == 2 else core_peer
        source = slots.at[number, 2] if slot == 3 else piece(number)
        return send(
            source,
            slots.at[number, slot],
            send_sem.at[number, slot - 1],
            recv_sem.at[number, slot - 1],
            peer,
        )

    def cot_trade(other):
        return send(
            cot_ref, cots_ref.at[other], cot_send.at[other], cot_recv.at[other], cot_peers[other]
        )

    def early_trade(stage):
        return send(
            early_sent[stage],
            early_arrived[stage],
            early_sem.at[stage],
            early_recv.at[stage],
            {"tensor": flipped(tensor, (trades + 1) >> (stage + 1))},
        )

    def normed_trade(other):
        return send(
            early_normed,
            others_ref.at[other],
            normed_sem.at[other],
            normed_recv.at[other],
            cot_peers[other],
        )

    def save(number, slot):
        return pltpu.make_async_copy(
            slots.at[number, slot], slots_ref.at[number, slot], save_sem.at[number, slot]
        )

    @pl.when(step == 0)
    def _():
        greet([core_peer, far_peer] + cot_peers)

        @pl.loop(0, near_steps)
        def _(number):
            own_copy(number).start()
            trade(number, 1).start()
            trade(number, 2).start()

        for other in range(trades):
            cot_trade(other).start()

    @pl.when(step == 2 * pairs)
    def _():
        early_trade(0).start()

    @pl.when(step == 3 * pairs)
    def _():
        kept = early_kept[...]
        for stage in range(stages):
            early_trade(stage).wait_recv()
            kept = kept + early_arrived[stage][...].astype(F32)
            if stage + 1 < stages:
                half = kept.shape[0] // 2
                early_sent[stage + 1][...] = kept[half:].astype(BF16)
                early_trade(stage + 1).start()
                kept = kept[:half]
        middle = x_ref[...].astype(F32) + kept
        middle_ref[...] = middle
        normed = (normalise(middle)[0] * norms_ref[2:3, :] + norms_ref[3:4, :]).astype(BF16)
        normed_ref[...] = normed
        early_normed[...] = normed

    @pl.when(step == 3 * pairs + 1)
    def _():
        for other in range(trades):
            normed_trade(other).start()

    relayed = step // (2 * pairs) * pairs + turn - (pairs - 1)

    @pl.when(jnp.logical_and(turn >= pairs - 1, turn < 2 * pairs - 1))
    def _():
        trade(relayed, 2).wait_recv()
        trade(relayed, 3).start()
        save(relayed, 2).start()

    @pl.when(jnp.logical_not(is_far))
    def _():
        own_copy(number).wait()
        trade(number, 1).wait_recv()
        save(number, 0).start()
        save(number, 1).start()
        acc_all[number] = jnp.zeros(acc_all.shape[1:], F32)
        total_all[number] = jnp.zeros(acc_all.shape[1:], F32)
        top_all[number] = jnp.full(acc_all.shape[1:], -1e30, F32)

    @pl.when(is_far)
    def _():
        trade(number, 3).wait_recv()
        save(number, 3).start()

    query = q_ref[0]
    is_first = first_head(query.shape)
    base = jnp.where(is_far, 2, 0)
    carried_top = top_all[number]
    outs, tops = [], []
    for head in range(2):
        mine = is_first if head == 0 else jnp.logical_not(is_first)
        own_query = jnp.where(mine, query, jnp.zeros_like(query))
        scores = [dot_nt(own_query, slots[number, base + slot, 0]) for slot in range(2)]
        at = head * HEAD_DIM
        top = carried_top[:, at : at + 1]
        for one in scores:
            top = jnp.maximum(top, one.max(axis=1, keepdims=True))
        shift = top * exp_scale
        mixed = None
        for slot, one in enumerate(scores):
            weight = jnp.exp2(one * exp_scale - shift).astype(BF16)
            value = slots[number, base + slot, 1]
            lane_first = first_head(value.shape)
            lane_mine = lane_first if head == 0 else jnp.logical_not(lane_first)
            term = dot_nn(weight, jnp.where(lane_mine, value, jnp.ones_like(value)))
            mixed = term if mixed is None else mixed + term
        outs.append(mixed)
        tops.append(jnp.broadcast_to(top, mixed.shape))
    top = jnp.where(is_first, tops[0], tops[1])
    fade = jnp.exp2((carried_top - top) * exp_scale)
    acc = jnp.where(is_first, outs[0], outs[1]) + acc_all[number] * fade
    total = pltpu.roll(jnp.where(is_first, outs[1], outs[0]), HEAD_DIM, 1) + total_all[number] * fade

    @pl.when(jnp.logical_not(is_far))
    def _():
        acc_all[number] = acc
        top_all[number] = top
        total_all[number] = total

    @pl.when(is_far)
    def _():
        attended = acc / total
        low = attended.astype(BF16)
        low_ref[0] = low
        wide_ref[0] = attended
        log_ref[0] = (top * exp_scale + jnp.log2(total)).T
        term = dot_nt(low, w_ref[...])
        pair = number % pairs

        @pl.when(pair == 0)
        def _():
            mixed_rows[...] = term

        @pl.when(pair > 0)
        def _():
            mixed_rows[...] += term

        @pl.when(jnp.logical_and(pair == pairs - 1, number >= pairs))
        def _():
            half = kept_ref.shape[1]
            kept_ref[0] = mixed_rows[:half]
            sent_ref[0] = mixed_rows[half:].astype(BF16)

        @pl.when(number == pairs - 1)
        def _():
            half = kept_ref.shape[1]
            early_kept[...] = mixed_rows[:half]
            early_sent[0][...] = mixed_rows[half:].astype(BF16)

    @pl.when(step == steps - 1)
    def _():
        @pl.loop(0, near_steps)
        def _(number):
            for slot in range(1, 4):
                trade(number, slot).wait_send()
            for slot in range(4):
                save(number, slot).wait()

        for stage in range(stages):
            early_trade(stage).wait_send()
        for other in range(trades):
            cot_trade(other).wait_send()
            cot_trade(other).wait_recv()
            normed_trade(other).wait_send()
            normed_trade(other).wait_recv()


def attend(queries, own_kv, w_att, cotangent, tokens, norms, trades):
    windows, rows, cols = queries.shape
    width = w_att.shape[0]
    pairs = cols // PAIR
    near = windows * pairs
    out_at = 3 * pairs

    def far(i):
        turn = i % (2 * pairs)
        done = i // (2 * pairs) * pairs
        return jnp.where(turn >= pairs, done + turn - pairs, jnp.maximum(done - 1, 0))

    anywhere = pl.BlockSpec(memory_space=pl.ANY)
    wide = pl.BlockSpec((1, rows, PAIR), lambda i: (far(i) // pairs, 0, far(i) % pairs))
    half = pl.BlockSpec(
        (1, rows // 2, width), lambda i: (jnp.maximum(far(i) // pairs, 1) - 1, 0, 0)
    )
    own_rows = tokens.shape[1]
    own = pl.BlockSpec((own_rows, width), lambda i: (0, 0))
    stages = [rows >> (stage + 1) for stage in range((trades + 1).bit_length() - 1)]
    state = pltpu.VMEM((near, rows, PAIR), F32)
    dma = pltpu.SemaphoreType.DMA
    return run(
        functools.partial(attend_kernel, windows, pairs, trades, LOG2E / math.sqrt(HEAD_DIM)),
        "attend",
        [
            shaped((windows, rows, cols), BF16),
            shaped((windows, rows, cols), F32),
            shaped((windows, cols, rows), F32),
            shaped((windows - 1, rows // 2, width), F32),
            shaped((windows - 1, rows // 2, width), BF16),
            shaped((near, 4, 2, rows, PAIR), BF16),
            shaped((trades,) + cotangent.shape, BF16),
            shaped((own_rows, width), F32),
            shaped((own_rows, width), BF16),
            shaped((trades, own_rows, width), BF16),
        ],
        64 * windows * rows * rows * cols,
        [queries, w_att, own_kv, cotangent, tokens, norms],
        collective_id=0,
        grid=(2 * near,),
        in_specs=[
            pl.BlockSpec((1, rows, PAIR), lambda i: (i // (2 * pairs), 0, i % pairs)),
            pl.BlockSpec((width, PAIR), lambda i: (0, out_at + far(i) % pairs)),
            anywhere,
            anywhere,
            pl.BlockSpec((None, own_rows, width), lambda i: (0, 0, 0)),
            pl.BlockSpec(norms.shape, lambda i: (0, 0)),
        ],
        out_specs=[
            wide,
            wide,
            pl.BlockSpec((1, PAIR, rows), lambda i: (far(i) // pairs, far(i) % pairs, 0)),
            half,
            half,
            anywhere,
            anywhere,
            own,
            own,
            anywhere,
        ],
        scratch_shapes=[
            pltpu.VMEM((near, 4, 2, rows, PAIR), BF16),
            state,
            state,
            state,
            pltpu.VMEM((rows, width), F32),
            dma((near,)),
            dma((near, 3)),
            dma((near, 3)),
            dma((near, 4)),
            dma((trades,)),
            dma((trades,)),
            pltpu.VMEM((rows // 2, width), F32),
            pltpu.VMEM((own_rows, width), BF16),
            dma((len(stages),)),
            dma((len(stages),)),
            dma((trades,)),
            dma((trades,)),
        ]
        + [pltpu.VMEM((count, width), BF16) for count in stages] * 2,
    )


def attend_back_kernel(windows, pairs, blocks, exp_scale, score_scale, *refs):
    q_ref, wide_ref, log_ref, slots_ref, w_ref, cos_ref, sin_ref, last_ref = refs[:8]
    trades = blocks - 1
    known = (windows - 1) * blocks + 1
    grad_refs = list(refs[8 : 8 + known])
    refs = refs[8 + known :]
    sent_refs, refs = refs[:windows], refs[windows:]
    gq_ref, gk_ref, gv_ref, rows_ref = refs[:4]
    arrived_refs, refs = refs[4 : 4 + windows], refs[4 + windows :]
    dq_all, do_all, far_kept, far_sent, far_core, far_x, near_kept, near_sent, near_core = refs[:9]
    send_sem, recv_sem, result_send, result_recv, last_send, last_recv, last_others = refs[9:]
    grad_refs += [last_others.at[other] for other in range(trades)]
    step = pl.program_id(0)
    count = windows * pairs
    tensor = lax.axis_index("tensor")
    core_peer = {"core": 1 - lax.axis_index("core")}
    far_peer = {"x": 1 - lax.axis_index("x")}
    result_peer = {"tensor": flipped(tensor, lax.axis_size("tensor") // 2)}

    def trade(kind, number):
        source, target, peer = (
            (far_sent, far_core, core_peer),
            (far_kept, far_x, far_peer),
            (near_sent, near_core, core_peer),
        )[kind]
        return send(
            source.at[number],
            target.at[number],
            send_sem.at[kind, number],
            recv_sem.at[kind, number],
            peer,
        )

    def result_trade(w):
        return send(
            sent_refs[w], arrived_refs[w], result_send.at[w], result_recv.at[w], result_peer
        )

    others = [{"tensor": flipped(tensor, other + 1)} for other in range(trades)]

    def last_trade(other):
        return send(
            last_ref, last_others.at[other], last_send.at[other], last_recv.at[other], others[other]
        )

    @pl.when(step == 0)
    def _():
        greet([core_peer, far_peer] + others)
        for other in range(trades):
            last_trade(other).start()
        for w in range(windows):
            result_trade(w).start()

    def at_step(first, body):
        number = step - first

        @pl.when(jnp.logical_and(number >= 0, number < count))
        def _():
            body(number)

    def send_far(number):
        trade(0, number).start()

    def add_far(number):
        trade(0, number).wait_recv()
        far_kept[number] = (
            far_kept[number].astype(F32) + far_core[number].astype(F32)
        ).astype(BF16)

    def send_x(number):
        trade(1, number).start()

    def send_near(number):
        trade(2, number).start()

    def finish(number):
        trade(2, number).wait_recv()
        trade(1, number).wait_recv()
        total = (
            near_kept[number].astype(F32)
            + near_core[number].astype(F32)
            + far_x[number].astype(F32)
        )
        key = total[0]
        gk_ref[0] = (key * cos_ref[...] - swap_halves(key) * sin_ref[...]).astype(BF16)
        gv_ref[0] = total[1].astype(BF16)

    at_step(1, send_far)
    at_step(3, send_x)
    at_step(count + 1, send_near)
    at_step(2, add_far)
    at_step(count + 2, finish)

    for w in range(windows):

        @pl.when(step == w * pairs)
        def _(w=w):
            if w == windows - 1:
                for other in range(trades):
                    last_trade(other).wait_recv()
            at_row = 0
            for grad_ref in grad_refs[w * blocks : (w + 1) * blocks]:
                rows_ref[0, at_row : at_row + grad_ref.shape[0], :] = grad_ref[...]
                at_row += grad_ref.shape[0]

    def gradients(number, grad_out, kept, sent):
        query = q_ref[0]
        is_first = first_head(query.shape)
        overlap = (grad_out.astype(F32) * wide_ref[0]).T
        logs = log_ref[0]
        zero = jnp.zeros_like(query)
        own_q, own_do, row_log, row_sum = [], [], [], []
        for head in range(2):
            mine = is_first if head == 0 else jnp.logical_not(is_first)
            own_q.append(jnp.where(mine, query, zero))
            own_do.append(jnp.where(mine, grad_out, zero))
            at = head * HEAD_DIM
            row_log.append(logs[at : at + 1, :])
            row_sum.append(jnp.sum(overlap[at : at + HEAD_DIM, :], axis=0, keepdims=True))
        dq_parts = [None, None]
        for slot, target in enumerate((kept, sent)):
            key, value = slots_ref[0, slot, 0], slots_ref[0, slot, 1]
            key_turned = key.T
            grad_key, grad_value = None, None
            for head in range(2):
                scores = dot_nt(key, own_q[head])
                probs = jnp.exp2(scores * exp_scale - row_log[head])
                grad_probs = dot_nt(value, own_do[head])
                grad_scores = (probs * (grad_probs - row_sum[head])).astype(BF16)
                term_v = dot_nn(probs.astype(BF16), own_do[head])
                term_k = dot_nn(grad_scores, own_q[head])
                at = head * HEAD_DIM
                term_q = dot_nn(key_turned[at : at + HEAD_DIM, :], grad_scores)
                grad_value = term_v if grad_value is None else grad_value + term_v
                grad_key = term_k if grad_key is None else grad_key + term_k
                dq_parts[head] = term_q if dq_parts[head] is None else dq_parts[head] + term_q
            target[number, 0] = (grad_key * score_scale).astype(BF16)
            target[number, 1] = grad_value.astype(BF16)
        return jnp.concatenate(dq_parts, axis=0).T * score_scale

    @pl.when(step < count)
    def _():
        grad_out = dot_nn(rows_ref[0], w_ref[...]).astype(BF16)
        do_all[step] = grad_out
        dq_all[step] = gradients(step, grad_out, far_kept, far_sent)

    @pl.when(jnp.logical_and(step >= count, step < 2 * count))
    def _():
        number = step - count
        grad_query = dq_all[number] + gradients(number, do_all[number], near_kept, near_sent)
        gq_ref[0] = (grad_query * cos_ref[...] - swap_halves(grad_query) * sin_ref[...]).astype(
            BF16
        )

    @pl.when(step == pl.num_programs(0) - 1)
    def _():
        @pl.loop(0, count)
        def _(number):
            for kind in range(3):
                trade(kind, number).wait_send()

        for other in range(trades):
            last_trade(other).wait_send()
        for w in range(windows):
            result_trade(w).wait_send()
            result_trade(w).wait_recv()


def attend_back(queries, wide, logs, slots_all, grad_blocks, w_att, tables, sent):
    windows, rows, cols = queries.shape
    width = w_att.shape[0]
    pairs = cols // PAIR
    count = windows * pairs
    out_at = 3 * pairs
    score_scale = 1.0 / math.sqrt(HEAD_DIM)
    blocks = lax.axis_size("tensor")
    grads = [block for one in grad_blocks for block in one]
    last = grads[-1]

    def spot(lag, last=None):
        def index(i):
            number = jnp.clip(i - lag, 0, count - 1)
            return (number // pairs, 0, number % pairs)

        return pl.BlockSpec((1, rows, PAIR), index)

    def both(i):
        return jnp.minimum(i, 2 * count - 1) % count

    dma = pltpu.SemaphoreType.DMA
    piece = pltpu.VMEM((count, 2, rows, PAIR), BF16)
    anywhere = pl.BlockSpec(memory_space=pl.ANY)
    return run(
        functools.partial(
            attend_back_kernel, windows, pairs, blocks, score_scale * LOG2E, score_scale
        ),
        "attend_back",
        [shaped((windows, rows, cols), BF16)] * 3
        + [shaped((windows, rows, width), BF16)]
        + [shaped(one.shape, BF16) for one in sent],
        160 * windows * rows * rows * cols,
        [queries, wide, logs, slots_all, w_att, *tables, last, *grads, *sent],
        collective_id=2,
        grid=(2 * count + 2,),
        in_specs=[
            pl.BlockSpec((1, rows, PAIR), lambda i: (both(i) // pairs, 0, both(i) % pairs)),
            pl.BlockSpec((1, rows, PAIR), lambda i: (both(i) // pairs, 0, both(i) % pairs)),
            pl.BlockSpec((1, PAIR, rows), lambda i: (both(i) // pairs, both(i) % pairs, 0)),
            pl.BlockSpec(
                (1, 2, 2, rows, PAIR),
                lambda i: (both(i), jnp.where(i < count, 1, 0), 0, 0, 0),
            ),
            pl.BlockSpec((width, PAIR), lambda i: (0, out_at + jnp.minimum(i, count - 1) % pairs)),
            pl.BlockSpec((rows, PAIR), lambda i: (0, 0)),
            pl.BlockSpec((rows, PAIR), lambda i: (0, 0)),
            anywhere,
        ]
        + [pl.BlockSpec(block.shape, lambda i: (0, 0)) for block in grads]
        + [anywhere] * windows,
        out_specs=[
            spot(count),
            spot(count + 2),
            spot(count + 2),
            pl.BlockSpec((1, rows, width), lambda i: (jnp.minimum(i // pairs, windows - 1), 0, 0)),
        ]
        + [anywhere] * windows,
        scratch_shapes=[pltpu.VMEM((count, rows, PAIR), F32), pltpu.VMEM((count, rows, PAIR), BF16)]
        + [piece] * 7
        + [dma((3, count)), dma((3, count)), dma((windows,)), dma((windows,))]
        + [dma((blocks - 1,)), dma((blocks - 1,)), pltpu.VMEM((blocks - 1,) + last.shape, BF16)],
    )


def middle_kernel(x_ref, kept_ref, arrived_ref, norms_ref, middle_ref, normed_ref):
    middle = x_ref[...].astype(F32) + (kept_ref[...] + arrived_ref[...].astype(F32))
    middle_ref[...] = middle
    normed_ref[...] = (
        normalise(middle)[0] * norms_ref[2:3, :] + norms_ref[3:4, :]
    ).astype(BF16)


def second_norm(x_rows, kept, arrived, norms):
    args, in_specs = row_planes((x_rows, kept, arrived))
    rows, width = arrived.shape
    block = pl.BlockSpec((rows // NORM_BLOCKS, width), lambda i: (i, 0))
    return run(
        middle_kernel,
        "second_norm",
        [shaped((rows, width), F32), shaped((rows, width), BF16)],
        20 * rows * width,
        [*args, norms],
        grid=(NORM_BLOCKS,),
        in_specs=[*in_specs, full(*norms.shape)],
        out_specs=[block, block],
    )


def feed_kernel(blocks, swaps, first, slots, *refs):
    refs = list(refs)

    def take(count):
        taken = refs[:count]
        del refs[:count]
        return taken

    w_refs = take(3)
    if first:
        weight_ref, norms_ref = take(2)
        x_refs, cot_refs = take(blocks), take(blocks)
        sources = take(len(swaps))
        both_ref, wide_ref, total_ref, grad_ref = take(4)
    else:
        both_ref, total_in, grad_in, _ = take(4)
        sources = take(len(swaps))
        wide_ref, kept_ref, sent_ref, grad_kept_ref, grad_sent_ref = take(5)
    trades = tensor_trades(sources, take(len(swaps)), swaps, *take(2 if swaps else 0))
    block = pl.program_id(0)

    def weights_of(ref):
        if len(ref.shape) == 2:
            return ref[...]
        depths, cores, halves = ref.shape[:3]
        return jnp.concatenate(
            [
                ref[depth, core, half]
                for depth in range(depths)
                for half in range(halves)
                for core in range(cores)
            ],
            axis=0,
        )

    gate_w, up_w, down_w = [weights_of(ref) for ref in w_refs]

    @pl.when(block == 0)
    def _():
        start_trades(trades, swaps)

    if first:
        factor = factor_of(weight_ref, norms_ref, slots)
        for at in range(blocks):

            @pl.when(block == at)
            def _(at=at):
                both_ref[0] = x_refs[at][...]
                both_ref[1] = (cot_refs[at][...].astype(F32) * factor).astype(BF16)

    x_rows = both_ref[0]
    gate = dot_nn(x_rows, gate_w)
    up = dot_nn(x_rows, up_w)
    grad_hidden = dot_nn(both_ref[1], down_w)
    sig = jax.nn.sigmoid(gate)
    swish = gate * sig
    hidden = (swish * up).astype(BF16)
    grad_gate = (grad_hidden * up * sig * (1.0 + gate * (1.0 - sig))).astype(BF16)
    grad_up = (grad_hidden * swish).astype(BF16)
    wide_ref[0] = grad_gate
    wide_ref[1] = grad_up
    wide_ref[2] = hidden
    grad_total = dot_nt(grad_gate, gate_w) + dot_nt(grad_up, up_w)
    total = dot_nt(hidden, down_w)
    if first:
        total_ref[...] = total
        grad_ref[...] = grad_total
    else:
        total = total + total_in[...]
        grad_total = grad_total + grad_in[...]
        rows = total.shape[0]
        for at in range(blocks):

            @pl.when(block == at)
            def _(at=at):
                start = (at % (blocks // 2)) * rows
                if at < blocks // 2:
                    kept_ref[start : start + rows] = total
                    grad_kept_ref[start : start + rows] = grad_total
                else:
                    sent_ref[start : start + rows] = total.astype(BF16)
                    grad_sent_ref[start : start + rows] = grad_total.astype(BF16)

    @pl.when(block == blocks - 1)
    def _():
        for trade in trades:
            trade.wait()


def tensor_trades(sources, targets, masks, send_sem=None, recv_sem=None):
    tensor = lax.axis_index("tensor")
    trades = []
    for source, target, kinds in zip(sources, targets, masks):
        for number, mask in enumerate(kinds):
            sems = (send_sem.at[len(trades)], recv_sem.at[len(trades)])
            peer = {"tensor": flipped(tensor, mask)}
            trades.append(send(source, target.at[number], *sems, peer))
    return trades


def start_trades(trades, masks):
    if trades:
        tensor = lax.axis_index("tensor")
        peers = sorted({mask for kinds in masks for mask in kinds})
        greet([{"tensor": flipped(tensor, mask)} for mask in peers])
        for trade in trades:
            trade.start()


def feed_specs(weights):
    lead = weights.shape[:-1]
    part_cols = weights.shape[-1] // 3
    zeros = (0,) * len(lead)
    return part_cols, [
        pl.BlockSpec(lead + (part_cols,), functools.partial(lambda at, i: zeros + (at,), k))
        for k in range(3)
    ]


def full(*shape):
    return pl.BlockSpec(shape, lambda i: (0,) * len(shape))


def feed_call(name, collective_id, blocks, rows, width, part_cols, out, args, swaps, **options):
    masks = [kinds for _, kinds in swaps]
    anywhere = pl.BlockSpec(memory_space=pl.ANY)
    total = sum(len(kinds) for kinds in masks)
    out_shape, out_specs = out
    return run(
        functools.partial(
            feed_kernel, blocks, masks, name == "feed_first", options.pop("slots", None)
        ),
        name,
        out_shape + [shaped((len(kinds),) + array.shape, BF16) for array, kinds in swaps],
        12 * rows * width * part_cols,
        args + [array for array, _ in swaps],
        collective_id=collective_id if swaps else None,
        grid=(blocks,),
        in_specs=options.pop("in_specs") + [anywhere] * len(swaps),
        out_specs=out_specs + [anywhere] * len(swaps),
        scratch_shapes=[pltpu.SemaphoreType.DMA((total,))] * 2 if swaps else [],
        **options,
    )


def feed_first(x_blocks, cot_blocks, weight, norms, slots, weights, swaps=()):
    operands, specs = zip(*[plane(block) for block in (*x_blocks, *cot_blocks)])
    width = math.prod(weights.shape[:-1])
    blocks, own = len(x_blocks), specs[0].block_shape[-2]
    rows = blocks * own
    part_cols, w_specs = feed_specs(weights)
    row_block = pl.BlockSpec((own, width), lambda i: (i, 0))
    out_shape = [shaped((2, rows, width), BF16), shaped((3, rows, 2 * part_cols), BF16)]
    out_shape += [shaped((rows, width), F32)] * 2
    out_specs = [
        pl.BlockSpec((2, own, width), lambda i: (0, i, 0)),
        pl.BlockSpec((3, own, part_cols), lambda i: (0, i, 0)),
        row_block,
        row_block,
    ]
    return feed_call(
        "feed_first",
        6,
        blocks,
        rows,
        width,
        part_cols,
        (out_shape, out_specs),
        [weights, weights, weights, weight, norms, *operands],
        swaps,
        in_specs=w_specs + [SCALAR, full(*norms.shape)] + list(specs),
        slots=slots,
    )


def feed_last(both, wide, totals, weights, blocks, swaps=()):
    rows, width = both.shape[1:]
    own = rows // blocks
    part_cols, w_specs = feed_specs(weights)
    half = full(rows // 2, width)
    row_block = pl.BlockSpec((own, width), lambda i: (i, 0))
    out_shape = [shaped(wide.shape, BF16)]
    out_shape += [shaped((rows // 2, width), F32), shaped((rows // 2, width), BF16)] * 2
    return feed_call(
        "feed_last",
        5,
        blocks,
        rows,
        width,
        part_cols,
        (out_shape, [pl.BlockSpec((3, own, part_cols), lambda i: (0, i, 1))] + [half] * 4),
        [weights, weights, weights, both, *totals, wide],
        swaps,
        in_specs=w_specs
        + [pl.BlockSpec((2, own, width), lambda i: (0, i, 0)), row_block, row_block]
        + [pl.BlockSpec(memory_space=pl.ANY)],
        input_output_aliases={6: 0},
    )


def weights_kernel(windows, masks, *refs):
    lefts, rights = refs[:windows], refs[windows : 2 * windows]
    refs = refs[2 * windows :]
    sources, out_ref, targets = refs[: len(masks)], refs[len(masks)], refs[len(masks) + 1 :]
    at = pl.program_id(0)
    trades = tensor_trades(refs[: len(masks)], targets[: len(masks)], masks, *targets[len(masks) :])

    @pl.when(at == 0)
    def _():
        start_trades(trades, masks)

    total = None
    for left, right in zip(lefts, rights):
        term = dot_tn(left[...], right[...])
        total = term if total is None else total + term
    total = total.astype(BF16)
    depths, cores, halves, shard = out_ref.shape[:4]
    for depth in range(depths):
        for half in range(halves):
            for core in range(cores):
                start = ((depth * halves + half) * cores + core) * shard
                out_ref[depth, core, half] = total[start : start + shard]

    if masks:

        @pl.when(at == pl.num_programs(0) - 1)
        def _():
            for trade in trades:
                trade.wait()


def feed_weights(boths, wides, part, swaps):
    windows = len(boths)
    rows, width = boths[0].shape[1:]
    hidden_cols = wides[0].shape[2] // 2
    step = min(512, hidden_cols)
    steps = hidden_cols // step
    lead = (lax.axis_size("dp"), lax.axis_size("core"), lax.axis_size("x"))
    lead += (width // math.prod(lead),)
    masks = [kinds for _, kinds in swaps]
    anywhere = pl.BlockSpec(memory_space=pl.ANY)
    left = pl.BlockSpec((None, rows, width), lambda i: (i // (2 * steps), 0, 0))
    right = pl.BlockSpec((None, rows, step), lambda i: (i // steps, 0, part * steps + i % steps))
    total = sum(len(kinds) for kinds in masks)
    return run(
        functools.partial(weights_kernel, windows, masks),
        "feed_weights",
        [shaped(lead + (3 * hidden_cols,), BF16)]
        + [shaped((len(kinds),) + array.shape, BF16) for array, kinds in swaps],
        6 * windows * rows * width * hidden_cols,
        [*boths, *wides] + [array for array, _ in swaps],
        collective_id=(6 if part else 4) if swaps else None,
        grid=(3 * steps,),
        in_specs=[left] * windows + [right] * windows + [anywhere] * len(swaps),
        out_specs=[pl.BlockSpec(lead + (step,), lambda i: (0, 0, 0, 0, i))]
        + [anywhere] * len(swaps),
        scratch_shapes=[pltpu.SemaphoreType.DMA((total,))] * 2 if swaps else [],
    )


def norm_grad(kept_ref, arrived_ref, stream, gain, sums_ref):
    grad_normed = kept_ref[...] + arrived_ref[...].astype(F32)
    normed, inv_std = normalise(stream)
    sums = [
        jnp.sum(one, axis=0, keepdims=True) for one in (grad_normed * normed, grad_normed)
    ]

    @pl.when(pl.program_id(0) == 0)
    def _():
        for at, one in enumerate(sums):
            sums_ref[at : at + 1, :] = one

    @pl.when(pl.program_id(0) > 0)
    def _():
        for at, one in enumerate(sums):
            sums_ref[at : at + 1, :] += one

    return norm_back(grad_normed, normed, inv_std, gain)


def middle_back_kernel(
    slots, weight_ref, kept_ref, arrived_ref, middle_ref, cot_ref, norms_ref, grad_ref, low_ref, sums_ref
):
    grad_y = cot_ref[...].astype(F32) * factor_of(weight_ref, norms_ref, slots)
    grad = grad_y + norm_grad(
        kept_ref, arrived_ref, middle_ref[...], norms_ref[2:3, :], sums_ref
    )
    grad_ref[...] = grad
    low_ref[...] = grad.astype(BF16)


NORM_BLOCKS = 1


def row_planes(operands):
    pairs = []
    for one in operands:
        array, at = one if isinstance(one, tuple) else (one, ())
        rows, width = array.shape[len(at) :]
        pairs.append(plane(one, (rows // NORM_BLOCKS, width), lambda i: (i, 0)))
    return [list(part) for part in zip(*pairs)]


def second_norm_back(weight, slots, kept, arrived, middle, cot_rows, norms):
    args, in_specs = row_planes((kept, arrived, middle, cot_rows))
    rows, width = kept.shape
    block = pl.BlockSpec((rows // NORM_BLOCKS, width), lambda i: (i, 0))
    return run(
        functools.partial(middle_back_kernel, slots),
        "second_norm_back",
        [shaped(kept.shape, F32), shaped(kept.shape, BF16), shaped((2, width), F32)],
        40 * kept.size,
        [weight, *args, norms],
        grid=(NORM_BLOCKS,),
        in_specs=[SCALAR, *in_specs, full(*norms.shape)],
        out_specs=[block, block, full(2, width)],
    )


class SumRoute:
    def __init__(self, part, rows, core_in, mine, x_in, z_in, send_sem, recv_sem):
        self.read, self.rows = part, rows
        self.core_in, self.mine, self.x_in, self.z_in = core_in, mine, x_in, z_in
        self.send_sem, self.recv_sem = send_sem, recv_sem
        self.seq, self.depth = seq_index(), lax.axis_index("dp")
        self.peers = half_chip_peers()

    def place(self, number, other_core):
        seq = flipped(self.seq, 2) if number >= 4 else self.seq
        seq = flipped(seq, 1) if other_core else seq
        turn = (self.depth + number % 4) % lax.axis_size("dp")
        return pl.ds(
            pl.multiple_of((turn * seq_size() + seq) * self.rows, self.rows), self.rows
        )

    def message(self, number):
        if number < 8:
            source, target, peer = self.read.at[self.place(number, True), :], self.core_in, "core"
            target = target.at[number]
        elif number < 12:
            source, target, peer = self.mine.at[number - 4], self.x_in.at[number - 8], "far"
        else:
            turn, peer = ((2, "up"), (1, "up"), (3, "down"))[number - 12]
            source, target = self.mine.at[turn], self.z_in.at[number - 12]
        return send(
            source, target, self.send_sem.at[number], self.recv_sem.at[number], self.peers[peer]
        )

    def start(self, *numbers):
        for number in numbers:
            self.message(number).start()

    def add_core(self, number):
        self.message(number).wait_recv()
        own = self.read[self.place(number, False), :].astype(F32)
        self.mine[number] = (own + self.core_in[number].astype(F32)).astype(self.mine.dtype)

    def add_x(self, number):
        self.message(8 + number).wait_recv()
        total = self.mine[number].astype(F32) + self.x_in[number].astype(F32)
        self.mine[number] = total.astype(self.mine.dtype)

    def add_up(self):
        self.message(12).wait_recv()
        total = self.mine[1].astype(F32) + self.z_in[0].astype(F32)
        self.mine[1] = total.astype(self.mine.dtype)

    def total(self):
        self.message(13).wait_recv()
        self.message(14).wait_recv()
        return (
            self.mine[0].astype(F32) + self.z_in[1].astype(F32) + self.z_in[2].astype(F32)
        )

    def sent(self):
        for number in range(SUM_MESSAGES):
            self.message(number).wait_send()


SUM_MESSAGES = 15


def finish_kernel(windows, trades, score_cols, *refs):
    stages = (trades + 1).bit_length() - 1
    refs = list(refs)

    def take(count):
        taken = refs[:count]
        del refs[:count]
        return taken

    far_inputs = take(8)
    shard_ref = take(1)[0]
    norms_ref = take(1)[0]
    second_refs = take(windows)
    grad_refs = take(windows)
    weights_ref, vectors_ref, input_ref, shard_arrived = take(4)
    loads = take(8)
    grad_loads = take(windows)
    part, core_in, mine, x_in, z_in = take(5)
    tiles, own_tiles, arrived_tiles = take(3)
    small_core, small_mine, small_x, small_z = take(4)
    kept_all = take(windows)
    stage_sent = [take(stages) for _ in range(windows)]
    stage_arrived = [take(stages) for _ in range(windows)]
    load_sem, big_send, big_recv, small_send, small_recv = take(5)
    y_send, y_recv, tile_send, tile_recv, shard_sem = take(5)
    assert not refs
    (grad_q, grad_k, grad_v, normed, grad_mid, attended, w_qkv, tokens) = loads[:8]
    tensor = lax.axis_index("tensor")
    others = [{"tensor": flipped(tensor, other + 1)} for other in range(trades)]
    shards = lax.axis_size("dp") * seq_size()
    devices = shards * (trades + 1)
    group = tiles.shape[0] // shards
    width = part.shape[1]
    cols = score_cols
    rows = width // shards

    w_source = far_inputs[6].at[:, pl.ds(0, 3 * cols)]
    sources = [*far_inputs[:6], w_source, far_inputs[7]]
    sources += [*grad_refs]
    targets = [*loads, *grad_loads]
    copies = [
        pltpu.make_async_copy(source, target, load_sem.at[at])
        for at, (source, target) in enumerate(zip(sources, targets))
    ]
    order = [4, 5, 6, 0, 1, 2, 3, 7] + list(range(8, len(copies)))
    for at in order:
        copies[at].start()

    def block_route(block):
        return SumRoute(
            part.at[block],
            rows,
            core_in.at[block],
            mine.at[block],
            x_in.at[block],
            z_in.at[block],
            big_send.at[block],
            big_recv.at[block],
        )

    routes = [block_route(block) for block in range(4)]
    small = SumRoute(
        tiles, group, small_core, small_mine, small_x, small_z, small_send, small_recv
    )
    greet(list(small.peers.values()) + others)
    everything = (6, 7, 5, 4, 2, 3, 1, 0)

    def product(block, left, right):
        total = None
        for w in range(windows):
            term = dot_tn(left[w], right[w])
            total = term if total is None else total + term
        part[block] = total.astype(BF16)

    def y_trade(w, stage):
        return send(
            stage_sent[w][stage],
            stage_arrived[w][stage],
            y_send.at[w, stage],
            y_recv.at[w, stage],
            {"tensor": flipped(tensor, (trades + 1) >> (stage + 1))},
        )

    def turn_back(w):
        total = None
        for at, grad in enumerate((grad_q, grad_k, grad_v)):
            term = dot_nt(grad[w], w_qkv[:, at * cols : (at + 1) * cols])
            total = term if total is None else total + term
        half = total.shape[0] // 2
        kept_all[w][...] = total[:half]
        stage_sent[w][0][...] = total[half:].astype(BF16)

    def fill_tiles(row, values):
        span = width // devices
        for device in range(devices):
            at = device * 8 + row
            tiles[at : at + 2, :span] = values[:, device * span : (device + 1) * span]

    def add_cores(route):
        for number in everything:
            route.add_core(number)

    def across(route):
        route.start(10, 11, 9, 8)

    def add_across(route):
        for number in (2, 3, 1, 0):
            route.add_x(number)

    count = shard_ref.shape[0] // 2
    far_rows = pl.ds(pl.multiple_of((1 - lax.axis_index("x")) * count, count), count)
    shard_trade = send(
        shard_ref.at[far_rows, :],
        shard_arrived,
        shard_sem.at[0],
        shard_sem.at[1],
        small.peers["far"],
    )
    shard_trade.start()
    for at in (6, 0, 1, 2):
        copies[at].wait()
    turn_back(0)
    copies[4].wait()
    copies[5].wait()
    product(3, grad_mid, attended)
    y_trade(0, 0).start()
    tiles[...] = jnp.zeros_like(tiles)
    fill_tiles(2, sum(ref[...] for ref in second_refs))
    copies[3].wait()
    routes[3].start(*everything)
    product(0, normed, grad_q)
    add_cores(routes[3])
    routes[0].start(*everything)
    across(routes[3])
    for w in range(1, windows):
        turn_back(w)
    add_cores(routes[0])
    across(routes[0])
    for w in range(1, windows):
        y_trade(w, 0).start()
    product(1, normed, grad_k)
    add_across(routes[3])
    routes[1].start(*everything)
    product(2, normed, grad_v)
    routes[3].start(12, 14)
    add_cores(routes[1])
    across(routes[1])
    for at in range(7, 8 + windows):
        copies[at].wait()
    sums = [None, None]

    def first_norm(w):
        kept = kept_all[w][...]
        for stage in range(stages):
            y_trade(w, stage).wait_recv()
            kept = kept + stage_arrived[w][stage][...].astype(F32)
            if stage + 1 < stages:
                half = kept.shape[0] // 2
                stage_sent[w][stage + 1][...] = kept[half:].astype(BF16)
                y_trade(w, stage + 1).start()
                kept = kept[:half]
        normed_rows, inv_std = normalise(tokens[w].astype(F32))
        for at, one in enumerate((kept * normed_rows, kept)):
            one = jnp.sum(one, axis=0, keepdims=True)
            sums[at] = one if sums[at] is None else sums[at] + one
        input_ref[w] = grad_loads[w][...] + norm_back(
            kept, normed_rows, inv_std, norms_ref[0:1, :]
        )

    first_norm(0)
    routes[2].start(*everything)
    add_across(routes[0])
    add_cores(routes[2])
    across(routes[2])
    routes[3].add_up()
    routes[0].start(12, 14)
    routes[3].start(13)
    for w in range(1, windows):
        first_norm(w)
    fill_tiles(0, jnp.concatenate(sums, axis=0))
    add_across(routes[1])
    small.start(*everything)
    routes[0].add_up()
    routes[1].start(12, 14)
    add_cores(small)
    routes[0].start(13)
    across(small)
    add_across(routes[2])
    routes[1].add_up()
    routes[2].start(12, 14)
    add_across(small)
    routes[1].start(13)
    small.start(12, 14)
    for block in (3, 0):
        weights_ref[:, block * cols : (block + 1) * cols] = routes[block].total()
    small.add_up()
    routes[2].add_up()
    small.start(13)
    weights_ref[:, cols : 2 * cols] = routes[1].total()
    routes[2].start(13)
    own_tiles[...] = small.total()

    def tile_trade(other):
        place = pl.ds(pl.multiple_of(flipped(tensor, other + 1) * 8, 8), 8)
        return send(
            own_tiles.at[place, :],
            arrived_tiles.at[other],
            tile_send.at[other],
            tile_recv.at[other],
            others[other],
        )

    weights_ref[:, 2 * cols : 3 * cols] = routes[2].total()
    for other in range(trades):
        tile_trade(other).start()
    vectors = own_tiles[pl.ds(pl.multiple_of(tensor * 8, 8), 8), :]
    for other in range(trades):
        tile_trade(other).wait_recv()
        vectors = vectors + arrived_tiles[other]
    vectors_ref[...] = vectors
    shard_trade.wait()
    for route in (*routes, small):
        route.sent()
    for w in range(windows):
        for stage in range(stages):
            y_trade(w, stage).wait_send()
    for other in range(trades):
        tile_trade(other).wait_send()


def finish(
    grads,
    normed,
    grad_mid,
    attended,
    w_att,
    tokens,
    ffn_shard,
    norms,
    second_sums,
    grad_middles,
    trades,
):
    windows, rows, cols = grads[0].shape
    width = w_att.shape[0]
    own_rows = tokens.shape[1]
    shards = lax.axis_size("dp") * seq_size()
    shard = width // shards
    group = 8 * (trades + 1)
    stages = [rows >> (stage + 1) for stage in range((trades + 1).bit_length() - 1)]
    dma = pltpu.SemaphoreType.DMA
    anywhere = pl.BlockSpec(memory_space=pl.ANY)
    vmem = pl.BlockSpec(memory_space=pltpu.VMEM)
    far_inputs = [*grads, normed, grad_mid, attended, w_att, tokens]
    kinds = (8, 8, 4, 3)

    def like(array):
        return pltpu.VMEM(array.shape, array.dtype)

    loads = [like(array) for array in far_inputs]
    loads[6] = pltpu.VMEM((width, 3 * cols), BF16)
    return run(
        functools.partial(finish_kernel, windows, trades, cols),
        "finish",
        [
            shaped((shard, 4 * cols), F32),
            shaped((8, 128), F32),
            shaped((windows, own_rows, width), F32),
            shaped((ffn_shard.shape[0] // 2, ffn_shard.shape[1]), BF16),
        ],
        8 * windows * rows * width * cols + 6 * windows * rows * width * cols,
        [*far_inputs, ffn_shard, norms, *second_sums, *grad_middles],
        collective_id=3,
        in_specs=[anywhere] * 9
        + [vmem] * (1 + windows)
        + [anywhere] * windows,
        out_specs=[vmem] * 3 + [anywhere],
        scratch_shapes=loads
        + [like(array) for array in grad_middles]
        + [pltpu.VMEM((4, width, cols), BF16)]
        + [pltpu.VMEM((4, count, shard, cols), BF16) for count in kinds]
        + [
            pltpu.VMEM((shards * group, 128), F32),
            pltpu.VMEM((group, 128), F32),
            pltpu.VMEM((trades, 8, 128), F32),
        ]
        + [pltpu.VMEM((count, group, 128), F32) for count in kinds]
        + [pltpu.VMEM((rows // 2, width), F32)] * windows
        + [pltpu.VMEM((count, width), BF16) for count in stages] * (2 * windows)
        + [
            dma((8 + windows,)),
            dma((4, SUM_MESSAGES)),
            dma((4, SUM_MESSAGES)),
            dma((SUM_MESSAGES,)),
            dma((SUM_MESSAGES,)),
            dma((windows, len(stages))),
            dma((windows, len(stages))),
            dma((trades,)),
            dma((trades,)),
            dma((2,)),
        ],
    )


def result_kernel(windows, *refs):
    out_ref = refs[-1]
    for w in range(windows):
        middle_ref, kept_ref, arrived_ref = refs[3 * w : 3 * w + 3]
        out_ref[w] = (
            middle_ref[...] + (kept_ref[...] + arrived_ref[...].astype(F32))
        ).astype(BF16)


def results(parts):
    rows, width = parts[0][0].shape
    return run(
        functools.partial(result_kernel, len(parts)),
        "results",
        shaped((len(parts), rows, width), BF16),
        2 * len(parts) * rows * width,
        [array for part in parts for array in part],
    )


def local(
    tokens,
    cotangent,
    species,
    counts,
    species_scale,
    norm1_gain,
    norm1_bias,
    w_query,
    w_key,
    w_value,
    w_out,
    norm2_gain,
    norm2_bias,
    w_gate,
    w_up,
    w_down,
):
    windows_here, own_rows, model_width = tokens.shape
    tensor_size = lax.axis_size("tensor")
    block_rows = own_rows * tensor_size
    head_cols = w_query.shape[1]
    hidden_cols = w_gate.shape[1]
    shards = ("dp", "x", "core")

    labels = lax.broadcasted_iota(jnp.int32, (windows_here, species_scale.shape[0]), 1)
    chosen = jnp.sum(jnp.where(species[:, None] == labels, species_scale[None, :], 0.0), axis=1)
    weighted = counts.astype(F32) * chosen

    lanes = jnp.zeros((8, 128), F32)
    vectors = jnp.stack([norm1_gain, norm1_bias, norm2_gain, norm2_bias])
    tile = lanes.at[:4, : vectors.shape[1]].set(vectors).at[4, :].set(jnp.sum(weighted))
    part = hidden_cols // 2
    turned = w_down.T
    first_ffn = jnp.concatenate([w_gate[:, :part], w_up[:, :part], turned[:, :part]], axis=1)
    last_ffn = jnp.concatenate([w_gate[:, part:], w_up[:, part:], turned[:, part:]], axis=1)
    upper = lax.axis_index("x") == 1

    def gather_ffn(own, across):
        pair = jnp.where(
            upper,
            jnp.concatenate([across, own], axis=0),
            jnp.concatenate([own, across], axis=0),
        )
        whole = lax.all_gather(pair, ("dp", "core"), axis=0, tiled=True)
        return whole.reshape(
            lax.axis_size("dp"), lax.axis_size("core"), lax.axis_size("x"), -1, whole.shape[1]
        )

    first_ffn = lax.all_gather(first_ffn, shards, axis=0, tiled=True)
    last_across = swap(last_ffn, "x", 1)
    w_att, norms, arrived_tokens, cosine, sine = gather(
        jnp.concatenate([w_query, w_key, w_value, w_out.T], axis=1),
        tile,
        tokens,
        tensor_size - 1,
    )
    slots = float(windows_here * lax.axis_size("dp"))

    windows = range(windows_here)
    weights = [weighted[w].reshape(1, 1) for w in windows]

    token_blocks = [tokens] + [arrived_tokens[other] for other in range(tensor_size - 1)]
    normed_rows, queries, own_kv = project(token_blocks, norms, w_att, cosine, sine)
    last_ffn = gather_ffn(last_ffn, hold(last_across, w_att))
    (
        attended,
        wide_attended,
        logs,
        kept_all,
        sent_all,
        slots_all,
        cots,
        first_middle,
        first_normed,
        first_others,
    ) = attend(queries, own_kv, w_att, cotangent, tokens, norms, tensor_size - 1)
    others = range(tensor_size - 1)
    cot_blocks = [
        [(cotangent, (w,))] + [(cots, (other, w)) for other in others] for w in windows
    ]
    middles = [first_middle]

    def reduce_ffn(partial):
        partial = partial.reshape(-1, partial.shape[-1])
        mine = lax.psum_scatter(partial, ("dp", "core"), scatter_dimension=0, tiled=True)
        count = mine.shape[0] // 2
        kept = jnp.where(upper, mine[count:], mine[:count])
        return kept, mine

    blocks = [first_normed] + [first_others[other] for other in others]
    begun, fed, lows, arrived_lows = [], [], [], []
    grad_middles, second_sums = [], []
    masks = [other + 1 for other in others]

    def through_second_norm(w, kept, arrived):
        grad_middle, low, sums = second_norm_back(
            weights[w], slots, kept, arrived, middles[w], (cotangent, (w,)), norms
        )
        grad_middles.append(grad_middle)
        second_sums.append(sums)
        return low

    for w in windows:
        begun.append(
            feed_first(blocks, cot_blocks[w], weights[w], norms, slots, first_ffn)
        )
        if w + 1 < windows_here:
            kept, arrived = scatter_pair(kept_all[w], sent_all[w], "tensor")
            middle, normed_mid = second_norm(
                (tokens, (w + 1,)), hold(kept, begun[-1]), arrived, norms
            )
            middles.append(middle)
            blocks = hold(spread(normed_mid, "tensor"), fed)
            after = normed_mid
        else:
            g_first_part, *arrived = feed_weights(
                [one[0] for one in begun],
                [one[0] for one in fed] + [one[1] for one in begun[len(fed) :]],
                0,
                [(one[4], [tensor_size // 2]) for one in fed],
            )
            first_kept, first_sent = reduce_ffn(g_first_part)
            after = g_first_part
        swaps = ()
        if w > 0:
            kept, arrived = later_pair(fed[-1][3], arrived[-1][0], "tensor")
            low = through_second_norm(w - 1, hold(kept, g_first_part), arrived)
            lows.append(low)
            swaps = [(low, masks)]
            after = low
        both, wide, *totals = hold(begun[w], after)
        ended = feed_last(both, wide, totals, last_ffn, tensor_size, swaps)
        fed.append(ended[:5])
        arrived_lows += ended[5:]
        if w + 1 < windows_here:
            blocks = hold(blocks, ended[3])
    g_ffn_part, arrived = feed_weights(
        [one[0] for one in begun],
        [one[0] for one in fed],
        1,
        [(fed[-1][4], [tensor_size // 2])],
    )
    last_kept, last_sent = reduce_ffn(g_ffn_part)
    kept, arrived = later_pair(fed[-1][3], arrived[0], "tensor")
    last_low = through_second_norm(windows[-1], hold(kept, g_ffn_part), arrived)
    grad_mid_blocks = [
        [low] + [arrived[other] for other in others] for low, arrived in zip(lows, arrived_lows)
    ] + [[last_low]]

    grad_q, grad_k, grad_v, grad_mid_rows, *arrived_results = attend_back(
        hold(queries, g_ffn_part),
        wide_attended,
        logs,
        slots_all,
        grad_mid_blocks,
        w_att,
        (cosine, sine),
        [fed[w][2] for w in windows],
    )
    parts = [
        (middles[w], *later_pair(fed[w][1], arrived_results[w], "tensor")) for w in windows
    ]

    g_att, vectors, input_grad, first_arrived = finish(
        (grad_q, grad_k, grad_v),
        normed_rows,
        grad_mid_rows,
        attended,
        w_att,
        tokens,
        first_sent,
        norms,
        second_sums,
        grad_middles,
        tensor_size - 1,
    )
    output = results(hold(parts, input_grad))
    g_first = first_kept.astype(F32) + first_arrived.astype(F32)
    last_sent = hold(last_sent, input_grad)
    count = last_sent.shape[0] // 2
    last_sent = jnp.where(upper, last_sent[:count], last_sent[count:])
    last_arrived = swap(last_sent, "x", 1)
    g_last = last_kept.astype(F32) + last_arrived.astype(F32)
    norm_sums = vectors[:4, : norm1_gain.shape[0]]
    ffn_grads = [
        jnp.concatenate(
            [g_first[:, at * part : (at + 1) * part], g_last[:, at * part : (at + 1) * part]],
            axis=1,
        )
        for at in range(3)
    ]

    return (
        output,
        input_grad,
        norm_sums[0],
        norm_sums[1],
        g_att[:, :head_cols],
        g_att[:, head_cols : 2 * head_cols],
        g_att[:, 2 * head_cols : 3 * head_cols],
        g_att[:, 3 * head_cols :].T,
        norm_sums[2],
        norm_sums[3],
        ffn_grads[0],
        ffn_grads[1],
        ffn_grads[2].T,
    )


def solution(mesh):
    depth, seq, tensor = mesh.devices.shape
    finer = jax.sharding.Mesh(
        mesh.devices.reshape(depth, seq // 2, 2, tensor), ("dp", "x", "core", "tensor")
    )
    rows = P("dp", ("x", "core", "tensor"), None)
    vector = P(("dp", "x", "core", "tensor"))
    tall = P(("dp", "x", "core"), "tensor")
    flat = P("tensor", ("dp", "x", "core"))
    return jax.shard_map(
        local,
        mesh=finer,
        in_specs=(
            rows, rows, P("dp"), P("dp"), P(), vector, vector,
            tall, tall, tall, flat, vector, vector, tall, tall, flat,
        ),
        out_specs=(
            rows, rows, vector, vector, tall, tall, tall, flat,
            vector, vector, tall, tall, flat,
        ),
        check_vma=False,
    )
```

```python
import functools
import math

import jax
import jax.numpy as jnp
from jax import lax
from jax.experimental import pallas as pl
from jax.experimental.pallas import tpu as pltpu
from jax.sharding import PartitionSpec as P

HEAD_DIM = 64
EPSILON = 1e-05
ROPE_BASE = 10000.0
PAIR = 2 * HEAD_DIM
LOG2E = math.log2(math.e)
BF16 = jnp.bfloat16
F32 = jnp.float32
VMEM_BYTES = 56 * 1024 * 1024
MESH = pl.DeviceIdType.MESH


def dot_nn(left, right):
    return lax.dot_general(left, right, (((1,), (0,)), ((), ())), preferred_element_type=F32)


def dot_nt(left, right):
    return lax.dot_general(left, right, (((1,), (1,)), ((), ())), preferred_element_type=F32)


def dot_tn(left, right):
    return lax.dot_general(left, right, (((0,), (0,)), ((), ())), preferred_element_type=F32)


def swap(array, axis, bit):
    size = lax.axis_size(axis)
    return lax.ppermute(array, axis, [(i, i ^ bit) for i in range(size)])


def spread(array, axis):
    blocks = [array]
    bit = 1
    while bit < lax.axis_size(axis):
        blocks = blocks + [swap(block, axis, bit) for block in blocks]
        bit *= 2
    return blocks


def scatter_pair(kept, sent, axis):
    return later_pair(kept, swap(sent, axis, lax.axis_size(axis) // 2), axis)


def later_pair(kept, arrived, axis):
    bit = lax.axis_size(axis) // 2
    while bit > 1:
        partial = kept + arrived.astype(F32)
        bit //= 2
        rows = partial.shape[0] // 2
        kept, arrived = partial[:rows], swap(partial[rows:].astype(BF16), axis, bit)
    return kept, arrived


def seq_size():
    return lax.axis_size("x") * lax.axis_size("core")


def seq_index():
    return lax.axis_index("x") * lax.axis_size("core") + lax.axis_index("core")


def hold(values, *others):
    return lax.optimization_barrier((values, others))[0]


def run(kernel, name, out_shape, flops, args, collective_id=None, **options):
    trading = {} if collective_id is None else dict(collective_id=collective_id, has_side_effects=True)
    moved = sum(math.prod(array.shape) * array.dtype.itemsize for array in args)
    outs = out_shape if isinstance(out_shape, list) else [out_shape]
    moved += sum(math.prod(array.shape) * array.dtype.itemsize for array in outs)
    return pl.pallas_call(
        kernel,
        out_shape=out_shape,
        compiler_params=pltpu.CompilerParams(vmem_limit_bytes=VMEM_BYTES, **trading),
        cost_estimate=pl.CostEstimate(
            flops=int(flops), bytes_accessed=int(moved), transcendentals=0
        ),
        name=name,
        **options,
    )(*args)


def shaped(shape, dtype):
    return jax.ShapeDtypeStruct(shape, dtype)


SCALAR = pl.BlockSpec(memory_space=pltpu.SMEM)


def plane(operand, block=None, index=None):
    array, at = operand if isinstance(operand, tuple) else (operand, ())
    shape = array.shape[len(at) :] if block is None else block
    place = (lambda *i: (0,) * len(shape)) if index is None else index
    return array, pl.BlockSpec((None,) * len(at) + tuple(shape), lambda *i: at + place(*i))


def normalise(stream):
    row_mean = jnp.mean(stream, axis=-1, keepdims=True)
    centred = stream - row_mean
    variance = jnp.mean(centred * centred, axis=-1, keepdims=True)
    inv_std = lax.rsqrt(variance + EPSILON)
    return centred * inv_std, inv_std


def norm_back(grad_normed, normed, inv_std, norm_gain):
    scaled_grad = grad_normed * norm_gain
    return inv_std * (
        scaled_grad
        - jnp.mean(scaled_grad, axis=-1, keepdims=True)
        - normed * jnp.mean(scaled_grad * normed, axis=-1, keepdims=True)
    )


def factor_of(weight_ref, norms_ref, slots):
    return weight_ref[0, 0] * slots / norms_ref[4:5, 0:1]


def first_head(shape):
    return lax.broadcasted_iota(jnp.int32, shape, 1) % PAIR < HEAD_DIM


def swap_halves(values):
    half = HEAD_DIM // 2
    lane = lax.broadcasted_iota(jnp.int32, values.shape, 1)
    ahead = pltpu.roll(values, PAIR - half, 1)
    behind = pltpu.roll(values, half, 1)
    return jnp.where(lane % HEAD_DIM < half, ahead, behind)


def project_kernel(blocks, norms_ref, w_ref, cos_ref, sin_ref, *refs):
    x_refs = refs[:blocks]
    normed_ref, q_ref, kv_ref = refs[blocks:]
    cols = q_ref.shape[2]
    gain, bias = norms_ref[0:1, :], norms_ref[1:2, :]
    at_row = 0
    for x_ref in x_refs:
        rows = slice(at_row, at_row + x_ref.shape[1])
        at_row += x_ref.shape[1]
        normed = (normalise(x_ref[0].astype(F32))[0] * gain + bias).astype(BF16)
        normed_ref[0, rows, :] = normed
        cosine, sine = cos_ref[rows, :], sin_ref[rows, :]
        query = dot_nn(normed, w_ref[:, :cols])
        key = dot_nn(normed, w_ref[:, cols : 2 * cols])
        value = dot_nn(normed, w_ref[:, 2 * cols : 3 * cols]).astype(BF16)
        for at in range(0, cols, PAIR):
            part, pair = slice(at, at + PAIR), at // PAIR
            one = query[:, part]
            q_ref[0, rows, part] = (one * cosine + swap_halves(one) * sine).astype(BF16)
            one = key[:, part]
            kv_ref[0, pair, 0, rows, :] = (one * cosine + swap_halves(one) * sine).astype(BF16)
            kv_ref[0, pair, 1, rows, :] = value[:, part]


def project(x_blocks, norms, w_att, cosine, sine):
    windows = x_blocks[0].shape[0]
    width, cols = w_att.shape[0], w_att.shape[1] // 4
    rows = sum(block.shape[1] for block in x_blocks)
    pieces = (cols // PAIR, 2, rows, PAIR)
    args = [norms, w_att, cosine, sine, *x_blocks]
    return run(
        functools.partial(project_kernel, len(x_blocks)),
        "project",
        [
            shaped((windows, rows, width), BF16),
            shaped((windows, rows, cols), BF16),
            shaped((windows,) + pieces, BF16),
        ],
        6 * windows * rows * width * cols,
        args,
        grid=(windows,),
        in_specs=[pl.BlockSpec(array.shape, lambda i: (0, 0)) for array in args[:4]]
        + [pl.BlockSpec((1,) + block.shape[1:], lambda i: (i, 0, 0)) for block in x_blocks],
        out_specs=[
            pl.BlockSpec((1, rows, width), lambda i: (i, 0, 0)),
            pl.BlockSpec((1, rows, cols), lambda i: (i, 0, 0)),
            pl.BlockSpec((1,) + pieces, lambda i: (i, 0, 0, 0, 0)),
        ],
    )


def flipped(index, mask):
    bit = 1
    while bit <= mask:
        if mask & bit:
            index = index + bit - 2 * bit * ((index // bit) % 2)
        bit *= 2
    return index


def greet(peers):
    barrier = pltpu.get_barrier_semaphore()
    for peer in peers:
        pl.semaphore_signal(barrier, inc=1, device_id=peer, device_id_type=MESH)
    pl.semaphore_wait(barrier, len(peers))


def send(source, target, send_sem, recv_sem, peer):
    return pltpu.make_async_remote_copy(
        src_ref=source,
        dst_ref=target,
        send_sem=send_sem,
        recv_sem=recv_sem,
        device_id=peer,
        device_id_type=MESH,
    )


def half_chip_peers():
    depth = lax.axis_index("dp")
    size = lax.axis_size("dp")
    return {
        "far": {"x": 1 - lax.axis_index("x")},
        "up": {"dp": (depth + 1) % size},
        "down": {"dp": (depth + size - 1) % size},
        "core": {"core": 1 - lax.axis_index("core")},
    }


class Route:
    PARTS = ((0, 0), (3, 0), (1, 0), (2, 0), (0, 1), (3, 1), (1, 1), (2, 1))

    def __init__(self, whole, rows, send_sem, recv_sem, own):
        self.whole, self.rows, self.own = whole, rows, own
        self.send_sem, self.recv_sem = send_sem, recv_sem
        self.seq, self.depth = seq_index(), lax.axis_index("dp")
        self.peers = half_chip_peers()

    def part(self, place):
        turn, other = place
        seq = flipped(self.seq, 2) if other else self.seq
        at = (((self.depth + turn) % lax.axis_size("dp")) * seq_size() + seq) * self.rows
        return self.whole.at[pl.ds(pl.multiple_of(at, self.rows), self.rows), :]

    def message(self, number):
        if number >= 7:
            place, peer = self.PARTS[number - 7], "core"
        else:
            place, peer = (
                ((0, 0), "up"),
                ((0, 0), "down"),
                ((3, 0), "up"),
                ((0, 0), "far"),
                ((3, 0), "far"),
                ((1, 0), "far"),
                ((2, 0), "far"),
            )[number]
        target = self.part(place)
        return send(
            self.own if place == (0, 0) else target,
            target,
            self.send_sem.at[number],
            self.recv_sem.at[number],
            self.peers[peer],
        )

    def start(self, *numbers):
        for number in numbers:
            self.message(number).start()

    def arrived(self, *numbers):
        for number in numbers:
            self.message(number).wait_recv()

    def sent(self, *numbers):
        for number in numbers:
            self.message(number).wait_send()


MESSAGES = 15


def tables(cos_ref, sin_ref, trades):
    own_rows = cos_ref.shape[0] // (trades + 1)
    tensor = lax.axis_index("tensor")
    half = HEAD_DIM // 2
    shape = (own_rows, PAIR)
    lane = lax.broadcasted_iota(jnp.int32, shape, 1)
    exponent = -(math.log(ROPE_BASE) * 2.0 / HEAD_DIM) * (lane % half).astype(F32)
    inverse = jnp.exp(exponent)
    row = lax.broadcasted_iota(jnp.int32, shape, 0)
    for other in range(trades + 1):
        start = (seq_index() * (trades + 1) + flipped(tensor, other)) * own_rows
        phase = (row + start).astype(F32) * inverse
        rows = slice(other * own_rows, (other + 1) * own_rows)
        cos_ref[rows, :] = jnp.cos(phase)
        sine = jnp.sin(phase)
        sin_ref[rows, :] = jnp.where(lane % HEAD_DIM < half, -sine, sine)


def gather_kernel(trades, att_ref, tile_ref, tokens_ref, *refs):
    att_all, norms_ref, tokens_all, cos_ref, sin_ref = refs[:5]
    tiles, pair_of_tiles = refs[5:7]
    att_send, att_recv, tile_send, tile_recv = refs[7:11]
    own_sem, tokens_send, tokens_recv, pair_send, pair_recv = refs[11:]
    tensor = lax.axis_index("tensor")
    others = [{"tensor": flipped(tensor, other + 1)} for other in range(trades)]
    att = Route(att_all, att_ref.shape[0], att_send, att_recv, att_ref)
    tile_rows = tile_ref.shape[0]
    small = Route(tiles, pair_of_tiles.shape[0], tile_send, tile_recv, pair_of_tiles)

    def tokens_trade(other):
        return send(
            tokens_ref,
            tokens_all.at[other],
            tokens_send.at[other],
            tokens_recv.at[other],
            others[other],
        )

    own_rows = pl.ds(pl.multiple_of(tensor * tile_rows, tile_rows), tile_rows)

    def pair_trade(other):
        return send(
            tile_ref,
            pair_of_tiles.at[own_rows, :],
            pair_send.at[other],
            pair_recv.at[other],
            others[other],
        )

    own_copies = [
        pltpu.make_async_copy(att_ref, att.part((0, 0)), own_sem.at[0]),
        pltpu.make_async_copy(tile_ref, pair_of_tiles.at[own_rows, :], own_sem.at[1]),
        pltpu.make_async_copy(pair_of_tiles, small.part((0, 0)), own_sem.at[2]),
    ]

    greet(list(att.peers.values()) + others)
    for other in range(trades):
        pair_trade(other).start()
    own_copies[1].start()
    att.start(0, 1, 3, 7)
    own_copies[1].wait()
    for other in range(trades):
        pair_trade(other).wait_recv()
    small.start(0, 1, 3, 7)
    own_copies[0].start()
    own_copies[2].start()
    for other in range(trades):
        tokens_trade(other).start()
    tables(cos_ref, sin_ref, trades)
    for route in (small, att):
        route.arrived(0)
        route.start(2, 4, 8)
    for route in (small, att):
        route.arrived(3)
        route.start(11)
    for route in (small, att):
        route.arrived(1)
        route.start(5, 9)
    for route in (small, att):
        route.arrived(2)
        route.start(6, 10)
    for route in (small, att):
        route.arrived(4)
        route.start(12)
        route.arrived(5)
        route.start(13)
        route.arrived(6)
        route.start(14)
    for route in (small, att):
        route.arrived(*range(7, MESSAGES))
    own_copies[2].wait()
    shard = norms_ref.shape[1] // (tiles.shape[0] // tile_rows)
    total = None
    for device in range(tiles.shape[0] // tile_rows):
        tile = tiles[device * tile_rows : (device + 1) * tile_rows, :]
        norms_ref[:, device * shard : (device + 1) * shard] = tile[:, :shard]
    for depth in range(lax.axis_size("dp")):
        at = depth * (tiles.shape[0] // lax.axis_size("dp"))
        one = tiles[at + 4 : at + 5, :]
        total = one if total is None else total + one
    norms_ref[4:5, : total.shape[1]] = total
    for route in (att, small):
        route.sent(*range(MESSAGES))
    own_copies[0].wait()
    for other in range(trades):
        pair_trade(other).wait_send()
        tokens_trade(other).wait_recv()
        tokens_trade(other).wait_send()


def gather(att, tile, tokens, trades):
    count = lax.axis_size("dp") * seq_size()
    rows = att.shape[0]
    group = tile.shape[0] * (trades + 1)
    anywhere = pl.BlockSpec(memory_space=pl.ANY)
    vmem = pl.BlockSpec(memory_space=pltpu.VMEM)
    dma = pltpu.SemaphoreType.DMA
    return run(
        functools.partial(gather_kernel, trades),
        "gather",
        [
            shaped((count * rows, att.shape[1]), BF16),
            shaped((tile.shape[0], count * rows), F32),
            shaped((trades,) + tokens.shape, BF16),
        ]
        + [shaped((tokens.shape[1] * (trades + 1), PAIR), F32)] * 2,
        0,
        [att, tile, tokens],
        collective_id=1,
        in_specs=[vmem, vmem, anywhere],
        out_specs=[anywhere, vmem, anywhere, vmem, vmem],
        scratch_shapes=[pltpu.VMEM((count * group, 128), F32), pltpu.VMEM((group, 128), F32)]
        + [dma((MESSAGES,))] * 4
        + [dma((3,)), dma((trades,)), dma((trades,)), dma((trades,)), dma((trades,))],
    )


def attend_kernel(windows, pairs, trades, exp_scale, *refs):
    stages = (trades + 1).bit_length() - 1
    q_ref, w_ref, kv_ref, cot_ref, x_ref, norms_ref = refs[:6]
    low_ref, wide_ref, log_ref, kept_ref, sent_ref, slots_ref, cots_ref = refs[6:13]
    middle_ref, normed_ref, others_ref = refs[13:16]
    slots, acc_all, top_all, total_all, mixed_rows = refs[16:21]
    own_sem, send_sem, recv_sem, save_sem, cot_send, cot_recv = refs[21:27]
    early_kept, early_normed, early_sem, early_recv, normed_sem, normed_recv = refs[27:33]
    early_sent, early_arrived = refs[33 : 33 + stages], refs[33 + stages :]
    step = pl.program_id(0)
    near_steps = windows * pairs
    steps = 2 * near_steps
    turn = step % (2 * pairs)
    is_far = turn >= pairs
    number = step // (2 * pairs) * pairs + turn % pairs
    tensor = lax.axis_index("tensor")
    core_peer = {"core": 1 - lax.axis_index("core")}
    far_peer = {"x": 1 - lax.axis_index("x")}
    cot_peers = [{"tensor": flipped(tensor, other + 1)} for other in range(trades)]

    def piece(number):
        return kv_ref.at[number // pairs, number % pairs]

    def own_copy(number):
        return pltpu.make_async_copy(piece(number), slots.at[number, 0], own_sem.at[number])

    def trade(number, slot):
        peer = far_peer if slot == 2 else core_peer
        source = slots.at[number, 2] if slot == 3 else piece(number)
        return send(
            source,
            slots.at[number, slot],
            send_sem.at[number, slot - 1],
            recv_sem.at[number, slot - 1],
            peer,
        )

    def cot_trade(other):
        return send(
            cot_ref, cots_ref.at[other], cot_send.at[other], cot_recv.at[other], cot_peers[other]
        )

    def early_trade(stage):
        return send(
            early_sent[stage],
            early_arrived[stage],
            early_sem.at[stage],
            early_recv.at[stage],
            {"tensor": flipped(tensor, (trades + 1) >> (stage + 1))},
        )

    def normed_trade(other):
        return send(
            early_normed,
            others_ref.at[other],
            normed_sem.at[other],
            normed_recv.at[other],
            cot_peers[other],
        )

    def save(number, slot):
        return pltpu.make_async_copy(
            slots.at[number, slot], slots_ref.at[number, slot], save_sem.at[number, slot]
        )

    @pl.when(step == 0)
    def _():
        greet([core_peer, far_peer] + cot_peers)

        @pl.loop(0, near_steps)
        def _(number):
            own_copy(number).start()
            trade(number, 1).start()
            trade(number, 2).start()

        for other in range(trades):
            cot_trade(other).start()

    @pl.when(step == 2 * pairs)
    def _():
        early_trade(0).start()

    @pl.when(step == 3 * pairs)
    def _():
        kept = early_kept[...]
        for stage in range(stages):
            early_trade(stage).wait_recv()
            kept = kept + early_arrived[stage][...].astype(F32)
            if stage + 1 < stages:
                half = kept.shape[0] // 2
                early_sent[stage + 1][...] = kept[half:].astype(BF16)
                early_trade(stage + 1).start()
                kept = kept[:half]
        middle = x_ref[...].astype(F32) + kept
        middle_ref[...] = middle
        normed = (normalise(middle)[0] * norms_ref[2:3, :] + norms_ref[3:4, :]).astype(BF16)
        normed_ref[...] = normed
        early_normed[...] = normed

    @pl.when(step == 3 * pairs + 1)
    def _():
        for other in range(trades):
            normed_trade(other).start()

    relayed = step // (2 * pairs) * pairs + turn - (pairs - 1)

    @pl.when(jnp.logical_and(turn >= pairs - 1, turn < 2 * pairs - 1))
    def _():
        trade(relayed, 2).wait_recv()
        trade(relayed, 3).start()
        save(relayed, 2).start()

    @pl.when(jnp.logical_not(is_far))
    def _():
        own_copy(number).wait()
        trade(number, 1).wait_recv()
        save(number, 0).start()
        save(number, 1).start()
        acc_all[number] = jnp.zeros(acc_all.shape[1:], F32)
        total_all[number] = jnp.zeros(acc_all.shape[1:], F32)
        top_all[number] = jnp.full(acc_all.shape[1:], -1e30, F32)

    @pl.when(is_far)
    def _():
        trade(number, 3).wait_recv()
        save(number, 3).start()

    query = q_ref[0]
    is_first = first_head(query.shape)
    base = jnp.where(is_far, 2, 0)
    carried_top = top_all[number]
    outs, tops = [], []
    for head in range(2):
        mine = is_first if head == 0 else jnp.logical_not(is_first)
        own_query = jnp.where(mine, query, jnp.zeros_like(query))
        scores = [dot_nt(own_query, slots[number, base + slot, 0]) for slot in range(2)]
        at = head * HEAD_DIM
        top = carried_top[:, at : at + 1]
        for one in scores:
            top = jnp.maximum(top, one.max(axis=1, keepdims=True))
        shift = top * exp_scale
        mixed = None
        for slot, one in enumerate(scores):
            weight = jnp.exp2(one * exp_scale - shift).astype(BF16)
            value = slots[number, base + slot, 1]
            lane_first = first_head(value.shape)
            lane_mine = lane_first if head == 0 else jnp.logical_not(lane_first)
            term = dot_nn(weight, jnp.where(lane_mine, value, jnp.ones_like(value)))
            mixed = term if mixed is None else mixed + term
        outs.append(mixed)
        tops.append(jnp.broadcast_to(top, mixed.shape))
    top = jnp.where(is_first, tops[0], tops[1])
    fade = jnp.exp2((carried_top - top) * exp_scale)
    acc = jnp.where(is_first, outs[0], outs[1]) + acc_all[number] * fade
    total = pltpu.roll(jnp.where(is_first, outs[1], outs[0]), HEAD_DIM, 1) + total_all[number] * fade

    @pl.when(jnp.logical_not(is_far))
    def _():
        acc_all[number] = acc
        top_all[number] = top
        total_all[number] = total

    @pl.when(is_far)
    def _():
        attended = acc / total
        low = attended.astype(BF16)
        low_ref[0] = low
        wide_ref[0] = attended
        log_ref[0] = (top * exp_scale + jnp.log2(total)).T
        term = dot_nt(low, w_ref[...])
        pair = number % pairs

        @pl.when(pair == 0)
        def _():
            mixed_rows[...] = term

        @pl.when(pair > 0)
        def _():
            mixed_rows[...] += term

        @pl.when(jnp.logical_and(pair == pairs - 1, number >= pairs))
        def _():
            half = kept_ref.shape[1]
            kept_ref[0] = mixed_rows[:half]
            sent_ref[0] = mixed_rows[half:].astype(BF16)

        @pl.when(number == pairs - 1)
        def _():
            half = kept_ref.shape[1]
            early_kept[...] = mixed_rows[:half]
            early_sent[0][...] = mixed_rows[half:].astype(BF16)

    @pl.when(step == steps - 1)
    def _():
        @pl.loop(0, near_steps)
        def _(number):
            for slot in range(1, 4):
                trade(number, slot).wait_send()
            for slot in range(4):
                save(number, slot).wait()

        for stage in range(stages):
            early_trade(stage).wait_send()
        for other in range(trades):
            cot_trade(other).wait_send()
            cot_trade(other).wait_recv()
            normed_trade(other).wait_send()
            normed_trade(other).wait_recv()


def attend(queries, own_kv, w_att, cotangent, tokens, norms, trades):
    windows, rows, cols = queries.shape
    width = w_att.shape[0]
    pairs = cols // PAIR
    near = windows * pairs
    out_at = 3 * pairs

    def far(i):
        turn = i % (2 * pairs)
        done = i // (2 * pairs) * pairs
        return jnp.where(turn >= pairs, done + turn - pairs, jnp.maximum(done - 1, 0))

    anywhere = pl.BlockSpec(memory_space=pl.ANY)
    wide = pl.BlockSpec((1, rows, PAIR), lambda i: (far(i) // pairs, 0, far(i) % pairs))
    half = pl.BlockSpec(
        (1, rows // 2, width), lambda i: (jnp.maximum(far(i) // pairs, 1) - 1, 0, 0)
    )
    own_rows = tokens.shape[1]
    own = pl.BlockSpec((own_rows, width), lambda i: (0, 0))
    stages = [rows >> (stage + 1) for stage in range((trades + 1).bit_length() - 1)]
    state = pltpu.VMEM((near, rows, PAIR), F32)
    dma = pltpu.SemaphoreType.DMA
    return run(
        functools.partial(attend_kernel, windows, pairs, trades, LOG2E / math.sqrt(HEAD_DIM)),
        "attend",
        [
            shaped((windows, rows, cols), BF16),
            shaped((windows, rows, cols), F32),
            shaped((windows, cols, rows), F32),
            shaped((windows - 1, rows // 2, width), F32),
            shaped((windows - 1, rows // 2, width), BF16),
            shaped((near, 4, 2, rows, PAIR), BF16),
            shaped((trades,) + cotangent.shape, BF16),
            shaped((own_rows, width), F32),
            shaped((own_rows, width), BF16),
            shaped((trades, own_rows, width), BF16),
        ],
        64 * windows * rows * rows * cols,
        [queries, w_att, own_kv, cotangent, tokens, norms],
        collective_id=0,
        grid=(2 * near,),
        in_specs=[
            pl.BlockSpec((1, rows, PAIR), lambda i: (i // (2 * pairs), 0, i % pairs)),
            pl.BlockSpec((width, PAIR), lambda i: (0, out_at + far(i) % pairs)),
            anywhere,
            anywhere,
            pl.BlockSpec((None, own_rows, width), lambda i: (0, 0, 0)),
            pl.BlockSpec(norms.shape, lambda i: (0, 0)),
        ],
        out_specs=[
            wide,
            wide,
            pl.BlockSpec((1, PAIR, rows), lambda i: (far(i) // pairs, far(i) % pairs, 0)),
            half,
            half,
            anywhere,
            anywhere,
            own,
            own,
            anywhere,
        ],
        scratch_shapes=[
            pltpu.VMEM((near, 4, 2, rows, PAIR), BF16),
            state,
            state,
            state,
            pltpu.VMEM((rows, width), F32),
            dma((near,)),
            dma((near, 3)),
            dma((near, 3)),
            dma((near, 4)),
            dma((trades,)),
            dma((trades,)),
            pltpu.VMEM((rows // 2, width), F32),
            pltpu.VMEM((own_rows, width), BF16),
            dma((len(stages),)),
            dma((len(stages),)),
            dma((trades,)),
            dma((trades,)),
        ]
        + [pltpu.VMEM((count, width), BF16) for count in stages] * 2,
    )


def attend_back_kernel(windows, pairs, blocks, exp_scale, score_scale, *refs):
    q_ref, wide_ref, log_ref, slots_ref, w_ref, cos_ref, sin_ref, last_ref = refs[:8]
    trades = blocks - 1
    known = (windows - 1) * blocks + 1
    grad_refs = list(refs[8 : 8 + known])
    refs = refs[8 + known :]
    sent_refs, refs = refs[:windows], refs[windows:]
    gq_ref, gk_ref, gv_ref, rows_ref = refs[:4]
    arrived_refs, refs = refs[4 : 4 + windows], refs[4 + windows :]
    dq_all, do_all, far_kept, far_sent, far_core, far_x, near_kept, near_sent, near_core = refs[:9]
    send_sem, recv_sem, result_send, result_recv, last_send, last_recv, last_others = refs[9:]
    grad_refs += [last_others.at[other] for other in range(trades)]
    step = pl.program_id(0)
    count = windows * pairs
    tensor = lax.axis_index("tensor")
    core_peer = {"core": 1 - lax.axis_index("core")}
    far_peer = {"x": 1 - lax.axis_index("x")}
    result_peer = {"tensor": flipped(tensor, lax.axis_size("tensor") // 2)}

    def trade(kind, number):
        source, target, peer = (
            (far_sent, far_core, core_peer),
            (far_kept, far_x, far_peer),
            (near_sent, near_core, core_peer),
        )[kind]
        return send(
            source.at[number],
            target.at[number],
            send_sem.at[kind, number],
            recv_sem.at[kind, number],
            peer,
        )

    def result_trade(w):
        return send(
            sent_refs[w], arrived_refs[w], result_send.at[w], result_recv.at[w], result_peer
        )

    others = [{"tensor": flipped(tensor, other + 1)} for other in range(trades)]

    def last_trade(other):
        return send(
            last_ref, last_others.at[other], last_send.at[other], last_recv.at[other], others[other]
        )

    @pl.when(step == 0)
    def _():
        greet([core_peer, far_peer] + others)
        for other in range(trades):
            last_trade(other).start()
        for w in range(windows):
            result_trade(w).start()

    def at_step(first, body):
        number = step - first

        @pl.when(jnp.logical_and(number >= 0, number < count))
        def _():
            body(number)

    def send_far(number):
        trade(0, number).start()

    def add_far(number):
        trade(0, number).wait_recv()
        far_kept[number] = (
            far_kept[number].astype(F32) + far_core[number].astype(F32)
        ).astype(BF16)

    def send_x(number):
        trade(1, number).start()

    def send_near(number):
        trade(2, number).start()

    def finish(number):
        trade(2, number).wait_recv()
        trade(1, number).wait_recv()
        total = (
            near_kept[number].astype(F32)
            + near_core[number].astype(F32)
            + far_x[number].astype(F32)
        )
        key = total[0]
        gk_ref[0] = (key * cos_ref[...] - swap_halves(key) * sin_ref[...]).astype(BF16)
        gv_ref[0] = total[1].astype(BF16)

    at_step(1, send_far)
    at_step(3, send_x)
    at_step(count + 1, send_near)
    at_step(2, add_far)
    at_step(count + 2, finish)

    for w in range(windows):

        @pl.when(step == w * pairs)
        def _(w=w):
            if w == windows - 1:
                for other in range(trades):
                    last_trade(other).wait_recv()
            at_row = 0
            for grad_ref in grad_refs[w * blocks : (w + 1) * blocks]:
                rows_ref[0, at_row : at_row + grad_ref.shape[0], :] = grad_ref[...]
                at_row += grad_ref.shape[0]

    def gradients(number, grad_out, kept, sent):
        query = q_ref[0]
        is_first = first_head(query.shape)
        overlap = (grad_out.astype(F32) * wide_ref[0]).T
        logs = log_ref[0]
        zero = jnp.zeros_like(query)
        own_q, own_do, row_log, row_sum = [], [], [], []
        for head in range(2):
            mine = is_first if head == 0 else jnp.logical_not(is_first)
            own_q.append(jnp.where(mine, query, zero))
            own_do.append(jnp.where(mine, grad_out, zero))
            at = head * HEAD_DIM
            row_log.append(logs[at : at + 1, :])
            row_sum.append(jnp.sum(overlap[at : at + HEAD_DIM, :], axis=0, keepdims=True))
        dq_parts = [None, None]
        for slot, target in enumerate((kept, sent)):
            key, value = slots_ref[0, slot, 0], slots_ref[0, slot, 1]
            key_turned = key.T
            grad_key, grad_value = None, None
            for head in range(2):
                scores = dot_nt(key, own_q[head])
                probs = jnp.exp2(scores * exp_scale - row_log[head])
                grad_probs = dot_nt(value, own_do[head])
                grad_scores = (probs * (grad_probs - row_sum[head])).astype(BF16)
                term_v = dot_nn(probs.astype(BF16), own_do[head])
                term_k = dot_nn(grad_scores, own_q[head])
                at = head * HEAD_DIM
                term_q = dot_nn(key_turned[at : at + HEAD_DIM, :], grad_scores)
                grad_value = term_v if grad_value is None else grad_value + term_v
                grad_key = term_k if grad_key is None else grad_key + term_k
                dq_parts[head] = term_q if dq_parts[head] is None else dq_parts[head] + term_q
            target[number, 0] = (grad_key * score_scale).astype(BF16)
            target[number, 1] = grad_value.astype(BF16)
        return jnp.concatenate(dq_parts, axis=0).T * score_scale

    @pl.when(step < count)
    def _():
        grad_out = dot_nn(rows_ref[0], w_ref[...]).astype(BF16)
        do_all[step] = grad_out
        dq_all[step] = gradients(step, grad_out, far_kept, far_sent)

    @pl.when(jnp.logical_and(step >= count, step < 2 * count))
    def _():
        number = step - count
        grad_query = dq_all[number] + gradients(number, do_all[number], near_kept, near_sent)
        gq_ref[0] = (grad_query * cos_ref[...] - swap_halves(grad_query) * sin_ref[...]).astype(
            BF16
        )

    @pl.when(step == pl.num_programs(0) - 1)
    def _():
        @pl.loop(0, count)
        def _(number):
            for kind in range(3):
                trade(kind, number).wait_send()

        for other in range(trades):
            last_trade(other).wait_send()
        for w in range(windows):
            result_trade(w).wait_send()
            result_trade(w).wait_recv()


def attend_back(queries, wide, logs, slots_all, grad_blocks, w_att, tables, sent):
    windows, rows, cols = queries.shape
    width = w_att.shape[0]
    pairs = cols // PAIR
    count = windows * pairs
    out_at = 3 * pairs
    score_scale = 1.0 / math.sqrt(HEAD_DIM)
    blocks = lax.axis_size("tensor")
    grads = [block for one in grad_blocks for block in one]
    last = grads[-1]

    def spot(lag, last=None):
        def index(i):
            number = jnp.clip(i - lag, 0, count - 1)
            return (number // pairs, 0, number % pairs)

        return pl.BlockSpec((1, rows, PAIR), index)

    def both(i):
        return jnp.minimum(i, 2 * count - 1) % count

    dma = pltpu.SemaphoreType.DMA
    piece = pltpu.VMEM((count, 2, rows, PAIR), BF16)
    anywhere = pl.BlockSpec(memory_space=pl.ANY)
    return run(
        functools.partial(
            attend_back_kernel, windows, pairs, blocks, score_scale * LOG2E, score_scale
        ),
        "attend_back",
        [shaped((windows, rows, cols), BF16)] * 3
        + [shaped((windows, rows, width), BF16)]
        + [shaped(one.shape, BF16) for one in sent],
        160 * windows * rows * rows * cols,
        [queries, wide, logs, slots_all, w_att, *tables, last, *grads, *sent],
        collective_id=2,
        grid=(2 * count + 2,),
        in_specs=[
            pl.BlockSpec((1, rows, PAIR), lambda i: (both(i) // pairs, 0, both(i) % pairs)),
            pl.BlockSpec((1, rows, PAIR), lambda i: (both(i) // pairs, 0, both(i) % pairs)),
            pl.BlockSpec((1, PAIR, rows), lambda i: (both(i) // pairs, both(i) % pairs, 0)),
            pl.BlockSpec(
                (1, 2, 2, rows, PAIR),
                lambda i: (both(i), jnp.where(i < count, 1, 0), 0, 0, 0),
            ),
            pl.BlockSpec((width, PAIR), lambda i: (0, out_at + jnp.minimum(i, count - 1) % pairs)),
            pl.BlockSpec((rows, PAIR), lambda i: (0, 0)),
            pl.BlockSpec((rows, PAIR), lambda i: (0, 0)),
            anywhere,
        ]
        + [pl.BlockSpec(block.shape, lambda i: (0, 0)) for block in grads]
        + [anywhere] * windows,
        out_specs=[
            spot(count),
            spot(count + 2),
            spot(count + 2),
            pl.BlockSpec((1, rows, width), lambda i: (jnp.minimum(i // pairs, windows - 1), 0, 0)),
        ]
        + [anywhere] * windows,
        scratch_shapes=[pltpu.VMEM((count, rows, PAIR), F32), pltpu.VMEM((count, rows, PAIR), BF16)]
        + [piece] * 7
        + [dma((3, count)), dma((3, count)), dma((windows,)), dma((windows,))]
        + [dma((blocks - 1,)), dma((blocks - 1,)), pltpu.VMEM((blocks - 1,) + last.shape, BF16)],
    )


def middle_kernel(x_ref, kept_ref, arrived_ref, norms_ref, middle_ref, normed_ref):
    middle = x_ref[...].astype(F32) + (kept_ref[...] + arrived_ref[...].astype(F32))
    middle_ref[...] = middle
    normed_ref[...] = (
        normalise(middle)[0] * norms_ref[2:3, :] + norms_ref[3:4, :]
    ).astype(BF16)


def second_norm(x_rows, kept, arrived, norms):
    args, in_specs = row_planes((x_rows, kept, arrived))
    rows, width = arrived.shape
    block = pl.BlockSpec((rows // NORM_BLOCKS, width), lambda i: (i, 0))
    return run(
        middle_kernel,
        "second_norm",
        [shaped((rows, width), F32), shaped((rows, width), BF16)],
        20 * rows * width,
        [*args, norms],
        grid=(NORM_BLOCKS,),
        in_specs=[*in_specs, full(*norms.shape)],
        out_specs=[block, block],
    )


def feed_kernel(blocks, swaps, first, slots, *refs):
    refs = list(refs)

    def take(count):
        taken = refs[:count]
        del refs[:count]
        return taken

    w_refs = take(3)
    if first:
        weight_ref, norms_ref = take(2)
        x_refs, cot_refs = take(blocks), take(blocks)
        sources = take(len(swaps))
        both_ref, wide_ref, total_ref, grad_ref = take(4)
    else:
        both_ref, total_in, grad_in, _ = take(4)
        sources = take(len(swaps))
        wide_ref, kept_ref, sent_ref, grad_kept_ref, grad_sent_ref = take(5)
    trades = tensor_trades(sources, take(len(swaps)), swaps, *take(2 if swaps else 0))
    block = pl.program_id(0)

    def weights_of(ref):
        if len(ref.shape) == 2:
            return ref[...]
        depths, cores, halves = ref.shape[:3]
        return jnp.concatenate(
            [
                ref[depth, core, half]
                for depth in range(depths)
                for half in range(halves)
                for core in range(cores)
            ],
            axis=0,
        )

    gate_w, up_w, down_w = [weights_of(ref) for ref in w_refs]

    @pl.when(block == 0)
    def _():
        start_trades(trades, swaps)

    if first:
        factor = factor_of(weight_ref, norms_ref, slots)
        for at in range(blocks):

            @pl.when(block == at)
            def _(at=at):
                both_ref[0] = x_refs[at][...]
                both_ref[1] = (cot_refs[at][...].astype(F32) * factor).astype(BF16)

    x_rows = both_ref[0]
    gate = dot_nn(x_rows, gate_w)
    up = dot_nn(x_rows, up_w)
    grad_hidden = dot_nn(both_ref[1], down_w)
    sig = jax.nn.sigmoid(gate)
    swish = gate * sig
    hidden = (swish * up).astype(BF16)
    grad_gate = (grad_hidden * up * sig * (1.0 + gate * (1.0 - sig))).astype(BF16)
    grad_up = (grad_hidden * swish).astype(BF16)
    wide_ref[0] = grad_gate
    wide_ref[1] = grad_up
    wide_ref[2] = hidden
    grad_total = dot_nt(grad_gate, gate_w) + dot_nt(grad_up, up_w)
    total = dot_nt(hidden, down_w)
    if first:
        total_ref[...] = total
        grad_ref[...] = grad_total
    else:
        total = total + total_in[...]
        grad_total = grad_total + grad_in[...]
        rows = total.shape[0]
        for at in range(blocks):

            @pl.when(block == at)
            def _(at=at):
                start = (at % (blocks // 2)) * rows
                if at < blocks // 2:
                    kept_ref[start : start + rows] = total
                    grad_kept_ref[start : start + rows] = grad_total
                else:
                    sent_ref[start : start + rows] = total.astype(BF16)
                    grad_sent_ref[start : start + rows] = grad_total.astype(BF16)

    @pl.when(block == blocks - 1)
    def _():
        for trade in trades:
            trade.wait()


def tensor_trades(sources, targets, masks, send_sem=None, recv_sem=None):
    tensor = lax.axis_index("tensor")
    trades = []
    for source, target, kinds in zip(sources, targets, masks):
        for number, mask in enumerate(kinds):
            sems = (send_sem.at[len(trades)], recv_sem.at[len(trades)])
            peer = {"tensor": flipped(tensor, mask)}
            trades.append(send(source, target.at[number], *sems, peer))
    return trades


def start_trades(trades, masks):
    if trades:
        tensor = lax.axis_index("tensor")
        peers = sorted({mask for kinds in masks for mask in kinds})
        greet([{"tensor": flipped(tensor, mask)} for mask in peers])
        for trade in trades:
            trade.start()


def feed_specs(weights):
    lead = weights.shape[:-1]
    part_cols = weights.shape[-1] // 3
    zeros = (0,) * len(lead)
    return part_cols, [
        pl.BlockSpec(lead + (part_cols,), functools.partial(lambda at, i: zeros + (at,), k))
        for k in range(3)
    ]


def full(*shape):
    return pl.BlockSpec(shape, lambda i: (0,) * len(shape))


def feed_call(name, collective_id, blocks, rows, width, part_cols, out, args, swaps, **options):
    masks = [kinds for _, kinds in swaps]
    anywhere = pl.BlockSpec(memory_space=pl.ANY)
    total = sum(len(kinds) for kinds in masks)
    out_shape, out_specs = out
    return run(
        functools.partial(
            feed_kernel, blocks, masks, name == "feed_first", options.pop("slots", None)
        ),
        name,
        out_shape + [shaped((len(kinds),) + array.shape, BF16) for array, kinds in swaps],
        12 * rows * width * part_cols,
        args + [array for array, _ in swaps],
        collective_id=collective_id if swaps else None,
        grid=(blocks,),
        in_specs=options.pop("in_specs") + [anywhere] * len(swaps),
        out_specs=out_specs + [anywhere] * len(swaps),
        scratch_shapes=[pltpu.SemaphoreType.DMA((total,))] * 2 if swaps else [],
        **options,
    )


def feed_first(x_blocks, cot_blocks, weight, norms, slots, weights, swaps=()):
    operands, specs = zip(*[plane(block) for block in (*x_blocks, *cot_blocks)])
    width = math.prod(weights.shape[:-1])
    blocks, own = len(x_blocks), specs[0].block_shape[-2]
    rows = blocks * own
    part_cols, w_specs = feed_specs(weights)
    row_block = pl.BlockSpec((own, width), lambda i: (i, 0))
    out_shape = [shaped((2, rows, width), BF16), shaped((3, rows, 2 * part_cols), BF16)]
    out_shape += [shaped((rows, width), F32)] * 2
    out_specs = [
        pl.BlockSpec((2, own, width), lambda i: (0, i, 0)),
        pl.BlockSpec((3, own, part_cols), lambda i: (0, i, 0)),
        row_block,
        row_block,
    ]
    return feed_call(
        "feed_first",
        6,
        blocks,
        rows,
        width,
        part_cols,
        (out_shape, out_specs),
        [weights, weights, weights, weight, norms, *operands],
        swaps,
        in_specs=w_specs + [SCALAR, full(*norms.shape)] + list(specs),
        slots=slots,
    )


def feed_last(both, wide, totals, weights, blocks, swaps=()):
    rows, width = both.shape[1:]
    own = rows // blocks
    part_cols, w_specs = feed_specs(weights)
    half = full(rows // 2, width)
    row_block = pl.BlockSpec((own, width), lambda i: (i, 0))
    out_shape = [shaped(wide.shape, BF16)]
    out_shape += [shaped((rows // 2, width), F32), shaped((rows // 2, width), BF16)] * 2
    return feed_call(
        "feed_last",
        5,
        blocks,
        rows,
        width,
        part_cols,
        (out_shape, [pl.BlockSpec((3, own, part_cols), lambda i: (0, i, 1))] + [half] * 4),
        [weights, weights, weights, both, *totals, wide],
        swaps,
        in_specs=w_specs
        + [pl.BlockSpec((2, own, width), lambda i: (0, i, 0)), row_block, row_block]
        + [pl.BlockSpec(memory_space=pl.ANY)],
        input_output_aliases={6: 0},
    )


def weights_kernel(windows, masks, *refs):
    lefts, rights = refs[:windows], refs[windows : 2 * windows]
    refs = refs[2 * windows :]
    sources, out_ref, targets = refs[: len(masks)], refs[len(masks)], refs[len(masks) + 1 :]
    at = pl.program_id(0)
    trades = tensor_trades(refs[: len(masks)], targets[: len(masks)], masks, *targets[len(masks) :])

    @pl.when(at == 0)
    def _():
        start_trades(trades, masks)

    total = None
    for left, right in zip(lefts, rights):
        term = dot_tn(left[...], right[...])
        total = term if total is None else total + term
    total = total.astype(BF16)
    depths, cores, halves, shard = out_ref.shape[:4]
    for depth in range(depths):
        for half in range(halves):
            for core in range(cores):
                start = ((depth * halves + half) * cores + core) * shard
                out_ref[depth, core, half] = total[start : start + shard]

    if masks:

        @pl.when(at == pl.num_programs(0) - 1)
        def _():
            for trade in trades:
                trade.wait()


def feed_weights(boths, wides, part, swaps):
    windows = len(boths)
    rows, width = boths[0].shape[1:]
    hidden_cols = wides[0].shape[2] // 2
    step = min(1024, hidden_cols)
    steps = hidden_cols // step
    lead = (lax.axis_size("dp"), lax.axis_size("core"), lax.axis_size("x"))
    lead += (width // math.prod(lead),)
    masks = [kinds for _, kinds in swaps]
    anywhere = pl.BlockSpec(memory_space=pl.ANY)
    left = pl.BlockSpec((None, rows, width), lambda i: (i // (2 * steps), 0, 0))
    right = pl.BlockSpec((None, rows, step), lambda i: (i // steps, 0, part * steps + i % steps))
    total = sum(len(kinds) for kinds in masks)
    return run(
        functools.partial(weights_kernel, windows, masks),
        "feed_weights",
        [shaped(lead + (3 * hidden_cols,), BF16)]
        + [shaped((len(kinds),) + array.shape, BF16) for array, kinds in swaps],
        6 * windows * rows * width * hidden_cols,
        [*boths, *wides] + [array for array, _ in swaps],
        collective_id=(6 if part else 4) if swaps else None,
        grid=(3 * steps,),
        in_specs=[left] * windows + [right] * windows + [anywhere] * len(swaps),
        out_specs=[pl.BlockSpec(lead + (step,), lambda i: (0, 0, 0, 0, i))]
        + [anywhere] * len(swaps),
        scratch_shapes=[pltpu.SemaphoreType.DMA((total,))] * 2 if swaps else [],
    )


def norm_grad(kept_ref, arrived_ref, stream, gain, sums_ref):
    grad_normed = kept_ref[...] + arrived_ref[...].astype(F32)
    normed, inv_std = normalise(stream)
    sums = [
        jnp.sum(one, axis=0, keepdims=True) for one in (grad_normed * normed, grad_normed)
    ]

    @pl.when(pl.program_id(0) == 0)
    def _():
        for at, one in enumerate(sums):
            sums_ref[at : at + 1, :] = one

    @pl.when(pl.program_id(0) > 0)
    def _():
        for at, one in enumerate(sums):
            sums_ref[at : at + 1, :] += one

    return norm_back(grad_normed, normed, inv_std, gain)


def middle_back_kernel(
    slots, weight_ref, kept_ref, arrived_ref, middle_ref, cot_ref, norms_ref, grad_ref, low_ref, sums_ref
):
    grad_y = cot_ref[...].astype(F32) * factor_of(weight_ref, norms_ref, slots)
    grad = grad_y + norm_grad(
        kept_ref, arrived_ref, middle_ref[...], norms_ref[2:3, :], sums_ref
    )
    grad_ref[...] = grad
    low_ref[...] = grad.astype(BF16)


NORM_BLOCKS = 1


def row_planes(operands):
    pairs = []
    for one in operands:
        array, at = one if isinstance(one, tuple) else (one, ())
        rows, width = array.shape[len(at) :]
        pairs.append(plane(one, (rows // NORM_BLOCKS, width), lambda i: (i, 0)))
    return [list(part) for part in zip(*pairs)]


def second_norm_back(weight, slots, kept, arrived, middle, cot_rows, norms):
    args, in_specs = row_planes((kept, arrived, middle, cot_rows))
    rows, width = kept.shape
    block = pl.BlockSpec((rows // NORM_BLOCKS, width), lambda i: (i, 0))
    return run(
        functools.partial(middle_back_kernel, slots),
        "second_norm_back",
        [shaped(kept.shape, F32), shaped(kept.shape, BF16), shaped((2, width), F32)],
        40 * kept.size,
        [weight, *args, norms],
        grid=(NORM_BLOCKS,),
        in_specs=[SCALAR, *in_specs, full(*norms.shape)],
        out_specs=[block, block, full(2, width)],
    )


class SumRoute:
    def __init__(self, part, rows, core_in, mine, x_in, z_in, send_sem, recv_sem):
        self.read, self.rows = part, rows
        self.core_in, self.mine, self.x_in, self.z_in = core_in, mine, x_in, z_in
        self.send_sem, self.recv_sem = send_sem, recv_sem
        self.seq, self.depth = seq_index(), lax.axis_index("dp")
        self.peers = half_chip_peers()

    def place(self, number, other_core):
        seq = flipped(self.seq, 2) if number >= 4 else self.seq
        seq = flipped(seq, 1) if other_core else seq
        turn = (self.depth + number % 4) % lax.axis_size("dp")
        return pl.ds(
            pl.multiple_of((turn * seq_size() + seq) * self.rows, self.rows), self.rows
        )

    def message(self, number):
        if number < 8:
            source, target, peer = self.read.at[self.place(number, True), :], self.core_in, "core"
            target = target.at[number]
        elif number < 12:
            source, target, peer = self.mine.at[number - 4], self.x_in.at[number - 8], "far"
        else:
            turn, peer = ((2, "up"), (1, "up"), (3, "down"))[number - 12]
            source, target = self.mine.at[turn], self.z_in.at[number - 12]
        return send(
            source, target, self.send_sem.at[number], self.recv_sem.at[number], self.peers[peer]
        )

    def start(self, *numbers):
        for number in numbers:
            self.message(number).start()

    def add_core(self, number):
        self.message(number).wait_recv()
        own = self.read[self.place(number, False), :].astype(F32)
        self.mine[number] = (own + self.core_in[number].astype(F32)).astype(self.mine.dtype)

    def add_x(self, number):
        self.message(8 + number).wait_recv()
        total = self.mine[number].astype(F32) + self.x_in[number].astype(F32)
        self.mine[number] = total.astype(self.mine.dtype)

    def add_up(self):
        self.message(12).wait_recv()
        total = self.mine[1].astype(F32) + self.z_in[0].astype(F32)
        self.mine[1] = total.astype(self.mine.dtype)

    def total(self):
        self.message(13).wait_recv()
        self.message(14).wait_recv()
        return (
            self.mine[0].astype(F32) + self.z_in[1].astype(F32) + self.z_in[2].astype(F32)
        )

    def sent(self):
        for number in range(SUM_MESSAGES):
            self.message(number).wait_send()


SUM_MESSAGES = 15


def finish_kernel(windows, trades, score_cols, *refs):
    stages = (trades + 1).bit_length() - 1
    refs = list(refs)

    def take(count):
        taken = refs[:count]
        del refs[:count]
        return taken

    far_inputs = take(8)
    shard_ref = take(1)[0]
    norms_ref = take(1)[0]
    second_refs = take(windows)
    grad_refs = take(windows)
    weights_ref, vectors_ref, input_ref, shard_arrived = take(4)
    loads = take(8)
    grad_loads = take(windows)
    part, core_in, mine, x_in, z_in = take(5)
    tiles, own_tiles, arrived_tiles = take(3)
    small_core, small_mine, small_x, small_z = take(4)
    kept_all = take(windows)
    stage_sent = [take(stages) for _ in range(windows)]
    stage_arrived = [take(stages) for _ in range(windows)]
    load_sem, big_send, big_recv, small_send, small_recv = take(5)
    y_send, y_recv, tile_send, tile_recv, shard_sem = take(5)
    assert not refs
    (grad_q, grad_k, grad_v, normed, grad_mid, attended, w_qkv, tokens) = loads[:8]
    tensor = lax.axis_index("tensor")
    others = [{"tensor": flipped(tensor, other + 1)} for other in range(trades)]
    shards = lax.axis_size("dp") * seq_size()
    devices = shards * (trades + 1)
    group = tiles.shape[0] // shards
    width = part.shape[1]
    cols = score_cols
    rows = width // shards

    w_source = far_inputs[6].at[:, pl.ds(0, 3 * cols)]
    sources = [*far_inputs[:6], w_source, far_inputs[7]]
    sources += [*grad_refs]
    targets = [*loads, *grad_loads]
    copies = [
        pltpu.make_async_copy(source, target, load_sem.at[at])
        for at, (source, target) in enumerate(zip(sources, targets))
    ]
    order = [4, 5, 6, 0, 1, 2, 3, 7] + list(range(8, len(copies)))
    for at in order:
        copies[at].start()

    def block_route(block):
        return SumRoute(
            part.at[block],
            rows,
            core_in.at[block],
            mine.at[block],
            x_in.at[block],
            z_in.at[block],
            big_send.at[block],
            big_recv.at[block],
        )

    routes = [block_route(block) for block in range(4)]
    small = SumRoute(
        tiles, group, small_core, small_mine, small_x, small_z, small_send, small_recv
    )
    greet(list(small.peers.values()) + others)
    everything = (6, 7, 5, 4, 2, 3, 1, 0)

    def product(block, left, right):
        total = None
        for w in range(windows):
            term = dot_tn(left[w], right[w])
            total = term if total is None else total + term
        part[block] = total.astype(BF16)

    def y_trade(w, stage):
        return send(
            stage_sent[w][stage],
            stage_arrived[w][stage],
            y_send.at[w, stage],
            y_recv.at[w, stage],
            {"tensor": flipped(tensor, (trades + 1) >> (stage + 1))},
        )

    def turn_back(w):
        total = None
        for at, grad in enumerate((grad_q, grad_k, grad_v)):
            term = dot_nt(grad[w], w_qkv[:, at * cols : (at + 1) * cols])
            total = term if total is None else total + term
        half = total.shape[0] // 2
        kept_all[w][...] = total[:half]
        stage_sent[w][0][...] = total[half:].astype(BF16)

    def fill_tiles(row, values):
        span = width // devices
        for device in range(devices):
            at = device * 8 + row
            tiles[at : at + 2, :span] = values[:, device * span : (device + 1) * span]

    def add_cores(route):
        for number in everything:
            route.add_core(number)

    def across(route):
        route.start(10, 11, 9, 8)

    def add_across(route):
        for number in (2, 3, 1, 0):
            route.add_x(number)

    count = shard_ref.shape[0] // 2
    far_rows = pl.ds(pl.multiple_of((1 - lax.axis_index("x")) * count, count), count)
    shard_trade = send(
        shard_ref.at[far_rows, :],
        shard_arrived,
        shard_sem.at[0],
        shard_sem.at[1],
        small.peers["far"],
    )
    for at in (6, 0, 1, 2):
        copies[at].wait()
    turn_back(0)
    copies[4].wait()
    copies[5].wait()
    product(3, grad_mid, attended)
    y_trade(0, 0).start()
    tiles[...] = jnp.zeros_like(tiles)
    fill_tiles(2, sum(ref[...] for ref in second_refs))
    copies[3].wait()
    routes[3].start(*everything)
    product(0, normed, grad_q)
    add_cores(routes[3])
    routes[0].start(*everything)
    across(routes[3])
    for w in range(1, windows):
        turn_back(w)
    add_cores(routes[0])
    across(routes[0])
    for w in range(1, windows):
        y_trade(w, 0).start()
    product(1, normed, grad_k)
    add_across(routes[3])
    routes[1].start(*everything)
    product(2, normed, grad_v)
    routes[3].start(12, 14)
    add_cores(routes[1])
    across(routes[1])
    for at in range(7, 8 + windows):
        copies[at].wait()
    sums = [None, None]

    def first_norm(w):
        kept = kept_all[w][...]
        for stage in range(stages):
            y_trade(w, stage).wait_recv()
            kept = kept + stage_arrived[w][stage][...].astype(F32)
            if stage + 1 < stages:
                half = kept.shape[0] // 2
                stage_sent[w][stage + 1][...] = kept[half:].astype(BF16)
                y_trade(w, stage + 1).start()
                kept = kept[:half]
        normed_rows, inv_std = normalise(tokens[w].astype(F32))
        for at, one in enumerate((kept * normed_rows, kept)):
            one = jnp.sum(one, axis=0, keepdims=True)
            sums[at] = one if sums[at] is None else sums[at] + one
        input_ref[w] = grad_loads[w][...] + norm_back(
            kept, normed_rows, inv_std, norms_ref[0:1, :]
        )

    first_norm(0)
    routes[2].start(*everything)
    add_across(routes[0])
    add_cores(routes[2])
    across(routes[2])
    shard_trade.start()
    routes[3].add_up()
    routes[0].start(12, 14)
    routes[3].start(13)
    for w in range(1, windows):
        first_norm(w)
    fill_tiles(0, jnp.concatenate(sums, axis=0))
    add_across(routes[1])
    small.start(*everything)
    routes[0].add_up()
    routes[1].start(12, 14)
    add_cores(small)
    routes[0].start(13)
    across(small)
    add_across(routes[2])
    routes[1].add_up()
    routes[2].start(12, 14)
    add_across(small)
    routes[1].start(13)
    small.start(12, 14)
    for block in (3, 0):
        weights_ref[:, block * cols : (block + 1) * cols] = routes[block].total()
    small.add_up()
    routes[2].add_up()
    small.start(13)
    weights_ref[:, cols : 2 * cols] = routes[1].total()
    routes[2].start(13)
    own_tiles[...] = small.total()

    def tile_trade(other):
        place = pl.ds(pl.multiple_of(flipped(tensor, other + 1) * 8, 8), 8)
        return send(
            own_tiles.at[place, :],
            arrived_tiles.at[other],
            tile_send.at[other],
            tile_recv.at[other],
            others[other],
        )

    weights_ref[:, 2 * cols : 3 * cols] = routes[2].total()
    for other in range(trades):
        tile_trade(other).start()
    vectors = own_tiles[pl.ds(pl.multiple_of(tensor * 8, 8), 8), :]
    for other in range(trades):
        tile_trade(other).wait_recv()
        vectors = vectors + arrived_tiles[other]
    vectors_ref[...] = vectors
    shard_trade.wait()
    for route in (*routes, small):
        route.sent()
    for w in range(windows):
        for stage in range(stages):
            y_trade(w, stage).wait_send()
    for other in range(trades):
        tile_trade(other).wait_send()


def finish(
    grads,
    normed,
    grad_mid,
    attended,
    w_att,
    tokens,
    ffn_shard,
    norms,
    second_sums,
    grad_middles,
    trades,
):
    windows, rows, cols = grads[0].shape
    width = w_att.shape[0]
    own_rows = tokens.shape[1]
    shards = lax.axis_size("dp") * seq_size()
    shard = width // shards
    group = 8 * (trades + 1)
    stages = [rows >> (stage + 1) for stage in range((trades + 1).bit_length() - 1)]
    dma = pltpu.SemaphoreType.DMA
    anywhere = pl.BlockSpec(memory_space=pl.ANY)
    vmem = pl.BlockSpec(memory_space=pltpu.VMEM)
    far_inputs = [*grads, normed, grad_mid, attended, w_att, tokens]
    kinds = (8, 8, 4, 3)

    def like(array):
        return pltpu.VMEM(array.shape, array.dtype)

    loads = [like(array) for array in far_inputs]
    loads[6] = pltpu.VMEM((width, 3 * cols), BF16)
    return run(
        functools.partial(finish_kernel, windows, trades, cols),
        "finish",
        [
            shaped((shard, 4 * cols), F32),
            shaped((8, 128), F32),
            shaped((windows, own_rows, width), F32),
            shaped((ffn_shard.shape[0] // 2, ffn_shard.shape[1]), BF16),
        ],
        8 * windows * rows * width * cols + 6 * windows * rows * width * cols,
        [*far_inputs, ffn_shard, norms, *second_sums, *grad_middles],
        collective_id=3,
        in_specs=[anywhere] * 9
        + [vmem] * (1 + windows)
        + [anywhere] * windows,
        out_specs=[vmem] * 3 + [anywhere],
        scratch_shapes=loads
        + [like(array) for array in grad_middles]
        + [pltpu.VMEM((4, width, cols), BF16)]
        + [pltpu.VMEM((4, count, shard, cols), BF16) for count in kinds]
        + [
            pltpu.VMEM((shards * group, 128), F32),
            pltpu.VMEM((group, 128), F32),
            pltpu.VMEM((trades, 8, 128), F32),
        ]
        + [pltpu.VMEM((count, group, 128), F32) for count in kinds]
        + [pltpu.VMEM((rows // 2, width), F32)] * windows
        + [pltpu.VMEM((count, width), BF16) for count in stages] * (2 * windows)
        + [
            dma((8 + windows,)),
            dma((4, SUM_MESSAGES)),
            dma((4, SUM_MESSAGES)),
            dma((SUM_MESSAGES,)),
            dma((SUM_MESSAGES,)),
            dma((windows, len(stages))),
            dma((windows, len(stages))),
            dma((trades,)),
            dma((trades,)),
            dma((2,)),
        ],
    )


def result_kernel(windows, *refs):
    out_ref = refs[-1]
    for w in range(windows):
        middle_ref, kept_ref, arrived_ref = refs[3 * w : 3 * w + 3]
        out_ref[w] = (
            middle_ref[...] + (kept_ref[...] + arrived_ref[...].astype(F32))
        ).astype(BF16)


def results(parts):
    rows, width = parts[0][0].shape
    return run(
        functools.partial(result_kernel, len(parts)),
        "results",
        shaped((len(parts), rows, width), BF16),
        2 * len(parts) * rows * width,
        [array for part in parts for array in part],
    )


def local(
    tokens,
    cotangent,
    species,
    counts,
    species_scale,
    norm1_gain,
    norm1_bias,
    w_query,
    w_key,
    w_value,
    w_out,
    norm2_gain,
    norm2_bias,
    w_gate,
    w_up,
    w_down,
):
    windows_here, own_rows, model_width = tokens.shape
    tensor_size = lax.axis_size("tensor")
    block_rows = own_rows * tensor_size
    head_cols = w_query.shape[1]
    hidden_cols = w_gate.shape[1]
    shards = ("dp", "x", "core")

    labels = lax.broadcasted_iota(jnp.int32, (windows_here, species_scale.shape[0]), 1)
    chosen = jnp.sum(jnp.where(species[:, None] == labels, species_scale[None, :], 0.0), axis=1)
    weighted = counts.astype(F32) * chosen

    lanes = jnp.zeros((8, 128), F32)
    vectors = jnp.stack([norm1_gain, norm1_bias, norm2_gain, norm2_bias])
    tile = lanes.at[:4, : vectors.shape[1]].set(vectors).at[4, :].set(jnp.sum(weighted))
    part = hidden_cols // 2
    turned = w_down.T
    first_ffn = jnp.concatenate([w_gate[:, :part], w_up[:, :part], turned[:, :part]], axis=1)
    last_ffn = jnp.concatenate([w_gate[:, part:], w_up[:, part:], turned[:, part:]], axis=1)
    upper = lax.axis_index("x") == 1

    def gather_ffn(own, across):
        pair = jnp.where(
            upper,
            jnp.concatenate([across, own], axis=0),
            jnp.concatenate([own, across], axis=0),
        )
        whole = lax.all_gather(pair, ("dp", "core"), axis=0, tiled=True)
        return whole.reshape(
            lax.axis_size("dp"), lax.axis_size("core"), lax.axis_size("x"), -1, whole.shape[1]
        )

    first_ffn = lax.all_gather(first_ffn, shards, axis=0, tiled=True)
    last_across = swap(last_ffn, "x", 1)
    w_att, norms, arrived_tokens, cosine, sine = gather(
        jnp.concatenate([w_query, w_key, w_value, w_out.T], axis=1),
        tile,
        tokens,
        tensor_size - 1,
    )
    slots = float(windows_here * lax.axis_size("dp"))

    windows = range(windows_here)
    weights = [weighted[w].reshape(1, 1) for w in windows]

    token_blocks = [tokens] + [arrived_tokens[other] for other in range(tensor_size - 1)]
    normed_rows, queries, own_kv = project(token_blocks, norms, w_att, cosine, sine)
    last_ffn = gather_ffn(last_ffn, hold(last_across, w_att))
    (
        attended,
        wide_attended,
        logs,
        kept_all,
        sent_all,
        slots_all,
        cots,
        first_middle,
        first_normed,
        first_others,
    ) = attend(queries, own_kv, w_att, cotangent, tokens, norms, tensor_size - 1)
    others = range(tensor_size - 1)
    cot_blocks = [
        [(cotangent, (w,))] + [(cots, (other, w)) for other in others] for w in windows
    ]
    middles = [first_middle]

    def reduce_ffn(partial):
        partial = partial.reshape(-1, partial.shape[-1])
        mine = lax.psum_scatter(partial, ("dp", "core"), scatter_dimension=0, tiled=True)
        count = mine.shape[0] // 2
        kept = jnp.where(upper, mine[count:], mine[:count])
        return kept, mine

    blocks = [first_normed] + [first_others[other] for other in others]
    begun, fed, lows, arrived_lows = [], [], [], []
    grad_middles, second_sums = [], []
    masks = [other + 1 for other in others]

    def through_second_norm(w, kept, arrived):
        grad_middle, low, sums = second_norm_back(
            weights[w], slots, kept, arrived, middles[w], (cotangent, (w,)), norms
        )
        grad_middles.append(grad_middle)
        second_sums.append(sums)
        return low

    for w in windows:
        begun.append(
            feed_first(blocks, cot_blocks[w], weights[w], norms, slots, first_ffn)
        )
        if w + 1 < windows_here:
            kept, arrived = scatter_pair(kept_all[w], sent_all[w], "tensor")
            middle, normed_mid = second_norm(
                (tokens, (w + 1,)), hold(kept, begun[-1]), arrived, norms
            )
            middles.append(middle)
            blocks = hold(spread(normed_mid, "tensor"), fed)
            after = normed_mid
        else:
            g_first_part, *arrived = feed_weights(
                [one[0] for one in begun],
                [one[0] for one in fed] + [one[1] for one in begun[len(fed) :]],
                0,
                [(one[4], [tensor_size // 2]) for one in fed],
            )
            first_kept, first_sent = reduce_ffn(g_first_part)
            after = g_first_part
        swaps = ()
        if w > 0:
            kept, arrived = later_pair(fed[-1][3], arrived[-1][0], "tensor")
            low = through_second_norm(w - 1, hold(kept, g_first_part), arrived)
            lows.append(low)
            swaps = [(low, masks)]
            after = low
        both, wide, *totals = hold(begun[w], after)
        ended = feed_last(both, wide, totals, last_ffn, tensor_size, swaps)
        fed.append(ended[:5])
        arrived_lows += ended[5:]
        if w + 1 < windows_here:
            blocks = hold(blocks, ended[3])
    g_ffn_part, arrived = feed_weights(
        [one[0] for one in begun],
        [one[0] for one in fed],
        1,
        [(fed[-1][4], [tensor_size // 2])],
    )
    last_kept, last_sent = reduce_ffn(g_ffn_part)
    kept, arrived = later_pair(fed[-1][3], arrived[0], "tensor")
    last_low = through_second_norm(windows[-1], hold(kept, g_ffn_part), arrived)
    grad_mid_blocks = [
        [low] + [arrived[other] for other in others] for low, arrived in zip(lows, arrived_lows)
    ] + [[last_low]]

    grad_q, grad_k, grad_v, grad_mid_rows, *arrived_results = attend_back(
        hold(queries, g_ffn_part),
        wide_attended,
        logs,
        slots_all,
        grad_mid_blocks,
        w_att,
        (cosine, sine),
        [fed[w][2] for w in windows],
    )
    parts = [
        (middles[w], *later_pair(fed[w][1], arrived_results[w], "tensor")) for w in windows
    ]

    g_att, vectors, input_grad, first_arrived = finish(
        (grad_q, grad_k, grad_v),
        normed_rows,
        grad_mid_rows,
        attended,
        w_att,
        tokens,
        first_sent,
        norms,
        second_sums,
        grad_middles,
        tensor_size - 1,
    )
    output = results(hold(parts, input_grad))
    g_first = first_kept.astype(F32) + first_arrived.astype(F32)
    last_sent = hold(last_sent, input_grad)
    count = last_sent.shape[0] // 2
    last_sent = jnp.where(upper, last_sent[:count], last_sent[count:])
    last_arrived = swap(last_sent, "x", 1)
    g_last = last_kept.astype(F32) + last_arrived.astype(F32)
    norm_sums = vectors[:4, : norm1_gain.shape[0]]
    ffn_grads = [
        jnp.concatenate(
            [g_first[:, at * part : (at + 1) * part], g_last[:, at * part : (at + 1) * part]],
            axis=1,
        )
        for at in range(3)
    ]

    return (
        output,
        input_grad,
        norm_sums[0],
        norm_sums[1],
        g_att[:, :head_cols],
        g_att[:, head_cols : 2 * head_cols],
        g_att[:, 2 * head_cols : 3 * head_cols],
        g_att[:, 3 * head_cols :].T,
        norm_sums[2],
        norm_sums[3],
        ffn_grads[0],
        ffn_grads[1],
        ffn_grads[2].T,
    )


def solution(mesh):
    depth, seq, tensor = mesh.devices.shape
    finer = jax.sharding.Mesh(
        mesh.devices.reshape(depth, seq // 2, 2, tensor), ("dp", "x", "core", "tensor")
    )
    rows = P("dp", ("x", "core", "tensor"), None)
    vector = P(("dp", "x", "core", "tensor"))
    tall = P(("dp", "x", "core"), "tensor")
    flat = P("tensor", ("dp", "x", "core"))
    return jax.shard_map(
        local,
        mesh=finer,
        in_specs=(
            rows, rows, P("dp"), P("dp"), P(), vector, vector,
            tall, tall, tall, flat, vector, vector, tall, tall, flat,
        ),
        out_specs=(
            rows, rows, vector, vector, tall, tall, tall, flat,
            vector, vector, tall, tall, flat,
        ),
        check_vma=False,
    )
```
